32 devices in a mesh: row: 4 (over y, core), col: 8 (over z, x).
Axes of the slice: x: 2, y: 2, z: 4, core: 2. Of those that a mesh axis runs over, the one named last changes fastest.
Arguments:
- inputs: bfloat16 [8192, 2048], P('row', 'col'), may hold values from -6 to 6
- prefix_len: int32 [4], P('row'), may hold values from 204 to 1024
- w_qkv: bfloat16 [2048, 16, 384], P('row', 'col'), may hold values from -0.125 to 0.125
- w_out: bfloat16 [2048, 2048], P('col', 'row'), may hold values from -1.5 to 1.5
- w_up_gate: bfloat16 [2048, 2, 8192], P('row', None, 'col'), may hold values from -0.125 to 0.125
- w_down: bfloat16 [8192, 2048], P('col', 'row'), may hold values from -0.0625 to 0.0625
- cotangent: bfloat16 [8192, 2048], P('row', 'col'), may hold values from -6 to 6
Outputs:
- outputs: bfloat16 [8192, 2048], P('row', 'col')
- input_grad: float32 [8192, 2048], P('row', 'col')
- grad_qkv: float32 [2048, 16, 384], P('row', 'col')
- grad_out: float32 [2048, 2048], P('col', 'row')
- grad_up_gate: float32 [2048, 2, 8192], P('row', None, 'col')
- grad_down: float32 [8192, 2048], P('col', 'row')
The draws below stay inside these ranges and needn't reach their ends.
Inputs may be any that keep to these rules, and one draw needn't show every extreme that they name: prefix_len gives, for each sequence, how many of its first tokens attend to each other in both directions.
All inputs are finite; a program needn't handle non-finite values.
Results may differ from the reference program's by a relative error of at most 0.014.
Values may be sent and summed in bfloat16 or wider, within the bound.
A program may use at most 192 MiB of HBM per device.

```python
import jax
import jax.numpy as jnp
from jax import lax

D = 2048
HEADS = 16
HEAD_DIM = 128
FF = 8192
SEQ = 2048
QBLOCK = 512
SEQS = 4
TOKENS = 8192


def with_ends(array, stream_key, smallest, top_value):
    longest = array.shape.index(max(array.shape))
    spots = []
    for shift in (0, 1):
        where = [jax.random.randint(jax.random.fold_in(stream_key, axis), (), 0, length) for axis, length in enumerate(array.shape)]
        where[longest] = (where[longest] + shift) % array.shape[longest]
        spots.append(tuple(where))
    return array.at[spots[0]].set(smallest).at[spots[1]].set(top_value)


def levels(rng, dims, cuts, low, top_value):
    gain, own = 1.0, jax.random.fold_in(rng, 6)
    for position, shards_of in cuts:
        draws = jnp.exp(jax.random.uniform(jax.random.fold_in(own, position), (shards_of,), jnp.float32, low / len(cuts), top_value / len(cuts)))
        gain = gain * jnp.repeat(draws, dims[position] // shards_of).reshape([-1 if axis == position else 1 for axis in range(len(dims))])
    return gain


def gaussian(own_key, shape, scale, most, shards=(), kind=jnp.bfloat16):
    drawn = scale * jax.random.normal(own_key, shape, jnp.float32)
    if shards:
        drawn = drawn * levels(own_key, shape, shards, -0.22, 0.18)
    return jnp.clip(drawn, -most, most).astype(kind)


def setup_inputs(seed: int = 0) -> dict:
    key_of = jax.random.split(jax.random.key(seed), 8)
    inputs = gaussian(key_of[0], (TOKENS, D), 1.0, 6.0, ((0, 4), (1, 8)))
    prefix_len = with_ends(jax.random.randint(key_of[1], (SEQS,), SEQ // 10, SEQ // 2 + 1), jax.random.fold_in(key_of[1], 1), SEQ // 10, (SEQ // 2 + 1) - 1).astype(jnp.int32)
    w_qkv = gaussian(key_of[2], (D, HEADS, 3 * HEAD_DIM), D ** -0.5, 0.125, ((0, 4), (1, 8)))
    w_out = gaussian(key_of[3], (D, D), (max(D // 128, 4)) ** -0.5, 1.5, ((0, 8), (1, 4)))
    w_up_gate = gaussian(key_of[4], (D, 2, FF), D ** -0.5, 0.125, ((0, 4), (2, 8)))
    w_down = gaussian(key_of[5], (FF, D), FF ** -0.5, 0.0625, ((0, 8), (1, 4)))
    cotangent = gaussian(key_of[6], (TOKENS, D), 1.0, 6.0, ((0, 4), (1, 8)))
    return {"inputs": inputs, "prefix_len": prefix_len, "w_qkv": w_qkv, "w_out": w_out, "w_up_gate": w_up_gate, "w_down": w_down, "cotangent": cotangent}


EPSILON = 1e-05
NEGATIVE = -1e+30

@jax.custom_vjp
def low(v):
    return lax.optimization_barrier(v.astype(jnp.bfloat16)).astype(jnp.float32)

@jax.custom_vjp
def low_back(v):
    return v

def low_keep(v):
    return (low(v), None)

def low_pass(kept, grad):
    return (grad,)

def back_keep(v):
    return (v, None)

def back_low(kept, grad):
    return (low(grad),)
low.defvjp(low_keep, low_pass)
low_back.defvjp(back_keep, back_low)

def matmul_high(spec, left, right):
    return jnp.einsum(spec, left, right, precision=lax.Precision.HIGHEST)

def layer_norm(values):
    center = values - lax.optimization_barrier(jnp.mean(values, axis=-1, keepdims=True))
    return center * lax.rsqrt(lax.optimization_barrier(jnp.mean(center * center, axis=-1, keepdims=True)) + EPSILON)

def rope_tables(count, head_dim):
    positions = jnp.arange(count).astype(jnp.float32)
    frequency = 10000.0 ** (-(jnp.arange(head_dim // 2).astype(jnp.float32) * 2.0 / head_dim))
    angles = positions[:, None] * frequency[None, :]
    return (jnp.cos(angles)[:, None, :], jnp.sin(angles)[:, None, :])

def rotate(values, cosine_table, sine_table):
    half_dim = values.shape[-1] // 2
    first_half = values[..., :half_dim]
    second_half = values[..., half_dim:]
    return jnp.concatenate([first_half * cosine_table - second_half * sine_table, second_half * cosine_table + first_half * sine_table], axis=-1)

def attention(query_rot, key_rot, value_rows, prefix_one):
    score_scale = HEAD_DIM ** (-0.5)
    key_pos = jnp.arange(SEQ, dtype=jnp.int32)

    def block_fn(block_index):
        first_row = block_index * QBLOCK
        query_block = lax.dynamic_slice_in_dim(query_rot, first_row, QBLOCK, 0)
        scores = low_back(matmul_high('qhe,khe->hqk', query_block, key_rot) * score_scale)
        query_pos = first_row + jnp.arange(QBLOCK, dtype=jnp.int32)
        allowed = (key_pos[None, :] <= query_pos[:, None]) | (key_pos[None, :] < prefix_one)
        scores = jnp.where(allowed[None], scores, NEGATIVE)
        row_top = lax.optimization_barrier(jnp.max(scores, axis=-1, keepdims=True))
        exp_scores = jnp.exp(scores - row_top)
        prob_rows = exp_scores / lax.optimization_barrier(jnp.sum(exp_scores, axis=-1, keepdims=True))
        return matmul_high('hqk,khe->qhe', low(prob_rows), value_rows)
    blocks = lax.map(jax.checkpoint(block_fn), jnp.arange(SEQ // QBLOCK, dtype=jnp.int32))
    return blocks.reshape(SEQ, HEADS, HEAD_DIM)

def layer(row_in, prefix_one, w_qkv, w_out, w_up_gate, w_down):
    normed_in = low(layer_norm(row_in))
    qkv_rows = low_back(matmul_high('td,dhe->the', normed_in, w_qkv))
    cosine_table, sine_table = rope_tables(SEQ, HEAD_DIM)
    query_rot = low(rotate(qkv_rows[..., :HEAD_DIM], cosine_table, sine_table))
    key_rot = low(rotate(qkv_rows[..., HEAD_DIM:2 * HEAD_DIM], cosine_table, sine_table))
    value_rows = low(qkv_rows[..., 2 * HEAD_DIM:])
    mixed_rows = attention(query_rot, key_rot, value_rows, prefix_one)
    mixed_rows = low(low_back(mixed_rows)).reshape(SEQ, HEADS * HEAD_DIM)
    branch = low_back(matmul_high('tc,cd->td', mixed_rows, w_out))
    middle = row_in + branch
    normed_mid = low(layer_norm(middle))
    gate_up = low_back(matmul_high('td,dkf->tkf', normed_mid, w_up_gate))
    hidden = low(jax.nn.silu(gate_up[:, 0]) * gate_up[:, 1])
    return middle + low_back(matmul_high('tf,fd->td', hidden, w_down))

def reference(inputs, prefix_len, w_qkv, w_out, w_up_gate, w_down, cotangent):
    weights = (w_qkv.astype(jnp.float32), w_out.astype(jnp.float32), w_up_gate.astype(jnp.float32), w_down.astype(jnp.float32))
    rows_in = inputs.astype(jnp.float32).reshape(SEQS, SEQ, D)
    cot_rows = cotangent.astype(jnp.float32).reshape(SEQS, SEQ, D)

    def scan_step(totals, packed):
        row_in, cot_one, prefix_one = packed

        def forward(row_arg, qkv_arg, out_arg, up_arg, down_arg):
            return layer(row_arg, prefix_one, qkv_arg, out_arg, up_arg, down_arg)
        result, pullback = jax.vjp(forward, row_in, weights[0], weights[1], weights[2], weights[3])
        gradients = pullback(cot_one)
        totals = (totals[0] + gradients[1], totals[1] + gradients[2], totals[2] + gradients[3], totals[3] + gradients[4])
        return (totals, (result.astype(jnp.bfloat16), gradients[0]))
    zeros_init = tuple((jnp.zeros(weight.shape, jnp.float32) for weight in weights))
    totals, (out_rows, grad_rows) = lax.scan(scan_step, zeros_init, (rows_in, cot_rows, prefix_len))
    return (out_rows.reshape(TOKENS, D), grad_rows.reshape(TOKENS, D), totals[0], totals[1], totals[2], totals[3])
```

```python
import functools

import jax
import jax.numpy as jnp
from jax import lax
from jax.experimental import pallas as pl
from jax.experimental.pallas import tpu as pltpu
from jax.sharding import Mesh
from jax.sharding import PartitionSpec as P

EPSILON = 1e-05
NEG = -1e30
F32 = jnp.float32
BF = jnp.bfloat16
NN = (((1,), (0,)), ((), ()))
NT = (((1,), (1,)), ((), ()))
TN = (((0,), (0,)), ((), ()))
def dot(a, b, dims):
    return lax.dot_general(a, b, dims, preferred_element_type=F32)

def fwd_kernel(prefix_ref, q_ref, k_ref, v_ref, o_ref, lse_ref, *, bq, bk, scale):
    i = pl.program_id(1)
    first = i * bq
    prefix = prefix_ref[0]
    q = q_ref[...]
    limit = jnp.maximum(first + bq, prefix)
    total = (limit + bk - 1) // bk
    clear = jnp.maximum(first, prefix) // bk
    def step(masked, j, carry):
        top, tot, acc = carry
        rows = pl.ds(pl.multiple_of(j * bk, bk), bk)
        s = dot(q, k_ref[rows, :], NT) * scale
        if masked:
            kp = j * bk + lax.broadcasted_iota(jnp.int32, (bq, bk), 1)
            qp = first + lax.broadcasted_iota(jnp.int32, (bq, bk), 0)
            s = jnp.where(kp < jnp.maximum(qp + 1, prefix), s, NEG)
        new = jnp.maximum(top, jnp.max(s, axis=1, keepdims=True))
        alpha = jnp.exp(top - new)
        p = jnp.exp(s - new)
        tot = tot * alpha + jnp.sum(p, axis=1, keepdims=True)
        acc = acc * alpha + dot(p.astype(BF), v_ref[rows, :], NN)
        return new, tot, acc
    carry = (jnp.full((bq, 1), NEG, F32), jnp.zeros((bq, 1), F32), jnp.zeros((bq, q.shape[1]), F32))
    carry = lax.fori_loop(0, clear, functools.partial(step, False), carry)
    top, tot, acc = lax.fori_loop(clear, total, functools.partial(step, True), carry)
    o_ref[...] = (acc / tot).astype(o_ref.dtype)
    lse = jnp.broadcast_to(top + jnp.log(tot), (bq, 128))
    lse_ref[0] = lse.T[0:8, :]

def attend_fwd(qkv, prefix, heads, *, bq=512, bk=512, hd=128):
    seq = qkv.shape[0]
    return pl.pallas_call(
        functools.partial(fwd_kernel, bq=bq, bk=bk, scale=hd ** -0.5),
        grid_spec=pltpu.PrefetchScalarGridSpec(
            num_scalar_prefetch=1, grid=(heads, seq // bq),
            in_specs=[pl.BlockSpec((bq, hd), lambda h, i, p: (i, 3 * h)),
                      pl.BlockSpec((seq, hd), lambda h, i, p: (0, 3 * h + 1)),
                      pl.BlockSpec((seq, hd), lambda h, i, p: (0, 3 * h + 2))],
            out_specs=[pl.BlockSpec((bq, hd), lambda h, i, p: (i, h)),
                       pl.BlockSpec((1, 8, bq), lambda h, i, p: (h, 0, i))]),
        out_shape=[jax.ShapeDtypeStruct((seq, heads * hd), BF), jax.ShapeDtypeStruct((heads, 8, seq), F32)],
        cost_estimate=pl.CostEstimate(flops=4 * heads * seq * seq * hd, bytes_accessed=8 * heads * seq * hd, transcendentals=heads * seq * seq),
        name="attend_forward",
    )(prefix, qkv, qkv, qkv)

def bwd_kernel(prefix_ref, qkv_ref, o_ref, do_ref, lse_ref, cos_ref, sin_ref, out_ref, dk_ref, dv_ref, delta_ref, *, bq, bk, hd, scale):
    seq = qkv_ref.shape[0]
    prefix = prefix_ref[0]
    dk_ref[...] = jnp.zeros_like(dk_ref)
    dv_ref[...] = jnp.zeros_like(dv_ref)
    def deltas(i, _):
        rows = pl.ds(pl.multiple_of(i * bq, bq), bq)
        prod = (do_ref[rows, :].astype(F32) * o_ref[rows, :].astype(F32)).T
        delta_ref[:, rows] = jnp.broadcast_to(jnp.sum(prod, axis=0, keepdims=True), (8, bq))
        return 0
    lax.fori_loop(0, seq // bq, deltas, 0)
    def unrotate(g, rows):
        cos, sin = cos_ref[rows, :], sin_ref[rows, :]
        half = hd // 2
        a, b = g[:, :half], g[:, half:]
        return jnp.concatenate([a * cos + b * sin, b * cos - a * sin], axis=1)
    def q_step(i, _):
        first = i * bq
        qrows = pl.ds(pl.multiple_of(first, bq), bq)
        q = qkv_ref[qrows, 0:hd]
        do = do_ref[qrows, :]
        lse = lse_ref[0, 0:1, qrows]
        delta = delta_ref[0:1, qrows]
        limit = jnp.maximum(first + bq, prefix)
        total = (limit + bk - 1) // bk
        clear = jnp.maximum(first, prefix) // bk
        def step(masked, j, dq):
            krows = pl.ds(pl.multiple_of(j * bk, bk), bk)
            k = qkv_ref[krows, hd:2 * hd]
            v = qkv_ref[krows, 2 * hd:3 * hd]
            s = dot(k, q, NT) * scale
            p = jnp.exp(s - lse)
            if masked:
                kp = j * bk + lax.broadcasted_iota(jnp.int32, (bk, bq), 0)
                qp = first + lax.broadcasted_iota(jnp.int32, (bk, bq), 1)
                p = jnp.where(kp < jnp.maximum(qp + 1, prefix), p, 0.0)
            dp = dot(v, do, NT)
            dv_ref[krows, :] += dot(p.astype(BF), do, NN)
            ds = (p * (dp - delta)).astype(BF)
            dk_ref[krows, :] += dot(ds, q, NN)
            return dq + dot(ds, k, TN)
        dq = lax.fori_loop(0, clear, functools.partial(step, False), jnp.zeros((bq, hd), F32))
        dq = lax.fori_loop(clear, total, functools.partial(step, True), dq)
        out_ref[qrows, 0:hd] = unrotate(dq * scale, qrows).astype(BF)
        return 0
    lax.fori_loop(0, seq // bq, q_step, 0)
    def fin(i, _):
        rows = pl.ds(pl.multiple_of(i * bq, bq), bq)
        out_ref[rows, hd:2 * hd] = unrotate(dk_ref[rows, :] * scale, rows).astype(BF)
        out_ref[rows, 2 * hd:3 * hd] = dv_ref[rows, :].astype(BF)
        return 0
    lax.fori_loop(0, seq // bq, fin, 0)

def attend_bwd(qkv, mixed, dmixed, lse, prefix, cos, sin, heads, *, bq=512, bk=512, hd=128):
    seq = qkv.shape[0]
    return pl.pallas_call(
        functools.partial(bwd_kernel, bq=bq, bk=bk, hd=hd, scale=hd ** -0.5),
        grid_spec=pltpu.PrefetchScalarGridSpec(
            num_scalar_prefetch=1, grid=(heads,),
            in_specs=[pl.BlockSpec((seq, 3 * hd), lambda h, p: (0, h)),
                      pl.BlockSpec((seq, hd), lambda h, p: (0, h)),
                      pl.BlockSpec((seq, hd), lambda h, p: (0, h)),
                      pl.BlockSpec((1, 8, seq), lambda h, p: (h, 0, 0)),
                      pl.BlockSpec((seq, hd // 2), lambda h, p: (0, 0)),
                      pl.BlockSpec((seq, hd // 2), lambda h, p: (0, 0))],
            out_specs=[pl.BlockSpec((seq, 3 * hd), lambda h, p: (0, h))],
            scratch_shapes=[pltpu.VMEM((seq, hd), F32), pltpu.VMEM((seq, hd), F32), pltpu.VMEM((8, seq), F32)]),
        out_shape=[jax.ShapeDtypeStruct((seq, heads * 3 * hd), BF)],
        cost_estimate=pl.CostEstimate(flops=10 * heads * seq * seq * hd, bytes_accessed=20 * heads * seq * hd, transcendentals=heads * seq * seq),
        name="attend_backward",
    )(prefix, qkv, mixed, dmixed, lse, cos, sin)[0]


def rope_tables(count, head_dim):
    positions = jnp.arange(count, dtype=jnp.int32).astype(F32)
    frequency = 10000.0 ** (-(jnp.arange(head_dim // 2).astype(F32) * 2.0 / head_dim))
    angles = positions[:, None] * frequency[None, :]
    return jnp.cos(angles), jnp.sin(angles)


def rotate(values, cosine, sine):
    half = values.shape[-1] // 2
    a, b = values[..., :half], values[..., half:]
    return jnp.concatenate([a * cosine - b * sine, b * cosine + a * sine], axis=-1)


def norm(values):
    center = values - jnp.mean(values, axis=-1, keepdims=True)
    inv_std = lax.rsqrt(jnp.mean(center * center, axis=-1, keepdims=True) + EPSILON)
    return center * inv_std, inv_std


def norm_back(grad, normed, inv_std):
    mean_grad = jnp.mean(grad, axis=-1, keepdims=True)
    mean_cross = jnp.mean(grad * normed, axis=-1, keepdims=True)
    return inv_std * (grad - mean_grad - normed * mean_cross)


def mm(spec, left, right):
    return jnp.einsum(spec, left, right, preferred_element_type=F32)


def local(swap, inputs, prefix_len, w_qkv, w_out, w_up_gate, w_down, cotangent):
    rows = ("rmaj", "cmin") if swap else ("rmaj", "core")
    cols = ("cmaj", "core") if swap else ("cmaj", "cmin")

    def exchange(value):
        if not swap:
            return value
        return lax.ppermute(value, ("core", "cmin"), [(0, 0), (1, 2), (2, 1), (3, 3)])

    def scatter(value):
        return lax.psum_scatter(value.astype(BF), cols, scatter_dimension=0, tiled=True).astype(F32)

    def spread(value):
        return lax.all_to_all(value, cols, 1, 0, tiled=True)

    prefix_len = exchange(prefix_len)
    inputs, cotangent = exchange(inputs), exchange(cotangent)
    w_qkv, w_out = exchange(w_qkv), exchange(w_out)
    w_up_gate, w_down = exchange(w_up_gate), exchange(w_down)
    tokens = inputs.shape[0]
    heads, head_dim = w_qkv.shape[1], w_qkv.shape[2] // 3
    hidden_width = w_down.shape[0]
    full_in = lax.all_gather(inputs, cols, axis=1, tiled=True)
    width = full_in.shape[1]
    qkv_all = lax.all_gather(w_qkv, rows, axis=0, tiled=True).reshape(width, heads * 3 * head_dim)
    out_all = lax.all_gather(w_out, rows, axis=1, tiled=True)
    up_all = lax.all_gather(w_up_gate, rows, axis=0, tiled=True).reshape(width, 2 * hidden_width)
    down_all = lax.all_gather(w_down, rows, axis=1, tiled=True)
    cot_full = lax.all_gather(cotangent, cols, axis=1, tiled=True)
    piece = tokens // lax.axis_size(cols)
    first = lax.axis_index(cols) * piece
    own_in = lax.dynamic_slice_in_dim(full_in, first, piece, 0).astype(F32)
    own_cot = lax.dynamic_slice_in_dim(cot_full, first, piece, 0).astype(F32)

    normed_in = norm(full_in.astype(F32))[0].astype(BF)
    qkv_rows = mm("td,de->te", normed_in, qkv_all).reshape(tokens, heads, 3, head_dim)
    cosine, sine = rope_tables(tokens, head_dim)
    turned = rotate(qkv_rows[:, :, :2], cosine[:, None, None], sine[:, None, None])
    qkv = jnp.concatenate([turned, qkv_rows[:, :, 2:]], axis=2).astype(BF)
    qkv = qkv.reshape(tokens, heads * 3 * head_dim)
    mixed, lse = attend_fwd(qkv, prefix_len, heads, hd=head_dim)
    middle = own_in + scatter(mm("tc,cd->td", mixed, out_all))
    normed_two, inv_two = norm(middle)
    normed_mid = lax.all_gather(normed_two.astype(BF), cols, axis=0, tiled=True)
    gate_up = mm("td,df->tf", normed_mid, up_all)
    gate, up = gate_up[:, :hidden_width], gate_up[:, hidden_width:]
    sig = jax.nn.sigmoid(gate)
    active = gate * sig
    hidden = (active * up).astype(BF)
    outputs = middle + scatter(mm("tf,fd->td", hidden, down_all))
    outputs = exchange(spread(outputs.astype(BF)))

    grad_hidden = mm("td,fd->tf", cot_full, down_all)
    grad_gate = grad_hidden * up * sig * (1.0 + gate * (1.0 - sig))
    grad_gate_up = jnp.concatenate([grad_gate, grad_hidden * active], axis=1).astype(BF)
    grad_down = mm("tf,td->fd", hidden, cot_full).astype(BF)
    grad_down = lax.psum_scatter(grad_down, rows, scatter_dimension=1, tiled=True)
    grad_up = mm("td,tf->df", normed_mid, grad_gate_up).astype(BF)
    grad_up = lax.psum_scatter(grad_up, rows, scatter_dimension=0, tiled=True)
    grad_normed = scatter(mm("tf,df->td", grad_gate_up, up_all))
    grad_middle = own_cot + norm_back(grad_normed, normed_two, inv_two)
    grad_branch = lax.all_gather(grad_middle.astype(BF), cols, axis=0, tiled=True)
    grad_out = mm("tc,td->cd", mixed, grad_branch).astype(BF)
    grad_out = lax.psum_scatter(grad_out, rows, scatter_dimension=1, tiled=True)
    grad_mixed = mm("td,cd->tc", grad_branch, out_all).astype(BF)
    grad_rows = attend_bwd(qkv, mixed, grad_mixed, lse, prefix_len, cosine, sine, heads, hd=head_dim)
    grad_in = scatter(mm("te,de->td", grad_rows, qkv_all))
    grad_qkv = mm("td,te->de", normed_in, grad_rows).astype(BF)
    grad_qkv = lax.psum_scatter(grad_qkv, rows, scatter_dimension=0, tiled=True)
    normed_own, inv_own = norm(own_in)
    input_grad = grad_middle + norm_back(grad_in, normed_own, inv_own)
    input_grad = exchange(spread(input_grad.astype(BF))).astype(F32)
    return (
        outputs,
        input_grad,
        exchange(grad_qkv).astype(F32).reshape(-1, heads, 3 * head_dim),
        exchange(grad_out).astype(F32),
        exchange(grad_up).astype(F32).reshape(-1, 2, hidden_width),
        exchange(grad_down).astype(F32),
    )


def solution(mesh):
    row_size, col_size = mesh.shape["row"], mesh.shape["col"]
    col_major = 4
    shape = (row_size // 2, 2, col_major, col_size // col_major)
    fine = Mesh(mesh.devices.reshape(shape), ("rmaj", "core", "cmaj", "cmin"))
    row, col = ("rmaj", "core"), ("cmaj", "cmin")
    outs = (P(row, col), P(row, col), P(row, col, None), P(col, row), P(row, None, col), P(col, row))
    return jax.shard_map(
        functools.partial(local, shape[3] == 2),
        mesh=fine,
        in_specs=(P(row, col), P(row), P(row, col, None), P(col, row), P(row, None, col), P(col, row), P(row, col)),
        out_specs=outs,
        check_vma=False,
    )
```

```python
import functools

import jax
import jax.numpy as jnp
from jax import lax
from jax.experimental import pallas as pl
from jax.experimental.pallas import tpu as pltpu
from jax.sharding import Mesh
from jax.sharding import PartitionSpec as P

EPSILON = 1e-05
NEG = -1e30
F32 = jnp.float32
BF = jnp.bfloat16
NN = (((1,), (0,)), ((), ()))
NT = (((1,), (1,)), ((), ()))
TN = (((0,), (0,)), ((), ()))
def dot(a, b, dims):
    return lax.dot_general(a, b, dims, preferred_element_type=F32)

def fwd_kernel(prefix_ref, q_ref, k_ref, v_ref, o_ref, lse_ref, *, bq, bk, scale):
    i = pl.program_id(1)
    first = i * bq
    prefix = prefix_ref[0]
    q = q_ref[...]
    limit = jnp.maximum(first + bq, prefix)
    total = (limit + bk - 1) // bk
    clear = jnp.maximum(first, prefix) // bk
    def step(masked, j, carry):
        top, tot, acc = carry
        rows = pl.ds(pl.multiple_of(j * bk, bk), bk)
        s = dot(q, k_ref[rows, :], NT) * scale
        if masked:
            kp = j * bk + lax.broadcasted_iota(jnp.int32, (bq, bk), 1)
            qp = first + lax.broadcasted_iota(jnp.int32, (bq, bk), 0)
            s = jnp.where(kp < jnp.maximum(qp + 1, prefix), s, NEG)
        new = jnp.maximum(top, jnp.max(s, axis=1, keepdims=True))
        alpha = jnp.exp(top - new)
        p = jnp.exp(s - new)
        tot = tot * alpha + jnp.sum(p, axis=1, keepdims=True)
        acc = acc * alpha + dot(p.astype(BF), v_ref[rows, :], NN)
        return new, tot, acc
    carry = (jnp.full((bq, 1), NEG, F32), jnp.zeros((bq, 1), F32), jnp.zeros((bq, q.shape[1]), F32))
    carry = lax.fori_loop(0, clear, functools.partial(step, False), carry)
    top, tot, acc = lax.fori_loop(clear, total, functools.partial(step, True), carry)
    o_ref[...] = (acc / tot).astype(o_ref.dtype)
    lse = jnp.broadcast_to(top + jnp.log(tot), (bq, 128))
    lse_ref[0] = lse.T[0:8, :]

def attend_fwd(qkv, prefix, heads, *, bq=512, bk=512, hd=128):
    seq = qkv.shape[0]
    return pl.pallas_call(
        functools.partial(fwd_kernel, bq=bq, bk=bk, scale=hd ** -0.5),
        grid_spec=pltpu.PrefetchScalarGridSpec(
            num_scalar_prefetch=1, grid=(heads, seq // bq),
            in_specs=[pl.BlockSpec((bq, hd), lambda h, i, p: (i, 3 * h)),
                      pl.BlockSpec((seq, hd), lambda h, i, p: (0, 3 * h + 1)),
                      pl.BlockSpec((seq, hd), lambda h, i, p: (0, 3 * h + 2))],
            out_specs=[pl.BlockSpec((bq, hd), lambda h, i, p: (i, h)),
                       pl.BlockSpec((1, 8, bq), lambda h, i, p: (h, 0, i))]),
        out_shape=[jax.ShapeDtypeStruct((seq, heads * hd), BF), jax.ShapeDtypeStruct((heads, 8, seq), F32)],
        cost_estimate=pl.CostEstimate(flops=4 * heads * seq * seq * hd, bytes_accessed=8 * heads * seq * hd, transcendentals=heads * seq * seq),
        name="attend_forward",
    )(prefix, qkv, qkv, qkv)

def bwd_kernel(prefix_ref, qkv_ref, o_ref, do_ref, lse_ref, cos_ref, sin_ref, out_ref, dk_ref, dv_ref, delta_ref, *, bq, bk, hd, scale):
    seq = qkv_ref.shape[0]
    prefix = prefix_ref[0]
    dk_ref[...] = jnp.zeros_like(dk_ref)
    dv_ref[...] = jnp.zeros_like(dv_ref)
    def deltas(i, _):
        rows = pl.ds(pl.multiple_of(i * bq, bq), bq)
        prod = (do_ref[rows, :].astype(F32) * o_ref[rows, :].astype(F32)).T
        delta_ref[:, rows] = jnp.broadcast_to(jnp.sum(prod, axis=0, keepdims=True), (8, bq))
        return 0
    lax.fori_loop(0, seq // bq, deltas, 0)
    def unrotate(g, rows):
        cos, sin = cos_ref[rows, :], sin_ref[rows, :]
        half = hd // 2
        a, b = g[:, :half], g[:, half:]
        return jnp.concatenate([a * cos + b * sin, b * cos - a * sin], axis=1)
    def q_step(i, _):
        first = i * bq
        qrows = pl.ds(pl.multiple_of(first, bq), bq)
        q = qkv_ref[qrows, 0:hd]
        do = do_ref[qrows, :]
        lse = lse_ref[0, 0:1, qrows]
        delta = delta_ref[0:1, qrows]
        limit = jnp.maximum(first + bq, prefix)
        total = (limit + bk - 1) // bk
        clear = jnp.maximum(first, prefix) // bk
        def step(masked, j, dq):
            krows = pl.ds(pl.multiple_of(j * bk, bk), bk)
            k = qkv_ref[krows, hd:2 * hd]
            v = qkv_ref[krows, 2 * hd:3 * hd]
            s = dot(k, q, NT) * scale
            p = jnp.exp(s - lse)
            if masked:
                kp = j * bk + lax.broadcasted_iota(jnp.int32, (bk, bq), 0)
                qp = first + lax.broadcasted_iota(jnp.int32, (bk, bq), 1)
                p = jnp.where(kp < jnp.maximum(qp + 1, prefix), p, 0.0)
            dp = dot(v, do, NT)
            dv_ref[krows, :] += dot(p.astype(BF), do, NN)
            ds = (p * (dp - delta)).astype(BF)
            dk_ref[krows, :] += dot(ds, q, NN)
            return dq + dot(ds, k, TN)
        dq = lax.fori_loop(0, clear, functools.partial(step, False), jnp.zeros((bq, hd), F32))
        dq = lax.fori_loop(clear, total, functools.partial(step, True), dq)
        out_ref[qrows, 0:hd] = unrotate(dq * scale, qrows).astype(BF)
        return 0
    lax.fori_loop(0, seq // bq, q_step, 0)
    def fin(i, _):
        rows = pl.ds(pl.multiple_of(i * bq, bq), bq)
        out_ref[rows, hd:2 * hd] = unrotate(dk_ref[rows, :] * scale, rows).astype(BF)
        out_ref[rows, 2 * hd:3 * hd] = dv_ref[rows, :].astype(BF)
        return 0
    lax.fori_loop(0, seq // bq, fin, 0)

def attend_bwd(qkv, mixed, dmixed, lse, prefix, cos, sin, heads, *, bq=512, bk=512, hd=128):
    seq = qkv.shape[0]
    return pl.pallas_call(
        functools.partial(bwd_kernel, bq=bq, bk=bk, hd=hd, scale=hd ** -0.5),
        grid_spec=pltpu.PrefetchScalarGridSpec(
            num_scalar_prefetch=1, grid=(heads,),
            in_specs=[pl.BlockSpec((seq, 3 * hd), lambda h, p: (0, h)),
                      pl.BlockSpec((seq, hd), lambda h, p: (0, h)),
                      pl.BlockSpec((seq, hd), lambda h, p: (0, h)),
                      pl.BlockSpec((1, 8, seq), lambda h, p: (h, 0, 0)),
                      pl.BlockSpec((seq, hd // 2), lambda h, p: (0, 0)),
                      pl.BlockSpec((seq, hd // 2), lambda h, p: (0, 0))],
            out_specs=[pl.BlockSpec((seq, 3 * hd), lambda h, p: (0, h))],
            scratch_shapes=[pltpu.VMEM((seq, hd), F32), pltpu.VMEM((seq, hd), F32), pltpu.VMEM((8, seq), F32)]),
        out_shape=[jax.ShapeDtypeStruct((seq, heads * 3 * hd), BF)],
        cost_estimate=pl.CostEstimate(flops=10 * heads * seq * seq * hd, bytes_accessed=20 * heads * seq * hd, transcendentals=heads * seq * seq),
        name="attend_backward",
    )(prefix, qkv, mixed, dmixed, lse, cos, sin)[0]


def rope_tables(count, head_dim):
    positions = jnp.arange(count, dtype=jnp.int32).astype(F32)
    frequency = 10000.0 ** (-(jnp.arange(head_dim // 2).astype(F32) * 2.0 / head_dim))
    angles = positions[:, None] * frequency[None, :]
    return jnp.cos(angles), jnp.sin(angles)


def rotate(values, cosine, sine):
    half = values.shape[-1] // 2
    a, b = values[..., :half], values[..., half:]
    return jnp.concatenate([a * cosine - b * sine, b * cosine + a * sine], axis=-1)


def norm(values):
    center = values - jnp.mean(values, axis=-1, keepdims=True)
    inv_std = lax.rsqrt(jnp.mean(center * center, axis=-1, keepdims=True) + EPSILON)
    return center * inv_std, inv_std


def norm_back(grad, normed, inv_std):
    mean_grad = jnp.mean(grad, axis=-1, keepdims=True)
    mean_cross = jnp.mean(grad * normed, axis=-1, keepdims=True)
    return inv_std * (grad - mean_grad - normed * mean_cross)


def mm(spec, left, right):
    return jnp.einsum(spec, left, right, preferred_element_type=F32)


def local(swap, inputs, prefix_len, w_qkv, w_out, w_up_gate, w_down, cotangent):
    rows = ("rmaj", "cmin") if swap else ("rmaj", "core")
    cols = ("cmaj", "core") if swap else ("cmaj", "cmin")

    def exchange(value):
        if not swap:
            return value
        return lax.ppermute(value, ("core", "cmin"), [(0, 0), (1, 2), (2, 1), (3, 3)])

    def scatter(value):
        return lax.psum_scatter(value.astype(BF), cols, scatter_dimension=0, tiled=True).astype(F32)

    def spread(value):
        return lax.all_to_all(value, cols, 1, 0, tiled=True)

    prefix_len = exchange(prefix_len)
    inputs, cotangent = exchange(inputs), exchange(cotangent)
    w_qkv, w_out = exchange(w_qkv), exchange(w_out)
    w_up_gate, w_down = exchange(w_up_gate), exchange(w_down)
    tokens = inputs.shape[0]
    heads, head_dim = w_qkv.shape[1], w_qkv.shape[2] // 3
    hidden_width = w_down.shape[0]
    full_in = lax.all_gather(inputs, cols, axis=1, tiled=True)
    width = full_in.shape[1]
    qkv_all = lax.all_gather(w_qkv, rows, axis=0, tiled=True).reshape(width, heads * 3 * head_dim)
    out_all = lax.all_gather(w_out, rows, axis=1, tiled=True)
    up_all = lax.all_gather(w_up_gate, rows, axis=0, tiled=True).reshape(width, 2 * hidden_width)
    down_all = lax.all_gather(w_down, rows, axis=1, tiled=True)
    cot_full = lax.all_gather(cotangent, cols, axis=1, tiled=True)
    piece = tokens // lax.axis_size(cols)
    first = lax.axis_index(cols) * piece
    own_in = lax.dynamic_slice_in_dim(full_in, first, piece, 0).astype(F32)
    own_cot = lax.dynamic_slice_in_dim(cot_full, first, piece, 0).astype(F32)

    normed_in = norm(full_in.astype(F32))[0].astype(BF)
    qkv_rows = mm("td,de->te", normed_in, qkv_all).reshape(tokens, heads, 3, head_dim)
    cosine, sine = rope_tables(tokens, head_dim)
    turned = rotate(qkv_rows[:, :, :2], cosine[:, None, None], sine[:, None, None])
    qkv = jnp.concatenate([turned, qkv_rows[:, :, 2:]], axis=2).astype(BF)
    qkv = qkv.reshape(tokens, heads * 3 * head_dim)
    mixed, lse = attend_fwd(qkv, prefix_len, heads, hd=head_dim)
    middle = own_in + scatter(mm("tc,cd->td", mixed, out_all))
    normed_two, inv_two = norm(middle)
    normed_mid = lax.all_gather(normed_two.astype(BF), cols, axis=0, tiled=True)
    gate_up = mm("td,df->tf", normed_mid, up_all)
    gate, up = gate_up[:, :hidden_width], gate_up[:, hidden_width:]
    sig = jax.nn.sigmoid(gate)
    active = gate * sig
    hidden = (active * up).astype(BF)
    outputs = middle + scatter(mm("tf,fd->td", hidden, down_all))
    outputs = exchange(spread(outputs.astype(BF)))

    grad_hidden = mm("td,fd->tf", cot_full, down_all)
    grad_gate = grad_hidden * up * sig * (1.0 + gate * (1.0 - sig))
    grad_gate_up = jnp.concatenate([grad_gate, grad_hidden * active], axis=1).astype(BF)
    grad_down = mm("tf,td->fd", hidden, cot_full).astype(BF)
    grad_down = lax.psum_scatter(grad_down, rows, scatter_dimension=1, tiled=True)
    grad_up = mm("td,tf->df", normed_mid, grad_gate_up).astype(BF)
    grad_up = lax.psum_scatter(grad_up, rows, scatter_dimension=0, tiled=True)
    grad_normed = scatter(mm("tf,df->td", grad_gate_up, up_all))
    grad_middle = own_cot + norm_back(grad_normed, normed_two, inv_two)
    grad_branch = lax.all_gather(grad_middle.astype(BF), cols, axis=0, tiled=True)
    grad_out = mm("tc,td->cd", mixed, grad_branch).astype(BF)
    grad_out = lax.psum_scatter(grad_out, rows, scatter_dimension=1, tiled=True)
    grad_mixed = mm("td,cd->tc", grad_branch, out_all).astype(BF)
    grad_rows = attend_bwd(qkv, mixed, grad_mixed, lse, prefix_len, cosine, sine, heads, hd=head_dim)
    grad_in = scatter(mm("te,de->td", grad_rows, qkv_all))
    grad_qkv = mm("td,te->de", normed_in, grad_rows).astype(BF)
    grad_qkv = lax.psum_scatter(grad_qkv, rows, scatter_dimension=0, tiled=True)
    normed_own, inv_own = norm(own_in)
    input_grad = grad_middle + norm_back(grad_in, normed_own, inv_own)
    input_grad = exchange(spread(input_grad.astype(BF))).astype(F32)
    return (
        outputs,
        input_grad,
        exchange(grad_qkv).astype(F32).reshape(-1, heads, 3 * head_dim),
        exchange(grad_out).astype(F32),
        exchange(grad_up).astype(F32).reshape(-1, 2, hidden_width),
        exchange(grad_down).astype(F32),
    )


AXES = ("y", "core", "zh", "zl", "x")
GROUP = ("core", "zl", "x")
MESH = pl.DeviceIdType.MESH


def place():
    y, c, zh, zl, x = (lax.axis_index(name) for name in AXES)
    sibling = (y, 1 - c, zh, zl, x)

    def peer(dz, dx):
        return (y, c, zh, lax.rem(zl + dz, 2), lax.rem(x + dx, 2))

    def chip(dz, dx):
        return lax.rem(zl + dz, 2) * 2 + lax.rem(x + dx, 2)

    order = [2 * y + zh, 2 * y + 1 - zh, 2 * (1 - y) + zh, 2 * (1 - y) + 1 - zh]
    return c, sibling, peer, chip, order


def meet(devices):
    barrier = pltpu.get_barrier_semaphore()
    for device in devices:
        pl.semaphore_signal(barrier, inc=1, device_id=device, device_id_type=MESH)
    pl.semaphore_wait(barrier, len(devices))


def span(start, size):
    return pl.ds(pl.multiple_of(start, size), size)


def remote(src, dst, send_sem, recv_sem, device):
    return pltpu.make_async_remote_copy(
        src_ref=src, dst_ref=dst, send_sem=send_sem, recv_sem=recv_sem, device_id=device, device_id_type=MESH
    )


def each_rows(count, body, size=32):
    def step(i, carry):
        body(span(i * size, size))
        return carry

    lax.fori_loop(0, count // size, step, 0)


def row_norm(values):
    center = values - jnp.mean(values, axis=-1, keepdims=True)
    inv_std = lax.rsqrt(jnp.mean(center * center, axis=-1, keepdims=True) + EPSILON)
    return center * inv_std, inv_std


def reduce_kernel(kind, transposed, a_ref, w0, w1, w2, w3, *refs):
    if kind == "mid":
        base_ref, total_ref, norm_ref = refs[:3]
        rest = refs[3:]
    elif kind == "out":
        base_ref, result_ref = refs[:2]
        rest = refs[2:]
    elif kind == "back":
        base_ref, value_ref, total_ref, result_ref = refs[:4]
        rest = refs[4:]
    else:
        base_ref, value_ref, result_ref = refs[:3]
        rest = refs[3:]
    (sib_out, sib_in, own, diag_out, diag_in, near_out, near_in,
     sib_send, sib_recv, diag_send, diag_recv, near_send, near_recv) = rest
    piece = own.shape[1]
    half = piece // 2
    c, sibling, peer, chip, order = place()
    across, along = peer(0, 1), peer(1, 0)
    meet([sibling, across, along])
    weights = (w0, w1, w2, w3)
    block = weights[0].shape[0] if transposed else weights[0].shape[1]

    def compute(owner, out_ref):
        left = a_ref[span(owner * piece, piece), :]
        for weight, index in zip(weights, order):
            part = dot(left, weight[...], NT if transposed else NN)
            out_ref[:, span(index * block, block)] = part.astype(out_ref.dtype)

    def sib_copy(step):
        return remote(sib_out.at[step], sib_in.at[step], sib_send.at[step], sib_recv.at[step], sibling)

    def diag_copy(part):
        return remote(
            diag_out.at[pl.ds(part * half, half)], diag_in.at[part], diag_send.at[part], diag_recv.at[part],
            across if part == 0 else along,
        )

    def near_copy(part):
        return remote(
            near_out.at[part], near_in.at[part], near_send.at[part], near_recv.at[part], across if part == 0 else along
        )

    def step(s, carry):
        target = chip(1 - lax.rem(s, 2), 1 - s // 2)
        compute((1 - c) * 4 + target, sib_out.at[s])
        sib_copy(s).start()

        @pl.when(s == 1)
        def _():
            finish_diag()

        @pl.when(s == 2)
        def _():
            finish_near(0)

        @pl.when(s == 3)
        def _():
            finish_near(1)

        compute(c * 4 + target, own.at[lax.rem(s, 2)])
        return carry

    def finish_diag():
        sib_copy(0).wait_recv()

        def body(rows):
            diag_out[rows, :] = (own[0, rows, :] + sib_in[0, rows, :].astype(F32)).astype(BF)

        each_rows(piece, body)
        diag_copy(0).start()
        diag_copy(1).start()

    def finish_near(part):
        step_index = part + 1
        slot = step_index % 2
        sib_copy(step_index).wait_recv()
        source = 1 - part
        diag_copy(source).wait_recv()
        low = source * half

        def plain(i, carry):
            rows = span((1 - source) * half + i * 32, 32)
            near_out[part, rows, :] = (own[slot, rows, :] + sib_in[step_index, rows, :].astype(F32)).astype(BF)
            return carry

        def added(i, carry):
            rows = span(low + i * 32, 32)
            total = own[slot, rows, :] + sib_in[step_index, rows, :].astype(F32)
            near_out[part, rows, :] = (total + diag_in[source, span(i * 32, 32), :].astype(F32)).astype(BF)
            return carry

        lax.fori_loop(0, half // 32, plain, 0)
        lax.fori_loop(0, half // 32, added, 0)
        near_copy(part).start()

    lax.fori_loop(0, 4, step, 0)
    sib_copy(3).wait_recv()
    near_copy(0).wait_recv()
    near_copy(1).wait_recv()

    def last(rows):
        total = own[1, rows, :] + sib_in[3, rows, :].astype(F32)
        total = total + near_in[0, rows, :].astype(F32) + near_in[1, rows, :].astype(F32)
        if kind == "mid":
            middle = base_ref[rows, :].astype(F32) + total
            total_ref[rows, :] = middle
            norm_ref[rows, :] = row_norm(middle)[0].astype(BF)
        elif kind == "out":
            result_ref[rows, :] = (base_ref[rows, :] + total).astype(BF)
        else:
            normed, inv_std = row_norm(value_ref[rows, :].astype(F32))
            mean_grad = jnp.mean(total, axis=-1, keepdims=True)
            mean_cross = jnp.mean(total * normed, axis=-1, keepdims=True)
            grad = base_ref[rows, :].astype(F32) + inv_std * (total - mean_grad - normed * mean_cross)
            if kind == "back":
                total_ref[rows, :] = grad
            result_ref[rows, :] = grad.astype(BF)

    each_rows(piece, last, 16)
    for s in range(4):
        sib_copy(s).wait_send()
    for part in range(2):
        diag_copy(part).wait_send()
        near_copy(part).wait_send()


VMEM_WHOLE = pl.BlockSpec(memory_space=pltpu.VMEM)


def reduce_call(kind, transposed, left, weights, extras, ident):
    piece, width = extras[0].shape
    steps = 4
    shape = functools.partial(jax.ShapeDtypeStruct, (piece, width))
    outs = {"mid": [shape(F32), shape(BF)], "out": [shape(BF)], "back": [shape(F32), shape(BF)], "end": [shape(BF)]}[kind]
    tokens, depth = left.shape
    dma = pltpu.SemaphoreType.DMA
    return pl.pallas_call(
        functools.partial(reduce_kernel, kind, transposed),
        out_shape=outs,
        in_specs=[VMEM_WHOLE] * (5 + len(extras)),
        out_specs=[VMEM_WHOLE] * len(outs),
        scratch_shapes=[
            pltpu.VMEM((steps, piece, width), BF),
            pltpu.VMEM((steps, piece, width), BF),
            pltpu.VMEM((2, piece, width), F32),
            pltpu.VMEM((piece, width), BF),
            pltpu.VMEM((2, piece // 2, width), BF),
            pltpu.VMEM((2, piece, width), BF),
            pltpu.VMEM((2, piece, width), BF),
            dma((steps,)), dma((steps,)), dma((2,)), dma((2,)), dma((2,)), dma((2,)),
        ],
        compiler_params=pltpu.CompilerParams(
            collective_id=ident, has_side_effects=True, vmem_limit_bytes=60 << 20
        ),
        cost_estimate=pl.CostEstimate(
            flops=2 * tokens * depth * width + (20 << 30), bytes_accessed=4 * tokens * width, transcendentals=0
        ),
        name="reduce_" + kind,
    )(left, *weights, *extras)


def gather_body(own_ref, full, sems, process):
    near_send, near_recv, diag_send, diag_recv, sib_send, sib_recv = sems
    piece = own_ref.shape[0]
    half = piece // 2
    c, sibling, peer, chip, order = place()
    across, along = peer(0, 1), peer(1, 0)
    meet([sibling, across, along])
    mine = chip(0, 0)

    def rows_of(core, target):
        return span((core * 4 + target) * piece, piece)

    def near_copy(part, target):
        rows = rows_of(c, target)
        return remote(full.at[rows], full.at[rows], near_send.at[part], near_recv.at[part], across if part == 0 else along)

    def diag_copy(part, target):
        rows = span((c * 4 + target) * piece + part * half, half)
        return remote(full.at[rows], full.at[rows], diag_send.at[part], diag_recv.at[part], along if part == 0 else across)

    def sib_copy(slot, core, target):
        rows = rows_of(core, target)
        return remote(full.at[rows], full.at[rows], sib_send.at[slot], sib_recv.at[slot], sibling)

    full[rows_of(c, mine), :] = own_ref[...]
    near_copy(0, mine).start()
    near_copy(1, mine).start()
    sib_copy(0, c, mine).start()
    process(c * 4 + mine)
    sib_copy(0, 1 - c, mine).wait_recv()
    process((1 - c) * 4 + mine)
    x_chip, z_chip, d_chip = chip(0, 1), chip(1, 0), chip(1, 1)
    near_copy(0, x_chip).wait_recv()
    diag_copy(0, x_chip).start()
    sib_copy(1, c, x_chip).start()
    near_copy(1, z_chip).wait_recv()
    diag_copy(1, z_chip).start()
    sib_copy(2, c, z_chip).start()
    process(c * 4 + x_chip)
    process(c * 4 + z_chip)
    sib_copy(1, 1 - c, x_chip).wait_recv()
    process((1 - c) * 4 + x_chip)
    diag_copy(0, d_chip).wait_recv()
    diag_copy(1, d_chip).wait_recv()
    sib_copy(3, c, d_chip).start()
    sib_copy(2, 1 - c, z_chip).wait_recv()
    process((1 - c) * 4 + z_chip)
    process(c * 4 + d_chip)
    sib_copy(3, 1 - c, d_chip).wait_recv()
    process((1 - c) * 4 + d_chip)
    near_copy(0, mine).wait_send()
    near_copy(1, mine).wait_send()
    diag_copy(0, x_chip).wait_send()
    diag_copy(1, z_chip).wait_send()
    for slot in range(4):
        sib_copy(slot, c, mine).wait_send()


def gather_sems():
    dma = pltpu.SemaphoreType.DMA
    return [dma((2,)), dma((2,)), dma((2,)), dma((2,)), dma((4,)), dma((4,))]


def feed_kernel(own_ref, cot_ref, u0, u1, u2, u3, d0, d1, d2, d3, full, hidden_ref, grad_ref, *sems):
    piece = own_ref.shape[0]
    order = place()[4]
    block = u0.shape[0]
    width = hidden_ref.shape[1]
    tile = 256

    def process(owner):
        rows = span(owner * piece, piece)

        def tile_step(t, carry):
            cols, up_cols = span(t * tile, tile), span(width + t * tile, tile)
            gate = up = grad = None
            for u_ref, d_ref, index in zip((u0, u1, u2, u3), (d0, d1, d2, d3), order):
                deep = span(index * block, block)
                normed = full[rows, deep]
                terms = (
                    dot(normed, u_ref[:, cols], NN),
                    dot(normed, u_ref[:, up_cols], NN),
                    dot(cot_ref[rows, deep], d_ref[cols, :], NT),
                )
                gate, up, grad = terms if gate is None else (gate + terms[0], up + terms[1], grad + terms[2])
            sig = 1.0 / (1.0 + jnp.exp(-gate))
            active = gate * sig
            hidden_ref[rows, cols] = (active * up).astype(BF)
            grad_ref[rows, cols] = (grad * up * sig * (1.0 + gate * (1.0 - sig))).astype(BF)
            grad_ref[rows, up_cols] = (grad * active).astype(BF)
            return carry

        lax.fori_loop(0, width // tile, tile_step, 0)

    gather_body(own_ref, full, sems, process)


def feed_call(own, cot, ups, downs, ident):
    tokens, width = cot.shape
    hidden = downs[0].shape[0]
    return pl.pallas_call(
        feed_kernel,
        out_shape=[
            jax.ShapeDtypeStruct((tokens, width), BF),
            jax.ShapeDtypeStruct((tokens, hidden), BF),
            jax.ShapeDtypeStruct((tokens, 2 * hidden), BF),
        ],
        in_specs=[VMEM_WHOLE] * 10,
        out_specs=[VMEM_WHOLE] * 3,
        scratch_shapes=gather_sems(),
        compiler_params=pltpu.CompilerParams(collective_id=ident, has_side_effects=True, vmem_limit_bytes=60 << 20),
        cost_estimate=pl.CostEstimate(
            flops=6 * tokens * hidden * width + (20 << 30), bytes_accessed=8 * tokens * width, transcendentals=tokens * hidden
        ),
        name="gather_feed",
    )(own, cot, *ups, *downs)


def mix_kernel(own_ref, w0, w1, w2, w3, full, mixed_ref, *sems):
    piece = own_ref.shape[0]
    order = place()[4]
    block = w0.shape[1]

    def process(owner):
        rows = span(owner * piece, piece)
        total = None
        for weight, index in zip((w0, w1, w2, w3), order):
            part = dot(full[rows, span(index * block, block)], weight[...], NT)
            total = part if total is None else total + part
        mixed_ref[rows, :] = total.astype(BF)

    gather_body(own_ref, full, sems, process)


def mix_call(own, weights, tokens, ident):
    width = own.shape[1]
    inner = weights[0].shape[0]
    return pl.pallas_call(
        mix_kernel,
        out_shape=[jax.ShapeDtypeStruct((tokens, width), BF), jax.ShapeDtypeStruct((tokens, inner), BF)],
        in_specs=[VMEM_WHOLE] * 5,
        out_specs=[VMEM_WHOLE] * 2,
        scratch_shapes=gather_sems(),
        compiler_params=pltpu.CompilerParams(collective_id=ident, has_side_effects=True, vmem_limit_bytes=60 << 20),
        cost_estimate=pl.CostEstimate(
            flops=2 * tokens * inner * width + (20 << 30), bytes_accessed=4 * tokens * width, transcendentals=0
        ),
        name="gather_mix",
    )(own, *weights)


def swapped(value, flip=0):
    pairs = (
        [(0, 0), (1, 2), (2, 1), (3, 3)],
        [(0, 1), (1, 3), (2, 0), (3, 2)],
        [(1, 0), (3, 1), (0, 2), (2, 3)],
    )[flip]
    return lax.ppermute(value, ("core", "zh"), pairs)


def over_y(value):
    return lax.ppermute(value, "y", [(0, 1), (1, 0)])


def weight_blocks(weight):
    first, second = swapped(weight, 0), swapped(weight, 1)
    return first, second, over_y(first), over_y(second)


def weight_scatter(grad, axis):
    y, zh = lax.axis_index("y"), lax.axis_index("zh")
    half = grad.shape[axis] // 2
    other = lax.dynamic_slice_in_dim(grad, (1 - y) * half, half, axis).astype(BF)
    mine = lax.dynamic_slice_in_dim(grad, y * half, half, axis).astype(F32)
    total = (mine + over_y(other).astype(F32)).astype(BF)
    block = half // 2
    first = swapped(lax.dynamic_slice_in_dim(total, zh * block, block, axis), 0)
    second = swapped(lax.dynamic_slice_in_dim(total, (1 - zh) * block, block, axis), 2)
    return first.astype(F32) + second.astype(F32)


def local_fine(inputs, prefix_len, w_qkv, w_out, w_up_gate, w_down, cotangent):
    heads, head_dim = w_qkv.shape[1], w_qkv.shape[2] // 3
    hidden_width = w_down.shape[0]
    prefix_len = swapped(prefix_len)
    inputs, cotangent = swapped(inputs), swapped(cotangent)
    qkv_blocks = weight_blocks(w_qkv.reshape(w_qkv.shape[0], -1))
    out_blocks = weight_blocks(w_out)
    up_blocks = weight_blocks(w_up_gate.reshape(w_up_gate.shape[0], -1))
    down_blocks = weight_blocks(w_down)
    tokens = inputs.shape[0]
    full_in = lax.all_gather(inputs, GROUP, axis=1, tiled=True)
    cot_full = lax.all_gather(cotangent, GROUP, axis=1, tiled=True)
    width = full_in.shape[1]
    piece = tokens // lax.axis_size(GROUP)
    first = lax.axis_index(GROUP) * piece
    own_in = lax.dynamic_slice_in_dim(full_in, first, piece, 0)
    own_cot = lax.dynamic_slice_in_dim(cot_full, first, piece, 0)
    y, zh = lax.axis_index("y"), lax.axis_index("zh")
    order = [2 * y + zh, 2 * y + 1 - zh, 2 * (1 - y) + zh, 2 * (1 - y) + 1 - zh]

    normed_in = norm(full_in.astype(F32))[0].astype(BF)
    block = qkv_blocks[0].shape[0]
    qkv_rows = 0.0
    for weight, index in zip(qkv_blocks, order):
        qkv_rows = qkv_rows + mm("td,de->te", lax.dynamic_slice_in_dim(normed_in, index * block, block, 1), weight)
    qkv_rows = qkv_rows.reshape(tokens, heads, 3, head_dim)
    cosine, sine = rope_tables(tokens, head_dim)
    turned = rotate(qkv_rows[:, :, :2], cosine[:, None, None], sine[:, None, None])
    qkv = jnp.concatenate([turned, qkv_rows[:, :, 2:]], axis=2).astype(BF)
    qkv = qkv.reshape(tokens, heads * 3 * head_dim)
    mixed, lse = attend_fwd(qkv, prefix_len, heads, hd=head_dim)
    middle, normed_own = reduce_call("mid", False, mixed, out_blocks, (own_in,), 1)
    normed_mid, hidden, grad_gate_up = feed_call(normed_own, cot_full, up_blocks, down_blocks, 2)
    grad_middle, branch_own = reduce_call("back", True, grad_gate_up, up_blocks, (own_cot, middle), 3)
    grad_branch, grad_mixed = mix_call(branch_own, out_blocks, tokens, 4)
    grad_up = weight_scatter(mm("td,tf->df", normed_mid, grad_gate_up), 0)
    grad_down = weight_scatter(mm("tf,td->fd", hidden, cot_full), 1)
    grad_rows = attend_bwd(qkv, mixed, grad_mixed, lse, prefix_len, cosine, sine, heads, hd=head_dim)
    (input_grad,) = reduce_call("end", True, grad_rows, qkv_blocks, (grad_middle, own_in), 5)
    (outputs,) = reduce_call("out", False, hidden, down_blocks, (middle,), 6)
    grad_out = weight_scatter(mm("tc,td->cd", mixed, grad_branch), 1)
    grad_qkv = weight_scatter(mm("td,te->de", normed_in, grad_rows), 0)

    def spread(value):
        return swapped(lax.all_to_all(value, GROUP, 1, 0, tiled=True))

    return (
        spread(outputs),
        spread(input_grad).astype(F32),
        grad_qkv.reshape(-1, heads, 3 * head_dim),
        grad_out,
        grad_up.reshape(-1, 2, hidden_width),
        grad_down,
    )


def solution(mesh):
    row_size, col_size = mesh.shape["row"], mesh.shape["col"]
    fine = (row_size, col_size) == (4, 8)
    if fine:
        names, shape, body = AXES, (2,) * 5, local_fine
        row, col = AXES[:2], AXES[2:]
    else:
        names = ("rmaj", "core", "cmaj", "cmin")
        shape = (row_size // 2, 2, 4, col_size // 4)
        body = functools.partial(local, shape[3] == 2)
        row, col = names[:2], names[2:]
    outs = (P(row, col), P(row, col), P(row, col, None), P(col, row), P(row, None, col), P(col, row))
    return jax.shard_map(
        body,
        mesh=Mesh(mesh.devices.reshape(shape), names),
        in_specs=(P(row, col), P(row), P(row, col, None), P(col, row), P(row, None, col), P(col, row), P(row, col)),
        out_specs=outs,
        check_vma=False,
    )
```

```python
import functools

import jax
import jax.numpy as jnp
from jax import lax
from jax.experimental import pallas as pl
from jax.experimental.pallas import tpu as pltpu
from jax.sharding import Mesh
from jax.sharding import PartitionSpec as P

EPSILON = 1e-05
NEG = -1e30
F32 = jnp.float32
BF = jnp.bfloat16
NN = (((1,), (0,)), ((), ()))
NT = (((1,), (1,)), ((), ()))
TN = (((0,), (0,)), ((), ()))
def dot(a, b, dims):
    return lax.dot_general(a, b, dims, preferred_element_type=F32)

def fwd_kernel(prefix_ref, q_ref, k_ref, v_ref, o_ref, lse_ref, *, bq, bk, scale):
    i = pl.program_id(1)
    first = i * bq
    prefix = prefix_ref[0]
    q = q_ref[...]
    limit = jnp.maximum(first + bq, prefix)
    total = (limit + bk - 1) // bk
    clear = jnp.maximum(first, prefix) // bk
    def step(masked, j, carry):
        top, tot, acc = carry
        rows = pl.ds(pl.multiple_of(j * bk, bk), bk)
        s = dot(q, k_ref[rows, :], NT) * scale
        if masked:
            kp = j * bk + lax.broadcasted_iota(jnp.int32, (bq, bk), 1)
            qp = first + lax.broadcasted_iota(jnp.int32, (bq, bk), 0)
            s = jnp.where(kp < jnp.maximum(qp + 1, prefix), s, NEG)
        new = jnp.maximum(top, jnp.max(s, axis=1, keepdims=True))
        alpha = jnp.exp(top - new)
        p = jnp.exp(s - new)
        tot = tot * alpha + jnp.sum(p, axis=1, keepdims=True)
        acc = acc * alpha + dot(p.astype(BF), v_ref[rows, :], NN)
        return new, tot, acc
    carry = (jnp.full((bq, 1), NEG, F32), jnp.zeros((bq, 1), F32), jnp.zeros((bq, q.shape[1]), F32))
    carry = lax.fori_loop(0, clear, functools.partial(step, False), carry)
    top, tot, acc = lax.fori_loop(clear, total, functools.partial(step, True), carry)
    o_ref[...] = (acc / tot).astype(o_ref.dtype)
    lse = jnp.broadcast_to(top + jnp.log(tot), (bq, 128))
    lse_ref[0] = lse.T[0:8, :]

def attend_fwd(qkv, prefix, heads, *, bq=512, bk=512, hd=128):
    seq = qkv.shape[0]
    return pl.pallas_call(
        functools.partial(fwd_kernel, bq=bq, bk=bk, scale=hd ** -0.5),
        grid_spec=pltpu.PrefetchScalarGridSpec(
            num_scalar_prefetch=1, grid=(heads, seq // bq),
            in_specs=[pl.BlockSpec((bq, hd), lambda h, i, p: (i, 3 * h)),
                      pl.BlockSpec((seq, hd), lambda h, i, p: (0, 3 * h + 1)),
                      pl.BlockSpec((seq, hd), lambda h, i, p: (0, 3 * h + 2))],
            out_specs=[pl.BlockSpec((bq, hd), lambda h, i, p: (i, h)),
                       pl.BlockSpec((1, 8, bq), lambda h, i, p: (h, 0, i))]),
        out_shape=[jax.ShapeDtypeStruct((seq, heads * hd), BF), jax.ShapeDtypeStruct((heads, 8, seq), F32)],
        cost_estimate=pl.CostEstimate(flops=4 * heads * seq * seq * hd, bytes_accessed=8 * heads * seq * hd, transcendentals=heads * seq * seq),
        name="attend_forward",
    )(prefix, qkv, qkv, qkv)

def bwd_kernel(prefix_ref, qkv_ref, o_ref, do_ref, lse_ref, cos_ref, sin_ref, out_ref, dk_ref, dv_ref, delta_ref, *, bq, bk, hd, scale):
    seq = qkv_ref.shape[0]
    prefix = prefix_ref[0]
    dk_ref[...] = jnp.zeros_like(dk_ref)
    dv_ref[...] = jnp.zeros_like(dv_ref)
    def deltas(i, _):
        rows = pl.ds(pl.multiple_of(i * bq, bq), bq)
        prod = (do_ref[rows, :].astype(F32) * o_ref[rows, :].astype(F32)).T
        delta_ref[:, rows] = jnp.broadcast_to(jnp.sum(prod, axis=0, keepdims=True), (8, bq))
        return 0
    lax.fori_loop(0, seq // bq, deltas, 0)
    def unrotate(g, rows):
        cos, sin = cos_ref[rows, :], sin_ref[rows, :]
        half = hd // 2
        a, b = g[:, :half], g[:, half:]
        return jnp.concatenate([a * cos + b * sin, b * cos - a * sin], axis=1)
    def q_step(i, _):
        first = i * bq
        qrows = pl.ds(pl.multiple_of(first, bq), bq)
        q = qkv_ref[qrows, 0:hd]
        do = do_ref[qrows, :]
        lse = lse_ref[0, 0:1, qrows]
        delta = delta_ref[0:1, qrows]
        limit = jnp.maximum(first + bq, prefix)
        total = (limit + bk - 1) // bk
        clear = jnp.maximum(first, prefix) // bk
        def step(masked, j, dq):
            krows = pl.ds(pl.multiple_of(j * bk, bk), bk)
            k = qkv_ref[krows, hd:2 * hd]
            v = qkv_ref[krows, 2 * hd:3 * hd]
            s = dot(k, q, NT) * scale
            p = jnp.exp(s - lse)
            if masked:
                kp = j * bk + lax.broadcasted_iota(jnp.int32, (bk, bq), 0)
                qp = first + lax.broadcasted_iota(jnp.int32, (bk, bq), 1)
                p = jnp.where(kp < jnp.maximum(qp + 1, prefix), p, 0.0)
            dp = dot(v, do, NT)
            dv_ref[krows, :] += dot(p.astype(BF), do, NN)
            ds = (p * (dp - delta)).astype(BF)
            dk_ref[krows, :] += dot(ds, q, NN)
            return dq + dot(ds, k, TN)
        dq = lax.fori_loop(0, clear, functools.partial(step, False), jnp.zeros((bq, hd), F32))
        dq = lax.fori_loop(clear, total, functools.partial(step, True), dq)
        out_ref[qrows, 0:hd] = unrotate(dq * scale, qrows).astype(BF)
        return 0
    lax.fori_loop(0, seq // bq, q_step, 0)
    def fin(i, _):
        rows = pl.ds(pl.multiple_of(i * bq, bq), bq)
        out_ref[rows, hd:2 * hd] = unrotate(dk_ref[rows, :] * scale, rows).astype(BF)
        out_ref[rows, 2 * hd:3 * hd] = dv_ref[rows, :].astype(BF)
        return 0
    lax.fori_loop(0, seq // bq, fin, 0)

def attend_bwd(qkv, mixed, dmixed, lse, prefix, cos, sin, heads, *, bq=512, bk=512, hd=128):
    seq = qkv.shape[0]
    return pl.pallas_call(
        functools.partial(bwd_kernel, bq=bq, bk=bk, hd=hd, scale=hd ** -0.5),
        grid_spec=pltpu.PrefetchScalarGridSpec(
            num_scalar_prefetch=1, grid=(heads,),
            in_specs=[pl.BlockSpec((seq, 3 * hd), lambda h, p: (0, h)),
                      pl.BlockSpec((seq, hd), lambda h, p: (0, h)),
                      pl.BlockSpec((seq, hd), lambda h, p: (0, h)),
                      pl.BlockSpec((1, 8, seq), lambda h, p: (h, 0, 0)),
                      pl.BlockSpec((seq, hd // 2), lambda h, p: (0, 0)),
                      pl.BlockSpec((seq, hd // 2), lambda h, p: (0, 0))],
            out_specs=[pl.BlockSpec((seq, 3 * hd), lambda h, p: (0, h))],
            scratch_shapes=[pltpu.VMEM((seq, hd), F32), pltpu.VMEM((seq, hd), F32), pltpu.VMEM((8, seq), F32)]),
        out_shape=[jax.ShapeDtypeStruct((seq, heads * 3 * hd), BF)],
        cost_estimate=pl.CostEstimate(flops=10 * heads * seq * seq * hd, bytes_accessed=20 * heads * seq * hd, transcendentals=heads * seq * seq),
        name="attend_backward",
    )(prefix, qkv, mixed, dmixed, lse, cos, sin)[0]


def rope_tables(count, head_dim):
    positions = jnp.arange(count, dtype=jnp.int32).astype(F32)
    frequency = 10000.0 ** (-(jnp.arange(head_dim // 2).astype(F32) * 2.0 / head_dim))
    angles = positions[:, None] * frequency[None, :]
    return jnp.cos(angles), jnp.sin(angles)


def rotate(values, cosine, sine):
    half = values.shape[-1] // 2
    a, b = values[..., :half], values[..., half:]
    return jnp.concatenate([a * cosine - b * sine, b * cosine + a * sine], axis=-1)


def norm(values):
    center = values - jnp.mean(values, axis=-1, keepdims=True)
    inv_std = lax.rsqrt(jnp.mean(center * center, axis=-1, keepdims=True) + EPSILON)
    return center * inv_std, inv_std


def norm_back(grad, normed, inv_std):
    mean_grad = jnp.mean(grad, axis=-1, keepdims=True)
    mean_cross = jnp.mean(grad * normed, axis=-1, keepdims=True)
    return inv_std * (grad - mean_grad - normed * mean_cross)


def mm(spec, left, right):
    return jnp.einsum(spec, left, right, preferred_element_type=F32)


def local(swap, inputs, prefix_len, w_qkv, w_out, w_up_gate, w_down, cotangent):
    rows = ("rmaj", "cmin") if swap else ("rmaj", "core")
    cols = ("cmaj", "core") if swap else ("cmaj", "cmin")

    def exchange(value):
        if not swap:
            return value
        return lax.ppermute(value, ("core", "cmin"), [(0, 0), (1, 2), (2, 1), (3, 3)])

    def scatter(value):
        return lax.psum_scatter(value.astype(BF), cols, scatter_dimension=0, tiled=True).astype(F32)

    def spread(value):
        return lax.all_to_all(value, cols, 1, 0, tiled=True)

    prefix_len = exchange(prefix_len)
    inputs, cotangent = exchange(inputs), exchange(cotangent)
    w_qkv, w_out = exchange(w_qkv), exchange(w_out)
    w_up_gate, w_down = exchange(w_up_gate), exchange(w_down)
    tokens = inputs.shape[0]
    heads, head_dim = w_qkv.shape[1], w_qkv.shape[2] // 3
    hidden_width = w_down.shape[0]
    full_in = lax.all_gather(inputs, cols, axis=1, tiled=True)
    width = full_in.shape[1]
    qkv_all = lax.all_gather(w_qkv, rows, axis=0, tiled=True).reshape(width, heads * 3 * head_dim)
    out_all = lax.all_gather(w_out, rows, axis=1, tiled=True)
    up_all = lax.all_gather(w_up_gate, rows, axis=0, tiled=True).reshape(width, 2 * hidden_width)
    down_all = lax.all_gather(w_down, rows, axis=1, tiled=True)
    cot_full = lax.all_gather(cotangent, cols, axis=1, tiled=True)
    piece = tokens // lax.axis_size(cols)
    first = lax.axis_index(cols) * piece
    own_in = lax.dynamic_slice_in_dim(full_in, first, piece, 0).astype(F32)
    own_cot = lax.dynamic_slice_in_dim(cot_full, first, piece, 0).astype(F32)

    normed_in = norm(full_in.astype(F32))[0].astype(BF)
    qkv_rows = mm("td,de->te", normed_in, qkv_all).reshape(tokens, heads, 3, head_dim)
    cosine, sine = rope_tables(tokens, head_dim)
    turned = rotate(qkv_rows[:, :, :2], cosine[:, None, None], sine[:, None, None])
    qkv = jnp.concatenate([turned, qkv_rows[:, :, 2:]], axis=2).astype(BF)
    qkv = qkv.reshape(tokens, heads * 3 * head_dim)
    mixed, lse = attend_fwd(qkv, prefix_len, heads, hd=head_dim)
    middle = own_in + scatter(mm("tc,cd->td", mixed, out_all))
    normed_two, inv_two = norm(middle)
    normed_mid = lax.all_gather(normed_two.astype(BF), cols, axis=0, tiled=True)
    gate_up = mm("td,df->tf", normed_mid, up_all)
    gate, up = gate_up[:, :hidden_width], gate_up[:, hidden_width:]
    sig = jax.nn.sigmoid(gate)
    active = gate * sig
    hidden = (active * up).astype(BF)
    outputs = middle + scatter(mm("tf,fd->td", hidden, down_all))
    outputs = exchange(spread(outputs.astype(BF)))

    grad_hidden = mm("td,fd->tf", cot_full, down_all)
    grad_gate = grad_hidden * up * sig * (1.0 + gate * (1.0 - sig))
    grad_gate_up = jnp.concatenate([grad_gate, grad_hidden * active], axis=1).astype(BF)
    grad_down = mm("tf,td->fd", hidden, cot_full).astype(BF)
    grad_down = lax.psum_scatter(grad_down, rows, scatter_dimension=1, tiled=True)
    grad_up = mm("td,tf->df", normed_mid, grad_gate_up).astype(BF)
    grad_up = lax.psum_scatter(grad_up, rows, scatter_dimension=0, tiled=True)
    grad_normed = scatter(mm("tf,df->td", grad_gate_up, up_all))
    grad_middle = own_cot + norm_back(grad_normed, normed_two, inv_two)
    grad_branch = lax.all_gather(grad_middle.astype(BF), cols, axis=0, tiled=True)
    grad_out = mm("tc,td->cd", mixed, grad_branch).astype(BF)
    grad_out = lax.psum_scatter(grad_out, rows, scatter_dimension=1, tiled=True)
    grad_mixed = mm("td,cd->tc", grad_branch, out_all).astype(BF)
    grad_rows = attend_bwd(qkv, mixed, grad_mixed, lse, prefix_len, cosine, sine, heads, hd=head_dim)
    grad_in = scatter(mm("te,de->td", grad_rows, qkv_all))
    grad_qkv = mm("td,te->de", normed_in, grad_rows).astype(BF)
    grad_qkv = lax.psum_scatter(grad_qkv, rows, scatter_dimension=0, tiled=True)
    normed_own, inv_own = norm(own_in)
    input_grad = grad_middle + norm_back(grad_in, normed_own, inv_own)
    input_grad = exchange(spread(input_grad.astype(BF))).astype(F32)
    return (
        outputs,
        input_grad,
        exchange(grad_qkv).astype(F32).reshape(-1, heads, 3 * head_dim),
        exchange(grad_out).astype(F32),
        exchange(grad_up).astype(F32).reshape(-1, 2, hidden_width),
        exchange(grad_down).astype(F32),
    )


AXES = ("y", "core", "zh", "zl", "x")
GROUP = ("core", "zl", "x")
MESH = pl.DeviceIdType.MESH
DMA = pltpu.SemaphoreType.DMA
VMEM_WHOLE = pl.BlockSpec(memory_space=pltpu.VMEM)
ANYWHERE = pl.BlockSpec(memory_space=pl.ANY)


class Place:
    def __init__(self):
        self.y, self.c, self.zh, self.zl, self.x = (lax.axis_index(name) for name in AXES)
        y, c, zh, zl, x = self.y, self.c, self.zh, self.zl, self.x
        self.sibling = (y, 1 - c, zh, zl, x)
        self.across = (y, c, zh, zl, 1 - x)
        self.along = (y, c, zh, 1 - zl, x)
        self.beyond = (1 - y, c, zh, zl, x)
        self.far = [(y, core, 1 - zh, zl, x) for core in (0, 1)]
        self.far_role = (y, zh, 1 - zh, zl, x)
        self.straight = c == zh
        self.outer = zl == zh
        self.order = [2 * y, 2 * y + 1, 2 * (1 - y), 2 * (1 - y) + 1]
        self.block = c * 4 + zl * 2 + x

    def chip(self, dz, dx):
        return lax.rem(self.zl + dz, 2) * 2 + lax.rem(self.x + dx, 2)

    def meet(self, greet=None):
        devices = [self.sibling, self.across, self.along, self.beyond, *self.far]
        barrier = pltpu.get_barrier_semaphore()
        for device in devices:
            pl.semaphore_signal(barrier, inc=1, device_id=device, device_id_type=MESH)
        more = greet(self, barrier) if greet else 0
        pl.semaphore_wait(barrier, len(devices) + more)


def span(start, size):
    return pl.ds(pl.multiple_of(start, size), size)


def remote(src, dst, send_sem, recv_sem, device):
    return pltpu.make_async_remote_copy(
        src_ref=src, dst_ref=dst, send_sem=send_sem, recv_sem=recv_sem, device_id=device, device_id_type=MESH
    )


class Beyond:
    along_z = False

    def __init__(self, place, src, dst, sem):
        self.copy = remote(src, dst, sem.at[0], sem.at[2], place.beyond)

    def start(self):
        self.copy.start()

    def wait_recv(self):
        self.copy.wait_recv()

    def wait_send(self):
        self.copy.wait_send()


class WeightHalf:
    along_z = True

    def __init__(self, place, src, dst, sem):
        c = place.c
        self.straight = place.straight
        self.outward = remote(src, dst.at[c], sem.at[0], sem.at[2 + c], place.far_role)
        self.aside = remote(src, dst.at[c], sem.at[1], sem.at[2 + c], place.sibling)
        self.here = pltpu.make_async_copy(src, dst.at[c], sem.at[1])
        self.from_sibling = remote(src, dst.at[1 - c], sem.at[1], sem.at[3 - c], place.sibling)
        self.from_far = [remote(src, dst.at[i], sem.at[0], sem.at[2 + i], place.far_role) for i in (0, 1)]

    def start(self):
        self.outward.start()

        @pl.when(self.straight)
        def _():
            self.here.start()

        @pl.when(jnp.logical_not(self.straight))
        def _():
            self.aside.start()

    def wait_recv(self):
        @pl.when(self.straight)
        def _():
            self.here.wait()
            self.from_sibling.wait_recv()

        @pl.when(jnp.logical_not(self.straight))
        def _():
            for copy in self.from_far:
                copy.wait_recv()

    def wait_send(self):
        self.outward.wait_send()

        @pl.when(jnp.logical_not(self.straight))
        def _():
            self.aside.wait_send()


class GradHalf:
    along_z = True

    def __init__(self, place, src, dst, sem):
        c, zh = place.c, place.zh
        self.straight = place.straight
        self.here = pltpu.make_async_copy(src.at[c], dst.at[zh], sem.at[0])
        self.aside = remote(src.at[1 - c], dst.at[zh], sem.at[1], sem.at[2 + zh], place.sibling)
        self.outward = [remote(src.at[i], dst.at[zh], sem.at[i], sem.at[2 + zh], place.far[i]) for i in (0, 1)]
        self.from_sibling = remote(src.at[c], dst.at[zh], sem.at[1], sem.at[2 + zh], place.sibling)
        self.from_far = remote(src.at[c], dst.at[1 - zh], sem.at[0], sem.at[3 - zh], place.far[0])

    def start(self):
        @pl.when(self.straight)
        def _():
            self.here.start()
            self.aside.start()

        @pl.when(jnp.logical_not(self.straight))
        def _():
            for copy in self.outward:
                copy.start()

    def wait_recv(self):
        self.from_far.wait_recv()

        @pl.when(self.straight)
        def _():
            self.here.wait()

        @pl.when(jnp.logical_not(self.straight))
        def _():
            self.from_sibling.wait_recv()

    def wait_send(self):
        @pl.when(self.straight)
        def _():
            self.aside.wait_send()

        @pl.when(jnp.logical_not(self.straight))
        def _():
            for copy in self.outward:
                copy.wait_send()


KINDS = {"beyond": Beyond, "weight": WeightHalf, "grad": GradHalf}


def moved_shape(kind, src):
    shape = (2, *src.shape) if kind == "weight" else src.shape
    return jax.ShapeDtypeStruct(shape, src.dtype)


class Under:
    def __init__(self, place, moves):
        self.place, self.moves = place, moves
        self.z = [move for kind, move in moves if move.along_z]
        self.y = [move for kind, move in moves if not move.along_z and not isinstance(kind, int)]
        self.follow = [(moves[kind][1], move) for kind, move in moves if isinstance(kind, int)]

    def start_y(self):
        for move in self.y:
            move.start()

    def start_z(self, outer=None):
        def start():
            for move in self.z:
                move.start()

        if outer is None:
            start()
        else:
            pl.when(self.place.outer if outer else jnp.logical_not(self.place.outer))(start)

    def start_follow(self):
        for ahead, move in self.follow:
            ahead.wait_recv()
            move.start()

    def end(self, skip=0):
        done = [ahead for ahead, _ in self.follow]
        for _, move in self.moves[skip:]:
            if move not in done:
                move.wait_recv()


def comm_call(
    body, name, ident, inputs, outs, scratch, moves=(), flops=0, transcendentals=0, spaces=None, greet=None
):
    n_in, n_out, n_move = len(inputs), len(outs), len(moves)
    own_source = [i for i, (kind, _) in enumerate(moves) if not isinstance(kind, int)]

    def kernel(*refs):
        ins, refs = refs[:n_in], refs[n_in:]
        sources, refs = refs[:len(own_source)], refs[len(own_source):]
        results, refs = refs[:n_out], refs[n_out:]
        targets, refs = refs[:n_move], refs[n_move:]
        sems, rest = refs[0], refs[1:]
        place = Place()
        place.meet(greet)
        made = []
        for i, (kind, _) in enumerate(moves):
            if isinstance(kind, int):
                made.append((kind, Beyond(place, targets[kind], targets[i], sems.at[i])))
            else:
                made.append((kind, KINDS[kind](place, sources[own_source.index(i)], targets[i], sems.at[i])))
        body(place, ins, results, rest, Under(place, made), targets)
        for _, move in made:
            move.wait_send()

    arrays = [*inputs, *(moves[i][1] for i in own_source)]
    shapes = list(outs)
    moved = []
    for kind, array in moves:
        moved.append(moved[kind] if isinstance(kind, int) else moved_shape(kind, array))
    shapes += moved
    in_specs = (spaces or [VMEM_WHOLE] * n_in) + [ANYWHERE] * len(own_source)
    size = sum(s.size * s.dtype.itemsize for s in (*arrays, *shapes))
    result = pl.pallas_call(
        kernel,
        out_shape=shapes,
        in_specs=in_specs,
        out_specs=[VMEM_WHOLE] * (n_out + n_move),
        scratch_shapes=[DMA((max(n_move, 1), 4)), *scratch],
        compiler_params=pltpu.CompilerParams(collective_id=ident, has_side_effects=True, vmem_limit_bytes=63 << 20),
        cost_estimate=pl.CostEstimate(
            flops=flops + (20 << 30), bytes_accessed=size, transcendentals=transcendentals
        ),
        name=name,
    )(*arrays)
    return result[:n_out], result[n_out:]


def each_rows(count, body, size=32):
    def step(i, carry):
        body(span(i * size, size))
        return carry

    lax.fori_loop(0, count // size, step, 0)


def row_norm(values):
    center = values - jnp.mean(values, axis=-1, keepdims=True)
    inv_std = lax.rsqrt(jnp.mean(center * center, axis=-1, keepdims=True) + EPSILON)
    return center * inv_std, inv_std


SLICES = 4


def reduce_scratch(piece, width):
    return [
        pltpu.VMEM((4, piece, width), BF),
        pltpu.VMEM((4, piece, width), BF),
        pltpu.VMEM((2, piece, width), F32),
        pltpu.VMEM((3, piece, width), BF),
        pltpu.VMEM((3, piece, width), BF),
        DMA((4,)), DMA((4,)), DMA((3, SLICES)), DMA((3, SLICES)),
    ]


def reduce_body(place, compute, last, scratch, under, started=False, before_wait=None):
    sib_out, sib_in, own, near_out, near_in, sib_send, sib_recv, near_send, near_recv = scratch
    piece = own.shape[1]
    c = place.c
    if not started:
        under.start_y()
        under.start_z(outer=True)

    def sib_copy(step):
        return remote(sib_out.at[step], sib_in.at[step], sib_send.at[step], sib_recv.at[step], place.sibling)

    size = piece // SLICES

    def near_copy(step, r):
        device = place.along if step == 2 else place.across
        rows = span(r * size, size)
        return remote(
            near_out.at[step, rows], near_in.at[step, rows], near_send.at[step, r], near_recv.at[step, r], device
        )

    def finish(step):
        slot = step % 2
        sib_copy(step).wait_recv()

        def send(r, carry):
            if step == 2:
                near_copy(0, r).wait_recv()
            rows = span(r * size, size)
            total = own[slot, rows, :] + sib_in[step, rows, :].astype(F32)
            if step == 2:
                total = total + near_in[0, rows, :].astype(F32)
            near_out[step, rows, :] = total.astype(BF)
            near_copy(step, r).start()
            return carry

        lax.fori_loop(0, SLICES, send, 0)

    def step(s, carry):
        target = place.chip(1 - lax.rem(s, 2), 1 - s // 2)
        compute((1 - c) * 4 + target, sib_out.at[s])
        sib_copy(s).start()
        for index in (0, 1):
            @pl.when(s == index + 1)
            def _(index=index):
                finish(index)

        compute(c * 4 + target, own.at[lax.rem(s, 2)])
        return carry

    lax.fori_loop(0, 4, step, 0)
    finish(2)
    if not started:
        under.start_z(outer=False)
        under.start_follow()
    if before_wait:
        before_wait()
    sib_copy(3).wait_recv()

    def arrive(r, carry):
        near_copy(1, r).wait_recv()
        near_copy(2, r).wait_recv()

        def final(i, carry):
            rows = span(r * size + i * 16, 16)
            total = own[1, rows, :] + sib_in[3, rows, :].astype(F32)
            last(rows, total + near_in[1, rows, :].astype(F32) + near_in[2, rows, :].astype(F32))
            return carry

        return lax.fori_loop(0, size // 16, final, carry)

    lax.fori_loop(0, SLICES, arrive, 0)
    for s in range(4):
        sib_copy(s).wait_send()

    def sent(r, carry):
        for s in range(3):
            near_copy(s, r).wait_send()
        return carry

    lax.fori_loop(0, SLICES, sent, 0)
    under.end()


def product(place, left_ref, weights, transposed):
    def compute(owner, out_ref):
        piece = out_ref.shape[0]
        left = left_ref[span(owner * piece, piece), :]
        for weight, index in zip(weights, place.order):
            size = weight.shape[0] if transposed else weight.shape[1]
            part = dot(left, weight[...], NT if transposed else NN)
            out_ref[:, span(index * size, size)] = part.astype(out_ref.dtype)

    return compute


def back_rows(base, value, total):
    normed, inv_std = row_norm(value)
    mean_grad = jnp.mean(total, axis=-1, keepdims=True)
    mean_cross = jnp.mean(total * normed, axis=-1, keepdims=True)
    return base + inv_std * (total - mean_grad - normed * mean_cross)


def quarters(first, second):
    return [first.at[0], first.at[1], second.at[0], second.at[1]]


def branch_call(mixed, halves, own_in, moves, ident):
    piece, width = own_in.shape

    def body(place, ins, outs, scratch, under, targets):
        mixed_ref, first, second, base_ref = ins
        total_ref, norm_ref = outs

        def last(rows, total):
            middle = base_ref[rows, :].astype(F32) + total
            total_ref[rows, :] = middle
            norm_ref[rows, :] = row_norm(middle)[0].astype(BF)

        reduce_body(place, product(place, mixed_ref, quarters(first, second), False), last, scratch, under)

    shape = functools.partial(jax.ShapeDtypeStruct, (piece, width))
    return comm_call(
        body, "reduce_branch", ident, [mixed, *halves, own_in], [shape(F32), shape(BF)],
        reduce_scratch(piece, width), moves, flops=2 * mixed.size * width,
    )


def down_call(hidden, firsts, seconds, middle, moves, ident):
    piece, width = middle.shape

    def body(place, ins, outs, scratch, under, targets):
        hidden_ref, first_a, first_b, second_a, second_b, base_ref = ins
        parts = list(zip(quarters(first_a, second_a), quarters(first_b, second_b), place.order))

        def compute(owner, out_ref):
            rows = span(owner * piece, piece)
            for upper, lower, index in parts:
                depth, size = upper.shape
                part = dot(hidden_ref[rows, 0:depth], upper[...], NN) + dot(hidden_ref[rows, depth:], lower[...], NN)
                out_ref[:, span(index * size, size)] = part.astype(out_ref.dtype)

        def last(rows, total):
            outs[0][rows, :] = (base_ref[rows, :] + total).astype(BF)

        reduce_body(place, compute, last, scratch, under)

    return comm_call(
        body, "reduce_down", ident, [hidden, *firsts, *seconds, middle], [jax.ShapeDtypeStruct((piece, width), BF)],
        reduce_scratch(piece, width), moves, flops=2 * hidden.size * width,
    )


def input_call(grad_rows, halves, grad_middle, own_in, ready, moves, ident):
    piece, width = own_in.shape

    def body(place, ins, outs, scratch, under, targets):
        rows_ref, first, second, base_ref, value_ref, ready_ref = ins
        spread = Spread(place, ready_ref, outs[1], scratch[:3])

        def last(rows, total):
            outs[0][rows, :] = back_rows(base_ref[rows, :], value_ref[rows, :].astype(F32), total).astype(BF)

        reduce_body(
            place, product(place, rows_ref, quarters(first, second), True), last, scratch[3:], under,
            before_wait=spread.start,
        )
        spread.wait()

    return comm_call(
        body, "reduce_input", ident, [grad_rows, *halves, grad_middle, own_in, ready],
        [jax.ShapeDtypeStruct((piece, width), BF), spread_shape(ready)],
        [*spread_scratch(), *reduce_scratch(piece, width)], moves, flops=2 * grad_rows.size * width,
        greet=spread_greet,
    )


def middle_call(cot, slopes, gates, ups, downs, down_last, moves, middle, ident):
    piece, width = middle.shape
    tokens, part_width = cot.shape[0], down_last.shape[1]
    hidden = 2 * part_width
    tile = 256
    tiles = part_width // tile

    def body(place, ins, outs, scratch, under, targets):
        cot_ref, slopes_ref, ga1, ga2, gb1, gb2, ua1, ua2, ub1, ub2, value_ref, da1, da2, db1 = ins
        total_ref, branch_ref, grad_ref = outs
        load_sem, *rest = scratch
        under.start_y()
        load = pltpu.make_async_copy(slopes_ref, grad_ref, load_sem.at[0])
        load.start()
        load.wait()
        rows_in = (quarters(da1, da2), quarters(db1, targets[0]))

        def fill(owner, part):
            rows = span(owner * piece, piece)

            def step(t, carry):
                grad = None
                for weight, index in zip(rows_in[part], place.order):
                    size = weight.shape[1]
                    term = dot(cot_ref[rows, span(index * size, size)], weight[span(t * tile, tile), :], NT)
                    grad = term if grad is None else grad + term
                for offset in (0, hidden):
                    cols = span(offset + part * part_width + t * tile, tile)
                    grad_ref[rows, cols] = (grad * grad_ref[rows, cols].astype(F32)).astype(BF)
                return carry

            lax.fori_loop(0, tiles, step, 0)

        def fill_first(i, carry):
            fill(i, 0)
            return carry

        lax.fori_loop(0, tokens // piece, fill_first, 0)
        under.moves[0][1].wait_recv()
        columns = [quarters(ga1, ga2), quarters(gb1, gb2), quarters(ua1, ua2), quarters(ub1, ub2)]

        def compute(owner, out_ref):
            rows = span(owner * piece, piece)
            fill(owner, 1)
            for quarter, index in enumerate(place.order):
                total = None
                for i, weights in enumerate(columns):
                    weight = weights[quarter]
                    size = weight.shape[0]
                    term = dot(grad_ref[rows, i * part_width:(i + 1) * part_width], weight[...], NT)
                    total = term if total is None else total + term
                out_ref[:, span(index * size, size)] = total.astype(out_ref.dtype)

        def last(rows, total):
            base = cot_ref[own_rows(rows), :].astype(F32)
            grad = back_rows(base, value_ref[rows, :], total)
            total_ref[rows, :] = grad
            branch_ref[rows, :] = grad.astype(BF)

        def own_rows(rows):
            return pl.ds(pl.multiple_of(place.block * piece + rows.start, 16), rows.size)

        reduce_body(place, compute, last, rest, Under(place, under.moves[1:]), started=True)

    shape = functools.partial(jax.ShapeDtypeStruct, (piece, width))
    return comm_call(
        body, "reduce_middle", ident, [cot, slopes, *gates, *ups, middle, *downs, down_last],
        [shape(F32), shape(BF), jax.ShapeDtypeStruct((tokens, 2 * hidden), BF)],
        [DMA((1,)), *reduce_scratch(piece, width)],
        moves, flops=6 * tokens * hidden * width,
        spaces=[VMEM_WHOLE, ANYWHERE] + [VMEM_WHOLE] * 12,
    )


def gather_scratch():
    return [DMA((3, SLICES)), DMA((3, SLICES)), DMA((4,)), DMA((4,))]


def gather_body(place, own_ref, full, sems, process, under):
    near_send, near_recv, sib_send, sib_recv = sems
    piece = own_ref.shape[0]
    size = piece // SLICES
    c = place.c

    def near_copy(slot, r, target):
        where = full.at[span((c * 4 + target) * piece + r * size, size)]
        device = place.along if slot == 2 else place.across
        return remote(where, where, near_send.at[slot, r], near_recv.at[slot, r], device)

    def sib_copy(slot, core, target):
        where = full.at[span((core * 4 + target) * piece, piece)]
        return remote(where, where, sib_send.at[slot], sib_recv.at[slot], place.sibling)

    def slices(act):
        def step(r, carry):
            act(r)
            return carry

        lax.fori_loop(0, SLICES, step, 0)

    mine, x_chip, z_chip, d_chip = place.chip(0, 0), place.chip(0, 1), place.chip(1, 0), place.chip(1, 1)
    full[span((c * 4 + mine) * piece, piece), :] = own_ref[...]
    slices(lambda r: near_copy(2, r, mine).start())
    slices(lambda r: near_copy(1, r, mine).start())
    sib_copy(3, c, mine).start()
    under.start_y()
    under.start_z()

    def forward(r):
        near_copy(2, r, z_chip).wait_recv()
        near_copy(0, r, z_chip).start()

    process(c * 4 + mine)
    forward(0)
    sib_copy(3, 1 - c, mine).wait_recv()
    process((1 - c) * 4 + mine)
    forward(1)
    slices(lambda r: near_copy(1, r, x_chip).wait_recv())
    sib_copy(1, c, x_chip).start()
    process(c * 4 + x_chip)
    for r in range(2, SLICES):
        forward(r)
    sib_copy(2, c, z_chip).start()
    sib_copy(1, 1 - c, x_chip).wait_recv()
    process((1 - c) * 4 + x_chip)
    process(c * 4 + z_chip)
    under.start_follow()
    sib_copy(2, 1 - c, z_chip).wait_recv()
    process((1 - c) * 4 + z_chip)
    slices(lambda r: near_copy(0, r, d_chip).wait_recv())
    sib_copy(0, c, d_chip).start()
    process(c * 4 + d_chip)
    sib_copy(0, 1 - c, d_chip).wait_recv()
    process((1 - c) * 4 + d_chip)
    for slot in range(3):
        slices(lambda r: near_copy(slot, r, mine).wait_send())
    for slot in range(4):
        sib_copy(slot, c, mine).wait_send()


def feed_call(own, tokens, gates, ups, up_last, moves, ident):
    piece, width = own.shape
    part = up_last.shape[2]
    hidden = 2 * part
    tile = 256
    tiles = part // tile

    def body(place, ins, outs, scratch, under, targets):
        own_ref, ga1, ga2, gb1, gb2, ua1, ua2, ub1 = ins
        full, hidden_ref, slopes_ref = outs
        columns = (
            (quarters(ga1, ga2), quarters(ua1, ua2)),
            (quarters(gb1, gb2), quarters(ub1, targets[0])),
        )
        waiting = []

        def fill(owner, which):
            rows = span(owner * piece, piece)
            gates, ups = columns[which]

            def step(t, carry):
                taken = span(t * tile, tile)
                gate = up = None
                for gate_weight, up_weight, index in zip(gates, ups, place.order):
                    size = gate_weight.shape[0]
                    normed = full[rows, span(index * size, size)]
                    terms = dot(normed, gate_weight[:, taken], NN), dot(normed, up_weight[:, taken], NN)
                    gate, up = terms if gate is None else (gate + terms[0], up + terms[1])
                cols, up_cols = span(which * part + t * tile, tile), span(hidden + which * part + t * tile, tile)
                sig = 1.0 / (1.0 + jnp.exp(-gate))
                active = gate * sig
                hidden_ref[rows, cols] = (active * up).astype(BF)
                slopes_ref[rows, cols] = (up * sig * (1.0 + gate * (1.0 - sig))).astype(BF)
                slopes_ref[rows, up_cols] = active.astype(BF)
                return carry

            lax.fori_loop(0, tiles, step, 0)

        def process(owner):
            fill(owner, 0)
            waiting.append(owner)
            if len(waiting) == 3:
                under.moves[0][1].wait_recv()
                for earlier in waiting:
                    fill(earlier, 1)
            elif len(waiting) > 3:
                fill(owner, 1)

        gather_body(place, own_ref, full, scratch, process, under)
        under.end(skip=1)

    return comm_call(
        body, "gather_feed", ident, [own, *gates, *ups, up_last],
        [
            jax.ShapeDtypeStruct((tokens, width), BF),
            jax.ShapeDtypeStruct((tokens, hidden), BF),
            jax.ShapeDtypeStruct((tokens, 2 * hidden), BF),
        ],
        gather_scratch(),
        moves, flops=4 * tokens * hidden * width, transcendentals=tokens * hidden,
    )


def mix_call(own, halves, tokens, moves, ident):
    width = own.shape[1]
    inner = halves[0].shape[1]

    def body(place, ins, outs, scratch, under, targets):
        own_ref, first, second = ins
        full, mixed_ref = outs
        piece = own_ref.shape[0]

        def process(owner):
            rows = span(owner * piece, piece)
            total = None
            for weight, index in zip(quarters(first, second), place.order):
                size = weight.shape[1]
                part = dot(full[rows, span(index * size, size)], weight[...], NT)
                total = part if total is None else total + part
            mixed_ref[rows, :] = total.astype(BF)

        gather_body(place, own_ref, full, scratch, process, under)
        under.end()

    return comm_call(
        body, "gather_mix", ident, [own, *halves],
        [jax.ShapeDtypeStruct((tokens, width), BF), jax.ShapeDtypeStruct((tokens, inner), BF)],
        gather_scratch(), moves, flops=2 * tokens * inner * width,
    )


class ColumnGather:
    def __init__(self, place, src, full, sems):
        self.place, self.src, self.full = place, src, full
        self.near_send, self.near_recv, self.sib_send, self.sib_recv, self.own = sems
        self.width = src.shape[1]
        self.size = src.shape[0] // SLICES

    def where(self, core, target):
        return span((core * 4 + target) * self.width, self.width)

    def near(self, slot, r, target, first=False):
        place = self.place
        rows = pl.ds(r * self.size, self.size)
        dst = self.full.at[rows, self.where(place.c, target)]
        src = self.src.at[rows] if first else dst
        device = place.along if slot == 2 else place.across
        return remote(src, dst, self.near_send.at[slot, r], self.near_recv.at[slot, r], device)

    def sib(self, slot, core, target, first=False):
        dst = self.full.at[:, self.where(core, target)]
        src = self.src if first else dst
        return remote(src, dst, self.sib_send.at[slot], self.sib_recv.at[slot], self.place.sibling)

    def chips(self):
        place = self.place
        return place.chip(0, 0), place.chip(0, 1), place.chip(1, 0), place.chip(1, 1)

    def own_copy(self):
        return pltpu.make_async_copy(self.src, self.full.at[:, self.where(self.place.c, self.chips()[0])], self.own.at[0])

    def start(self):
        mine = self.chips()[0]
        self.own_copy().start()
        for slot in (2, 1):
            for r in range(SLICES):
                self.near(slot, r, mine, True).start()
        self.sib(3, self.place.c, mine, True).start()

    def forward(self, r):
        z_chip = self.chips()[2]
        self.near(2, r, z_chip).wait_recv()
        self.near(0, r, z_chip).start()

    def finish(self):
        mine, x_chip, z_chip, d_chip = self.chips()
        c = self.place.c
        self.sib(2, c, z_chip).start()
        for r in range(SLICES):
            self.near(1, r, x_chip).wait_recv()
        self.sib(1, c, x_chip).start()
        for r in range(SLICES):
            self.near(0, r, d_chip).wait_recv()
        self.sib(0, c, d_chip).start()
        self.own_copy().wait()
        for slot, target in enumerate((d_chip, x_chip, z_chip, mine)):
            self.sib(slot, 1 - c, target).wait_recv()
            self.sib(slot, c, mine).wait_send()
        for slot in range(3):
            for r in range(SLICES):
                self.near(slot, r, mine).wait_send()


def attend_call(qkv, prefix, cot_block, heads, hd, moves, ident):
    seq = qkv.shape[0]
    bq = bk = min(512, seq // 2)
    scale = hd ** -0.5

    def body(place, ins, outs, scratch, under, targets):
        qkv_ref, prefix_ref, block_ref = ins
        mixed_ref, lse_ref, cot_ref = outs
        gather = ColumnGather(place, block_ref, cot_ref, scratch)
        gather.start()
        under.start_y()
        under.start_z()
        bound = prefix_ref[0:1, 0:1]

        def head(h):
            base = h * 3 * hd
            for i in range(seq // bq):
                first = i * bq
                q = qkv_ref[first:first + bq, base:base + hd]
                total = max(i + 1, seq // 2 // bk)

                def step(masked, j, state, first=first, q=q):
                    top, tot, acc = state
                    rows = span(j * bk, bk)
                    s = dot(q, qkv_ref[rows, base + hd:base + 2 * hd], NT) * scale
                    if masked:
                        kp = j * bk + lax.broadcasted_iota(jnp.int32, (bq, bk), 1)
                        qp = first + lax.broadcasted_iota(jnp.int32, (bq, bk), 0)
                        s = jnp.where(kp < jnp.maximum(qp + 1, bound), s, NEG)
                    new = jnp.maximum(top, jnp.max(s, axis=1, keepdims=True))
                    alpha = jnp.exp(top - new)
                    p = jnp.exp(s - new)
                    tot = tot * alpha + jnp.sum(p, axis=1, keepdims=True)
                    acc = acc * alpha + dot(p.astype(BF), qkv_ref[rows, base + 2 * hd:base + 3 * hd], NN)
                    return new, tot, acc

                state = (jnp.full((bq, 1), NEG, F32), jnp.zeros((bq, 1), F32), jnp.zeros((bq, hd), F32))
                state = lax.fori_loop(0, i, functools.partial(step, False), state)
                top, tot, acc = lax.fori_loop(i, total, functools.partial(step, True), state)
                mixed_ref[first:first + bq, h * hd:(h + 1) * hd] = (acc / tot).astype(BF)
                lse = jnp.broadcast_to(top + jnp.log(tot), (bq, 128))
                lse_ref[h, :, first:first + bq] = lse.T[0:8, :]

        passed = 0
        for h in range(heads):
            head(h)
            if passed < SLICES:
                gather.forward(passed)
                passed += 1
        under.start_follow()
        for r in range(passed, SLICES):
            gather.forward(r)
        gather.finish()
        under.end()

    return comm_call(
        body, "attend", ident, [qkv, prefix, cot_block],
        [
            jax.ShapeDtypeStruct((seq, heads * hd), BF),
            jax.ShapeDtypeStruct((heads, 8, seq), F32),
            jax.ShapeDtypeStruct((seq, cot_block.shape[1] * 8), BF),
        ],
        [DMA((3, SLICES)), DMA((3, SLICES)), DMA((4,)), DMA((4,)), DMA((1,))],
        moves, flops=4 * heads * seq * seq * hd, transcendentals=heads * seq * seq,
    )


def attend_back_call(qkv, mixed, grad_mixed, lse, prefix, tables, heads, hd, moves, ident):
    seq = qkv.shape[0]
    bq = bk = min(512, seq // 2)
    scale = hd ** -0.5
    half = hd // 2

    def body(place, ins, outs, scratch, under, targets):
        qkv_ref, o_ref, do_ref, lse_ref, prefix_ref, cos_ref, sin_ref = ins
        (out_ref,) = outs
        under.start_y()
        under.start_z()
        dk_ref, dv_ref = scratch
        bound = prefix_ref[0:1, 0:1]

        def unrotate(g, rows):
            return g * cos_ref[rows, :] - pltpu.roll(g, half, 1) * sin_ref[rows, :]

        def head(h, carry):
            base = h * 3 * hd
            own = span(h * hd, hd)
            dk_ref[...] = jnp.zeros_like(dk_ref)
            dv_ref[...] = jnp.zeros_like(dv_ref)
            for i in range(seq // bq):
                first = i * bq
                rows = pl.ds(first, bq)
                q = qkv_ref[rows, span(base, hd)]
                do = do_ref[rows, own]
                row_sums = (do.astype(F32) * o_ref[rows, own].astype(F32)).T
                delta = jnp.sum(row_sums, axis=0, keepdims=True)
                tops = lse_ref[h, 0:1, first:first + bq]
                total = max(i + 1, seq // 2 // bk)

                def step(masked, j, dq, first=first, q=q, do=do, delta=delta, tops=tops):
                    keys = span(j * bk, bk)
                    k = qkv_ref[keys, span(base + hd, hd)]
                    v = qkv_ref[keys, span(base + 2 * hd, hd)]
                    p = jnp.exp(dot(k, q, NT) * scale - tops)
                    if masked:
                        kp = j * bk + lax.broadcasted_iota(jnp.int32, (bk, bq), 0)
                        qp = first + lax.broadcasted_iota(jnp.int32, (bk, bq), 1)
                        p = jnp.where(kp < jnp.maximum(qp + 1, bound), p, 0.0)
                    dv_ref[keys, :] += dot(p.astype(BF), do, NN)
                    ds = (p * (dot(v, do, NT) - delta)).astype(BF)
                    dk_ref[keys, :] += dot(ds, q, NN)
                    return dq + dot(ds, k, TN)

                dq = lax.fori_loop(0, i, functools.partial(step, False), jnp.zeros((bq, hd), F32))
                dq = lax.fori_loop(i, total, functools.partial(step, True), dq)
                out_ref[rows, span(base, hd)] = unrotate(dq * scale, rows).astype(BF)

            def fin(i, carry):
                rows = span(i * bq, bq)
                out_ref[rows, span(base + hd, hd)] = unrotate(dk_ref[rows, :] * scale, rows).astype(BF)
                out_ref[rows, span(base + 2 * hd, hd)] = dv_ref[rows, :].astype(BF)
                return carry

            return lax.fori_loop(0, seq // bq, fin, carry)

        lax.fori_loop(0, heads, head, 0)
        under.start_follow()
        under.end()

    return comm_call(
        body, "attend_back", ident, [qkv, mixed, grad_mixed, lse, prefix, *tables],
        [jax.ShapeDtypeStruct(qkv.shape, BF)],
        [pltpu.VMEM((seq, hd), F32), pltpu.VMEM((seq, hd), F32)],
        moves, flops=10 * heads * seq * seq * hd, transcendentals=heads * seq * seq,
    )


def start_call(inputs, cot, tables, moves, heads, hd, ident):
    tokens, slice_width = inputs.shape
    width = slice_width * 8
    piece = tokens // 8
    chunks = 4
    size = tokens // chunks
    half = size // 2

    def body(place, ins, outs, scratch, under, targets):
        in_ref, cot_ref, cos_ref, sin_ref = ins
        qkv_ref, normed_ref, own_ref, block_ref, second_qkv, second_out = outs
        (full, total_ref, swap_send, swap_recv, near_send, near_recv, diag_send, diag_recv, sib_send, sib_recv,
         y_sems) = scratch
        c, zl, x = place.c, place.zl, place.x
        crossed = jnp.logical_not(place.straight)
        partner = (place.y, 1 - c, 1 - place.zh, zl, x)

        def columns(core, target):
            return span((core * 4 + target) * slice_width, slice_width)

        mine = place.chip(0, 0)
        x_chip, z_chip, d_chip = place.chip(0, 1), place.chip(1, 0), place.chip(1, 1)

        def rows_of(r):
            return pl.ds(r * size, size)

        def swap_copy(r, core):
            return remote(
                in_ref.at[rows_of(r)], full.at[rows_of(r), columns(core, mine)], swap_send.at[r], swap_recv.at[r], partner
            )

        def own_copy(r):
            return pltpu.make_async_copy(in_ref.at[rows_of(r)], full.at[rows_of(r), columns(c, mine)], swap_send.at[r])

        def cot_swap():
            return remote(cot_ref, block_ref, swap_send.at[chunks], swap_recv.at[chunks], partner)

        def cot_own():
            return pltpu.make_async_copy(cot_ref, block_ref, swap_send.at[chunks])

        def near_copy(part, r, target):
            where = full.at[rows_of(r), columns(c, target)]
            device = place.across if part == 0 else place.along
            return remote(where, where, near_send.at[part, r], near_recv.at[part, r], device)

        def diag_copy(r, target):
            where = full.at[rows_of(r), columns(c, target)]
            return remote(where, where, diag_send.at[r], diag_recv.at[r], place.across)

        def sib_copy(slot, r, core, target):
            where = full.at[rows_of(r), columns(core, target)]
            return remote(where, where, sib_send.at[slot, r], sib_recv.at[slot, r], place.sibling)

        @pl.when(place.straight)
        def _():
            for r in range(chunks):
                own_copy(r).start()
            cot_own().start()

        @pl.when(crossed)
        def _():
            for r in range(chunks):
                swap_copy(r, 1 - c).start()

        for r in range(chunks):
            @pl.when(place.straight)
            def _(r=r):
                own_copy(r).wait()

            @pl.when(crossed)
            def _(r=r):
                swap_copy(r, c).wait_recv()

            near_copy(0, r, mine).start()
            near_copy(1, r, mine).start()
            sib_copy(0, r, c, mine).start()
        for r in range(chunks):
            near_copy(1, r, z_chip).wait_recv()
            diag_copy(r, z_chip).start()
            sib_copy(2, r, c, z_chip).start()
            near_copy(0, r, x_chip).wait_recv()
            sib_copy(1, r, c, x_chip).start()
            if r == 0:
                under.moves[0][1].start()

        under.moves[0][1].wait_recv()
        under.moves[1][1].start()
        pl.when(crossed)(lambda: cot_swap().start())
        beyond_qkv = Beyond(place, targets[0], second_qkv, y_sems.at[0])
        beyond_qkv.start()
        firsts = [targets[0].at[0], targets[0].at[1]]
        seconds = [second_qkv.at[0], second_qkv.at[1]]
        depth = firsts[0].shape[0]
        for r in range(chunks):
            diag_copy(r, d_chip).wait_recv()
            sib_copy(3, r, c, d_chip).start()
            for slot, target in enumerate((mine, x_chip, z_chip, d_chip)):
                sib_copy(slot, r, 1 - c, target).wait_recv()

            def norm_rows(i, carry, r=r):
                rows = span(r * size + i * 16, 16)
                normed_ref[rows, :] = row_norm(full[rows, :].astype(F32))[0].astype(BF)
                return carry

            lax.fori_loop(0, size // 16, norm_rows, 0)
            rows = rows_of(r)
            total = None
            for weight, index in zip(firsts, place.order[:2]):
                term = dot(normed_ref[rows, span(index * depth, depth)], weight[...], NN)
                total = term if total is None else total + term
            total_ref[rows, :] = total
        own_ref[...] = full[span(place.block * piece, piece), :]
        under.moves[1][1].wait_recv()
        beyond_out = Beyond(place, targets[1], second_out, y_sems.at[1])
        beyond_out.start()
        beyond_qkv.wait_recv()

        def project(r, carry):
            rows = span(r * half, half)
            total = total_ref[rows, :]
            for weight, index in zip(seconds, place.order[2:]):
                total = total + dot(normed_ref[rows, span(index * depth, depth)], weight[...], NN)
            cos, sin = cos_ref[rows, :], sin_ref[rows, :]
            for h in range(heads):
                for part in range(3):
                    cols = pl.ds((3 * h + part) * hd, hd)
                    value = total[:, (3 * h + part) * hd:(3 * h + part + 1) * hd]
                    if part < 2:
                        value = value * cos + pltpu.roll(value, hd // 2, 1) * sin
                    qkv_ref[rows, cols] = value.astype(BF)
            return carry

        lax.fori_loop(0, tokens // half, project, 0)
        beyond_out.wait_recv()

        @pl.when(place.straight)
        def _():
            cot_own().wait()

        @pl.when(crossed)
        def _():
            cot_swap().wait_recv()
            cot_swap().wait_send()
            for r in range(chunks):
                swap_copy(r, 1 - c).wait_send()

        beyond_qkv.wait_send()
        beyond_out.wait_send()
        for r in range(chunks):
            near_copy(0, r, mine).wait_send()
            near_copy(1, r, mine).wait_send()
            diag_copy(r, z_chip).wait_send()
            for slot in range(4):
                sib_copy(slot, r, c, mine).wait_send()

    qkv_half, out_half = (moved_shape(kind, array) for kind, array in moves)
    inner = qkv_half.shape[2]
    return comm_call(
        body, "start", ident, [inputs, cot, *tables],
        [
            jax.ShapeDtypeStruct((tokens, inner), BF),
            jax.ShapeDtypeStruct((tokens, width), BF),
            jax.ShapeDtypeStruct((piece, width), BF),
            jax.ShapeDtypeStruct(cot.shape, BF),
            qkv_half,
            out_half,
        ],
        [
            pltpu.VMEM((tokens, width), BF), pltpu.VMEM((tokens, inner), F32),
            DMA((chunks + 1,)), DMA((chunks + 1,)), DMA((2, chunks)), DMA((2, chunks)), DMA((chunks,)),
            DMA((chunks,)), DMA((4, chunks)), DMA((4, chunks)), DMA((2, 4)),
        ],
        moves, flops=2 * tokens * width * inner,
        spaces=[ANYWHERE, ANYWHERE, VMEM_WHOLE, VMEM_WHOLE],
    )


BLOCKS = [(core, zl, x) for core in (0, 1) for zl in (0, 1) for x in (0, 1)]


def spread_greet(place, barrier):
    for core, zl, x in BLOCKS:
        mine = jnp.logical_and(place.straight, core * 4 + zl * 2 + x == place.block)

        @pl.when(jnp.logical_not(mine))
        def _(core=core, zl=zl, x=x):
            pl.semaphore_signal(
                barrier, inc=1, device_id=(place.y, core, place.c, zl, x), device_id_type=MESH
            )

    return 8 - jnp.where(place.straight, 1, 0)


def spread_scratch():
    return [DMA((8,)), DMA((8,)), DMA((1,))]


def spread_shape(piece):
    return jax.ShapeDtypeStruct((piece.shape[0] * 8, piece.shape[1] // 8), piece.dtype)


class Spread:
    def __init__(self, place, src, dst, sems):
        self.place, self.src, self.dst = place, src, dst
        self.send, self.recv, self.own = sems
        self.piece, self.width = src.shape[0], src.shape[1] // 8

    def copy(self, f):
        place = self.place
        return remote(
            self.src.at[:, pl.ds(f * self.width, self.width)], self.dst.at[span(place.block * self.piece, self.piece)],
            self.send.at[f], self.recv.at[place.block], (place.y, place.zh, *BLOCKS[f]),
        )

    def incoming(self, f):
        core, zl, x = BLOCKS[f]
        place = self.place
        return remote(
            self.src.at[:, pl.ds(f * self.width, self.width)], self.dst.at[pl.ds(f * self.piece, self.piece)],
            self.send.at[f], self.recv.at[f], (place.y, core, place.c, zl, x),
        )

    def own_copy(self):
        block = self.place.block
        return pltpu.make_async_copy(
            self.src.at[:, span(block * self.width, self.width)], self.dst.at[span(block * self.piece, self.piece)],
            self.own.at[0],
        )

    def each(self, act):
        for f in range(8):
            mine = jnp.logical_and(self.place.straight, self.place.block == f)
            pl.when(jnp.logical_not(mine))(functools.partial(act, f))

    def start(self):
        self.each(lambda f: self.copy(f).start())
        pl.when(self.place.straight)(lambda: self.own_copy().start())

    def wait(self):
        self.each(lambda f: self.incoming(f).wait_recv())
        self.each(lambda f: self.copy(f).wait_send())
        pl.when(self.place.straight)(lambda: self.own_copy().wait())


def finish_call(piece, moves, ident):
    def body(place, ins, outs, scratch, under, targets):
        spread = Spread(place, ins[0], outs[0], scratch)
        spread.start()
        under.start_z()
        under.end()
        spread.wait()

    return comm_call(
        body, "finish", ident, [piece], [spread_shape(piece)], spread_scratch(), moves, greet=spread_greet,
    )


def local_fine(inputs, prefix_len, w_qkv, w_out, w_up_gate, w_down, cotangent):
    heads, hd = w_qkv.shape[1], w_qkv.shape[2] // 3
    hidden_width = w_down.shape[0]
    tokens = inputs.shape[0]
    y = lax.axis_index("y")
    prefix_len = lax.ppermute(prefix_len, ("core", "zh"), [(0, 0), (1, 2), (2, 1), (3, 3)])
    prefix = jnp.broadcast_to(prefix_len[:, None], (8, 128))
    cosine, sine = rope_tables(tokens, hd)
    tables = (jnp.concatenate([cosine, cosine], axis=1), jnp.concatenate([-sine, sine], axis=1))
    part = hidden_width // 2
    ga, gb = w_up_gate[:, 0, :part], w_up_gate[:, 0, part:]
    ua, ub = w_up_gate[:, 1, :part], w_up_gate[:, 1, part:]
    da, db = w_down[:part], w_down[part:]

    (qkv, normed_in, own_in, cot_block, qkv_2, out_2), (qkv_1, out_1) = start_call(
        inputs, cotangent, tables, [("weight", w_qkv.reshape(w_qkv.shape[0], -1)), ("weight", w_out)], heads, hd, 1
    )
    (mixed, lse, cot_full), (ga_1, gb_1, ga_2) = attend_call(
        qkv, prefix, cot_block, heads, hd, [("weight", ga), ("weight", gb), (0, None)], 2
    )
    (middle, normed_own), (gb_2, ua_1, ub_1, ua_2) = branch_call(
        mixed, (out_1, out_2), own_in, [("beyond", gb_1), ("weight", ua), ("weight", ub), (1, None)], 3
    )
    gates = (ga_1, ga_2, gb_1, gb_2)
    (normed_mid, hidden, slopes), (ub_2, da_1, db_1, da_2) = feed_call(
        normed_own, tokens, gates, (ua_1, ua_2), ub_1, [("beyond", ub_1), ("weight", da), ("weight", db), (1, None)], 4
    )

    def halves(spec, left, right, axis):
        side = left if axis == 0 else right
        half = side.shape[1] // 2

        def cut(which):
            taken = lax.dynamic_slice_in_dim(side, which * half, half, 1)
            return mm(spec, taken, right) if axis == 0 else mm(spec, left, taken)

        return cut(y), cut(1 - y).astype(BF)

    def joined(own, moved, axis):
        total = (own + moved.astype(F32)).astype(BF)
        if axis == 0:
            return total.reshape(2, total.shape[0] // 2, total.shape[1])
        return jnp.swapaxes(total.reshape(total.shape[0], 2, total.shape[1] // 2), 0, 1)

    down_own, down_other = halves("tf,td->fd", hidden, cot_full, 1)
    (grad_middle, branch_own, grad_gate_up), (db_2, down_moved) = middle_call(
        cot_full, slopes, gates, (ua_1, ua_2, ub_1, ub_2), (da_1, da_2), db_1,
        [("beyond", db_1), ("beyond", down_other)], middle, 5,
    )
    gate_grad, gate_other = halves("td,tf->df", normed_mid, grad_gate_up[:, :hidden_width], 0)
    up_grad, up_other = halves("td,tf->df", normed_mid, grad_gate_up[:, hidden_width:], 0)
    (outputs,), (down_final, gate_moved) = down_call(
        hidden, (da_1, db_1), (da_2, db_2), middle,
        [("grad", joined(down_own, down_moved, 1)), ("beyond", gate_other)], 6,
    )
    (grad_branch, grad_mixed), (gate_final, up_moved) = mix_call(
        branch_own, (out_1, out_2), tokens,
        [("grad", joined(gate_grad, gate_moved, 0)), ("beyond", up_other)], 7,
    )
    out_grad, out_other = halves("tc,td->cd", mixed, grad_branch, 1)
    (grad_rows,), (up_final, out_moved) = attend_back_call(
        qkv, mixed, grad_mixed, lse, prefix, tables, heads, hd,
        [("grad", joined(up_grad, up_moved, 0)), ("beyond", out_other)], 8,
    )
    qkv_grad, qkv_other = halves("td,te->de", normed_in, grad_rows, 0)
    (input_grad, outputs), (out_final, qkv_moved) = input_call(
        grad_rows, (qkv_1, qkv_2), grad_middle, own_in, outputs,
        [("grad", joined(out_grad, out_moved, 1)), ("beyond", qkv_other)], 9,
    )
    (input_grad,), (qkv_final,) = finish_call(input_grad, [("grad", joined(qkv_grad, qkv_moved, 0))], 10)

    def summed(parts):
        return parts[0].astype(F32) + parts[1].astype(F32)

    return (
        outputs,
        input_grad.astype(F32),
        summed(qkv_final).reshape(-1, heads, 3 * hd),
        summed(out_final),
        jnp.stack([summed(gate_final), summed(up_final)], axis=1),
        summed(down_final),
    )


def solution(mesh):
    row_size, col_size = mesh.shape["row"], mesh.shape["col"]
    fine = (row_size, col_size) == (4, 8)
    if fine:
        names, shape, body = AXES, (2,) * 5, local_fine
        row, col = AXES[:2], AXES[2:]
    else:
        names = ("rmaj", "core", "cmaj", "cmin")
        shape = (row_size // 2, 2, 4, col_size // 4)
        body = functools.partial(local, shape[3] == 2)
        row, col = names[:2], names[2:]
    outs = (P(row, col), P(row, col), P(row, col, None), P(col, row), P(row, None, col), P(col, row))
    return jax.shard_map(
        body,
        mesh=Mesh(mesh.devices.reshape(shape), names),
        in_specs=(P(row, col), P(row), P(row, col, None), P(col, row), P(row, None, col), P(col, row), P(row, col)),
        out_specs=outs,
        check_vma=False,
    )
```

```python
import functools

import jax
import jax.numpy as jnp
from jax import lax
from jax.experimental import pallas as pl
from jax.experimental.pallas import tpu as pltpu
from jax.sharding import Mesh
from jax.sharding import PartitionSpec as P

EPSILON = 1e-05
NEG = -1e30
F32 = jnp.float32
BF = jnp.bfloat16
NN = (((1,), (0,)), ((), ()))
NT = (((1,), (1,)), ((), ()))
TN = (((0,), (0,)), ((), ()))
def dot(a, b, dims):
    return lax.dot_general(a, b, dims, preferred_element_type=F32)

def fwd_kernel(prefix_ref, q_ref, k_ref, v_ref, o_ref, lse_ref, *, bq, bk, scale):
    i = pl.program_id(1)
    first = i * bq
    prefix = prefix_ref[0]
    q = q_ref[...]
    limit = jnp.maximum(first + bq, prefix)
    total = (limit + bk - 1) // bk
    clear = jnp.maximum(first, prefix) // bk
    def step(masked, j, carry):
        top, tot, acc = carry
        rows = pl.ds(pl.multiple_of(j * bk, bk), bk)
        s = dot(q, k_ref[rows, :], NT) * scale
        if masked:
            kp = j * bk + lax.broadcasted_iota(jnp.int32, (bq, bk), 1)
            qp = first + lax.broadcasted_iota(jnp.int32, (bq, bk), 0)
            s = jnp.where(kp < jnp.maximum(qp + 1, prefix), s, NEG)
        new = jnp.maximum(top, jnp.max(s, axis=1, keepdims=True))
        alpha = jnp.exp(top - new)
        p = jnp.exp(s - new)
        tot = tot * alpha + jnp.sum(p, axis=1, keepdims=True)
        acc = acc * alpha + dot(p.astype(BF), v_ref[rows, :], NN)
        return new, tot, acc
    carry = (jnp.full((bq, 1), NEG, F32), jnp.zeros((bq, 1), F32), jnp.zeros((bq, q.shape[1]), F32))
    carry = lax.fori_loop(0, clear, functools.partial(step, False), carry)
    top, tot, acc = lax.fori_loop(clear, total, functools.partial(step, True), carry)
    o_ref[...] = (acc / tot).astype(o_ref.dtype)
    lse = jnp.broadcast_to(top + jnp.log(tot), (bq, 128))
    lse_ref[0] = lse.T[0:8, :]

def attend_fwd(qkv, prefix, heads, *, bq=512, bk=512, hd=128):
    seq = qkv.shape[0]
    return pl.pallas_call(
        functools.partial(fwd_kernel, bq=bq, bk=bk, scale=hd ** -0.5),
        grid_spec=pltpu.PrefetchScalarGridSpec(
            num_scalar_prefetch=1, grid=(heads, seq // bq),
            in_specs=[pl.BlockSpec((bq, hd), lambda h, i, p: (i, 3 * h)),
                      pl.BlockSpec((seq, hd), lambda h, i, p: (0, 3 * h + 1)),
                      pl.BlockSpec((seq, hd), lambda h, i, p: (0, 3 * h + 2))],
            out_specs=[pl.BlockSpec((bq, hd), lambda h, i, p: (i, h)),
                       pl.BlockSpec((1, 8, bq), lambda h, i, p: (h, 0, i))]),
        out_shape=[jax.ShapeDtypeStruct((seq, heads * hd), BF), jax.ShapeDtypeStruct((heads, 8, seq), F32)],
        cost_estimate=pl.CostEstimate(flops=4 * heads * seq * seq * hd, bytes_accessed=8 * heads * seq * hd, transcendentals=heads * seq * seq),
        name="attend_forward",
    )(prefix, qkv, qkv, qkv)

def bwd_kernel(prefix_ref, qkv_ref, o_ref, do_ref, lse_ref, cos_ref, sin_ref, out_ref, dk_ref, dv_ref, delta_ref, *, bq, bk, hd, scale):
    seq = qkv_ref.shape[0]
    prefix = prefix_ref[0]
    dk_ref[...] = jnp.zeros_like(dk_ref)
    dv_ref[...] = jnp.zeros_like(dv_ref)
    def deltas(i, _):
        rows = pl.ds(pl.multiple_of(i * bq, bq), bq)
        prod = (do_ref[rows, :].astype(F32) * o_ref[rows, :].astype(F32)).T
        delta_ref[:, rows] = jnp.broadcast_to(jnp.sum(prod, axis=0, keepdims=True), (8, bq))
        return 0
    lax.fori_loop(0, seq // bq, deltas, 0)
    def unrotate(g, rows):
        cos, sin = cos_ref[rows, :], sin_ref[rows, :]
        half = hd // 2
        a, b = g[:, :half], g[:, half:]
        return jnp.concatenate([a * cos + b * sin, b * cos - a * sin], axis=1)
    def q_step(i, _):
        first = i * bq
        qrows = pl.ds(pl.multiple_of(first, bq), bq)
        q = qkv_ref[qrows, 0:hd]
        do = do_ref[qrows, :]
        lse = lse_ref[0, 0:1, qrows]
        delta = delta_ref[0:1, qrows]
        limit = jnp.maximum(first + bq, prefix)
        total = (limit + bk - 1) // bk
        clear = jnp.maximum(first, prefix) // bk
        def step(masked, j, dq):
            krows = pl.ds(pl.multiple_of(j * bk, bk), bk)
            k = qkv_ref[krows, hd:2 * hd]
            v = qkv_ref[krows, 2 * hd:3 * hd]
            s = dot(k, q, NT) * scale
            p = jnp.exp(s - lse)
            if masked:
                kp = j * bk + lax.broadcasted_iota(jnp.int32, (bk, bq), 0)
                qp = first + lax.broadcasted_iota(jnp.int32, (bk, bq), 1)
                p = jnp.where(kp < jnp.maximum(qp + 1, prefix), p, 0.0)
            dp = dot(v, do, NT)
            dv_ref[krows, :] += dot(p.astype(BF), do, NN)
            ds = (p * (dp - delta)).astype(BF)
            dk_ref[krows, :] += dot(ds, q, NN)
            return dq + dot(ds, k, TN)
        dq = lax.fori_loop(0, clear, functools.partial(step, False), jnp.zeros((bq, hd), F32))
        dq = lax.fori_loop(clear, total, functools.partial(step, True), dq)
        out_ref[qrows, 0:hd] = unrotate(dq * scale, qrows).astype(BF)
        return 0
    lax.fori_loop(0, seq // bq, q_step, 0)
    def fin(i, _):
        rows = pl.ds(pl.multiple_of(i * bq, bq), bq)
        out_ref[rows, hd:2 * hd] = unrotate(dk_ref[rows, :] * scale, rows).astype(BF)
        out_ref[rows, 2 * hd:3 * hd] = dv_ref[rows, :].astype(BF)
        return 0
    lax.fori_loop(0, seq // bq, fin, 0)

def attend_bwd(qkv, mixed, dmixed, lse, prefix, cos, sin, heads, *, bq=512, bk=512, hd=128):
    seq = qkv.shape[0]
    return pl.pallas_call(
        functools.partial(bwd_kernel, bq=bq, bk=bk, hd=hd, scale=hd ** -0.5),
        grid_spec=pltpu.PrefetchScalarGridSpec(
            num_scalar_prefetch=1, grid=(heads,),
            in_specs=[pl.BlockSpec((seq, 3 * hd), lambda h, p: (0, h)),
                      pl.BlockSpec((seq, hd), lambda h, p: (0, h)),
                      pl.BlockSpec((seq, hd), lambda h, p: (0, h)),
                      pl.BlockSpec((1, 8, seq), lambda h, p: (h, 0, 0)),
                      pl.BlockSpec((seq, hd // 2), lambda h, p: (0, 0)),
                      pl.BlockSpec((seq, hd // 2), lambda h, p: (0, 0))],
            out_specs=[pl.BlockSpec((seq, 3 * hd), lambda h, p: (0, h))],
            scratch_shapes=[pltpu.VMEM((seq, hd), F32), pltpu.VMEM((seq, hd), F32), pltpu.VMEM((8, seq), F32)]),
        out_shape=[jax.ShapeDtypeStruct((seq, heads * 3 * hd), BF)],
        cost_estimate=pl.CostEstimate(flops=10 * heads * seq * seq * hd, bytes_accessed=20 * heads * seq * hd, transcendentals=heads * seq * seq),
        name="attend_backward",
    )(prefix, qkv, mixed, dmixed, lse, cos, sin)[0]


def rope_tables(count, head_dim):
    positions = jnp.arange(count, dtype=jnp.int32).astype(F32)
    frequency = 10000.0 ** (-(jnp.arange(head_dim // 2).astype(F32) * 2.0 / head_dim))
    angles = positions[:, None] * frequency[None, :]
    return jnp.cos(angles), jnp.sin(angles)


def rotate(values, cosine, sine):
    half = values.shape[-1] // 2
    a, b = values[..., :half], values[..., half:]
    return jnp.concatenate([a * cosine - b * sine, b * cosine + a * sine], axis=-1)


def norm(values):
    center = values - jnp.mean(values, axis=-1, keepdims=True)
    inv_std = lax.rsqrt(jnp.mean(center * center, axis=-1, keepdims=True) + EPSILON)
    return center * inv_std, inv_std


def norm_back(grad, normed, inv_std):
    mean_grad = jnp.mean(grad, axis=-1, keepdims=True)
    mean_cross = jnp.mean(grad * normed, axis=-1, keepdims=True)
    return inv_std * (grad - mean_grad - normed * mean_cross)


def mm(spec, left, right):
    return jnp.einsum(spec, left, right, preferred_element_type=F32)


def local(swap, inputs, prefix_len, w_qkv, w_out, w_up_gate, w_down, cotangent):
    rows = ("rmaj", "cmin") if swap else ("rmaj", "core")
    cols = ("cmaj", "core") if swap else ("cmaj", "cmin")

    def exchange(value):
        if not swap:
            return value
        return lax.ppermute(value, ("core", "cmin"), [(0, 0), (1, 2), (2, 1), (3, 3)])

    def scatter(value):
        return lax.psum_scatter(value.astype(BF), cols, scatter_dimension=0, tiled=True).astype(F32)

    def spread(value):
        return lax.all_to_all(value, cols, 1, 0, tiled=True)

    prefix_len = exchange(prefix_len)
    inputs, cotangent = exchange(inputs), exchange(cotangent)
    w_qkv, w_out = exchange(w_qkv), exchange(w_out)
    w_up_gate, w_down = exchange(w_up_gate), exchange(w_down)
    tokens = inputs.shape[0]
    heads, head_dim = w_qkv.shape[1], w_qkv.shape[2] // 3
    hidden_width = w_down.shape[0]
    full_in = lax.all_gather(inputs, cols, axis=1, tiled=True)
    width = full_in.shape[1]
    qkv_all = lax.all_gather(w_qkv, rows, axis=0, tiled=True).reshape(width, heads * 3 * head_dim)
    out_all = lax.all_gather(w_out, rows, axis=1, tiled=True)
    up_all = lax.all_gather(w_up_gate, rows, axis=0, tiled=True).reshape(width, 2 * hidden_width)
    down_all = lax.all_gather(w_down, rows, axis=1, tiled=True)
    cot_full = lax.all_gather(cotangent, cols, axis=1, tiled=True)
    piece = tokens // lax.axis_size(cols)
    first = lax.axis_index(cols) * piece
    own_in = lax.dynamic_slice_in_dim(full_in, first, piece, 0).astype(F32)
    own_cot = lax.dynamic_slice_in_dim(cot_full, first, piece, 0).astype(F32)

    normed_in = norm(full_in.astype(F32))[0].astype(BF)
    qkv_rows = mm("td,de->te", normed_in, qkv_all).reshape(tokens, heads, 3, head_dim)
    cosine, sine = rope_tables(tokens, head_dim)
    turned = rotate(qkv_rows[:, :, :2], cosine[:, None, None], sine[:, None, None])
    qkv = jnp.concatenate([turned, qkv_rows[:, :, 2:]], axis=2).astype(BF)
    qkv = qkv.reshape(tokens, heads * 3 * head_dim)
    mixed, lse = attend_fwd(qkv, prefix_len, heads, hd=head_dim)
    middle = own_in + scatter(mm("tc,cd->td", mixed, out_all))
    normed_two, inv_two = norm(middle)
    normed_mid = lax.all_gather(normed_two.astype(BF), cols, axis=0, tiled=True)
    gate_up = mm("td,df->tf", normed_mid, up_all)
    gate, up = gate_up[:, :hidden_width], gate_up[:, hidden_width:]
    sig = jax.nn.sigmoid(gate)
    active = gate * sig
    hidden = (active * up).astype(BF)
    outputs = middle + scatter(mm("tf,fd->td", hidden, down_all))
    outputs = exchange(spread(outputs.astype(BF)))

    grad_hidden = mm("td,fd->tf", cot_full, down_all)
    grad_gate = grad_hidden * up * sig * (1.0 + gate * (1.0 - sig))
    grad_gate_up = jnp.concatenate([grad_gate, grad_hidden * active], axis=1).astype(BF)
    grad_down = mm("tf,td->fd", hidden, cot_full).astype(BF)
    grad_down = lax.psum_scatter(grad_down, rows, scatter_dimension=1, tiled=True)
    grad_up = mm("td,tf->df", normed_mid, grad_gate_up).astype(BF)
    grad_up = lax.psum_scatter(grad_up, rows, scatter_dimension=0, tiled=True)
    grad_normed = scatter(mm("tf,df->td", grad_gate_up, up_all))
    grad_middle = own_cot + norm_back(grad_normed, normed_two, inv_two)
    grad_branch = lax.all_gather(grad_middle.astype(BF), cols, axis=0, tiled=True)
    grad_out = mm("tc,td->cd", mixed, grad_branch).astype(BF)
    grad_out = lax.psum_scatter(grad_out, rows, scatter_dimension=1, tiled=True)
    grad_mixed = mm("td,cd->tc", grad_branch, out_all).astype(BF)
    grad_rows = attend_bwd(qkv, mixed, grad_mixed, lse, prefix_len, cosine, sine, heads, hd=head_dim)
    grad_in = scatter(mm("te,de->td", grad_rows, qkv_all))
    grad_qkv = mm("td,te->de", normed_in, grad_rows).astype(BF)
    grad_qkv = lax.psum_scatter(grad_qkv, rows, scatter_dimension=0, tiled=True)
    normed_own, inv_own = norm(own_in)
    input_grad = grad_middle + norm_back(grad_in, normed_own, inv_own)
    input_grad = exchange(spread(input_grad.astype(BF))).astype(F32)
    return (
        outputs,
        input_grad,
        exchange(grad_qkv).astype(F32).reshape(-1, heads, 3 * head_dim),
        exchange(grad_out).astype(F32),
        exchange(grad_up).astype(F32).reshape(-1, 2, hidden_width),
        exchange(grad_down).astype(F32),
    )


AXES = ("y", "core", "zh", "zl", "x")
GROUP = ("core", "zl", "x")
MESH = pl.DeviceIdType.MESH
DMA = pltpu.SemaphoreType.DMA
VMEM_WHOLE = pl.BlockSpec(memory_space=pltpu.VMEM)
ANYWHERE = pl.BlockSpec(memory_space=pl.ANY)


class Place:
    def __init__(self):
        self.y, self.c, self.zh, self.zl, self.x = (lax.axis_index(name) for name in AXES)
        y, c, zh, zl, x = self.y, self.c, self.zh, self.zl, self.x
        self.sibling = (y, 1 - c, zh, zl, x)
        self.across = (y, c, zh, zl, 1 - x)
        self.along = (y, c, zh, 1 - zl, x)
        self.beyond = (1 - y, c, zh, zl, x)
        self.far = [(y, core, 1 - zh, zl, x) for core in (0, 1)]
        self.far_role = (y, zh, 1 - zh, zl, x)
        self.straight = c == zh
        self.outer = zl == zh
        self.order = [2 * y, 2 * y + 1, 2 * (1 - y), 2 * (1 - y) + 1]
        self.block = c * 4 + zl * 2 + x

    def chip(self, dz, dx):
        return lax.rem(self.zl + dz, 2) * 2 + lax.rem(self.x + dx, 2)

    def meet(self, greet=None):
        devices = [self.sibling, self.across, self.along, self.beyond, *self.far]
        barrier = pltpu.get_barrier_semaphore()
        for device in devices:
            pl.semaphore_signal(barrier, inc=1, device_id=device, device_id_type=MESH)
        more = greet(self, barrier) if greet else 0
        pl.semaphore_wait(barrier, len(devices) + more)


def span(start, size):
    return pl.ds(pl.multiple_of(start, size), size)


def remote(src, dst, send_sem, recv_sem, device):
    return pltpu.make_async_remote_copy(
        src_ref=src, dst_ref=dst, send_sem=send_sem, recv_sem=recv_sem, device_id=device, device_id_type=MESH
    )


class Beyond:
    along_z = False

    def __init__(self, place, src, dst, sem):
        self.copy = remote(src, dst, sem.at[0], sem.at[2], place.beyond)

    def start(self):
        self.copy.start()

    def wait_recv(self):
        self.copy.wait_recv()

    def wait_send(self):
        self.copy.wait_send()


class WeightHalf:
    along_z = True

    def __init__(self, place, src, dst, sem):
        c = place.c
        self.straight = place.straight
        self.outward = remote(src, dst.at[c], sem.at[0], sem.at[2 + c], place.far_role)
        self.aside = remote(src, dst.at[c], sem.at[1], sem.at[2 + c], place.sibling)
        self.here = pltpu.make_async_copy(src, dst.at[c], sem.at[1])
        self.from_sibling = remote(src, dst.at[1 - c], sem.at[1], sem.at[3 - c], place.sibling)
        self.from_far = [remote(src, dst.at[i], sem.at[0], sem.at[2 + i], place.far_role) for i in (0, 1)]

    def start(self):
        self.outward.start()

        @pl.when(self.straight)
        def _():
            self.here.start()

        @pl.when(jnp.logical_not(self.straight))
        def _():
            self.aside.start()

    def wait_recv(self):
        @pl.when(self.straight)
        def _():
            self.here.wait()
            self.from_sibling.wait_recv()

        @pl.when(jnp.logical_not(self.straight))
        def _():
            for copy in self.from_far:
                copy.wait_recv()

    def wait_send(self):
        self.outward.wait_send()

        @pl.when(jnp.logical_not(self.straight))
        def _():
            self.aside.wait_send()


class GradHalf:
    along_z = True

    def __init__(self, place, src, dst, sem):
        c, zh = place.c, place.zh
        self.straight = place.straight
        self.here = pltpu.make_async_copy(src.at[c], dst.at[zh], sem.at[0])
        self.aside = remote(src.at[1 - c], dst.at[zh], sem.at[1], sem.at[2 + zh], place.sibling)
        self.outward = [remote(src.at[i], dst.at[zh], sem.at[i], sem.at[2 + zh], place.far[i]) for i in (0, 1)]
        self.from_sibling = remote(src.at[c], dst.at[zh], sem.at[1], sem.at[2 + zh], place.sibling)
        self.from_far = remote(src.at[c], dst.at[1 - zh], sem.at[0], sem.at[3 - zh], place.far[0])

    def start(self):
        @pl.when(self.straight)
        def _():
            self.here.start()
            self.aside.start()

        @pl.when(jnp.logical_not(self.straight))
        def _():
            for copy in self.outward:
                copy.start()

    def wait_recv(self):
        self.from_far.wait_recv()

        @pl.when(self.straight)
        def _():
            self.here.wait()

        @pl.when(jnp.logical_not(self.straight))
        def _():
            self.from_sibling.wait_recv()

    def wait_send(self):
        @pl.when(self.straight)
        def _():
            self.aside.wait_send()

        @pl.when(jnp.logical_not(self.straight))
        def _():
            for copy in self.outward:
                copy.wait_send()


KINDS = {"beyond": Beyond, "weight": WeightHalf, "grad": GradHalf}


def moved_shape(kind, src):
    shape = (2, *src.shape) if kind == "weight" else src.shape
    return jax.ShapeDtypeStruct(shape, src.dtype)


class Under:
    def __init__(self, place, moves):
        self.place, self.moves = place, moves
        self.z = [move for kind, move in moves if move.along_z]
        self.y = [move for kind, move in moves if not move.along_z and not isinstance(kind, int)]
        self.follow = [(moves[kind][1], move) for kind, move in moves if isinstance(kind, int)]

    def start_y(self):
        for move in self.y:
            move.start()

    def start_z(self, outer=None):
        def start():
            for move in self.z:
                move.start()

        if outer is None:
            start()
        else:
            pl.when(self.place.outer if outer else jnp.logical_not(self.place.outer))(start)

    def start_follow(self):
        for ahead, move in self.follow:
            ahead.wait_recv()
            move.start()

    def end(self, skip=0):
        done = [ahead for ahead, _ in self.follow]
        for _, move in self.moves[skip:]:
            if move not in done:
                move.wait_recv()


def comm_call(
    body, name, ident, inputs, outs, scratch, moves=(), flops=0, transcendentals=0, spaces=None, greet=None
):
    n_in, n_out, n_move = len(inputs), len(outs), len(moves)
    own_source = [i for i, (kind, _) in enumerate(moves) if not isinstance(kind, int)]

    def kernel(*refs):
        ins, refs = refs[:n_in], refs[n_in:]
        sources, refs = refs[:len(own_source)], refs[len(own_source):]
        results, refs = refs[:n_out], refs[n_out:]
        targets, refs = refs[:n_move], refs[n_move:]
        sems, rest = refs[0], refs[1:]
        place = Place()
        place.meet(greet)
        made = []
        for i, (kind, _) in enumerate(moves):
            if isinstance(kind, int):
                made.append((kind, Beyond(place, targets[kind], targets[i], sems.at[i])))
            else:
                made.append((kind, KINDS[kind](place, sources[own_source.index(i)], targets[i], sems.at[i])))
        body(place, ins, results, rest, Under(place, made), targets)
        for _, move in made:
            move.wait_send()

    arrays = [*inputs, *(moves[i][1] for i in own_source)]
    shapes = list(outs)
    moved = []
    for kind, array in moves:
        moved.append(moved[kind] if isinstance(kind, int) else moved_shape(kind, array))
    shapes += moved
    in_specs = (spaces or [VMEM_WHOLE] * n_in) + [ANYWHERE] * len(own_source)
    size = sum(s.size * s.dtype.itemsize for s in (*arrays, *shapes))
    result = pl.pallas_call(
        kernel,
        out_shape=shapes,
        in_specs=in_specs,
        out_specs=[VMEM_WHOLE] * (n_out + n_move),
        scratch_shapes=[DMA((max(n_move, 1), 4)), *scratch],
        compiler_params=pltpu.CompilerParams(collective_id=ident, has_side_effects=True, vmem_limit_bytes=63 << 20),
        cost_estimate=pl.CostEstimate(
            flops=flops + (20 << 30), bytes_accessed=size, transcendentals=transcendentals
        ),
        name=name,
    )(*arrays)
    return result[:n_out], result[n_out:]


def each_rows(count, body, size=32):
    def step(i, carry):
        body(span(i * size, size))
        return carry

    lax.fori_loop(0, count // size, step, 0)


def row_norm(values):
    center = values - jnp.mean(values, axis=-1, keepdims=True)
    inv_std = lax.rsqrt(jnp.mean(center * center, axis=-1, keepdims=True) + EPSILON)
    return center * inv_std, inv_std


SLICES = 4


def reduce_sems():
    return [DMA((4,)), DMA((4,)), DMA((3, SLICES)), DMA((3, SLICES))]


def reduce_scratch(piece, width):
    return [pltpu.VMEM((count, piece, width), BF) for count in (4, 4, 2, 3, 3)] + reduce_sems()


def nothing():
    pass


def reduce_body(place, compute, last, scratch, begin=nothing, before_z=nothing, after_z=nothing):
    sib_out, sib_in, own, near_out, near_in, sib_send, sib_recv, near_send, near_recv = scratch
    piece = own.shape[1]
    c = place.c
    size = piece // SLICES
    begin()

    def sib_copy(step):
        return remote(sib_out.at[step], sib_in.at[step], sib_send.at[step], sib_recv.at[step], place.sibling)

    def near_copy(step, r):
        device = place.along if step == 2 else place.across
        rows = span(r * size, size)
        return remote(
            near_out.at[step, rows], near_in.at[step, rows], near_send.at[step, r], near_recv.at[step, r], device
        )

    def finish(step):
        slot = step % 2
        sib_copy(step).wait_recv()

        def send(r, carry):
            if step == 2:
                near_copy(0, r).wait_recv()
            rows = span(r * size, size)
            total = own[slot, rows, :].astype(F32) + sib_in[step, rows, :].astype(F32)
            if step == 2:
                total = total + near_in[0, rows, :].astype(F32)
            near_out[step, rows, :] = total.astype(BF)
            near_copy(step, r).start()
            return carry

        lax.fori_loop(0, SLICES, send, 0)

    def step(s, carry):
        target = place.chip(1 - lax.rem(s, 2), 1 - s // 2)
        compute((1 - c) * 4 + target, sib_out.at[s])
        sib_copy(s).start()
        for index in (0, 1):
            @pl.when(s == index + 1)
            def _(index=index):
                finish(index)

        compute(c * 4 + target, own.at[lax.rem(s, 2)])
        return carry

    lax.fori_loop(0, 4, step, 0)
    before_z()
    finish(2)
    after_z()
    sib_copy(3).wait_recv()

    def arrive(r, carry):
        near_copy(1, r).wait_recv()
        near_copy(2, r).wait_recv()

        def final(i, carry):
            rows = span(r * size + i * 16, 16)
            total = own[1, rows, :].astype(F32) + sib_in[3, rows, :].astype(F32)
            last(rows, total + near_in[1, rows, :].astype(F32) + near_in[2, rows, :].astype(F32))
            return carry

        return lax.fori_loop(0, size // 16, final, carry)

    lax.fori_loop(0, SLICES, arrive, 0)
    for s in range(4):
        sib_copy(s).wait_send()

    def sent(r, carry):
        for s in range(3):
            near_copy(s, r).wait_send()
        return carry

    lax.fori_loop(0, SLICES, sent, 0)


def product(place, left_ref, weights, transposed):
    def compute(owner, out_ref):
        piece = out_ref.shape[0]
        left = left_ref[span(owner * piece, piece), :]
        for weight, index in zip(weights, place.order):
            size = weight.shape[0] if transposed else weight.shape[1]
            part = dot(left, weight[...], NT if transposed else NN)
            out_ref[:, span(index * size, size)] = part.astype(out_ref.dtype)

    return compute


def back_rows(base, value, total):
    normed, inv_std = row_norm(value)
    mean_grad = jnp.mean(total, axis=-1, keepdims=True)
    mean_cross = jnp.mean(total * normed, axis=-1, keepdims=True)
    return base + inv_std * (total - mean_grad - normed * mean_cross)


def quarters(first, second):
    return [first.at[0], first.at[1], second.at[0], second.at[1]]


def beside(under):
    def begin():
        under.start_y()
        under.start_z()

    return dict(begin=begin, after_z=under.start_follow)


def down_call(hidden, firsts, seconds, middle, moves, ident):
    piece, width = middle.shape

    def body(place, ins, outs, scratch, under, targets):
        hidden_ref, first_a, first_b, second_a, second_b, base_ref = ins
        parts = list(zip(quarters(first_a, second_a), quarters(first_b, second_b), place.order))

        def compute(owner, out_ref):
            rows = span(owner * piece, piece)
            for upper, lower, index in parts:
                depth, size = upper.shape
                part = dot(hidden_ref[rows, 0:depth], upper[...], NN) + dot(hidden_ref[rows, depth:], lower[...], NN)
                out_ref[:, span(index * size, size)] = part.astype(out_ref.dtype)

        def last(rows, total):
            outs[0][rows, :] = (base_ref[rows, :] + total).astype(BF)

        reduce_body(place, compute, last, scratch, **beside(under))
        under.end()

    return comm_call(
        body, "reduce_down", ident, [hidden, *firsts, *seconds, middle], [jax.ShapeDtypeStruct((piece, width), BF)],
        reduce_scratch(piece, width), moves, flops=2 * hidden.size * width,
    )


def input_call(grad_rows, halves, grad_middle, own_in, ready, moves, ident):
    piece, width = own_in.shape

    def body(place, ins, outs, scratch, under, targets):
        rows_ref, first, second, base_ref, value_ref, ready_ref = ins
        spread = Spread(place, ready_ref, outs[1], scratch[:3])

        def last(rows, total):
            outs[0][rows, :] = back_rows(base_ref[rows, :], value_ref[rows, :].astype(F32), total).astype(BF)

        def after_z():
            under.start_follow()
            spread.start()

        hooks = dict(beside(under), after_z=after_z)
        reduce_body(place, product(place, rows_ref, quarters(first, second), True), last, scratch[3:], **hooks)
        under.end()
        spread.wait()

    return comm_call(
        body, "reduce_input", ident, [grad_rows, *halves, grad_middle, own_in, ready],
        [jax.ShapeDtypeStruct((piece, width), BF), spread_shape(ready)],
        [*spread_scratch(), *reduce_scratch(piece, width)], moves, flops=2 * grad_rows.size * width,
        greet=spread_greet,
    )


def middle_call(cot, slopes, gates, ups, downs, down_last, moves, middle, ident):
    piece, width = middle.shape
    tokens, part_width = cot.shape[0], down_last.shape[1]
    hidden = 2 * part_width
    tile = 256
    tiles = part_width // tile

    def body(place, ins, outs, scratch, under, targets):
        cot_ref, slopes_ref, ga1, ga2, gb1, gb2, ua1, ua2, ub1, ub2, value_ref, da1, da2, db1 = ins
        total_ref, branch_ref, grad_ref = outs
        load_sem, *rest = scratch
        under.start_y()
        load = pltpu.make_async_copy(slopes_ref, grad_ref, load_sem.at[0])
        load.start()
        load.wait()
        rows_in = (quarters(da1, da2), quarters(db1, targets[0]))

        def fill(owner, part):
            rows = span(owner * piece, piece)

            def step(t, carry):
                grad = None
                for weight, index in zip(rows_in[part], place.order):
                    size = weight.shape[1]
                    term = dot(cot_ref[rows, span(index * size, size)], weight[span(t * tile, tile), :], NT)
                    grad = term if grad is None else grad + term
                for offset in (0, hidden):
                    cols = span(offset + part * part_width + t * tile, tile)
                    grad_ref[rows, cols] = (grad * grad_ref[rows, cols].astype(F32)).astype(BF)
                return carry

            lax.fori_loop(0, tiles, step, 0)

        def fill_first(i, carry):
            fill(i, 0)
            return carry

        lax.fori_loop(0, tokens // piece, fill_first, 0)
        under.moves[0][1].wait_recv()
        columns = [quarters(ga1, ga2), quarters(gb1, gb2), quarters(ua1, ua2), quarters(ub1, ub2)]

        def compute(owner, out_ref):
            rows = span(owner * piece, piece)
            fill(owner, 1)
            for quarter, index in enumerate(place.order):
                total = None
                for i, weights in enumerate(columns):
                    weight = weights[quarter]
                    size = weight.shape[0]
                    term = dot(grad_ref[rows, i * part_width:(i + 1) * part_width], weight[...], NT)
                    total = term if total is None else total + term
                out_ref[:, span(index * size, size)] = total.astype(out_ref.dtype)

        def last(rows, total):
            base = cot_ref[own_rows(rows), :].astype(F32)
            grad = back_rows(base, value_ref[rows, :], total)
            total_ref[rows, :] = grad
            branch_ref[rows, :] = grad.astype(BF)

        def own_rows(rows):
            return pl.ds(pl.multiple_of(place.block * piece + rows.start, 16), rows.size)

        reduce_body(place, compute, last, rest)
        under.end(skip=1)

    shape = functools.partial(jax.ShapeDtypeStruct, (piece, width))
    return comm_call(
        body, "reduce_middle", ident, [cot, slopes, *gates, *ups, middle, *downs, down_last],
        [shape(F32), shape(BF), jax.ShapeDtypeStruct((tokens, 2 * hidden), BF)],
        [DMA((1,)), *reduce_scratch(piece, width)],
        moves, flops=6 * tokens * hidden * width,
        spaces=[VMEM_WHOLE, ANYWHERE] + [VMEM_WHOLE] * 12,
    )


def gather_scratch():
    return [DMA((3, SLICES)), DMA((3, SLICES)), DMA((4,)), DMA((4,))]


def gather_body(place, own_ref, full, sems, process, begin=nothing, follow=nothing):
    near_send, near_recv, sib_send, sib_recv = sems
    piece = own_ref.shape[0]
    size = piece // SLICES
    c = place.c

    def near_copy(slot, r, target):
        where = full.at[span((c * 4 + target) * piece + r * size, size)]
        device = place.along if slot == 2 else place.across
        return remote(where, where, near_send.at[slot, r], near_recv.at[slot, r], device)

    def sib_copy(slot, core, target):
        where = full.at[span((core * 4 + target) * piece, piece)]
        return remote(where, where, sib_send.at[slot], sib_recv.at[slot], place.sibling)

    def slices(act):
        def step(r, carry):
            act(r)
            return carry

        lax.fori_loop(0, SLICES, step, 0)

    mine, x_chip, z_chip, d_chip = place.chip(0, 0), place.chip(0, 1), place.chip(1, 0), place.chip(1, 1)
    full[span((c * 4 + mine) * piece, piece), :] = own_ref[...]
    slices(lambda r: near_copy(2, r, mine).start())
    slices(lambda r: near_copy(1, r, mine).start())
    sib_copy(3, c, mine).start()
    begin()

    def forward(r):
        near_copy(2, r, z_chip).wait_recv()
        near_copy(0, r, z_chip).start()

    process(c * 4 + mine)
    forward(0)
    sib_copy(3, 1 - c, mine).wait_recv()
    process((1 - c) * 4 + mine)
    forward(1)
    slices(lambda r: near_copy(1, r, x_chip).wait_recv())
    sib_copy(1, c, x_chip).start()
    process(c * 4 + x_chip)
    for r in range(2, SLICES):
        forward(r)
    sib_copy(2, c, z_chip).start()
    sib_copy(1, 1 - c, x_chip).wait_recv()
    process((1 - c) * 4 + x_chip)
    process(c * 4 + z_chip)
    follow()
    sib_copy(2, 1 - c, z_chip).wait_recv()
    process((1 - c) * 4 + z_chip)
    slices(lambda r: near_copy(0, r, d_chip).wait_recv())
    sib_copy(0, c, d_chip).start()
    process(c * 4 + d_chip)
    sib_copy(0, 1 - c, d_chip).wait_recv()
    process((1 - c) * 4 + d_chip)
    for slot in range(3):
        slices(lambda r: near_copy(slot, r, mine).wait_send())
    for slot in range(4):
        sib_copy(slot, c, mine).wait_send()


def mix_call(own, halves, tokens, moves, ident):
    width = own.shape[1]
    inner = halves[0].shape[1]

    def body(place, ins, outs, scratch, under, targets):
        own_ref, first, second = ins
        full, mixed_ref = outs
        piece = own_ref.shape[0]

        def process(owner):
            rows = span(owner * piece, piece)
            total = None
            for weight, index in zip(quarters(first, second), place.order):
                size = weight.shape[1]
                part = dot(full[rows, span(index * size, size)], weight[...], NT)
                total = part if total is None else total + part
            mixed_ref[rows, :] = total.astype(BF)

        def begin():
            under.start_y()
            under.start_z()

        gather_body(place, own_ref, full, scratch, process, begin, under.start_follow)
        under.end()

    return comm_call(
        body, "gather_mix", ident, [own, *halves],
        [jax.ShapeDtypeStruct((tokens, width), BF), jax.ShapeDtypeStruct((tokens, inner), BF)],
        gather_scratch(), moves, flops=2 * tokens * inner * width,
    )


class ColumnGather:
    def __init__(self, place, src, full, sems):
        self.place, self.src, self.full = place, src, full
        self.near_send, self.near_recv, self.sib_send, self.sib_recv, self.own = sems
        self.width = src.shape[1]
        self.size = src.shape[0] // SLICES

    def where(self, core, target):
        return span((core * 4 + target) * self.width, self.width)

    def near(self, slot, r, target, first=False):
        place = self.place
        rows = pl.ds(r * self.size, self.size)
        dst = self.full.at[rows, self.where(place.c, target)]
        src = self.src.at[rows] if first else dst
        device = place.along if slot == 2 else place.across
        return remote(src, dst, self.near_send.at[slot, r], self.near_recv.at[slot, r], device)

    def sib(self, slot, core, target, first=False):
        dst = self.full.at[:, self.where(core, target)]
        src = self.src if first else dst
        return remote(src, dst, self.sib_send.at[slot], self.sib_recv.at[slot], self.place.sibling)

    def chips(self):
        place = self.place
        return place.chip(0, 0), place.chip(0, 1), place.chip(1, 0), place.chip(1, 1)

    def own_copy(self):
        return pltpu.make_async_copy(self.src, self.full.at[:, self.where(self.place.c, self.chips()[0])], self.own.at[0])

    def start(self):
        mine = self.chips()[0]
        self.own_copy().start()
        for slot in (2, 1):
            for r in range(SLICES):
                self.near(slot, r, mine, True).start()
        self.sib(3, self.place.c, mine, True).start()

    def forward(self, r):
        z_chip = self.chips()[2]
        self.near(2, r, z_chip).wait_recv()
        self.near(0, r, z_chip).start()

    def finish(self):
        mine, x_chip, z_chip, d_chip = self.chips()
        c = self.place.c
        self.sib(2, c, z_chip).start()
        for r in range(SLICES):
            self.near(1, r, x_chip).wait_recv()
        self.sib(1, c, x_chip).start()
        for r in range(SLICES):
            self.near(0, r, d_chip).wait_recv()
        self.sib(0, c, d_chip).start()
        self.own_copy().wait()
        for slot, target in enumerate((d_chip, x_chip, z_chip, mine)):
            self.sib(slot, 1 - c, target).wait_recv()
            self.sib(slot, c, mine).wait_send()
        for slot in range(3):
            for r in range(SLICES):
                self.near(slot, r, mine).wait_send()


def attend_back_call(qkv, mixed, grad_mixed, lse, prefix, tables, heads, hd, moves, ident):
    seq = qkv.shape[0]
    bq = bk = min(512, seq // 2)
    scale = hd ** -0.5
    half = hd // 2

    def body(place, ins, outs, scratch, under, targets):
        qkv_ref, o_ref, do_ref, lse_ref, prefix_ref, cos_ref, sin_ref = ins
        (out_ref,) = outs
        under.start_y()
        under.start_z()
        dk_ref, dv_ref = scratch
        bound = prefix_ref[0:1, 0:1]

        def unrotate(g, rows):
            return g * cos_ref[rows, :] - pltpu.roll(g, half, 1) * sin_ref[rows, :]

        def head(h, carry):
            base = h * 3 * hd
            own = span(h * hd, hd)
            dk_ref[...] = jnp.zeros_like(dk_ref)
            dv_ref[...] = jnp.zeros_like(dv_ref)
            for i in range(seq // bq):
                first = i * bq
                rows = pl.ds(first, bq)
                q = qkv_ref[rows, span(base, hd)]
                do = do_ref[rows, own]
                row_sums = (do.astype(F32) * o_ref[rows, own].astype(F32)).T
                delta = jnp.sum(row_sums, axis=0, keepdims=True)
                tops = lse_ref[h, 0:1, first:first + bq]
                total = max(i + 1, seq // 2 // bk)

                def step(masked, j, dq, first=first, q=q, do=do, delta=delta, tops=tops):
                    keys = span(j * bk, bk)
                    k = qkv_ref[keys, span(base + hd, hd)]
                    v = qkv_ref[keys, span(base + 2 * hd, hd)]
                    p = jnp.exp(dot(k, q, NT) * scale - tops)
                    if masked:
                        kp = j * bk + lax.broadcasted_iota(jnp.int32, (bk, bq), 0)
                        qp = first + lax.broadcasted_iota(jnp.int32, (bk, bq), 1)
                        p = jnp.where(kp < jnp.maximum(qp + 1, bound), p, 0.0)
                    dv_ref[keys, :] += dot(p.astype(BF), do, NN)
                    ds = (p * (dot(v, do, NT) - delta)).astype(BF)
                    dk_ref[keys, :] += dot(ds, q, NN)
                    return dq + dot(ds, k, TN)

                dq = lax.fori_loop(0, i, functools.partial(step, False), jnp.zeros((bq, hd), F32))
                dq = lax.fori_loop(i, total, functools.partial(step, True), dq)
                out_ref[rows, span(base, hd)] = unrotate(dq * scale, rows).astype(BF)

            def fin(i, carry):
                rows = span(i * bq, bq)
                out_ref[rows, span(base + hd, hd)] = unrotate(dk_ref[rows, :] * scale, rows).astype(BF)
                out_ref[rows, span(base + 2 * hd, hd)] = dv_ref[rows, :].astype(BF)
                return carry

            return lax.fori_loop(0, seq // bq, fin, carry)

        lax.fori_loop(0, heads, head, 0)
        under.start_follow()
        under.end()

    return comm_call(
        body, "attend_back", ident, [qkv, mixed, grad_mixed, lse, prefix, *tables],
        [jax.ShapeDtypeStruct(qkv.shape, BF)],
        [pltpu.VMEM((seq, hd), F32), pltpu.VMEM((seq, hd), F32)],
        moves, flops=10 * heads * seq * seq * hd, transcendentals=heads * seq * seq,
    )


def front_call(inputs, cot, prefix, tables, weights, heads, hd, ident):
    names = ("qkv", "out", "ga", "gb", "ua", "ub", "da", "db")
    tokens, slice_width = inputs.shape
    width = slice_width * 8
    piece = tokens // 8
    size = tokens // SLICES
    inner = weights[0].shape[1]
    part_width = weights[2].shape[1]
    hidden = 2 * part_width
    tile = 256
    bq = bk = min(512, tokens // 2)
    scale = hd ** -0.5

    def kernel(in_ref, cot_ref, prefix_ref, cos_ref, sin_ref, *refs):
        sources, refs = refs[:8], refs[8:]
        firsts, seconds, refs = refs[:8], refs[8:15], refs[15:]
        (qkv_ref, mixed_ref, lse_ref, own_in_ref, middle_ref, normed_in_out, cot_out, normed_mid_out, hidden_out,
         slopes_out), refs = refs[:10], refs[10:]
        (arena, acc, block_ref, normed_own, w_qkv, w_out, w_ga, w_gb, w_ua, w_ub, z_sems, y_sems, load_sems, out_sems,
         swap_send, swap_recv, phase, *sems) = refs
        start_sems, gather_sems, reduce_sems_, feed_sems = sems[:5], sems[5:10], sems[10:14], sems[14:]
        place = Place()
        c, zl, x = place.c, place.zl, place.x
        place.meet()
        z_moves = {n: WeightHalf(place, sources[i], firsts[i], z_sems.at[i]) for i, n in enumerate(names)}
        y_moves = {n: Beyond(place, firsts[i], seconds[i], y_sems.at[i]) for i, n in enumerate(names[:7])}
        held = dict(qkv=w_qkv, out=w_out, ga=w_ga, gb=w_gb, ua=w_ua, ub=w_ub)

        def go(name):
            z_moves[name].start()

        def pass_on(name):
            z_moves[name].wait_recv()
            y_moves[name].start()

        def half_load(name, side):
            i = names.index(name)
            source = (firsts, seconds)[side][i]
            return pltpu.make_async_copy(source, held[name].at[side], load_sems.at[i, side])

        def load_first(name):
            half_load(name, 0).start()

        def load_second(name):
            y_moves[name].wait_recv()
            half_load(name, 1).start()

        def parts(name):
            return [held[name].at[side, i] for side in (0, 1) for i in (0, 1)]

        full, normed = arena.at[pl.ds(0, tokens)], arena.at[pl.ds(tokens, tokens)]
        gather = ColumnGather(place, in_ref, full, start_sems)
        crossed = jnp.logical_not(place.straight)
        partner = (place.y, 1 - c, 1 - place.zh, zl, x)
        mine, x_chip, z_chip, d_chip = gather.chips()
        def rows_of(r):
            return pl.ds(r * size, size)

        def swap_copy(r, core):
            where = full.at[rows_of(r), gather.where(core, mine)]
            return remote(in_ref.at[rows_of(r)], where, swap_send.at[r], swap_recv.at[r], partner)

        def own_copy(r):
            where = full.at[rows_of(r), gather.where(c, mine)]
            return pltpu.make_async_copy(in_ref.at[rows_of(r)], where, swap_send.at[r])

        def cot_swap():
            return remote(cot_ref, block_ref, swap_send.at[SLICES], swap_recv.at[SLICES], partner)

        def cot_own():
            return pltpu.make_async_copy(cot_ref, block_ref, swap_send.at[SLICES])

        def sib(slot, r, core, target):
            where = full.at[rows_of(r), gather.where(core, target)]
            return remote(where, where, start_sems[2].at[slot, r], start_sems[3].at[slot, r], place.sibling)

        @pl.when(place.straight)
        def _():
            for r in range(SLICES):
                own_copy(r).start()
            cot_own().start()

        @pl.when(crossed)
        def _():
            for r in range(SLICES):
                swap_copy(r, 1 - c).start()

        for r in range(SLICES):
            @pl.when(place.straight)
            def _(r=r):
                own_copy(r).wait()

            @pl.when(crossed)
            def _(r=r):
                swap_copy(r, c).wait_recv()

            gather.near(2, r, mine).start()
            gather.near(1, r, mine).start()
            sib(3, r, c, mine).start()
        for r in range(SLICES):
            gather.forward(r)
            sib(2, r, c, z_chip).start()
            gather.near(1, r, x_chip).wait_recv()
            sib(1, r, c, x_chip).start()
            if r == 0:
                go("qkv")
        pass_on("qkv")
        load_first("qkv")
        go("out")
        pl.when(crossed)(lambda: cot_swap().start())
        half_load("qkv", 0).wait()
        depth = w_qkv.shape[2]
        for r in range(SLICES):
            gather.near(0, r, d_chip).wait_recv()
            sib(0, r, c, d_chip).start()
            for slot, target in enumerate((d_chip, x_chip, z_chip, mine)):
                sib(slot, r, 1 - c, target).wait_recv()

            def norm_rows(i, carry, r=r):
                rows = span(r * size + i * 16, 16)
                normed[rows, :] = row_norm(full[rows, :].astype(F32))[0].astype(BF)
                return carry

            lax.fori_loop(0, size // 16, norm_rows, 0)
            pltpu.make_async_copy(normed.at[rows_of(r)], normed_in_out.at[rows_of(r)], out_sems.at[r]).start()
            total = None
            for weight, index in zip(parts("qkv")[:2], place.order[:2]):
                term = dot(normed[rows_of(r), span(index * depth, depth)], weight[...], NN)
                total = term if total is None else total + term
            acc[rows_of(r), :] = total
        own_in_ref[...] = full[span(place.block * piece, piece), :]
        load_second("qkv")
        half_load("qkv", 1).wait()
        go("ga")
        half = size // 2

        def project(r, carry):
            rows = span(r * half, half)
            total = acc[rows, :]
            for weight, index in zip(parts("qkv")[2:], place.order[2:]):
                total = total + dot(normed[rows, span(index * depth, depth)], weight[...], NN)
            cos, sin = cos_ref[rows, :], sin_ref[rows, :]
            for h in range(heads):
                for part in range(3):
                    value = total[:, (3 * h + part) * hd:(3 * h + part + 1) * hd]
                    if part < 2:
                        value = value * cos + pltpu.roll(value, hd // 2, 1) * sin
                    qkv_ref[rows, pl.ds((3 * h + part) * hd, hd)] = value.astype(BF)
            return carry

        lax.fori_loop(0, tokens // half, project, 0)
        pass_on("out")
        load_first("out")

        @pl.when(place.straight)
        def _():
            cot_own().wait()

        @pl.when(crossed)
        def _():
            cot_swap().wait_recv()
            cot_swap().wait_send()
            for r in range(SLICES):
                swap_copy(r, 1 - c).wait_send()

        cot_gather = ColumnGather(place, block_ref, cot_out, gather_sems)
        cot_gather.start()
        bound = prefix_ref[0:1, 0:1]

        def head(h, carry):
            base = h * 3 * hd
            for i in range(tokens // bq):
                first = i * bq
                q = qkv_ref[first:first + bq, span(base, hd)]
                count = max(i + 1, tokens // 2 // bk)

                def step(masked, j, state, first=first, q=q):
                    top, tot, out = state
                    rows = span(j * bk, bk)
                    s = dot(q, qkv_ref[rows, span(base + hd, hd)], NT) * scale
                    if masked:
                        kp = j * bk + lax.broadcasted_iota(jnp.int32, (bq, bk), 1)
                        qp = first + lax.broadcasted_iota(jnp.int32, (bq, bk), 0)
                        s = jnp.where(kp < jnp.maximum(qp + 1, bound), s, NEG)
                    new = jnp.maximum(top, jnp.max(s, axis=1, keepdims=True))
                    alpha = jnp.exp(top - new)
                    p = jnp.exp(s - new)
                    tot = tot * alpha + jnp.sum(p, axis=1, keepdims=True)
                    out = out * alpha + dot(p.astype(BF), qkv_ref[rows, span(base + 2 * hd, hd)], NN)
                    return new, tot, out

                state = (jnp.full((bq, 1), NEG, F32), jnp.zeros((bq, 1), F32), jnp.zeros((bq, hd), F32))
                state = lax.fori_loop(0, i, functools.partial(step, False), state)
                top, tot, out = lax.fori_loop(i, count, functools.partial(step, True), state)
                mixed_ref[first:first + bq, span(h * hd, hd)] = (out / tot).astype(BF)
                lse = jnp.broadcast_to(top + jnp.log(tot), (bq, 128))
                lse_ref[h, :, first:first + bq] = lse.T[0:8, :]
            return carry

        lax.fori_loop(0, heads, head, 0)
        go("gb")
        load_second("out")
        half_load("out", 0).wait()
        half_load("out", 1).wait()
        cot_gather.forward(0)
        pass_on("ga")

        for r in range(SLICES):
            pltpu.make_async_copy(normed.at[rows_of(r)], normed_in_out.at[rows_of(r)], out_sems.at[r]).wait()
            for slot in range(3):
                gather.near(slot, r, mine).wait_send()
            for slot in range(4):
                sib(slot, r, c, mine).wait_send()
        for device in (place.sibling, place.across, place.along):
            pl.semaphore_signal(phase, inc=1, device_id=device, device_id_type=MESH)
        pl.semaphore_wait(phase, 3)

        class Blocks:
            def __init__(self, first, count):
                self.first, self.shape = first, (count, piece, width)

            def rows(self, index):
                if isinstance(index, tuple):
                    step, inside, *rest = index
                    start = (self.first + step) * piece + inside.start
                    return (pl.ds(pl.multiple_of(start, 16), inside.size), *rest)
                return (span((self.first + index) * piece, piece),)

            @property
            def at(self):
                return At(self)

            def __getitem__(self, index):
                return arena[self.rows(index)]

            def __setitem__(self, index, value):
                arena[self.rows(index)] = value

        class At:
            def __init__(self, blocks):
                self.blocks = blocks

            def __getitem__(self, index):
                return arena.at[self.blocks.rows(index)]

        buffers, first = [], 0
        for count in (4, 4, 2, 3, 3):
            buffers.append(Blocks(first, count))
            first += count

        def last(rows, total):
            middle = own_in_ref[rows, :].astype(F32) + total
            middle_ref[rows, :] = middle
            normed_own[rows, :] = row_norm(middle)[0].astype(BF)

        def before_z():
            go("ua")
            for r in range(1, SLICES):
                cot_gather.forward(r)

        def after_z():
            pass_on("gb")
            go("ub")
            load_first("ga")
            load_first("gb")
            load_second("ga")

        reduce_body(
            place, product(place, mixed_ref, parts("out"), False), last, [*buffers, *reduce_sems_],
            before_z=before_z, after_z=after_z,
        )

        full = arena.at[pl.ds(2 * tokens, tokens)]
        slopes_ref = arena.at[pl.ds(0, tokens)]
        hidden_ref = arena.at[pl.ds(tokens, tokens), pl.ds(0, hidden)]
        columns = (("ga", "ua"), ("gb", "ub"))
        waiting = []

        def fill(owner, which):
            rows = span(owner * piece, piece)
            gates, ups = (parts(name) for name in columns[which])

            def step(t, carry):
                taken = span(t * tile, tile)
                gate = up = None
                for gate_weight, up_weight, index in zip(gates, ups, place.order):
                    deep = gate_weight.shape[0]
                    value = full[rows, span(index * deep, deep)]
                    terms = dot(value, gate_weight[:, taken], NN), dot(value, up_weight[:, taken], NN)
                    gate, up = terms if gate is None else (gate + terms[0], up + terms[1])
                cols = span(which * part_width + t * tile, tile)
                up_cols = span(hidden + which * part_width + t * tile, tile)
                sig = 1.0 / (1.0 + jnp.exp(-gate))
                active = gate * sig
                hidden_ref[rows, cols] = (active * up).astype(BF)
                slopes_ref[rows, cols] = (up * sig * (1.0 + gate * (1.0 - sig))).astype(BF)
                slopes_ref[rows, up_cols] = active.astype(BF)
                return carry

            lax.fori_loop(0, part_width // tile, step, 0)

        def process(owner):
            waiting.append(owner)
            if len(waiting) == 1:
                for side in (0, 1):
                    half_load("ga", side).wait()
                pass_on("ua")
                load_second("gb")
                load_first("ua")
                load_second("ua")
                for side in (0, 1):
                    half_load("ua", side).wait()
            fill(owner, 0)
            if len(waiting) == 3:
                for side in (0, 1):
                    half_load("gb", side).wait()
                pass_on("ub")
                load_first("ub")
                go("db")
                load_second("ub")
                for side in (0, 1):
                    half_load("ub", side).wait()
                for i, earlier in enumerate(waiting):
                    fill(earlier, 1)
            elif len(waiting) > 3:
                fill(owner, 1)

        gather_body(place, normed_own, full, feed_sems, process, begin=lambda: go("da"))
        for i, (ref, out) in enumerate(((full, normed_mid_out), (hidden_ref, hidden_out), (slopes_ref, slopes_out))):
            pltpu.make_async_copy(ref, out, out_sems.at[SLICES + i]).start()
        pass_on("da")
        cot_gather.finish()
        z_moves["db"].wait_recv()
        y_moves["da"].wait_recv()
        for i, (ref, out) in enumerate(((full, normed_mid_out), (hidden_ref, hidden_out), (slopes_ref, slopes_out))):
            pltpu.make_async_copy(ref, out, out_sems.at[SLICES + i]).wait()
        for move in (*z_moves.values(), *y_moves.values()):
            move.wait_send()

    def half_shape(weight):
        return jax.ShapeDtypeStruct((2, *weight.shape), BF)

    shape = jax.ShapeDtypeStruct
    outs = [
        *(half_shape(weight) for weight in weights),
        *(half_shape(weight) for weight in weights[:7]),
        shape((tokens, inner), BF),
        shape((tokens, heads * hd), BF),
        shape((heads, 8, tokens), F32),
        shape((piece, width), BF),
        shape((piece, width), F32),
        shape((tokens, width), BF),
        shape((tokens, width), BF),
        shape((tokens, width), BF),
        shape((tokens, hidden), BF),
        shape((tokens, 2 * hidden), BF),
    ]
    column_sems = [DMA((3, SLICES)), DMA((3, SLICES)), DMA((4,)), DMA((4,)), DMA((1,))]
    start_sems = [DMA((3, SLICES)), DMA((3, SLICES)), DMA((4, SLICES)), DMA((4, SLICES)), DMA((1,))]
    result = pl.pallas_call(
        kernel,
        out_shape=outs,
        in_specs=[ANYWHERE, ANYWHERE, VMEM_WHOLE, VMEM_WHOLE, VMEM_WHOLE] + [ANYWHERE] * 8,
        out_specs=[ANYWHERE] * 15 + [VMEM_WHOLE] * 5 + [ANYWHERE] * 5,
        scratch_shapes=[
            pltpu.VMEM((3 * tokens, width), BF),
            pltpu.VMEM((tokens, inner), F32),
            pltpu.VMEM((tokens, slice_width), BF),
            pltpu.VMEM((piece, width), BF),
            *(pltpu.VMEM((2, 2, *weight.shape), BF) for weight in weights[:6]),
            DMA((8, 4)), DMA((8, 4)), DMA((8, 2)), DMA((SLICES + 3,)), DMA((SLICES + 1,)), DMA((SLICES + 1,)),
            pltpu.SemaphoreType.REGULAR,
            *start_sems, *column_sems, *reduce_sems(), *gather_scratch(),
        ],
        compiler_params=pltpu.CompilerParams(collective_id=ident, has_side_effects=True, vmem_limit_bytes=63 << 20),
        cost_estimate=pl.CostEstimate(
            flops=100 << 30, bytes_accessed=100 << 20, transcendentals=heads * tokens * tokens
        ),
        name="front",
    )(inputs, cot, prefix, *tables, *weights)
    return result[:8], result[8:15], result[15:]


BLOCKS = [(core, zl, x) for core in (0, 1) for zl in (0, 1) for x in (0, 1)]


def spread_greet(place, barrier):
    for core, zl, x in BLOCKS:
        mine = jnp.logical_and(place.straight, core * 4 + zl * 2 + x == place.block)

        @pl.when(jnp.logical_not(mine))
        def _(core=core, zl=zl, x=x):
            pl.semaphore_signal(
                barrier, inc=1, device_id=(place.y, core, place.c, zl, x), device_id_type=MESH
            )

    return 8 - jnp.where(place.straight, 1, 0)


def spread_scratch():
    return [DMA((8,)), DMA((8,)), DMA((1,))]


def spread_shape(piece):
    return jax.ShapeDtypeStruct((piece.shape[0] * 8, piece.shape[1] // 8), piece.dtype)


class Spread:
    def __init__(self, place, src, dst, sems):
        self.place, self.src, self.dst = place, src, dst
        self.send, self.recv, self.own = sems
        self.piece, self.width = src.shape[0], src.shape[1] // 8

    def copy(self, f):
        place = self.place
        return remote(
            self.src.at[:, pl.ds(f * self.width, self.width)], self.dst.at[span(place.block * self.piece, self.piece)],
            self.send.at[f], self.recv.at[place.block], (place.y, place.zh, *BLOCKS[f]),
        )

    def incoming(self, f):
        core, zl, x = BLOCKS[f]
        place = self.place
        return remote(
            self.src.at[:, pl.ds(f * self.width, self.width)], self.dst.at[pl.ds(f * self.piece, self.piece)],
            self.send.at[f], self.recv.at[f], (place.y, core, place.c, zl, x),
        )

    def own_copy(self):
        block = self.place.block
        return pltpu.make_async_copy(
            self.src.at[:, span(block * self.width, self.width)], self.dst.at[span(block * self.piece, self.piece)],
            self.own.at[0],
        )

    def each(self, act):
        for f in range(8):
            mine = jnp.logical_and(self.place.straight, self.place.block == f)
            pl.when(jnp.logical_not(mine))(functools.partial(act, f))

    def start(self):
        self.each(lambda f: self.copy(f).start())
        pl.when(self.place.straight)(lambda: self.own_copy().start())

    def wait(self):
        self.each(lambda f: self.incoming(f).wait_recv())
        self.each(lambda f: self.copy(f).wait_send())
        pl.when(self.place.straight)(lambda: self.own_copy().wait())


def finish_call(piece, moves, ident):
    def body(place, ins, outs, scratch, under, targets):
        spread = Spread(place, ins[0], outs[0], scratch)
        spread.start()
        under.start_z()
        under.end()
        spread.wait()

    return comm_call(
        body, "finish", ident, [piece], [spread_shape(piece)], spread_scratch(), moves, greet=spread_greet,
    )


def local_fine(inputs, prefix_len, w_qkv, w_out, w_up_gate, w_down, cotangent):
    heads, hd = w_qkv.shape[1], w_qkv.shape[2] // 3
    hidden_width = w_down.shape[0]
    tokens = inputs.shape[0]
    y = lax.axis_index("y")
    prefix_len = lax.ppermute(prefix_len, ("core", "zh"), [(0, 0), (1, 2), (2, 1), (3, 3)])
    prefix = jnp.broadcast_to(prefix_len[:, None], (8, 128))
    cosine, sine = rope_tables(tokens, hd)
    tables = (jnp.concatenate([cosine, cosine], axis=1), jnp.concatenate([-sine, sine], axis=1))
    part = hidden_width // 2
    ga, gb = w_up_gate[:, 0, :part], w_up_gate[:, 0, part:]
    ua, ub = w_up_gate[:, 1, :part], w_up_gate[:, 1, part:]
    da, db = w_down[:part], w_down[part:]

    weights = (w_qkv.reshape(w_qkv.shape[0], -1), w_out, ga, gb, ua, ub, da, db)
    firsts, seconds, results = front_call(inputs, cotangent, prefix, tables, weights, heads, hd, 1)
    qkv_1, out_1, ga_1, gb_1, ua_1, ub_1, da_1, db_1 = firsts
    qkv_2, out_2, ga_2, gb_2, ua_2, ub_2, da_2 = seconds
    qkv, mixed, lse, own_in, middle, normed_in, cot_full, normed_mid, hidden, slopes = results
    gates = (ga_1, ga_2, gb_1, gb_2)

    def halves(spec, left, right, axis):
        side = left if axis == 0 else right
        half = side.shape[1] // 2

        def cut(which):
            taken = lax.dynamic_slice_in_dim(side, which * half, half, 1)
            return mm(spec, taken, right) if axis == 0 else mm(spec, left, taken)

        return cut(y), cut(1 - y).astype(BF)

    def joined(own, moved, axis):
        total = (own + moved.astype(F32)).astype(BF)
        if axis == 0:
            return total.reshape(2, total.shape[0] // 2, total.shape[1])
        return jnp.swapaxes(total.reshape(total.shape[0], 2, total.shape[1] // 2), 0, 1)

    down_own, down_other = halves("tf,td->fd", hidden, cot_full, 1)
    (grad_middle, branch_own, grad_gate_up), (db_2, down_moved) = middle_call(
        cot_full, slopes, gates, (ua_1, ua_2, ub_1, ub_2), (da_1, da_2), db_1,
        [("beyond", db_1), ("beyond", down_other)], middle, 5,
    )
    gate_grad, gate_other = halves("td,tf->df", normed_mid, grad_gate_up[:, :hidden_width], 0)
    up_grad, up_other = halves("td,tf->df", normed_mid, grad_gate_up[:, hidden_width:], 0)
    (outputs,), (down_final, gate_moved) = down_call(
        hidden, (da_1, db_1), (da_2, db_2), middle,
        [("grad", joined(down_own, down_moved, 1)), ("beyond", gate_other)], 6,
    )
    (grad_branch, grad_mixed), (gate_final, up_moved) = mix_call(
        branch_own, (out_1, out_2), tokens,
        [("grad", joined(gate_grad, gate_moved, 0)), ("beyond", up_other)], 7,
    )
    out_grad, out_other = halves("tc,td->cd", mixed, grad_branch, 1)
    (grad_rows,), (up_final, out_moved) = attend_back_call(
        qkv, mixed, grad_mixed, lse, prefix, tables, heads, hd,
        [("grad", joined(up_grad, up_moved, 0)), ("beyond", out_other)], 8,
    )
    qkv_grad, qkv_other = halves("td,te->de", normed_in, grad_rows, 0)
    (input_grad, outputs), (out_final, qkv_moved) = input_call(
        grad_rows, (qkv_1, qkv_2), grad_middle, own_in, outputs,
        [("grad", joined(out_grad, out_moved, 1)), ("beyond", qkv_other)], 9,
    )
    (input_grad,), (qkv_final,) = finish_call(input_grad, [("grad", joined(qkv_grad, qkv_moved, 0))], 10)

    def summed(parts):
        return parts[0].astype(F32) + parts[1].astype(F32)

    return (
        outputs,
        input_grad.astype(F32),
        summed(qkv_final).reshape(-1, heads, 3 * hd),
        summed(out_final),
        jnp.stack([summed(gate_final), summed(up_final)], axis=1),
        summed(down_final),
    )


def solution(mesh):
    row_size, col_size = mesh.shape["row"], mesh.shape["col"]
    fine = (row_size, col_size) == (4, 8)
    if fine:
        names, shape, body = AXES, (2,) * 5, local_fine
        row, col = AXES[:2], AXES[2:]
    else:
        names = ("rmaj", "core", "cmaj", "cmin")
        shape = (row_size // 2, 2, 4, col_size // 4)
        body = functools.partial(local, shape[3] == 2)
        row, col = names[:2], names[2:]
    outs = (P(row, col), P(row, col), P(row, col, None), P(col, row), P(row, None, col), P(col, row))
    return jax.shard_map(
        body,
        mesh=Mesh(mesh.devices.reshape(shape), names),
        in_specs=(P(row, col), P(row), P(row, col, None), P(col, row), P(row, None, col), P(col, row), P(row, col)),
        out_specs=outs,
        check_vma=False,
    )
```

```python
import functools

import jax
import jax.numpy as jnp
from jax import lax
from jax.experimental import pallas as pl
from jax.experimental.pallas import tpu as pltpu
from jax.sharding import Mesh
from jax.sharding import PartitionSpec as P

EPSILON = 1e-05
NEG = -1e30
F32 = jnp.float32
BF = jnp.bfloat16
NN = (((1,), (0,)), ((), ()))
NT = (((1,), (1,)), ((), ()))
TN = (((0,), (0,)), ((), ()))
def dot(a, b, dims):
    return lax.dot_general(a, b, dims, preferred_element_type=F32)

def fwd_kernel(prefix_ref, q_ref, k_ref, v_ref, o_ref, lse_ref, *, bq, bk, scale):
    i = pl.program_id(1)
    first = i * bq
    prefix = prefix_ref[0]
    q = q_ref[...]
    limit = jnp.maximum(first + bq, prefix)
    total = (limit + bk - 1) // bk
    clear = jnp.maximum(first, prefix) // bk
    def step(masked, j, carry):
        top, tot, acc = carry
        rows = pl.ds(pl.multiple_of(j * bk, bk), bk)
        s = dot(q, k_ref[rows, :], NT) * scale
        if masked:
            kp = j * bk + lax.broadcasted_iota(jnp.int32, (bq, bk), 1)
            qp = first + lax.broadcasted_iota(jnp.int32, (bq, bk), 0)
            s = jnp.where(kp < jnp.maximum(qp + 1, prefix), s, NEG)
        new = jnp.maximum(top, jnp.max(s, axis=1, keepdims=True))
        alpha = jnp.exp(top - new)
        p = jnp.exp(s - new)
        tot = tot * alpha + jnp.sum(p, axis=1, keepdims=True)
        acc = acc * alpha + dot(p.astype(BF), v_ref[rows, :], NN)
        return new, tot, acc
    carry = (jnp.full((bq, 1), NEG, F32), jnp.zeros((bq, 1), F32), jnp.zeros((bq, q.shape[1]), F32))
    carry = lax.fori_loop(0, clear, functools.partial(step, False), carry)
    top, tot, acc = lax.fori_loop(clear, total, functools.partial(step, True), carry)
    o_ref[...] = (acc / tot).astype(o_ref.dtype)
    lse = jnp.broadcast_to(top + jnp.log(tot), (bq, 128))
    lse_ref[0] = lse.T[0:8, :]

def attend_fwd(qkv, prefix, heads, *, bq=512, bk=512, hd=128):
    seq = qkv.shape[0]
    return pl.pallas_call(
        functools.partial(fwd_kernel, bq=bq, bk=bk, scale=hd ** -0.5),
        grid_spec=pltpu.PrefetchScalarGridSpec(
            num_scalar_prefetch=1, grid=(heads, seq // bq),
            in_specs=[pl.BlockSpec((bq, hd), lambda h, i, p: (i, 3 * h)),
                      pl.BlockSpec((seq, hd), lambda h, i, p: (0, 3 * h + 1)),
                      pl.BlockSpec((seq, hd), lambda h, i, p: (0, 3 * h + 2))],
            out_specs=[pl.BlockSpec((bq, hd), lambda h, i, p: (i, h)),
                       pl.BlockSpec((1, 8, bq), lambda h, i, p: (h, 0, i))]),
        out_shape=[jax.ShapeDtypeStruct((seq, heads * hd), BF), jax.ShapeDtypeStruct((heads, 8, seq), F32)],
        cost_estimate=pl.CostEstimate(flops=4 * heads * seq * seq * hd, bytes_accessed=8 * heads * seq * hd, transcendentals=heads * seq * seq),
        name="attend_forward",
    )(prefix, qkv, qkv, qkv)

def bwd_kernel(prefix_ref, qkv_ref, o_ref, do_ref, lse_ref, cos_ref, sin_ref, out_ref, dk_ref, dv_ref, delta_ref, *, bq, bk, hd, scale):
    seq = qkv_ref.shape[0]
    prefix = prefix_ref[0]
    dk_ref[...] = jnp.zeros_like(dk_ref)
    dv_ref[...] = jnp.zeros_like(dv_ref)
    def deltas(i, _):
        rows = pl.ds(pl.multiple_of(i * bq, bq), bq)
        prod = (do_ref[rows, :].astype(F32) * o_ref[rows, :].astype(F32)).T
        delta_ref[:, rows] = jnp.broadcast_to(jnp.sum(prod, axis=0, keepdims=True), (8, bq))
        return 0
    lax.fori_loop(0, seq // bq, deltas, 0)
    def unrotate(g, rows):
        cos, sin = cos_ref[rows, :], sin_ref[rows, :]
        half = hd // 2
        a, b = g[:, :half], g[:, half:]
        return jnp.concatenate([a * cos + b * sin, b * cos - a * sin], axis=1)
    def q_step(i, _):
        first = i * bq
        qrows = pl.ds(pl.multiple_of(first, bq), bq)
        q = qkv_ref[qrows, 0:hd]
        do = do_ref[qrows, :]
        lse = lse_ref[0, 0:1, qrows]
        delta = delta_ref[0:1, qrows]
        limit = jnp.maximum(first + bq, prefix)
        total = (limit + bk - 1) // bk
        clear = jnp.maximum(first, prefix) // bk
        def step(masked, j, dq):
            krows = pl.ds(pl.multiple_of(j * bk, bk), bk)
            k = qkv_ref[krows, hd:2 * hd]
            v = qkv_ref[krows, 2 * hd:3 * hd]
            s = dot(k, q, NT) * scale
            p = jnp.exp(s - lse)
            if masked:
                kp = j * bk + lax.broadcasted_iota(jnp.int32, (bk, bq), 0)
                qp = first + lax.broadcasted_iota(jnp.int32, (bk, bq), 1)
                p = jnp.where(kp < jnp.maximum(qp + 1, prefix), p, 0.0)
            dp = dot(v, do, NT)
            dv_ref[krows, :] += dot(p.astype(BF), do, NN)
            ds = (p * (dp - delta)).astype(BF)
            dk_ref[krows, :] += dot(ds, q, NN)
            return dq + dot(ds, k, TN)
        dq = lax.fori_loop(0, clear, functools.partial(step, False), jnp.zeros((bq, hd), F32))
        dq = lax.fori_loop(clear, total, functools.partial(step, True), dq)
        out_ref[qrows, 0:hd] = unrotate(dq * scale, qrows).astype(BF)
        return 0
    lax.fori_loop(0, seq // bq, q_step, 0)
    def fin(i, _):
        rows = pl.ds(pl.multiple_of(i * bq, bq), bq)
        out_ref[rows, hd:2 * hd] = unrotate(dk_ref[rows, :] * scale, rows).astype(BF)
        out_ref[rows, 2 * hd:3 * hd] = dv_ref[rows, :].astype(BF)
        return 0
    lax.fori_loop(0, seq // bq, fin, 0)

def attend_bwd(qkv, mixed, dmixed, lse, prefix, cos, sin, heads, *, bq=512, bk=512, hd=128):
    seq = qkv.shape[0]
    return pl.pallas_call(
        functools.partial(bwd_kernel, bq=bq, bk=bk, hd=hd, scale=hd ** -0.5),
        grid_spec=pltpu.PrefetchScalarGridSpec(
            num_scalar_prefetch=1, grid=(heads,),
            in_specs=[pl.BlockSpec((seq, 3 * hd), lambda h, p: (0, h)),
                      pl.BlockSpec((seq, hd), lambda h, p: (0, h)),
                      pl.BlockSpec((seq, hd), lambda h, p: (0, h)),
                      pl.BlockSpec((1, 8, seq), lambda h, p: (h, 0, 0)),
                      pl.BlockSpec((seq, hd // 2), lambda h, p: (0, 0)),
                      pl.BlockSpec((seq, hd // 2), lambda h, p: (0, 0))],
            out_specs=[pl.BlockSpec((seq, 3 * hd), lambda h, p: (0, h))],
            scratch_shapes=[pltpu.VMEM((seq, hd), F32), pltpu.VMEM((seq, hd), F32), pltpu.VMEM((8, seq), F32)]),
        out_shape=[jax.ShapeDtypeStruct((seq, heads * 3 * hd), BF)],
        cost_estimate=pl.CostEstimate(flops=10 * heads * seq * seq * hd, bytes_accessed=20 * heads * seq * hd, transcendentals=heads * seq * seq),
        name="attend_backward",
    )(prefix, qkv, mixed, dmixed, lse, cos, sin)[0]


def rope_tables(count, head_dim):
    positions = jnp.arange(count, dtype=jnp.int32).astype(F32)
    frequency = 10000.0 ** (-(jnp.arange(head_dim // 2).astype(F32) * 2.0 / head_dim))
    angles = positions[:, None] * frequency[None, :]
    return jnp.cos(angles), jnp.sin(angles)


def rotate(values, cosine, sine):
    half = values.shape[-1] // 2
    a, b = values[..., :half], values[..., half:]
    return jnp.concatenate([a * cosine - b * sine, b * cosine + a * sine], axis=-1)


def norm(values):
    center = values - jnp.mean(values, axis=-1, keepdims=True)
    inv_std = lax.rsqrt(jnp.mean(center * center, axis=-1, keepdims=True) + EPSILON)
    return center * inv_std, inv_std


def norm_back(grad, normed, inv_std):
    mean_grad = jnp.mean(grad, axis=-1, keepdims=True)
    mean_cross = jnp.mean(grad * normed, axis=-1, keepdims=True)
    return inv_std * (grad - mean_grad - normed * mean_cross)


def mm(spec, left, right):
    return jnp.einsum(spec, left, right, preferred_element_type=F32)


def local(swap, inputs, prefix_len, w_qkv, w_out, w_up_gate, w_down, cotangent):
    rows = ("rmaj", "cmin") if swap else ("rmaj", "core")
    cols = ("cmaj", "core") if swap else ("cmaj", "cmin")

    def exchange(value):
        if not swap:
            return value
        return lax.ppermute(value, ("core", "cmin"), [(0, 0), (1, 2), (2, 1), (3, 3)])

    def scatter(value):
        return lax.psum_scatter(value.astype(BF), cols, scatter_dimension=0, tiled=True).astype(F32)

    def spread(value):
        return lax.all_to_all(value, cols, 1, 0, tiled=True)

    prefix_len = exchange(prefix_len)
    inputs, cotangent = exchange(inputs), exchange(cotangent)
    w_qkv, w_out = exchange(w_qkv), exchange(w_out)
    w_up_gate, w_down = exchange(w_up_gate), exchange(w_down)
    tokens = inputs.shape[0]
    heads, head_dim = w_qkv.shape[1], w_qkv.shape[2] // 3
    hidden_width = w_down.shape[0]
    full_in = lax.all_gather(inputs, cols, axis=1, tiled=True)
    width = full_in.shape[1]
    qkv_all = lax.all_gather(w_qkv, rows, axis=0, tiled=True).reshape(width, heads * 3 * head_dim)
    out_all = lax.all_gather(w_out, rows, axis=1, tiled=True)
    up_all = lax.all_gather(w_up_gate, rows, axis=0, tiled=True).reshape(width, 2 * hidden_width)
    down_all = lax.all_gather(w_down, rows, axis=1, tiled=True)
    cot_full = lax.all_gather(cotangent, cols, axis=1, tiled=True)
    piece = tokens // lax.axis_size(cols)
    first = lax.axis_index(cols) * piece
    own_in = lax.dynamic_slice_in_dim(full_in, first, piece, 0).astype(F32)
    own_cot = lax.dynamic_slice_in_dim(cot_full, first, piece, 0).astype(F32)

    normed_in = norm(full_in.astype(F32))[0].astype(BF)
    qkv_rows = mm("td,de->te", normed_in, qkv_all).reshape(tokens, heads, 3, head_dim)
    cosine, sine = rope_tables(tokens, head_dim)
    turned = rotate(qkv_rows[:, :, :2], cosine[:, None, None], sine[:, None, None])
    qkv = jnp.concatenate([turned, qkv_rows[:, :, 2:]], axis=2).astype(BF)
    qkv = qkv.reshape(tokens, heads * 3 * head_dim)
    mixed, lse = attend_fwd(qkv, prefix_len, heads, hd=head_dim)
    middle = own_in + scatter(mm("tc,cd->td", mixed, out_all))
    normed_two, inv_two = norm(middle)
    normed_mid = lax.all_gather(normed_two.astype(BF), cols, axis=0, tiled=True)
    gate_up = mm("td,df->tf", normed_mid, up_all)
    gate, up = gate_up[:, :hidden_width], gate_up[:, hidden_width:]
    sig = jax.nn.sigmoid(gate)
    active = gate * sig
    hidden = (active * up).astype(BF)
    outputs = middle + scatter(mm("tf,fd->td", hidden, down_all))
    outputs = exchange(spread(outputs.astype(BF)))

    grad_hidden = mm("td,fd->tf", cot_full, down_all)
    grad_gate = grad_hidden * up * sig * (1.0 + gate * (1.0 - sig))
    grad_gate_up = jnp.concatenate([grad_gate, grad_hidden * active], axis=1).astype(BF)
    grad_down = mm("tf,td->fd", hidden, cot_full).astype(BF)
    grad_down = lax.psum_scatter(grad_down, rows, scatter_dimension=1, tiled=True)
    grad_up = mm("td,tf->df", normed_mid, grad_gate_up).astype(BF)
    grad_up = lax.psum_scatter(grad_up, rows, scatter_dimension=0, tiled=True)
    grad_normed = scatter(mm("tf,df->td", grad_gate_up, up_all))
    grad_middle = own_cot + norm_back(grad_normed, normed_two, inv_two)
    grad_branch = lax.all_gather(grad_middle.astype(BF), cols, axis=0, tiled=True)
    grad_out = mm("tc,td->cd", mixed, grad_branch).astype(BF)
    grad_out = lax.psum_scatter(grad_out, rows, scatter_dimension=1, tiled=True)
    grad_mixed = mm("td,cd->tc", grad_branch, out_all).astype(BF)
    grad_rows = attend_bwd(qkv, mixed, grad_mixed, lse, prefix_len, cosine, sine, heads, hd=head_dim)
    grad_in = scatter(mm("te,de->td", grad_rows, qkv_all))
    grad_qkv = mm("td,te->de", normed_in, grad_rows).astype(BF)
    grad_qkv = lax.psum_scatter(grad_qkv, rows, scatter_dimension=0, tiled=True)
    normed_own, inv_own = norm(own_in)
    input_grad = grad_middle + norm_back(grad_in, normed_own, inv_own)
    input_grad = exchange(spread(input_grad.astype(BF))).astype(F32)
    return (
        outputs,
        input_grad,
        exchange(grad_qkv).astype(F32).reshape(-1, heads, 3 * head_dim),
        exchange(grad_out).astype(F32),
        exchange(grad_up).astype(F32).reshape(-1, 2, hidden_width),
        exchange(grad_down).astype(F32),
    )


AXES = ("y", "core", "zh", "zl", "x")
GROUP = ("core", "zl", "x")
MESH = pl.DeviceIdType.MESH
DMA = pltpu.SemaphoreType.DMA
VMEM_WHOLE = pl.BlockSpec(memory_space=pltpu.VMEM)
ANYWHERE = pl.BlockSpec(memory_space=pl.ANY)


class Place:
    def __init__(self):
        self.y, self.c, self.zh, self.zl, self.x = (lax.axis_index(name) for name in AXES)
        y, c, zh, zl, x = self.y, self.c, self.zh, self.zl, self.x
        self.sibling = (y, 1 - c, zh, zl, x)
        self.across = (y, c, zh, zl, 1 - x)
        self.along = (y, c, zh, 1 - zl, x)
        self.beyond = (1 - y, c, zh, zl, x)
        self.far = [(y, core, 1 - zh, zl, x) for core in (0, 1)]
        self.far_role = (y, zh, 1 - zh, zl, x)
        self.straight = c == zh
        self.outer = zl == zh
        self.order = [2 * y, 2 * y + 1, 2 * (1 - y), 2 * (1 - y) + 1]
        self.block = c * 4 + zl * 2 + x

    def chip(self, dz, dx):
        return lax.rem(self.zl + dz, 2) * 2 + lax.rem(self.x + dx, 2)

    def meet(self, greet=None):
        devices = [self.sibling, self.across, self.along, self.beyond, *self.far]
        barrier = pltpu.get_barrier_semaphore()
        for device in devices:
            pl.semaphore_signal(barrier, inc=1, device_id=device, device_id_type=MESH)
        more = greet(self, barrier) if greet else 0
        pl.semaphore_wait(barrier, len(devices) + more)


def span(start, size):
    return pl.ds(pl.multiple_of(start, size), size)


def remote(src, dst, send_sem, recv_sem, device):
    return pltpu.make_async_remote_copy(
        src_ref=src, dst_ref=dst, send_sem=send_sem, recv_sem=recv_sem, device_id=device, device_id_type=MESH
    )


class Beyond:
    along_z = False

    def __init__(self, place, src, dst, sem):
        self.copy = remote(src, dst, sem.at[0], sem.at[2], place.beyond)

    def start(self):
        self.copy.start()

    def wait_recv(self):
        self.copy.wait_recv()

    def wait_send(self):
        self.copy.wait_send()


class WeightHalf:
    along_z = True

    def __init__(self, place, src, dst, sem):
        c = place.c
        self.straight = place.straight
        self.outward = remote(src, dst.at[c], sem.at[0], sem.at[2 + c], place.far_role)
        self.aside = remote(src, dst.at[c], sem.at[1], sem.at[2 + c], place.sibling)
        self.here = pltpu.make_async_copy(src, dst.at[c], sem.at[1])
        self.from_sibling = remote(src, dst.at[1 - c], sem.at[1], sem.at[3 - c], place.sibling)
        self.from_far = [remote(src, dst.at[i], sem.at[0], sem.at[2 + i], place.far_role) for i in (0, 1)]

    def start(self):
        self.outward.start()

        @pl.when(self.straight)
        def _():
            self.here.start()

        @pl.when(jnp.logical_not(self.straight))
        def _():
            self.aside.start()

    def wait_recv(self):
        @pl.when(self.straight)
        def _():
            self.here.wait()
            self.from_sibling.wait_recv()

        @pl.when(jnp.logical_not(self.straight))
        def _():
            for copy in self.from_far:
                copy.wait_recv()

    def wait_send(self):
        self.outward.wait_send()

        @pl.when(jnp.logical_not(self.straight))
        def _():
            self.aside.wait_send()


class GradHalf:
    along_z = True

    def __init__(self, place, src, dst, sem):
        c, zh = place.c, place.zh
        self.straight = place.straight
        self.here = pltpu.make_async_copy(src.at[c], dst.at[zh], sem.at[0])
        self.aside = remote(src.at[1 - c], dst.at[zh], sem.at[1], sem.at[2 + zh], place.sibling)
        self.outward = [remote(src.at[i], dst.at[zh], sem.at[i], sem.at[2 + zh], place.far[i]) for i in (0, 1)]
        self.from_sibling = remote(src.at[c], dst.at[zh], sem.at[1], sem.at[2 + zh], place.sibling)
        self.from_far = remote(src.at[c], dst.at[1 - zh], sem.at[0], sem.at[3 - zh], place.far[0])

    def start(self):
        @pl.when(self.straight)
        def _():
            self.here.start()
            self.aside.start()

        @pl.when(jnp.logical_not(self.straight))
        def _():
            for copy in self.outward:
                copy.start()

    def wait_recv(self):
        self.from_far.wait_recv()

        @pl.when(self.straight)
        def _():
            self.here.wait()

        @pl.when(jnp.logical_not(self.straight))
        def _():
            self.from_sibling.wait_recv()

    def wait_send(self):
        @pl.when(self.straight)
        def _():
            self.aside.wait_send()

        @pl.when(jnp.logical_not(self.straight))
        def _():
            for copy in self.outward:
                copy.wait_send()


KINDS = {"beyond": Beyond, "weight": WeightHalf, "grad": GradHalf}


def moved_shape(kind, src):
    shape = (2, *src.shape) if kind == "weight" else src.shape
    return jax.ShapeDtypeStruct(shape, src.dtype)


class Under:
    def __init__(self, place, moves):
        self.place, self.moves = place, moves
        self.z = [move for kind, move in moves if move.along_z]
        self.y = [move for kind, move in moves if not move.along_z and not isinstance(kind, int)]
        self.follow = [(moves[kind][1], move) for kind, move in moves if isinstance(kind, int)]

    def start_y(self):
        for move in self.y:
            move.start()

    def start_z(self, outer=None):
        def start():
            for move in self.z:
                move.start()

        if outer is None:
            start()
        else:
            pl.when(self.place.outer if outer else jnp.logical_not(self.place.outer))(start)

    def start_follow(self):
        for ahead, move in self.follow:
            ahead.wait_recv()
            move.start()

    def end(self, skip=0):
        done = [ahead for ahead, _ in self.follow]
        for _, move in self.moves[skip:]:
            if move not in done:
                move.wait_recv()


def comm_call(
    body, name, ident, inputs, outs, scratch, moves=(), flops=0, transcendentals=0, spaces=None, greet=None
):
    n_in, n_out, n_move = len(inputs), len(outs), len(moves)
    own_source = [i for i, (kind, _) in enumerate(moves) if not isinstance(kind, int)]

    def kernel(*refs):
        ins, refs = refs[:n_in], refs[n_in:]
        sources, refs = refs[:len(own_source)], refs[len(own_source):]
        results, refs = refs[:n_out], refs[n_out:]
        targets, refs = refs[:n_move], refs[n_move:]
        sems, rest = refs[0], refs[1:]
        place = Place()
        place.meet(greet)
        made = []
        for i, (kind, _) in enumerate(moves):
            if isinstance(kind, int):
                made.append((kind, Beyond(place, targets[kind], targets[i], sems.at[i])))
            else:
                made.append((kind, KINDS[kind](place, sources[own_source.index(i)], targets[i], sems.at[i])))
        body(place, ins, results, rest, Under(place, made), targets)
        for _, move in made:
            move.wait_send()

    arrays = [*inputs, *(moves[i][1] for i in own_source)]
    shapes = list(outs)
    moved = []
    for kind, array in moves:
        moved.append(moved[kind] if isinstance(kind, int) else moved_shape(kind, array))
    shapes += moved
    in_specs = (spaces or [VMEM_WHOLE] * n_in) + [ANYWHERE] * len(own_source)
    size = sum(s.size * s.dtype.itemsize for s in (*arrays, *shapes))
    result = pl.pallas_call(
        kernel,
        out_shape=shapes,
        in_specs=in_specs,
        out_specs=[VMEM_WHOLE] * (n_out + n_move),
        scratch_shapes=[DMA((max(n_move, 1), 4)), *scratch],
        compiler_params=pltpu.CompilerParams(collective_id=ident, has_side_effects=True, vmem_limit_bytes=63 << 20),
        cost_estimate=pl.CostEstimate(
            flops=flops + (20 << 30), bytes_accessed=size, transcendentals=transcendentals
        ),
        name=name,
    )(*arrays)
    return result[:n_out], result[n_out:]


def each_rows(count, body, size=32):
    def step(i, carry):
        body(span(i * size, size))
        return carry

    lax.fori_loop(0, count // size, step, 0)


def row_norm(values):
    center = values - jnp.mean(values, axis=-1, keepdims=True)
    inv_std = lax.rsqrt(jnp.mean(center * center, axis=-1, keepdims=True) + EPSILON)
    return center * inv_std, inv_std


SLICES = 4
NORM_ROWS = 64
NORM_UNROLL = 1


def reduce_sems():
    return [DMA((4,)), DMA((4,)), DMA((3, SLICES)), DMA((3, SLICES))]


def reduce_scratch(piece, width):
    return [pltpu.VMEM((count, piece, width), BF) for count in (4, 4, 2, 3, 3)] + reduce_sems()


def nothing():
    pass


def reduce_body(place, compute, last, scratch, begin=nothing, before_z=nothing, after_z=nothing):
    sib_out, sib_in, own, near_out, near_in, sib_send, sib_recv, near_send, near_recv = scratch
    piece = own.shape[1]
    c = place.c
    size = piece // SLICES
    begin()

    def sib_copy(step):
        return remote(sib_out.at[step], sib_in.at[step], sib_send.at[step], sib_recv.at[step], place.sibling)

    def near_copy(step, r):
        device = place.along if step == 2 else place.across
        rows = span(r * size, size)
        return remote(
            near_out.at[step, rows], near_in.at[step, rows], near_send.at[step, r], near_recv.at[step, r], device
        )

    def finish(step):
        slot = step % 2
        sib_copy(step).wait_recv()

        def send(r, carry):
            if step == 2:
                near_copy(0, r).wait_recv()
            rows = span(r * size, size)
            total = own[slot, rows, :].astype(F32) + sib_in[step, rows, :].astype(F32)
            if step == 2:
                total = total + near_in[0, rows, :].astype(F32)
            near_out[step, rows, :] = total.astype(BF)
            near_copy(step, r).start()
            return carry

        lax.fori_loop(0, SLICES, send, 0)

    def step(s, carry):
        target = place.chip(1 - lax.rem(s, 2), 1 - s // 2)
        compute((1 - c) * 4 + target, sib_out.at[s])
        sib_copy(s).start()
        for index in (0, 1):
            @pl.when(s == index + 1)
            def _(index=index):
                finish(index)

        compute(c * 4 + target, own.at[lax.rem(s, 2)])
        return carry

    lax.fori_loop(0, 4, step, 0)
    before_z()
    finish(2)
    after_z()
    sib_copy(3).wait_recv()

    def arrive(r, carry):
        near_copy(1, r).wait_recv()
        near_copy(2, r).wait_recv()

        def final(i, carry):
            rows = span(r * size + i * 16, 16)
            total = own[1, rows, :].astype(F32) + sib_in[3, rows, :].astype(F32)
            last(rows, total + near_in[1, rows, :].astype(F32) + near_in[2, rows, :].astype(F32))
            return carry

        return lax.fori_loop(0, size // 16, final, carry)

    lax.fori_loop(0, SLICES, arrive, 0)
    for s in range(4):
        sib_copy(s).wait_send()

    def sent(r, carry):
        for s in range(3):
            near_copy(s, r).wait_send()
        return carry

    lax.fori_loop(0, SLICES, sent, 0)


def product(place, left_ref, weights, transposed):
    def compute(owner, out_ref):
        piece = out_ref.shape[0]
        left = left_ref[span(owner * piece, piece), :]
        for weight, index in zip(weights, place.order):
            size = weight.shape[0] if transposed else weight.shape[1]
            part = dot(left, weight[...], NT if transposed else NN)
            out_ref[:, span(index * size, size)] = part.astype(out_ref.dtype)

    return compute


def back_rows(base, value, total):
    normed, inv_std = row_norm(value)
    mean_grad = jnp.mean(total, axis=-1, keepdims=True)
    mean_cross = jnp.mean(total * normed, axis=-1, keepdims=True)
    return base + inv_std * (total - mean_grad - normed * mean_cross)


def quarters(first, second):
    return [first.at[0], first.at[1], second.at[0], second.at[1]]


def beside(under):
    def begin():
        under.start_y()
        under.start_z()

    return dict(begin=begin, after_z=under.start_follow)


def down_call(hidden, firsts, seconds, middle, moves, ident):
    piece, width = middle.shape

    def body(place, ins, outs, scratch, under, targets):
        hidden_ref, first_a, first_b, second_a, second_b, base_ref = ins
        parts = list(zip(quarters(first_a, second_a), quarters(first_b, second_b), place.order))

        def compute(owner, out_ref):
            rows = span(owner * piece, piece)
            for upper, lower, index in parts:
                depth, size = upper.shape
                part = dot(hidden_ref[rows, 0:depth], upper[...], NN) + dot(hidden_ref[rows, depth:], lower[...], NN)
                out_ref[:, span(index * size, size)] = part.astype(out_ref.dtype)

        def last(rows, total):
            outs[0][rows, :] = (base_ref[rows, :] + total).astype(BF)

        reduce_body(place, compute, last, scratch, **beside(under))
        under.end()

    return comm_call(
        body, "reduce_down", ident, [hidden, *firsts, *seconds, middle], [jax.ShapeDtypeStruct((piece, width), BF)],
        reduce_scratch(piece, width), moves, flops=2 * hidden.size * width,
    )


def middle_call(cot, slopes, gates, ups, downs, down_last, moves, middle, ident):
    piece, width = middle.shape
    tokens, part_width = cot.shape[0], down_last.shape[1]
    hidden = 2 * part_width
    tile = 256
    tiles = part_width // tile

    def body(place, ins, outs, scratch, under, targets):
        cot_ref, slopes_ref, ga1, ga2, gb1, gb2, ua1, ua2, ub1, ub2, value_ref, da1, da2, db1 = ins
        total_ref, branch_ref, grad_ref = outs
        load_sem, *rest = scratch
        under.start_y()
        load = pltpu.make_async_copy(slopes_ref, grad_ref, load_sem.at[0])
        load.start()
        load.wait()
        rows_in = (quarters(da1, da2), quarters(db1, targets[0]))

        def fill(owner, part):
            rows = span(owner * piece, piece)

            def step(t, carry):
                grad = None
                for weight, index in zip(rows_in[part], place.order):
                    size = weight.shape[1]
                    term = dot(cot_ref[rows, span(index * size, size)], weight[span(t * tile, tile), :], NT)
                    grad = term if grad is None else grad + term
                for offset in (0, hidden):
                    cols = span(offset + part * part_width + t * tile, tile)
                    grad_ref[rows, cols] = (grad * grad_ref[rows, cols].astype(F32)).astype(BF)
                return carry

            lax.fori_loop(0, tiles, step, 0)

        def fill_first(i, carry):
            fill(i, 0)
            return carry

        lax.fori_loop(0, tokens // piece, fill_first, 0)
        under.moves[0][1].wait_recv()
        columns = [quarters(ga1, ga2), quarters(gb1, gb2), quarters(ua1, ua2), quarters(ub1, ub2)]

        def compute(owner, out_ref):
            rows = span(owner * piece, piece)
            fill(owner, 1)
            for quarter, index in enumerate(place.order):
                total = None
                for i, weights in enumerate(columns):
                    weight = weights[quarter]
                    size = weight.shape[0]
                    term = dot(grad_ref[rows, i * part_width:(i + 1) * part_width], weight[...], NT)
                    total = term if total is None else total + term
                out_ref[:, span(index * size, size)] = total.astype(out_ref.dtype)

        def last(rows, total):
            base = cot_ref[own_rows(rows), :].astype(F32)
            grad = back_rows(base, value_ref[rows, :], total)
            total_ref[rows, :] = grad
            branch_ref[rows, :] = grad.astype(BF)

        def own_rows(rows):
            return pl.ds(pl.multiple_of(place.block * piece + rows.start, 16), rows.size)

        reduce_body(place, compute, last, rest)
        under.end(skip=1)

    shape = functools.partial(jax.ShapeDtypeStruct, (piece, width))
    return comm_call(
        body, "reduce_middle", ident, [cot, slopes, *gates, *ups, middle, *downs, down_last],
        [shape(F32), shape(BF), jax.ShapeDtypeStruct((tokens, 2 * hidden), BF)],
        [DMA((1,)), *reduce_scratch(piece, width)],
        moves, flops=6 * tokens * hidden * width,
        spaces=[VMEM_WHOLE, ANYWHERE] + [VMEM_WHOLE] * 12,
    )


def gather_scratch():
    return [DMA((3, SLICES)), DMA((3, SLICES)), DMA((4,)), DMA((4,))]


def gather_body(place, own_ref, full, sems, process, begin=nothing, follow=nothing):
    near_send, near_recv, sib_send, sib_recv = sems
    piece = own_ref.shape[0]
    size = piece // SLICES
    c = place.c

    def near_copy(slot, r, target):
        where = full.at[span((c * 4 + target) * piece + r * size, size)]
        device = place.along if slot == 2 else place.across
        return remote(where, where, near_send.at[slot, r], near_recv.at[slot, r], device)

    def sib_copy(slot, core, target):
        where = full.at[span((core * 4 + target) * piece, piece)]
        return remote(where, where, sib_send.at[slot], sib_recv.at[slot], place.sibling)

    def slices(act):
        def step(r, carry):
            act(r)
            return carry

        lax.fori_loop(0, SLICES, step, 0)

    mine, x_chip, z_chip, d_chip = place.chip(0, 0), place.chip(0, 1), place.chip(1, 0), place.chip(1, 1)
    full[span((c * 4 + mine) * piece, piece), :] = own_ref[...]
    slices(lambda r: near_copy(2, r, mine).start())
    slices(lambda r: near_copy(1, r, mine).start())
    sib_copy(3, c, mine).start()
    begin()

    def forward(r):
        near_copy(2, r, z_chip).wait_recv()
        near_copy(0, r, z_chip).start()

    process(c * 4 + mine)
    forward(0)
    sib_copy(3, 1 - c, mine).wait_recv()
    process((1 - c) * 4 + mine)
    forward(1)
    slices(lambda r: near_copy(1, r, x_chip).wait_recv())
    sib_copy(1, c, x_chip).start()
    process(c * 4 + x_chip)
    for r in range(2, SLICES):
        forward(r)
    sib_copy(2, c, z_chip).start()
    sib_copy(1, 1 - c, x_chip).wait_recv()
    process((1 - c) * 4 + x_chip)
    process(c * 4 + z_chip)
    follow()
    sib_copy(2, 1 - c, z_chip).wait_recv()
    process((1 - c) * 4 + z_chip)
    slices(lambda r: near_copy(0, r, d_chip).wait_recv())
    sib_copy(0, c, d_chip).start()
    process(c * 4 + d_chip)
    sib_copy(0, 1 - c, d_chip).wait_recv()
    process((1 - c) * 4 + d_chip)
    for slot in range(3):
        slices(lambda r: near_copy(slot, r, mine).wait_send())
    for slot in range(4):
        sib_copy(slot, c, mine).wait_send()


class ColumnGather:
    def __init__(self, place, src, full, sems):
        self.place, self.src, self.full = place, src, full
        self.near_send, self.near_recv, self.sib_send, self.sib_recv, self.own = sems
        self.width = src.shape[1]
        self.size = src.shape[0] // SLICES

    def where(self, core, target):
        return span((core * 4 + target) * self.width, self.width)

    def near(self, slot, r, target, first=False):
        place = self.place
        rows = pl.ds(r * self.size, self.size)
        dst = self.full.at[rows, self.where(place.c, target)]
        src = self.src.at[rows] if first else dst
        device = place.along if slot == 2 else place.across
        return remote(src, dst, self.near_send.at[slot, r], self.near_recv.at[slot, r], device)

    def sib(self, slot, core, target, first=False):
        dst = self.full.at[:, self.where(core, target)]
        src = self.src if first else dst
        return remote(src, dst, self.sib_send.at[slot], self.sib_recv.at[slot], self.place.sibling)

    def chips(self):
        place = self.place
        return place.chip(0, 0), place.chip(0, 1), place.chip(1, 0), place.chip(1, 1)

    def own_copy(self):
        return pltpu.make_async_copy(self.src, self.full.at[:, self.where(self.place.c, self.chips()[0])], self.own.at[0])

    def start(self):
        mine = self.chips()[0]
        self.own_copy().start()
        for slot in (2, 1):
            for r in range(SLICES):
                self.near(slot, r, mine, True).start()
        self.sib(3, self.place.c, mine, True).start()

    def forward(self, r):
        z_chip = self.chips()[2]
        self.near(2, r, z_chip).wait_recv()
        self.near(0, r, z_chip).start()

    def finish(self):
        mine, x_chip, z_chip, d_chip = self.chips()
        c = self.place.c
        self.sib(2, c, z_chip).start()
        for r in range(SLICES):
            self.near(1, r, x_chip).wait_recv()
        self.sib(1, c, x_chip).start()
        for r in range(SLICES):
            self.near(0, r, d_chip).wait_recv()
        self.sib(0, c, d_chip).start()
        self.own_copy().wait()
        for slot, target in enumerate((d_chip, x_chip, z_chip, mine)):
            self.sib(slot, 1 - c, target).wait_recv()
            self.sib(slot, c, mine).wait_send()
        for slot in range(3):
            for r in range(SLICES):
                self.near(slot, r, mine).wait_send()


def attend_back_body(qkv_ref, o_ref, do_ref, lse_ref, bound, cos_ref, sin_ref, out_ref, dk_ref, dv_ref, heads, hd):
    seq = qkv_ref.shape[0]
    bq = bk = min(512, seq // 2)
    scale = hd ** -0.5
    half = hd // 2

    def unrotate(g, rows):
        return g * cos_ref[rows, :] - pltpu.roll(g, half, 1) * sin_ref[rows, :]

    def head(h, carry):
        base = h * 3 * hd
        own = span(h * hd, hd)
        dk_ref[...] = jnp.zeros_like(dk_ref)
        dv_ref[...] = jnp.zeros_like(dv_ref)
        for i in range(seq // bq):
            first = i * bq
            rows = pl.ds(first, bq)
            q = qkv_ref[rows, span(base, hd)]
            do = do_ref[rows, own]
            row_sums = (do.astype(F32) * o_ref[rows, own].astype(F32)).T
            delta = jnp.sum(row_sums, axis=0, keepdims=True)
            tops = lse_ref[h, 0:1, first:first + bq]
            total = max(i + 1, seq // 2 // bk)

            def step(masked, j, dq, first=first, q=q, do=do, delta=delta, tops=tops):
                keys = span(j * bk, bk)
                k = qkv_ref[keys, span(base + hd, hd)]
                v = qkv_ref[keys, span(base + 2 * hd, hd)]
                p = jnp.exp(dot(k, q, NT) * scale - tops)
                if masked:
                    kp = j * bk + lax.broadcasted_iota(jnp.int32, (bk, bq), 0)
                    qp = first + lax.broadcasted_iota(jnp.int32, (bk, bq), 1)
                    p = jnp.where(kp < jnp.maximum(qp + 1, bound), p, 0.0)
                dv_ref[keys, :] += dot(p.astype(BF), do, NN)
                ds = (p * (dot(v, do, NT) - delta)).astype(BF)
                dk_ref[keys, :] += dot(ds, q, NN)
                return dq + dot(ds, k, TN)

            dq = lax.fori_loop(0, i, functools.partial(step, False), jnp.zeros((bq, hd), F32))
            dq = lax.fori_loop(i, total, functools.partial(step, True), dq)
            out_ref[rows, span(base, hd)] = unrotate(dq * scale, rows).astype(BF)

        def fin(i, carry):
            rows = span(i * bq, bq)
            out_ref[rows, span(base + hd, hd)] = unrotate(dk_ref[rows, :] * scale, rows).astype(BF)
            out_ref[rows, span(base + 2 * hd, hd)] = dv_ref[rows, :].astype(BF)
            return carry

        return lax.fori_loop(0, seq // bq, fin, carry)

    lax.fori_loop(0, heads, head, 0)


def front_call(inputs, cot, prefix, tables, weights, heads, hd, ident):
    names = ("qkv", "out", "ga", "gb", "ua", "ub", "da", "db")
    tokens, slice_width = inputs.shape
    width = slice_width * 8
    piece = tokens // 8
    size = tokens // SLICES
    inner = weights[0].shape[1]
    part_width = weights[2].shape[1]
    hidden = 2 * part_width
    tile = 256
    bq = bk = min(512, tokens // 2)
    scale = hd ** -0.5

    def kernel(in_ref, cot_ref, prefix_ref, cos_ref, sin_ref, *refs):
        sources, refs = refs[:8], refs[8:]
        firsts, seconds, refs = refs[:8], refs[8:15], refs[15:]
        (qkv_ref, mixed_ref, lse_ref, own_in_ref, middle_ref, normed_in_out, cot_out, normed_mid_out, hidden_out,
         slopes_out), refs = refs[:10], refs[10:]
        arena, acc, block_ref, normed_own, *refs = refs
        held, refs = dict(zip(names, refs[:8])), refs[8:]
        z_sems, y_sems, store_sems, out_sems, swap_send, swap_recv, phase, *sems = refs
        start_sems, gather_sems, reduce_sems_, feed_sems = sems[:5], sems[5:10], sems[10:14], sems[14:]
        place = Place()
        c, zl, x = place.c, place.zl, place.x
        place.meet()
        z_moves = {n: WeightHalf(place, sources[i], held[n].at[0], z_sems.at[i]) for i, n in enumerate(names)}
        y_moves = {n: Beyond(place, held[n].at[0], held[n].at[1], y_sems.at[i]) for i, n in enumerate(names[:7])}

        def go(name):
            z_moves[name].start()

        def stores(name):
            i = names.index(name)
            copies = [pltpu.make_async_copy(held[name].at[0], firsts[i], store_sems.at[i, 0])]
            if i < 7:
                copies.append(pltpu.make_async_copy(held[name].at[1], seconds[i], store_sems.at[i, 1]))
            return copies

        def pass_on(name):
            z_moves[name].wait_recv()
            y_moves[name].start()

        def got(name):
            y_moves[name].wait_recv()
            for copy in stores(name):
                copy.start()

        def parts(name):
            return [held[name].at[side, i] for side in (0, 1) for i in (0, 1)]

        full, normed = arena.at[pl.ds(0, tokens)], arena.at[pl.ds(tokens, tokens)]
        gather = ColumnGather(place, in_ref, full, start_sems)
        crossed = jnp.logical_not(place.straight)
        partner = (place.y, 1 - c, 1 - place.zh, zl, x)
        mine, x_chip, z_chip, d_chip = gather.chips()
        def rows_of(r):
            return pl.ds(r * size, size)

        def swap_copy(r, core):
            where = full.at[rows_of(r), gather.where(core, mine)]
            return remote(in_ref.at[rows_of(r)], where, swap_send.at[r], swap_recv.at[r], partner)

        def own_copy(r):
            where = full.at[rows_of(r), gather.where(c, mine)]
            return pltpu.make_async_copy(in_ref.at[rows_of(r)], where, swap_send.at[r])

        def cot_swap():
            return remote(cot_ref, block_ref, swap_send.at[SLICES], swap_recv.at[SLICES], partner)

        def cot_own():
            return pltpu.make_async_copy(cot_ref, block_ref, swap_send.at[SLICES])

        def sib(slot, r, core, target):
            where = full.at[rows_of(r), gather.where(core, target)]
            return remote(where, where, start_sems[2].at[slot, r], start_sems[3].at[slot, r], place.sibling)

        @pl.when(place.straight)
        def _():
            for r in range(SLICES):
                own_copy(r).start()
            cot_own().start()

        @pl.when(crossed)
        def _():
            for r in range(SLICES):
                swap_copy(r, 1 - c).start()

        for r in range(SLICES):
            @pl.when(place.straight)
            def _(r=r):
                own_copy(r).wait()

            @pl.when(crossed)
            def _(r=r):
                swap_copy(r, c).wait_recv()

            gather.near(2, r, mine).start()
            gather.near(1, r, mine).start()
            sib(3, r, c, mine).start()
        for r in range(SLICES):
            gather.forward(r)
            sib(2, r, c, z_chip).start()
            gather.near(1, r, x_chip).wait_recv()
            sib(1, r, c, x_chip).start()
            if r == 0:
                go("qkv")
        pass_on("qkv")
        go("out")
        pl.when(crossed)(lambda: cot_swap().start())
        depth = held["qkv"].shape[2]
        for r in range(SLICES):
            gather.near(0, r, d_chip).wait_recv()
            sib(0, r, c, d_chip).start()
            for slot, target in enumerate((d_chip, x_chip, z_chip, mine)):
                sib(slot, r, 1 - c, target).wait_recv()

            def norm_rows(i, carry, r=r):
                rows = span(r * size + i * NORM_ROWS, NORM_ROWS)
                normed[rows, :] = row_norm(full[rows, :].astype(F32))[0].astype(BF)
                return carry

            lax.fori_loop(0, size // NORM_ROWS, norm_rows, 0, unroll=NORM_UNROLL)
            pltpu.make_async_copy(normed.at[rows_of(r)], normed_in_out.at[rows_of(r)], out_sems.at[r]).start()
            total = None
            for weight, index in zip(parts("qkv")[:2], place.order[:2]):
                term = dot(normed[rows_of(r), span(index * depth, depth)], weight[...], NN)
                total = term if total is None else total + term
            acc[rows_of(r), :] = total
        own_in_ref[...] = full[span(place.block * piece, piece), :]
        pass_on("out")

        cot_gather = ColumnGather(place, block_ref, cot_out, gather_sems)

        def forward_cot():
            for r in range(SLICES):
                cot_gather.forward(r)

        @pl.when(place.straight)
        def _():
            cot_own().wait()
            cot_gather.start()
            go("ga")

        got("qkv")
        half = size // 2

        def project(r, carry):
            rows = span(r * half, half)
            total = acc[rows, :]
            for weight, index in zip(parts("qkv")[2:], place.order[2:]):
                total = total + dot(normed[rows, span(index * depth, depth)], weight[...], NN)
            cos, sin = cos_ref[rows, :], sin_ref[rows, :]
            for h in range(heads):
                for part in range(3):
                    value = total[:, (3 * h + part) * hd:(3 * h + part + 1) * hd]
                    if part < 2:
                        value = value * cos + pltpu.roll(value, hd // 2, 1) * sin
                    qkv_ref[rows, pl.ds((3 * h + part) * hd, hd)] = value.astype(BF)
            return carry

        lax.fori_loop(0, tokens // half, project, 0)
        @pl.when(crossed)
        def _():
            cot_swap().wait_recv()
            cot_gather.start()
            go("ga")
            cot_swap().wait_send()
            for r in range(SLICES):
                swap_copy(r, 1 - c).wait_send()

        pl.when(place.straight)(forward_cot)

        bound = prefix_ref[0:1, 0:1]

        def head(h, carry):
            base = h * 3 * hd
            for i in range(tokens // bq):
                first = i * bq
                q = qkv_ref[first:first + bq, span(base, hd)]
                count = max(i + 1, tokens // 2 // bk)

                def step(masked, j, state, first=first, q=q):
                    top, tot, out = state
                    rows = span(j * bk, bk)
                    s = dot(q, qkv_ref[rows, span(base + hd, hd)], NT) * scale
                    if masked:
                        kp = j * bk + lax.broadcasted_iota(jnp.int32, (bq, bk), 1)
                        qp = first + lax.broadcasted_iota(jnp.int32, (bq, bk), 0)
                        s = jnp.where(kp < jnp.maximum(qp + 1, bound), s, NEG)
                    new = jnp.maximum(top, jnp.max(s, axis=1, keepdims=True))
                    alpha = jnp.exp(top - new)
                    p = jnp.exp(s - new)
                    tot = tot * alpha + jnp.sum(p, axis=1, keepdims=True)
                    out = out * alpha + dot(p.astype(BF), qkv_ref[rows, span(base + 2 * hd, hd)], NN)
                    return new, tot, out

                state = (jnp.full((bq, 1), NEG, F32), jnp.zeros((bq, 1), F32), jnp.zeros((bq, hd), F32))
                state = lax.fori_loop(0, i, functools.partial(step, False), state)
                top, tot, out = lax.fori_loop(i, count, functools.partial(step, True), state)
                mixed_ref[first:first + bq, span(h * hd, hd)] = (out / tot).astype(BF)
                lse = jnp.broadcast_to(top + jnp.log(tot), (bq, 128))
                lse_ref[h, :, first:first + bq] = lse.T[0:8, :]
            return carry

        lax.fori_loop(0, heads, head, 0)
        go("gb")
        got("out")
        pl.when(crossed)(forward_cot)
        pass_on("ga")

        for r in range(SLICES):
            pltpu.make_async_copy(normed.at[rows_of(r)], normed_in_out.at[rows_of(r)], out_sems.at[r]).wait()
            for slot in range(3):
                gather.near(slot, r, mine).wait_send()
            for slot in range(4):
                sib(slot, r, c, mine).wait_send()
        for device in (place.sibling, place.across, place.along):
            pl.semaphore_signal(phase, inc=1, device_id=device, device_id_type=MESH)
        pl.semaphore_wait(phase, 3)

        class Blocks:
            def __init__(self, first, count):
                self.first, self.shape = first, (count, piece, width)

            def rows(self, index):
                if isinstance(index, tuple):
                    step, inside, *rest = index
                    start = (self.first + step) * piece + inside.start
                    return (pl.ds(pl.multiple_of(start, 16), inside.size), *rest)
                return (span((self.first + index) * piece, piece),)

            @property
            def at(self):
                return At(self)

            def __getitem__(self, index):
                return arena[self.rows(index)]

            def __setitem__(self, index, value):
                arena[self.rows(index)] = value

        class At:
            def __init__(self, blocks):
                self.blocks = blocks

            def __getitem__(self, index):
                return arena.at[self.blocks.rows(index)]

        buffers, first = [], 0
        for count in (4, 4, 2, 3, 3):
            buffers.append(Blocks(first, count))
            first += count

        def last(rows, total):
            middle = own_in_ref[rows, :].astype(F32) + total
            middle_ref[rows, :] = middle
            normed_own[rows, :] = row_norm(middle)[0].astype(BF)

        def after_z():
            go("ua")
            go("ub")
            pass_on("gb")
            got("ga")

        reduce_body(
            place, product(place, mixed_ref, parts("out"), False), last, [*buffers, *reduce_sems_],
            after_z=after_z,
        )

        full = arena.at[pl.ds(2 * tokens, tokens)]
        slopes_ref = arena.at[pl.ds(0, tokens)]
        hidden_ref = arena.at[pl.ds(tokens, tokens), pl.ds(0, hidden)]
        columns = (("ga", "ua"), ("gb", "ub"))
        waiting = []

        def fill(owner, which):
            rows = span(owner * piece, piece)
            gates, ups = (parts(name) for name in columns[which])

            def step(t, carry):
                taken = span(t * tile, tile)
                gate = up = None
                for gate_weight, up_weight, index in zip(gates, ups, place.order):
                    deep = gate_weight.shape[0]
                    value = full[rows, span(index * deep, deep)]
                    terms = dot(value, gate_weight[:, taken], NN), dot(value, up_weight[:, taken], NN)
                    gate, up = terms if gate is None else (gate + terms[0], up + terms[1])
                cols = span(which * part_width + t * tile, tile)
                up_cols = span(hidden + which * part_width + t * tile, tile)
                sig = 1.0 / (1.0 + jnp.exp(-gate))
                active = gate * sig
                hidden_ref[rows, cols] = (active * up).astype(BF)
                slopes_ref[rows, cols] = (up * sig * (1.0 + gate * (1.0 - sig))).astype(BF)
                slopes_ref[rows, up_cols] = active.astype(BF)
                return carry

            lax.fori_loop(0, part_width // tile, step, 0)

        def begin():
            go("da")
            go("db")

        def process(owner):
            waiting.append(owner)
            if len(waiting) == 1:
                pass_on("ua")
                got("gb")
                got("ua")
            fill(owner, 0)
            if len(waiting) == 3:
                pass_on("ub")
                got("ub")
                for earlier in waiting:
                    fill(earlier, 1)
            elif len(waiting) > 3:
                fill(owner, 1)

        gather_body(place, normed_own, full, feed_sems, process, begin=begin)
        for i, (ref, out) in enumerate(((full, normed_mid_out), (hidden_ref, hidden_out), (slopes_ref, slopes_out))):
            pltpu.make_async_copy(ref, out, out_sems.at[SLICES + i]).start()
        pass_on("da")
        cot_gather.finish()
        z_moves["db"].wait_recv()
        stores("db")[0].start()
        got("da")
        for i, (ref, out) in enumerate(((full, normed_mid_out), (hidden_ref, hidden_out), (slopes_ref, slopes_out))):
            pltpu.make_async_copy(ref, out, out_sems.at[SLICES + i]).wait()
        for move in (*z_moves.values(), *y_moves.values()):
            move.wait_send()
        for name in names:
            for copy in stores(name):
                copy.wait()

    def half_shape(weight):
        return jax.ShapeDtypeStruct((2, *weight.shape), BF)

    shape = jax.ShapeDtypeStruct
    outs = [
        *(half_shape(weight) for weight in weights),
        *(half_shape(weight) for weight in weights[:7]),
        shape((tokens, inner), BF),
        shape((tokens, heads * hd), BF),
        shape((heads, 8, tokens), F32),
        shape((piece, width), BF),
        shape((piece, width), F32),
        shape((tokens, width), BF),
        shape((tokens, width), BF),
        shape((tokens, width), BF),
        shape((tokens, hidden), BF),
        shape((tokens, 2 * hidden), BF),
    ]
    column_sems = [DMA((3, SLICES)), DMA((3, SLICES)), DMA((4,)), DMA((4,)), DMA((1,))]
    start_sems = [DMA((3, SLICES)), DMA((3, SLICES)), DMA((4, SLICES)), DMA((4, SLICES)), DMA((1,))]
    result = pl.pallas_call(
        kernel,
        out_shape=outs,
        in_specs=[ANYWHERE, ANYWHERE, VMEM_WHOLE, VMEM_WHOLE, VMEM_WHOLE] + [ANYWHERE] * 8,
        out_specs=[ANYWHERE] * 15 + [VMEM_WHOLE] * 5 + [ANYWHERE] * 5,
        scratch_shapes=[
            pltpu.VMEM((3 * tokens, width), BF),
            pltpu.VMEM((tokens, inner), F32),
            pltpu.VMEM((tokens, slice_width), BF),
            pltpu.VMEM((piece, width), BF),
            *(pltpu.VMEM((2, 2, *weight.shape), BF) for weight in weights[:7]),
            pltpu.VMEM((1, 2, *weights[7].shape), BF),
            DMA((8, 4)), DMA((8, 4)), DMA((8, 2)), DMA((SLICES + 3,)), DMA((SLICES + 1,)), DMA((SLICES + 1,)),
            pltpu.SemaphoreType.REGULAR,
            *start_sems, *column_sems, *reduce_sems(), *gather_scratch(),
        ],
        compiler_params=pltpu.CompilerParams(collective_id=ident, has_side_effects=True, vmem_limit_bytes=63 << 20),
        cost_estimate=pl.CostEstimate(
            flops=100 << 30, bytes_accessed=100 << 20, transcendentals=heads * tokens * tokens
        ),
        name="front",
    )(inputs, cot, prefix, *tables, *weights)
    return result[:8], result[8:15], result[15:]


BLOCKS = [(core, zl, x) for core in (0, 1) for zl in (0, 1) for x in (0, 1)]


def spread_greet(place, barrier):
    for core, zl, x in BLOCKS:
        mine = jnp.logical_and(place.straight, core * 4 + zl * 2 + x == place.block)

        @pl.when(jnp.logical_not(mine))
        def _(core=core, zl=zl, x=x):
            pl.semaphore_signal(
                barrier, inc=1, device_id=(place.y, core, place.c, zl, x), device_id_type=MESH
            )

    return 8 - jnp.where(place.straight, 1, 0)


def spread_scratch():
    return [DMA((8,)), DMA((8,)), DMA((1,))]


def spread_shape(piece):
    return jax.ShapeDtypeStruct((piece.shape[0] * 8, piece.shape[1] // 8), piece.dtype)


class Spread:
    def __init__(self, place, src, dst, sems):
        self.place, self.src, self.dst = place, src, dst
        self.send, self.recv, self.own = sems
        self.piece, self.width = src.shape[0], src.shape[1] // 8

    def copy(self, f):
        place = self.place
        return remote(
            self.src.at[:, pl.ds(f * self.width, self.width)], self.dst.at[span(place.block * self.piece, self.piece)],
            self.send.at[f], self.recv.at[place.block], (place.y, place.zh, *BLOCKS[f]),
        )

    def incoming(self, f):
        core, zl, x = BLOCKS[f]
        place = self.place
        return remote(
            self.src.at[:, pl.ds(f * self.width, self.width)], self.dst.at[pl.ds(f * self.piece, self.piece)],
            self.send.at[f], self.recv.at[f], (place.y, core, place.c, zl, x),
        )

    def own_copy(self):
        block = self.place.block
        return pltpu.make_async_copy(
            self.src.at[:, span(block * self.width, self.width)], self.dst.at[span(block * self.piece, self.piece)],
            self.own.at[0],
        )

    def each(self, act):
        for f in range(8):
            mine = jnp.logical_and(self.place.straight, self.place.block == f)
            pl.when(jnp.logical_not(mine))(functools.partial(act, f))

    def start(self):
        self.each(lambda f: self.copy(f).start())
        pl.when(self.place.straight)(lambda: self.own_copy().start())

    def wait(self):
        self.each(lambda f: self.incoming(f).wait_recv())
        self.each(lambda f: self.copy(f).wait_send())
        pl.when(self.place.straight)(lambda: self.own_copy().wait())


def rear_call(branch_own, out_halves, qkv_halves, qkv, mixed, lse, prefix, tables, grad_middle, own_in, ready, normed_in,
              gate_sum, up_own, up_other, heads, hd, ident):
    tokens, inner = qkv.shape
    piece, width = branch_own.shape
    inner_out = mixed.shape[1]
    block = width // 4
    tile = 256

    def kernel(
        branch_ref, out_1, out_2, qkv_1, qkv_2, qkv_ref, mixed_ref, lse_ref, prefix_ref, cos_ref, sin_ref, middle_ref,
        own_in_ref, ready_ref, normed_in_ref, gate_ref, up_own_ref, up_other_ref,
        gate_out, up_out, out_out, qkv_out, ready_out, result_out,
        full, grad_mixed, grad_rows, flipped, dk_ref, dv_ref, up_moved, out_grads, qkv_grads,
        y_sems, z_sems, load_sem, *sems
    ):
        place = Place()
        y = place.y
        reduce_refs, sems = sems[:9], sems[9:]
        gather_sems, ready_sems, result_sems = sems[:4], sems[4:7], sems[7:10]
        place.meet(spread_greet)
        y_up = Beyond(place, up_other_ref, up_moved, y_sems.at[0])
        y_out = Beyond(place, out_grads.at[0], out_grads.at[2], y_sems.at[1])
        y_qkv = Beyond(place, qkv_grads.at[0], qkv_grads.at[2], y_sems.at[2])
        z_gate = GradHalf(place, gate_ref, gate_out, z_sems.at[0])
        z_up = GradHalf(place, up_moved, up_out, z_sems.at[1])
        z_out = GradHalf(place, out_grads.at[1], out_out, z_sems.at[2])
        z_qkv = GradHalf(place, qkv_grads.at[1], qkv_out, z_sems.at[3])
        y_up.start()

        def add(own, moved, rows):
            def step(i, carry):
                where = span(i * 64, 64)
                for j in (0, 1):
                    total = own[j, where, :].astype(F32) + moved[j, where, :].astype(F32)
                    own[j, where, :] = total.astype(BF)
                return carry

            lax.fori_loop(0, rows // 64, step, 0)

        result_ref = full.at[pl.ds(0, piece)]

        out_parts = quarters(out_1, out_2)

        def process(owner):
            rows = span(owner * piece, piece)
            total = None
            for weight, index in zip(out_parts, place.order):
                part = dot(full[rows, span(index * block, block)], weight[...], NT)
                total = part if total is None else total + part
            grad_mixed[rows, :] = total.astype(BF)

        gather_body(place, branch_ref, full, gather_sems, process, begin=z_gate.start)
        ready_spread = Spread(place, ready_ref, ready_out, ready_sems)
        y_up.wait_recv()
        add(up_moved, up_own_ref, up_own.shape[1])
        z_up.start()
        ready_spread.start()

        def flip(source, columns):
            def step(i, carry):
                rows = span(i * tile, tile)
                flipped[0:columns, rows] = source[rows, :].T
                return carry

            lax.fori_loop(0, tokens // tile, step, 0)

        def weigh(grads, side, which, columns):
            def step(n, carry):
                i, m = n // (columns // tile), lax.rem(n, columns // tile)
                rows = span(m * tile, tile)
                value = dot(flipped[rows, :], full[:, span((which * 2 + i) * block, block)], NN)
                grads[side, i, rows, :] = value.astype(BF)
                return carry

            lax.fori_loop(0, 2 * (columns // tile), step, 0)

        flip(mixed_ref, inner_out)
        weigh(out_grads, 0, 1 - y, inner_out)
        y_out.start()
        weigh(out_grads, 1, y, inner_out)
        load = pltpu.make_async_copy(normed_in_ref, full, load_sem.at[0])
        load.start()
        attend_back_body(
            qkv_ref, mixed_ref, grad_mixed, lse_ref, prefix_ref[0:1, 0:1], cos_ref, sin_ref, grad_rows, dk_ref, dv_ref,
            heads, hd,
        )
        load.wait()

        def last(rows, total):
            value = back_rows(middle_ref[rows, :], own_in_ref[rows, :].astype(F32), total)
            result_ref[rows, :] = value.astype(BF)

        def before_z():
            flip(grad_rows, inner)
            weigh(qkv_grads, 0, 1 - y, inner)
            y_qkv.start()

        def after_z():
            y_out.wait_recv()
            add(out_grads.at[1], out_grads.at[2], inner_out)
            z_out.start()
            weigh(qkv_grads, 1, y, inner)

        reduce_body(
            place, product(place, grad_rows, quarters(qkv_1, qkv_2), True), last, reduce_refs,
            before_z=before_z, after_z=after_z,
        )
        result_spread = Spread(place, result_ref, result_out, result_sems)
        result_spread.start()
        y_qkv.wait_recv()
        add(qkv_grads.at[1], qkv_grads.at[2], inner)
        z_qkv.start()
        for move in (z_gate, z_up, z_out, z_qkv):
            move.wait_recv()
        ready_spread.wait()
        result_spread.wait()
        for move in (y_up, y_out, y_qkv, z_gate, z_up, z_out, z_qkv):
            move.wait_send()

    shape = jax.ShapeDtypeStruct
    spread = spread_shape(ready)
    return pl.pallas_call(
        kernel,
        out_shape=[
            shape(gate_sum.shape, BF), shape(up_own.shape, BF), shape((2, inner_out, block), BF),
            shape((2, inner, block), BF), spread, spread,
        ],
        in_specs=[VMEM_WHOLE] * 14 + [ANYWHERE, ANYWHERE, VMEM_WHOLE, ANYWHERE],
        out_specs=[ANYWHERE] * 6,
        scratch_shapes=[
            pltpu.VMEM((tokens, width), BF),
            pltpu.VMEM((tokens, inner_out), BF),
            pltpu.VMEM((tokens, inner), BF),
            pltpu.VMEM((inner, tokens), BF),
            pltpu.VMEM((tokens, hd), F32),
            pltpu.VMEM((tokens, hd), F32),
            pltpu.VMEM(up_own.shape, BF),
            pltpu.VMEM((3, 2, inner_out, block), BF),
            pltpu.VMEM((3, 2, inner, block), BF),
            DMA((3, 4)), DMA((4, 4)), DMA((1,)),
            *reduce_scratch(piece, width), *gather_scratch(), *spread_scratch(), *spread_scratch(),
        ],
        compiler_params=pltpu.CompilerParams(
            collective_id=ident, has_side_effects=True, vmem_limit_bytes=(64 << 20) - (64 << 10)
        ),
        cost_estimate=pl.CostEstimate(flops=100 << 30, bytes_accessed=100 << 20, transcendentals=heads * tokens * tokens),
        name="rear",
    )(
        branch_own, *out_halves, *qkv_halves, qkv, mixed, lse, prefix, *tables, grad_middle, own_in, ready, normed_in,
        gate_sum, up_own, up_other,
    )


def local_fine(inputs, prefix_len, w_qkv, w_out, w_up_gate, w_down, cotangent):
    heads, hd = w_qkv.shape[1], w_qkv.shape[2] // 3
    hidden_width = w_down.shape[0]
    tokens = inputs.shape[0]
    y = lax.axis_index("y")
    prefix_len = lax.ppermute(prefix_len, ("core", "zh"), [(0, 0), (1, 2), (2, 1), (3, 3)])
    prefix = jnp.broadcast_to(prefix_len[:, None], (8, 128))
    cosine, sine = rope_tables(tokens, hd)
    tables = (jnp.concatenate([cosine, cosine], axis=1), jnp.concatenate([-sine, sine], axis=1))
    part = hidden_width // 2
    ga, gb = w_up_gate[:, 0, :part], w_up_gate[:, 0, part:]
    ua, ub = w_up_gate[:, 1, :part], w_up_gate[:, 1, part:]
    da, db = w_down[:part], w_down[part:]

    weights = (w_qkv.reshape(w_qkv.shape[0], -1), w_out, ga, gb, ua, ub, da, db)
    firsts, seconds, results = front_call(inputs, cotangent, prefix, tables, weights, heads, hd, 1)
    qkv_1, out_1, ga_1, gb_1, ua_1, ub_1, da_1, db_1 = firsts
    qkv_2, out_2, ga_2, gb_2, ua_2, ub_2, da_2 = seconds
    qkv, mixed, lse, own_in, middle, normed_in, cot_full, normed_mid, hidden, slopes = results
    gates = (ga_1, ga_2, gb_1, gb_2)

    def halves(spec, left, right, axis):
        side = left if axis == 0 else right
        half = side.shape[1] // 2

        def cut(which):
            taken = lax.dynamic_slice_in_dim(side, which * half, half, 1)
            return mm(spec, taken, right) if axis == 0 else mm(spec, left, taken)

        return cut(y), cut(1 - y).astype(BF)

    def joined(own, moved, axis):
        total = (own + moved.astype(F32)).astype(BF)
        if axis == 0:
            return total.reshape(2, total.shape[0] // 2, total.shape[1])
        return jnp.swapaxes(total.reshape(total.shape[0], 2, total.shape[1] // 2), 0, 1)

    down_own, down_other = halves("tf,td->fd", hidden, cot_full, 1)
    (grad_middle, branch_own, grad_gate_up), (db_2, down_moved) = middle_call(
        cot_full, slopes, gates, (ua_1, ua_2, ub_1, ub_2), (da_1, da_2), db_1,
        [("beyond", db_1), ("beyond", down_other)], middle, 5,
    )
    gate_grad, gate_other = halves("td,tf->df", normed_mid, grad_gate_up[:, :hidden_width], 0)
    up_grad, up_other = halves("td,tf->df", normed_mid, grad_gate_up[:, hidden_width:], 0)
    (outputs,), (down_final, gate_moved) = down_call(
        hidden, (da_1, db_1), (da_2, db_2), middle,
        [("grad", joined(down_own, down_moved, 1)), ("beyond", gate_other)], 6,
    )
    def blocks(array):
        return array.reshape(2, array.shape[0] // 2, array.shape[1])

    gate_final, up_final, out_final, qkv_final, outputs, input_grad = rear_call(
        branch_own, (out_1, out_2), (qkv_1, qkv_2), qkv, mixed, lse, prefix, tables, grad_middle, own_in, outputs,
        normed_in, joined(gate_grad, gate_moved, 0), blocks(up_grad.astype(BF)), blocks(up_other), heads, hd, 7,
    )

    def summed(parts):
        return parts[0].astype(F32) + parts[1].astype(F32)

    return (
        outputs,
        input_grad.astype(F32),
        summed(qkv_final).T.reshape(-1, heads, 3 * hd),
        summed(out_final),
        jnp.stack([summed(gate_final), summed(up_final)], axis=1),
        summed(down_final),
    )


def solution(mesh):
    row_size, col_size = mesh.shape["row"], mesh.shape["col"]
    fine = (row_size, col_size) == (4, 8)
    if fine:
        names, shape, body = AXES, (2,) * 5, local_fine
        row, col = AXES[:2], AXES[2:]
    else:
        names = ("rmaj", "core", "cmaj", "cmin")
        shape = (row_size // 2, 2, 4, col_size // 4)
        body = functools.partial(local, shape[3] == 2)
        row, col = names[:2], names[2:]
    outs = (P(row, col), P(row, col), P(row, col, None), P(col, row), P(row, None, col), P(col, row))
    return jax.shard_map(
        body,
        mesh=Mesh(mesh.devices.reshape(shape), names),
        in_specs=(P(row, col), P(row), P(row, col, None), P(col, row), P(row, None, col), P(col, row), P(row, col)),
        out_specs=outs,
        check_vma=False,
    )
```

```python
import functools

import jax
import jax.numpy as jnp
from jax import lax
from jax.experimental import pallas as pl
from jax.experimental.pallas import tpu as pltpu
from jax.sharding import Mesh
from jax.sharding import PartitionSpec as P

EPSILON = 1e-05
NEG = -1e30
F32 = jnp.float32
BF = jnp.bfloat16
NN = (((1,), (0,)), ((), ()))
NT = (((1,), (1,)), ((), ()))
TN = (((0,), (0,)), ((), ()))
def dot(a, b, dims):
    return lax.dot_general(a, b, dims, preferred_element_type=F32)

def fwd_kernel(prefix_ref, q_ref, k_ref, v_ref, o_ref, lse_ref, *, bq, bk, scale):
    i = pl.program_id(1)
    first = i * bq
    prefix = prefix_ref[0]
    q = q_ref[...]
    limit = jnp.maximum(first + bq, prefix)
    total = (limit + bk - 1) // bk
    clear = jnp.maximum(first, prefix) // bk
    def step(masked, j, carry):
        top, tot, acc = carry
        rows = pl.ds(pl.multiple_of(j * bk, bk), bk)
        s = dot(q, k_ref[rows, :], NT) * scale
        if masked:
            kp = j * bk + lax.broadcasted_iota(jnp.int32, (bq, bk), 1)
            qp = first + lax.broadcasted_iota(jnp.int32, (bq, bk), 0)
            s = jnp.where(kp < jnp.maximum(qp + 1, prefix), s, NEG)
        new = jnp.maximum(top, jnp.max(s, axis=1, keepdims=True))
        alpha = jnp.exp(top - new)
        p = jnp.exp(s - new)
        tot = tot * alpha + jnp.sum(p, axis=1, keepdims=True)
        acc = acc * alpha + dot(p.astype(BF), v_ref[rows, :], NN)
        return new, tot, acc
    carry = (jnp.full((bq, 1), NEG, F32), jnp.zeros((bq, 1), F32), jnp.zeros((bq, q.shape[1]), F32))
    carry = lax.fori_loop(0, clear, functools.partial(step, False), carry)
    top, tot, acc = lax.fori_loop(clear, total, functools.partial(step, True), carry)
    o_ref[...] = (acc / tot).astype(o_ref.dtype)
    lse = jnp.broadcast_to(top + jnp.log(tot), (bq, 128))
    lse_ref[0] = lse.T[0:8, :]

def attend_fwd(qkv, prefix, heads, *, bq=512, bk=512, hd=128):
    seq = qkv.shape[0]
    return pl.pallas_call(
        functools.partial(fwd_kernel, bq=bq, bk=bk, scale=hd ** -0.5),
        grid_spec=pltpu.PrefetchScalarGridSpec(
            num_scalar_prefetch=1, grid=(heads, seq // bq),
            in_specs=[pl.BlockSpec((bq, hd), lambda h, i, p: (i, 3 * h)),
                      pl.BlockSpec((seq, hd), lambda h, i, p: (0, 3 * h + 1)),
                      pl.BlockSpec((seq, hd), lambda h, i, p: (0, 3 * h + 2))],
            out_specs=[pl.BlockSpec((bq, hd), lambda h, i, p: (i, h)),
                       pl.BlockSpec((1, 8, bq), lambda h, i, p: (h, 0, i))]),
        out_shape=[jax.ShapeDtypeStruct((seq, heads * hd), BF), jax.ShapeDtypeStruct((heads, 8, seq), F32)],
        cost_estimate=pl.CostEstimate(flops=4 * heads * seq * seq * hd, bytes_accessed=8 * heads * seq * hd, transcendentals=heads * seq * seq),
        name="attend_forward",
    )(prefix, qkv, qkv, qkv)

def bwd_kernel(prefix_ref, qkv_ref, o_ref, do_ref, lse_ref, cos_ref, sin_ref, out_ref, dk_ref, dv_ref, delta_ref, *, bq, bk, hd, scale):
    seq = qkv_ref.shape[0]
    prefix = prefix_ref[0]
    dk_ref[...] = jnp.zeros_like(dk_ref)
    dv_ref[...] = jnp.zeros_like(dv_ref)
    def deltas(i, _):
        rows = pl.ds(pl.multiple_of(i * bq, bq), bq)
        prod = (do_ref[rows, :].astype(F32) * o_ref[rows, :].astype(F32)).T
        delta_ref[:, rows] = jnp.broadcast_to(jnp.sum(prod, axis=0, keepdims=True), (8, bq))
        return 0
    lax.fori_loop(0, seq // bq, deltas, 0)
    def unrotate(g, rows):
        cos, sin = cos_ref[rows, :], sin_ref[rows, :]
        half = hd // 2
        a, b = g[:, :half], g[:, half:]
        return jnp.concatenate([a * cos + b * sin, b * cos - a * sin], axis=1)
    def q_step(i, _):
        first = i * bq
        qrows = pl.ds(pl.multiple_of(first, bq), bq)
        q = qkv_ref[qrows, 0:hd]
        do = do_ref[qrows, :]
        lse = lse_ref[0, 0:1, qrows]
        delta = delta_ref[0:1, qrows]
        limit = jnp.maximum(first + bq, prefix)
        total = (limit + bk - 1) // bk
        clear = jnp.maximum(first, prefix) // bk
        def step(masked, j, dq):
            krows = pl.ds(pl.multiple_of(j * bk, bk), bk)
            k = qkv_ref[krows, hd:2 * hd]
            v = qkv_ref[krows, 2 * hd:3 * hd]
            s = dot(k, q, NT) * scale
            p = jnp.exp(s - lse)
            if masked:
                kp = j * bk + lax.broadcasted_iota(jnp.int32, (bk, bq), 0)
                qp = first + lax.broadcasted_iota(jnp.int32, (bk, bq), 1)
                p = jnp.where(kp < jnp.maximum(qp + 1, prefix), p, 0.0)
            dp = dot(v, do, NT)
            dv_ref[krows, :] += dot(p.astype(BF), do, NN)
            ds = (p * (dp - delta)).astype(BF)
            dk_ref[krows, :] += dot(ds, q, NN)
            return dq + dot(ds, k, TN)
        dq = lax.fori_loop(0, clear, functools.partial(step, False), jnp.zeros((bq, hd), F32))
        dq = lax.fori_loop(clear, total, functools.partial(step, True), dq)
        out_ref[qrows, 0:hd] = unrotate(dq * scale, qrows).astype(BF)
        return 0
    lax.fori_loop(0, seq // bq, q_step, 0)
    def fin(i, _):
        rows = pl.ds(pl.multiple_of(i * bq, bq), bq)
        out_ref[rows, hd:2 * hd] = unrotate(dk_ref[rows, :] * scale, rows).astype(BF)
        out_ref[rows, 2 * hd:3 * hd] = dv_ref[rows, :].astype(BF)
        return 0
    lax.fori_loop(0, seq // bq, fin, 0)

def attend_bwd(qkv, mixed, dmixed, lse, prefix, cos, sin, heads, *, bq=512, bk=512, hd=128):
    seq = qkv.shape[0]
    return pl.pallas_call(
        functools.partial(bwd_kernel, bq=bq, bk=bk, hd=hd, scale=hd ** -0.5),
        grid_spec=pltpu.PrefetchScalarGridSpec(
            num_scalar_prefetch=1, grid=(heads,),
            in_specs=[pl.BlockSpec((seq, 3 * hd), lambda h, p: (0, h)),
                      pl.BlockSpec((seq, hd), lambda h, p: (0, h)),
                      pl.BlockSpec((seq, hd), lambda h, p: (0, h)),
                      pl.BlockSpec((1, 8, seq), lambda h, p: (h, 0, 0)),
                      pl.BlockSpec((seq, hd // 2), lambda h, p: (0, 0)),
                      pl.BlockSpec((seq, hd // 2), lambda h, p: (0, 0))],
            out_specs=[pl.BlockSpec((seq, 3 * hd), lambda h, p: (0, h))],
            scratch_shapes=[pltpu.VMEM((seq, hd), F32), pltpu.VMEM((seq, hd), F32), pltpu.VMEM((8, seq), F32)]),
        out_shape=[jax.ShapeDtypeStruct((seq, heads * 3 * hd), BF)],
        cost_estimate=pl.CostEstimate(flops=10 * heads * seq * seq * hd, bytes_accessed=20 * heads * seq * hd, transcendentals=heads * seq * seq),
        name="attend_backward",
    )(prefix, qkv, mixed, dmixed, lse, cos, sin)[0]


def rope_tables(count, head_dim):
    positions = jnp.arange(count, dtype=jnp.int32).astype(F32)
    frequency = 10000.0 ** (-(jnp.arange(head_dim // 2).astype(F32) * 2.0 / head_dim))
    angles = positions[:, None] * frequency[None, :]
    return jnp.cos(angles), jnp.sin(angles)


def rotate(values, cosine, sine):
    half = values.shape[-1] // 2
    a, b = values[..., :half], values[..., half:]
    return jnp.concatenate([a * cosine - b * sine, b * cosine + a * sine], axis=-1)


def norm(values):
    center = values - jnp.mean(values, axis=-1, keepdims=True)
    inv_std = lax.rsqrt(jnp.mean(center * center, axis=-1, keepdims=True) + EPSILON)
    return center * inv_std, inv_std


def norm_back(grad, normed, inv_std):
    mean_grad = jnp.mean(grad, axis=-1, keepdims=True)
    mean_cross = jnp.mean(grad * normed, axis=-1, keepdims=True)
    return inv_std * (grad - mean_grad - normed * mean_cross)


def mm(spec, left, right):
    return jnp.einsum(spec, left, right, preferred_element_type=F32)


def local(swap, inputs, prefix_len, w_qkv, w_out, w_up_gate, w_down, cotangent):
    rows = ("rmaj", "cmin") if swap else ("rmaj", "core")
    cols = ("cmaj", "core") if swap else ("cmaj", "cmin")

    def exchange(value):
        if not swap:
            return value
        return lax.ppermute(value, ("core", "cmin"), [(0, 0), (1, 2), (2, 1), (3, 3)])

    def scatter(value):
        return lax.psum_scatter(value.astype(BF), cols, scatter_dimension=0, tiled=True).astype(F32)

    def spread(value):
        return lax.all_to_all(value, cols, 1, 0, tiled=True)

    prefix_len = exchange(prefix_len)
    inputs, cotangent = exchange(inputs), exchange(cotangent)
    w_qkv, w_out = exchange(w_qkv), exchange(w_out)
    w_up_gate, w_down = exchange(w_up_gate), exchange(w_down)
    tokens = inputs.shape[0]
    heads, head_dim = w_qkv.shape[1], w_qkv.shape[2] // 3
    hidden_width = w_down.shape[0]
    full_in = lax.all_gather(inputs, cols, axis=1, tiled=True)
    width = full_in.shape[1]
    qkv_all = lax.all_gather(w_qkv, rows, axis=0, tiled=True).reshape(width, heads * 3 * head_dim)
    out_all = lax.all_gather(w_out, rows, axis=1, tiled=True)
    up_all = lax.all_gather(w_up_gate, rows, axis=0, tiled=True).reshape(width, 2 * hidden_width)
    down_all = lax.all_gather(w_down, rows, axis=1, tiled=True)
    cot_full = lax.all_gather(cotangent, cols, axis=1, tiled=True)
    piece = tokens // lax.axis_size(cols)
    first = lax.axis_index(cols) * piece
    own_in = lax.dynamic_slice_in_dim(full_in, first, piece, 0).astype(F32)
    own_cot = lax.dynamic_slice_in_dim(cot_full, first, piece, 0).astype(F32)

    normed_in = norm(full_in.astype(F32))[0].astype(BF)
    qkv_rows = mm("td,de->te", normed_in, qkv_all).reshape(tokens, heads, 3, head_dim)
    cosine, sine = rope_tables(tokens, head_dim)
    turned = rotate(qkv_rows[:, :, :2], cosine[:, None, None], sine[:, None, None])
    qkv = jnp.concatenate([turned, qkv_rows[:, :, 2:]], axis=2).astype(BF)
    qkv = qkv.reshape(tokens, heads * 3 * head_dim)
    mixed, lse = attend_fwd(qkv, prefix_len, heads, hd=head_dim)
    middle = own_in + scatter(mm("tc,cd->td", mixed, out_all))
    normed_two, inv_two = norm(middle)
    normed_mid = lax.all_gather(normed_two.astype(BF), cols, axis=0, tiled=True)
    gate_up = mm("td,df->tf", normed_mid, up_all)
    gate, up = gate_up[:, :hidden_width], gate_up[:, hidden_width:]
    sig = jax.nn.sigmoid(gate)
    active = gate * sig
    hidden = (active * up).astype(BF)
    outputs = middle + scatter(mm("tf,fd->td", hidden, down_all))
    outputs = exchange(spread(outputs.astype(BF)))

    grad_hidden = mm("td,fd->tf", cot_full, down_all)
    grad_gate = grad_hidden * up * sig * (1.0 + gate * (1.0 - sig))
    grad_gate_up = jnp.concatenate([grad_gate, grad_hidden * active], axis=1).astype(BF)
    grad_down = mm("tf,td->fd", hidden, cot_full).astype(BF)
    grad_down = lax.psum_scatter(grad_down, rows, scatter_dimension=1, tiled=True)
    grad_up = mm("td,tf->df", normed_mid, grad_gate_up).astype(BF)
    grad_up = lax.psum_scatter(grad_up, rows, scatter_dimension=0, tiled=True)
    grad_normed = scatter(mm("tf,df->td", grad_gate_up, up_all))
    grad_middle = own_cot + norm_back(grad_normed, normed_two, inv_two)
    grad_branch = lax.all_gather(grad_middle.astype(BF), cols, axis=0, tiled=True)
    grad_out = mm("tc,td->cd", mixed, grad_branch).astype(BF)
    grad_out = lax.psum_scatter(grad_out, rows, scatter_dimension=1, tiled=True)
    grad_mixed = mm("td,cd->tc", grad_branch, out_all).astype(BF)
    grad_rows = attend_bwd(qkv, mixed, grad_mixed, lse, prefix_len, cosine, sine, heads, hd=head_dim)
    grad_in = scatter(mm("te,de->td", grad_rows, qkv_all))
    grad_qkv = mm("td,te->de", normed_in, grad_rows).astype(BF)
    grad_qkv = lax.psum_scatter(grad_qkv, rows, scatter_dimension=0, tiled=True)
    normed_own, inv_own = norm(own_in)
    input_grad = grad_middle + norm_back(grad_in, normed_own, inv_own)
    input_grad = exchange(spread(input_grad.astype(BF))).astype(F32)
    return (
        outputs,
        input_grad,
        exchange(grad_qkv).astype(F32).reshape(-1, heads, 3 * head_dim),
        exchange(grad_out).astype(F32),
        exchange(grad_up).astype(F32).reshape(-1, 2, hidden_width),
        exchange(grad_down).astype(F32),
    )


AXES = ("y", "core", "zh", "zl", "x")
GROUP = ("core", "zl", "x")
MESH = pl.DeviceIdType.MESH
DMA = pltpu.SemaphoreType.DMA
VMEM_WHOLE = pl.BlockSpec(memory_space=pltpu.VMEM)
ANYWHERE = pl.BlockSpec(memory_space=pl.ANY)


class Place:
    def __init__(self):
        self.y, self.c, self.zh, self.zl, self.x = (lax.axis_index(name) for name in AXES)
        y, c, zh, zl, x = self.y, self.c, self.zh, self.zl, self.x
        self.sibling = (y, 1 - c, zh, zl, x)
        self.across = (y, c, zh, zl, 1 - x)
        self.along = (y, c, zh, 1 - zl, x)
        self.beyond = (1 - y, c, zh, zl, x)
        self.far = [(y, core, 1 - zh, zl, x) for core in (0, 1)]
        self.far_role = (y, zh, 1 - zh, zl, x)
        self.straight = c == zh
        self.outer = zl == zh
        self.order = [2 * y, 2 * y + 1, 2 * (1 - y), 2 * (1 - y) + 1]
        self.block = c * 4 + zl * 2 + x

    def chip(self, dz, dx):
        return lax.rem(self.zl + dz, 2) * 2 + lax.rem(self.x + dx, 2)

    def meet(self, greet=None):
        devices = [self.sibling, self.across, self.along, self.beyond, *self.far]
        barrier = pltpu.get_barrier_semaphore()
        for device in devices:
            pl.semaphore_signal(barrier, inc=1, device_id=device, device_id_type=MESH)
        more = greet(self, barrier) if greet else 0
        pl.semaphore_wait(barrier, len(devices) + more)


def span(start, size):
    return pl.ds(pl.multiple_of(start, size), size)


def remote(src, dst, send_sem, recv_sem, device):
    return pltpu.make_async_remote_copy(
        src_ref=src, dst_ref=dst, send_sem=send_sem, recv_sem=recv_sem, device_id=device, device_id_type=MESH
    )


class Beyond:
    along_z = False

    def __init__(self, place, src, dst, sem):
        self.copy = remote(src, dst, sem.at[0], sem.at[2], place.beyond)

    def start(self):
        self.copy.start()

    def wait_recv(self):
        self.copy.wait_recv()

    def wait_send(self):
        self.copy.wait_send()


class WeightHalf:
    along_z = True

    def __init__(self, place, src, dst, sem):
        c = place.c
        self.straight = place.straight
        self.outward = remote(src, dst.at[c], sem.at[0], sem.at[2 + c], place.far_role)
        self.aside = remote(src, dst.at[c], sem.at[1], sem.at[2 + c], place.sibling)
        self.here = pltpu.make_async_copy(src, dst.at[c], sem.at[1])
        self.from_sibling = remote(src, dst.at[1 - c], sem.at[1], sem.at[3 - c], place.sibling)
        self.from_far = [remote(src, dst.at[i], sem.at[0], sem.at[2 + i], place.far_role) for i in (0, 1)]

    def start(self):
        self.outward.start()

        @pl.when(self.straight)
        def _():
            self.here.start()

        @pl.when(jnp.logical_not(self.straight))
        def _():
            self.aside.start()

    def wait_recv(self):
        @pl.when(self.straight)
        def _():
            self.here.wait()
            self.from_sibling.wait_recv()

        @pl.when(jnp.logical_not(self.straight))
        def _():
            for copy in self.from_far:
                copy.wait_recv()

    def wait_send(self):
        self.outward.wait_send()

        @pl.when(jnp.logical_not(self.straight))
        def _():
            self.aside.wait_send()


class GradHalf:
    along_z = True

    def __init__(self, place, src, dst, sem):
        c, zh = place.c, place.zh
        self.straight = place.straight
        self.here = pltpu.make_async_copy(src.at[c], dst.at[zh], sem.at[0])
        self.aside = remote(src.at[1 - c], dst.at[zh], sem.at[1], sem.at[2 + zh], place.sibling)
        self.outward = [remote(src.at[i], dst.at[zh], sem.at[i], sem.at[2 + zh], place.far[i]) for i in (0, 1)]
        self.from_sibling = remote(src.at[c], dst.at[zh], sem.at[1], sem.at[2 + zh], place.sibling)
        self.from_far = remote(src.at[c], dst.at[1 - zh], sem.at[0], sem.at[3 - zh], place.far[0])

    def start(self):
        @pl.when(self.straight)
        def _():
            self.here.start()
            self.aside.start()

        @pl.when(jnp.logical_not(self.straight))
        def _():
            for copy in self.outward:
                copy.start()

    def wait_recv(self):
        self.from_far.wait_recv()

        @pl.when(self.straight)
        def _():
            self.here.wait()

        @pl.when(jnp.logical_not(self.straight))
        def _():
            self.from_sibling.wait_recv()

    def wait_send(self):
        @pl.when(self.straight)
        def _():
            self.aside.wait_send()

        @pl.when(jnp.logical_not(self.straight))
        def _():
            for copy in self.outward:
                copy.wait_send()


KINDS = {"beyond": Beyond, "weight": WeightHalf, "grad": GradHalf}


def moved_shape(kind, src):
    shape = (2, *src.shape) if kind == "weight" else src.shape
    return jax.ShapeDtypeStruct(shape, src.dtype)


class Under:
    def __init__(self, place, moves):
        self.place, self.moves = place, moves
        self.z = [move for kind, move in moves if move.along_z]
        self.y = [move for kind, move in moves if not move.along_z and not isinstance(kind, int)]
        self.follow = [(moves[kind][1], move) for kind, move in moves if isinstance(kind, int)]

    def start_y(self):
        for move in self.y:
            move.start()

    def start_z(self, outer=None):
        def start():
            for move in self.z:
                move.start()

        if outer is None:
            start()
        else:
            pl.when(self.place.outer if outer else jnp.logical_not(self.place.outer))(start)

    def start_follow(self):
        for ahead, move in self.follow:
            ahead.wait_recv()
            move.start()

    def end(self, skip=0):
        done = [ahead for ahead, _ in self.follow]
        for _, move in self.moves[skip:]:
            if move not in done:
                move.wait_recv()


def comm_call(
    body, name, ident, inputs, outs, scratch, moves=(), flops=0, transcendentals=0, spaces=None, greet=None
):
    n_in, n_out, n_move = len(inputs), len(outs), len(moves)
    own_source = [i for i, (kind, _) in enumerate(moves) if not isinstance(kind, int)]

    def kernel(*refs):
        ins, refs = refs[:n_in], refs[n_in:]
        sources, refs = refs[:len(own_source)], refs[len(own_source):]
        results, refs = refs[:n_out], refs[n_out:]
        targets, refs = refs[:n_move], refs[n_move:]
        sems, rest = refs[0], refs[1:]
        place = Place()
        place.meet(greet)
        made = []
        for i, (kind, _) in enumerate(moves):
            if isinstance(kind, int):
                made.append((kind, Beyond(place, targets[kind], targets[i], sems.at[i])))
            else:
                made.append((kind, KINDS[kind](place, sources[own_source.index(i)], targets[i], sems.at[i])))
        body(place, ins, results, rest, Under(place, made), targets)
        for _, move in made:
            move.wait_send()

    arrays = [*inputs, *(moves[i][1] for i in own_source)]
    shapes = list(outs)
    moved = []
    for kind, array in moves:
        moved.append(moved[kind] if isinstance(kind, int) else moved_shape(kind, array))
    shapes += moved
    in_specs = (spaces or [VMEM_WHOLE] * n_in) + [ANYWHERE] * len(own_source)
    size = sum(s.size * s.dtype.itemsize for s in (*arrays, *shapes))
    result = pl.pallas_call(
        kernel,
        out_shape=shapes,
        in_specs=in_specs,
        out_specs=[VMEM_WHOLE] * (n_out + n_move),
        scratch_shapes=[DMA((max(n_move, 1), 4)), *scratch],
        compiler_params=pltpu.CompilerParams(collective_id=ident, has_side_effects=True, vmem_limit_bytes=63 << 20),
        cost_estimate=pl.CostEstimate(
            flops=flops + (20 << 30), bytes_accessed=size, transcendentals=transcendentals
        ),
        name=name,
    )(*arrays)
    return result[:n_out], result[n_out:]


def each_rows(count, body, size=32):
    def step(i, carry):
        body(span(i * size, size))
        return carry

    lax.fori_loop(0, count // size, step, 0)


def row_norm(values):
    center = values - jnp.mean(values, axis=-1, keepdims=True)
    inv_std = lax.rsqrt(jnp.mean(center * center, axis=-1, keepdims=True) + EPSILON)
    return center * inv_std, inv_std


SLICES = 4
NORM_ROWS = 64
NORM_UNROLL = 1


def reduce_sems():
    return [DMA((4,)), DMA((4,)), DMA((3, SLICES)), DMA((3, SLICES))]


def reduce_scratch(piece, width):
    return [pltpu.VMEM((count, piece, width), BF) for count in (4, 4, 2, 3, 3)] + reduce_sems()


def nothing():
    pass


def reduce_body(place, compute, last, scratch, begin=nothing, before_z=nothing, after_z=nothing, split=0):
    sib_out, sib_in, own, near_out, near_in, sib_send, sib_recv, near_send, near_recv = scratch
    piece = own.shape[1]
    c = place.c
    size = piece // SLICES
    begin()

    def sib_copy(step):
        return remote(sib_out.at[step], sib_in.at[step], sib_send.at[step], sib_recv.at[step], place.sibling)

    def near_copy(step, r, turned=False):
        device = place.along if step == 2 or turned else place.across
        rows = span(r * size, size)
        return remote(
            near_out.at[step, rows], near_in.at[step, rows], near_send.at[step, r], near_recv.at[step, r], device
        )

    def finish(step):
        slot = step % 2
        sib_copy(step).wait_recv()

        def send(joins, turned, r, carry):
            if joins:
                near_copy(0, r).wait_recv()
            rows = span(r * size, size)
            total = own[slot, rows, :].astype(F32) + sib_in[step, rows, :].astype(F32)
            if joins:
                total = total + near_in[0, rows, :].astype(F32)
            near_out[step, rows, :] = total.astype(BF)
            near_copy(step, r, turned).start()
            return carry

        lax.fori_loop(0, SLICES - split, functools.partial(send, step == 2, False), 0)
        if split:
            lax.fori_loop(SLICES - split, SLICES, functools.partial(send, step == 1, step == 0), 0)

    def step(s, carry):
        target = place.chip(1 - lax.rem(s, 2), 1 - s // 2)
        compute((1 - c) * 4 + target, sib_out.at[s])
        sib_copy(s).start()
        for index in (0, 1):
            @pl.when(s == index + 1)
            def _(index=index):
                finish(index)

        compute(c * 4 + target, own.at[lax.rem(s, 2)])
        return carry

    lax.fori_loop(0, 4, step, 0)
    before_z()
    finish(2)
    after_z()
    sib_copy(3).wait_recv()

    def arrive(r, carry):
        near_copy(1, r).wait_recv()
        near_copy(2, r).wait_recv()

        def final(i, carry):
            rows = span(r * size + i * 16, 16)
            total = own[1, rows, :].astype(F32) + sib_in[3, rows, :].astype(F32)
            last(rows, total + near_in[1, rows, :].astype(F32) + near_in[2, rows, :].astype(F32))
            return carry

        return lax.fori_loop(0, size // 16, final, carry)

    lax.fori_loop(0, SLICES, arrive, 0)
    for s in range(4):
        sib_copy(s).wait_send()

    def sent(r, carry):
        for s in range(3):
            near_copy(s, r).wait_send()
        return carry

    lax.fori_loop(0, SLICES, sent, 0)


def product(place, left_ref, weights, transposed):
    def compute(owner, out_ref):
        piece = out_ref.shape[0]
        left = left_ref[span(owner * piece, piece), :]
        for weight, index in zip(weights, place.order):
            size = weight.shape[0] if transposed else weight.shape[1]
            part = dot(left, weight[...], NT if transposed else NN)
            out_ref[:, span(index * size, size)] = part.astype(out_ref.dtype)

    return compute


def back_rows(base, value, total):
    normed, inv_std = row_norm(value)
    mean_grad = jnp.mean(total, axis=-1, keepdims=True)
    mean_cross = jnp.mean(total * normed, axis=-1, keepdims=True)
    return base + inv_std * (total - mean_grad - normed * mean_cross)


def quarters(first, second):
    return [first.at[0], first.at[1], second.at[0], second.at[1]]


def beside(under):
    def begin():
        under.start_y()
        under.start_z()

    return dict(begin=begin, after_z=under.start_follow)


class Turned:
    def __init__(self, source, stage, sems, flipped):
        self.source, self.stage, self.sems, self.flipped = source, stage, sems, flipped
        self.tile = stage.shape[1]
        self.count = flipped.shape[1] // self.tile

    def load(self, i):
        slot = lax.rem(i, 2)
        rows = span(i * self.tile, self.tile)
        return pltpu.make_async_copy(self.source.at[rows], self.stage.at[slot], self.sems.at[slot])

    def turn(self):
        def step(i, carry):
            self.load(i).wait()

            @pl.when(i + 1 < self.count)
            def _():
                self.load(i + 1).start()

            self.flipped[:, span(i * self.tile, self.tile)] = self.stage[lax.rem(i, 2)].T
            return carry

        self.load(0).start()
        lax.fori_loop(0, self.count, step, 0)

    def times(self, right, out, first, offset):
        block, columns = out.shape[1:]
        half = columns // 2
        each = block // self.tile

        def step(n, carry):
            m, t = n // 2, lax.rem(n, 2)
            left = self.flipped[span(first + m * self.tile, self.tile), :]
            value = dot(left, right[:, span(offset + t * half, half)], NN)
            out[m // each, span(lax.rem(m, each) * self.tile, self.tile), span(t * half, half)] = value.astype(BF)
            return carry

        lax.fori_loop(0, 4 * each, step, 0)


def down_call(hidden, firsts, seconds, middle, owns, moved, normed, grads, gate_other, ident):
    piece, width = middle.shape
    tokens, both = grads.shape
    part_width = both // 2
    block = width // 4
    tile = 256

    def kernel(
        hidden_ref, first_a, first_b, second_a, second_b, base_ref, own_0, own_1, moved_0, moved_1, grads_ref, normed_ref, gate_other,
        result_ref, down_out, gate_out, up_own_out, up_other_out,
        down_sum, stage, flipped, gate_moved, kept, spare,
        y_sems, z_sems, load_sems, store_sems, *reduce_refs
    ):
        place = Place()
        place.meet()
        y = place.y

        turned = Turned(normed_ref, stage, load_sems, flipped)
        for j, (own, came) in enumerate(((own_0, moved_0), (own_1, moved_1))):
            def step(i, carry, j=j, own=own, came=came):
                rows = span(i * 64, 64)
                down_sum[j, rows, :] = (own[rows, :].astype(F32) + came[rows, :].astype(F32)).astype(BF)
                return carry

            lax.fori_loop(0, own_0.shape[0] // 64, step, 0)
        z_down = GradHalf(place, down_sum, down_out, z_sems.at[0])
        y_gate = Beyond(place, gate_other, gate_moved, y_sems.at[0])
        y_gate.start()
        parts = list(zip(quarters(first_a, second_a), quarters(first_b, second_b), place.order))

        def compute(owner, out_ref):
            rows = span(owner * piece, piece)
            for upper, lower, index in parts:
                depth, size = upper.shape
                part = dot(hidden_ref[rows, 0:depth], upper[...], NN) + dot(hidden_ref[rows, depth:], lower[...], NN)
                out_ref[:, span(index * size, size)] = part.astype(out_ref.dtype)

        def last(rows, total):
            result_ref[rows, :] = (base_ref[rows, :] + total).astype(BF)

        def store(out, ref, i):
            return pltpu.make_async_copy(ref, out, store_sems.at[i])

        def after_z():
            turned.times(grads_ref, spare, (1 - y) * (width // 2), part_width)
            store(up_other_out, spare, 0).start()
            turned.times(grads_ref, kept, y * (width // 2), 0)
            store(up_other_out, spare, 0).wait()
            turned.times(grads_ref, spare, y * (width // 2), part_width)
            store(up_own_out, spare, 1).start()

        reduce_body(place, compute, last, reduce_refs, begin=z_down.start, before_z=turned.turn, after_z=after_z)
        y_gate.wait_recv()
        for i in (0, 1):
            def add(n, carry, i=i):
                rows = span(n * 64, 64)
                kept[i, rows, :] = (kept[i, rows, :].astype(F32) + gate_moved[i, rows, :].astype(F32)).astype(BF)
                return carry

            lax.fori_loop(0, block // 64, add, 0)
        store(gate_out, kept, 2).start()
        z_down.wait_recv()
        store(up_own_out, spare, 1).wait()
        store(gate_out, kept, 2).wait()
        for move in (z_down, y_gate):
            move.wait_send()

    shape = jax.ShapeDtypeStruct
    half = shape((2, block, part_width), BF)
    down_shape = (2, *owns[0].shape)
    held = pltpu.VMEM(half.shape, BF)
    return pl.pallas_call(
        kernel,
        out_shape=[shape((piece, width), BF), shape(down_shape, BF), half, half, half],
        in_specs=[VMEM_WHOLE] * 11 + [ANYWHERE] * 2,
        out_specs=[VMEM_WHOLE] + [ANYWHERE] * 4,
        scratch_shapes=[
            pltpu.VMEM(down_shape, BF),
            pltpu.VMEM((2, tile, width), BF),
            pltpu.VMEM((width, tokens), BF),
            held, held, held,
            DMA((1, 4)), DMA((1, 4)), DMA((2,)), DMA((3,)), *reduce_scratch(piece, width),
        ],
        compiler_params=pltpu.CompilerParams(collective_id=ident, has_side_effects=True, vmem_limit_bytes=63 << 20),
        cost_estimate=pl.CostEstimate(flops=60 << 30, bytes_accessed=60 << 20, transcendentals=0),
        name="reduce_down",
    )(hidden, *firsts, *seconds, middle, *owns, *moved, grads, normed, gate_other)


def middle_call(cot, slopes, gates, ups, downs, down_last, normed, moves, middle, ident):
    piece, width = middle.shape
    tokens, part_width = cot.shape[0], down_last.shape[1]
    hidden = 2 * part_width
    tile = 256
    tiles = part_width // tile

    def body(place, ins, outs, scratch, under, targets):
        cot_hbm, slopes_ref, normed_ref, ga1, ga2, gb1, gb2, ua1, ua2, ub1, ub2, value_ref, da1, da2, db1 = ins
        total_ref, branch_ref, grad_ref, gate_other = outs
        load_sem, cot_ref, base_ref, stage, *rest = scratch
        under.start_y()
        loads = [
            pltpu.make_async_copy(slopes_ref, grad_ref, load_sem.at[0]),
            pltpu.make_async_copy(cot_hbm, cot_ref, load_sem.at[1]),
        ]
        for load in loads:
            load.start()
        for load in loads:
            load.wait()
        base_ref[...] = cot_ref[span(place.block * piece, piece), :]
        rows_in = (quarters(da1, da2), quarters(db1, targets[0]))

        def fill(owner, part):
            rows = span(owner * piece, piece)

            def step(t, carry):
                grad = None
                for weight, index in zip(rows_in[part], place.order):
                    size = weight.shape[1]
                    term = dot(cot_ref[rows, span(index * size, size)], weight[span(t * tile, tile), :], NT)
                    grad = term if grad is None else grad + term
                for offset in (0, hidden):
                    cols = span(offset + part * part_width + t * tile, tile)
                    grad_ref[rows, cols] = (grad * grad_ref[rows, cols].astype(F32)).astype(BF)
                return carry

            lax.fori_loop(0, tiles, step, 0)

        def fill_first(i, carry):
            fill(i, 0)
            return carry

        lax.fori_loop(0, tokens // piece, fill_first, 0)
        under.moves[0][1].wait_recv()
        columns = [quarters(ga1, ga2), quarters(gb1, gb2), quarters(ua1, ua2), quarters(ub1, ub2)]

        def compute(owner, out_ref):
            rows = span(owner * piece, piece)
            fill(owner, 1)
            for quarter, index in enumerate(place.order):
                total = None
                for i, weights in enumerate(columns):
                    weight = weights[quarter]
                    size = weight.shape[0]
                    term = dot(grad_ref[rows, i * part_width:(i + 1) * part_width], weight[...], NT)
                    total = term if total is None else total + term
                out_ref[:, span(index * size, size)] = total.astype(out_ref.dtype)

        def last(rows, total):
            base = base_ref[rows, :].astype(F32)
            grad = back_rows(base, value_ref[rows, :], total)
            total_ref[rows, :] = grad
            branch_ref[rows, :] = grad.astype(BF)

        turned = Turned(normed_ref, stage, load_sem, cot_ref)

        def after_z():
            turned.turn()
            turned.times(grad_ref, gate_other, (1 - place.y) * (width // 2), 0)

        reduce_body(place, compute, last, rest, after_z=after_z, split=2)
        under.end(skip=1)

    shape = functools.partial(jax.ShapeDtypeStruct, (piece, width))
    return comm_call(
        body, "reduce_middle", ident, [cot, slopes, normed, *gates, *ups, middle, *downs, down_last],
        [
            shape(F32), shape(BF), jax.ShapeDtypeStruct((tokens, 2 * hidden), BF),
            jax.ShapeDtypeStruct((2, width // 4, hidden), BF),
        ],
        [
            DMA((2,)), pltpu.VMEM((tokens, width), BF), pltpu.VMEM((piece, width), BF), pltpu.VMEM((2, tile, width), BF),
            *reduce_scratch(piece, width),
        ],
        moves, flops=6 * tokens * hidden * width,
        spaces=[ANYWHERE] * 3 + [VMEM_WHOLE] * 12,
    )


def gather_scratch():
    return [DMA((3, SLICES)), DMA((3, SLICES)), DMA((4,)), DMA((4,))]


def gather_body(place, own_ref, full, sems, process, begin=nothing, follow=nothing, split=0):
    near_send, near_recv, sib_send, sib_recv = sems
    piece = own_ref.shape[0]
    size = piece // SLICES
    c = place.c

    def near_copy(slot, r, target, turned=False):
        where = full.at[span((c * 4 + target) * piece + r * size, size)]
        device = place.along if slot == 2 or turned else place.across
        return remote(where, where, near_send.at[slot, r], near_recv.at[slot, r], device)

    def sib_copy(slot, core, target):
        where = full.at[span((core * 4 + target) * piece, piece)]
        return remote(where, where, sib_send.at[slot], sib_recv.at[slot], place.sibling)

    def slices(act):
        def step(r, carry):
            act(r)
            return carry

        lax.fori_loop(0, SLICES, step, 0)

    mine, x_chip, z_chip, d_chip = place.chip(0, 0), place.chip(0, 1), place.chip(1, 0), place.chip(1, 1)
    full[span((c * 4 + mine) * piece, piece), :] = own_ref[...]
    slices(lambda r: near_copy(2, r, mine).start())
    slices(lambda r: near_copy(1, r, mine).start())
    sib_copy(3, c, mine).start()
    begin()

    def forward(r):
        near_copy(2, r, z_chip).wait_recv()
        if r < SLICES - split:
            near_copy(0, r, z_chip).start()

    process(c * 4 + mine)
    forward(0)
    sib_copy(3, 1 - c, mine).wait_recv()
    process((1 - c) * 4 + mine)
    forward(1)

    def arrived(r):
        near_copy(1, r, x_chip).wait_recv()

    for r in range(SLICES):
        arrived(r)
        if r >= SLICES - split:
            near_copy(0, r, x_chip, True).start()
    sib_copy(1, c, x_chip).start()
    process(c * 4 + x_chip)
    for r in range(2, SLICES):
        forward(r)
    sib_copy(2, c, z_chip).start()
    sib_copy(1, 1 - c, x_chip).wait_recv()
    process((1 - c) * 4 + x_chip)
    process(c * 4 + z_chip)
    follow()
    sib_copy(2, 1 - c, z_chip).wait_recv()
    process((1 - c) * 4 + z_chip)
    slices(lambda r: near_copy(0, r, d_chip).wait_recv())
    sib_copy(0, c, d_chip).start()
    process(c * 4 + d_chip)
    sib_copy(0, 1 - c, d_chip).wait_recv()
    process((1 - c) * 4 + d_chip)
    for slot in range(3):
        slices(lambda r: near_copy(slot, r, mine).wait_send())
    for slot in range(4):
        sib_copy(slot, c, mine).wait_send()


class ColumnGather:
    def __init__(self, place, src, full, sems):
        self.place, self.src, self.full = place, src, full
        self.near_send, self.near_recv, self.sib_send, self.sib_recv, self.own = sems
        self.width = src.shape[1]
        self.size = src.shape[0] // SLICES

    def where(self, core, target):
        return span((core * 4 + target) * self.width, self.width)

    def near(self, slot, r, target, first=False):
        place = self.place
        rows = pl.ds(r * self.size, self.size)
        dst = self.full.at[rows, self.where(place.c, target)]
        src = self.src.at[rows] if first else dst
        device = place.along if slot == 2 else place.across
        return remote(src, dst, self.near_send.at[slot, r], self.near_recv.at[slot, r], device)

    def sib(self, slot, core, target, first=False):
        dst = self.full.at[:, self.where(core, target)]
        src = self.src if first else dst
        return remote(src, dst, self.sib_send.at[slot], self.sib_recv.at[slot], self.place.sibling)

    def chips(self):
        place = self.place
        return place.chip(0, 0), place.chip(0, 1), place.chip(1, 0), place.chip(1, 1)

    def own_copy(self):
        return pltpu.make_async_copy(self.src, self.full.at[:, self.where(self.place.c, self.chips()[0])], self.own.at[0])

    def start(self):
        mine = self.chips()[0]
        self.own_copy().start()
        for slot in (2, 1):
            for r in range(SLICES):
                self.near(slot, r, mine, True).start()
        self.sib(3, self.place.c, mine, True).start()

    def forward(self, r):
        z_chip = self.chips()[2]
        self.near(2, r, z_chip).wait_recv()
        self.near(0, r, z_chip).start()

    def finish(self):
        mine, x_chip, z_chip, d_chip = self.chips()
        c = self.place.c
        self.sib(2, c, z_chip).start()
        for r in range(SLICES):
            self.near(1, r, x_chip).wait_recv()
        self.sib(1, c, x_chip).start()
        for r in range(SLICES):
            self.near(0, r, d_chip).wait_recv()
        self.sib(0, c, d_chip).start()
        self.own_copy().wait()
        for slot, target in enumerate((d_chip, x_chip, z_chip, mine)):
            self.sib(slot, 1 - c, target).wait_recv()
            self.sib(slot, c, mine).wait_send()
        for slot in range(3):
            for r in range(SLICES):
                self.near(slot, r, mine).wait_send()


def attend_back_body(qkv_ref, o_ref, do_ref, lse_ref, bound, cos_ref, sin_ref, out_ref, dk_ref, dv_ref, heads, hd):
    seq = qkv_ref.shape[0]
    bq = bk = min(512, seq // 2)
    scale = hd ** -0.5
    half = hd // 2

    def unrotate(g, rows):
        return g * cos_ref[rows, :] - pltpu.roll(g, half, 1) * sin_ref[rows, :]

    def head(h, carry):
        base = h * 3 * hd
        own = span(h * hd, hd)
        dk_ref[...] = jnp.zeros_like(dk_ref)
        dv_ref[...] = jnp.zeros_like(dv_ref)
        for i in range(seq // bq):
            first = i * bq
            rows = pl.ds(first, bq)
            q = qkv_ref[rows, span(base, hd)]
            do = do_ref[rows, own]
            row_sums = (do.astype(F32) * o_ref[rows, own].astype(F32)).T
            delta = jnp.sum(row_sums, axis=0, keepdims=True)
            tops = lse_ref[h, 0:1, first:first + bq]
            total = max(i + 1, seq // 2 // bk)

            def step(masked, j, dq, first=first, q=q, do=do, delta=delta, tops=tops):
                keys = span(j * bk, bk)
                k = qkv_ref[keys, span(base + hd, hd)]
                v = qkv_ref[keys, span(base + 2 * hd, hd)]
                p = jnp.exp(dot(k, q, NT) * scale - tops)
                if masked:
                    kp = j * bk + lax.broadcasted_iota(jnp.int32, (bk, bq), 0)
                    qp = first + lax.broadcasted_iota(jnp.int32, (bk, bq), 1)
                    p = jnp.where(kp < jnp.maximum(qp + 1, bound), p, 0.0)
                dv_ref[keys, :] += dot(p.astype(BF), do, NN)
                ds = (p * (dot(v, do, NT) - delta)).astype(BF)
                dk_ref[keys, :] += dot(ds, q, NN)
                return dq + dot(ds, k, TN)

            dq = lax.fori_loop(0, i, functools.partial(step, False), jnp.zeros((bq, hd), F32))
            dq = lax.fori_loop(i, total, functools.partial(step, True), dq)
            out_ref[rows, span(base, hd)] = unrotate(dq * scale, rows).astype(BF)

        def fin(i, carry):
            rows = span(i * bq, bq)
            out_ref[rows, span(base + hd, hd)] = unrotate(dk_ref[rows, :] * scale, rows).astype(BF)
            out_ref[rows, span(base + 2 * hd, hd)] = dv_ref[rows, :].astype(BF)
            return carry

        return lax.fori_loop(0, seq // bq, fin, carry)

    lax.fori_loop(0, heads, head, 0)


def front_call(inputs, cot, prefix, tables, weights, heads, hd, ident):
    names = ("qkv", "out", "ga", "gb", "ua", "ub", "da", "db")
    tokens, slice_width = inputs.shape
    width = slice_width * 8
    piece = tokens // 8
    size = tokens // SLICES
    inner = weights[0].shape[1]
    part_width = weights[2].shape[1]
    hidden = 2 * part_width
    tile = 256
    bq = bk = min(512, tokens // 2)
    scale = hd ** -0.5

    def kernel(in_ref, cot_ref, prefix_ref, cos_ref, sin_ref, *refs):
        sources, refs = refs[:8], refs[8:]
        firsts, seconds, refs = refs[:8], refs[8:15], refs[15:]
        (qkv_ref, mixed_ref, lse_ref, own_in_ref, middle_ref, normed_in_out, cot_out, normed_mid_out, hidden_out,
         slopes_out), refs = refs[:10], refs[10:]
        arena, acc, block_ref, normed_own, *refs = refs
        held, refs = dict(zip(names, refs[:8])), refs[8:]
        z_sems, y_sems, store_sems, out_sems, swap_send, swap_recv, phase, *sems = refs
        start_sems, gather_sems, reduce_sems_, feed_sems = sems[:5], sems[5:10], sems[10:14], sems[14:]
        place = Place()
        c, zl, x = place.c, place.zl, place.x
        place.meet()
        z_moves = {n: WeightHalf(place, sources[i], held[n].at[0], z_sems.at[i]) for i, n in enumerate(names)}
        y_moves = {n: Beyond(place, held[n].at[0], held[n].at[1], y_sems.at[i]) for i, n in enumerate(names[:7])}

        def go(name):
            z_moves[name].start()

        def stores(name):
            i = names.index(name)
            return [
                pltpu.make_async_copy(held[name].at[side], out[i], store_sems.at[i, side])
                for side, out in enumerate((firsts, seconds[:7]))
                if i < len(out)
            ]

        def pass_on(name):
            z_moves[name].wait_recv()
            y_moves[name].start()

        def got(name):
            y_moves[name].wait_recv()
            for copy in stores(name):
                copy.start()

        def parts(name):
            return [held[name].at[side, i] for side in (0, 1) for i in (0, 1)]

        full, normed = arena.at[pl.ds(0, tokens)], arena.at[pl.ds(tokens, tokens)]
        gather = ColumnGather(place, in_ref, full, start_sems)
        crossed = jnp.logical_not(place.straight)
        partner = (place.y, 1 - c, 1 - place.zh, zl, x)
        mine, x_chip, z_chip, d_chip = gather.chips()
        def rows_of(r):
            return pl.ds(r * size, size)

        def swap_copy(r, core):
            where = full.at[rows_of(r), gather.where(core, mine)]
            return remote(in_ref.at[rows_of(r)], where, swap_send.at[r], swap_recv.at[r], partner)

        def own_copy(r):
            where = full.at[rows_of(r), gather.where(c, mine)]
            return pltpu.make_async_copy(in_ref.at[rows_of(r)], where, swap_send.at[r])

        def cot_swap():
            return remote(cot_ref, block_ref, swap_send.at[SLICES], swap_recv.at[SLICES], partner)

        def cot_own():
            return pltpu.make_async_copy(cot_ref, block_ref, swap_send.at[SLICES])

        def sib(slot, r, core, target):
            where = full.at[rows_of(r), gather.where(core, target)]
            return remote(where, where, start_sems[2].at[slot, r], start_sems[3].at[slot, r], place.sibling)

        @pl.when(place.straight)
        def _():
            for r in range(SLICES):
                own_copy(r).start()
            cot_own().start()

        @pl.when(crossed)
        def _():
            for r in range(SLICES):
                swap_copy(r, 1 - c).start()

        for r in range(SLICES):
            @pl.when(place.straight)
            def _(r=r):
                own_copy(r).wait()

            @pl.when(crossed)
            def _(r=r):
                swap_copy(r, c).wait_recv()

            gather.near(2, r, mine).start()
            gather.near(1, r, mine).start()
            sib(3, r, c, mine).start()
        for r in range(SLICES):
            gather.forward(r)
            sib(2, r, c, z_chip).start()
            gather.near(1, r, x_chip).wait_recv()
            sib(1, r, c, x_chip).start()
            if r == 0:
                go("qkv")
        pass_on("qkv")
        go("out")
        pl.when(crossed)(lambda: cot_swap().start())
        depth = held["qkv"].shape[2]
        for r in range(SLICES):
            gather.near(0, r, d_chip).wait_recv()
            sib(0, r, c, d_chip).start()
            for slot, target in enumerate((d_chip, x_chip, z_chip, mine)):
                sib(slot, r, 1 - c, target).wait_recv()

            def norm_rows(i, carry, r=r):
                rows = span(r * size + i * NORM_ROWS, NORM_ROWS)
                normed[rows, :] = row_norm(full[rows, :].astype(F32))[0].astype(BF)
                return carry

            lax.fori_loop(0, size // NORM_ROWS, norm_rows, 0, unroll=NORM_UNROLL)
            pltpu.make_async_copy(normed.at[rows_of(r)], normed_in_out.at[rows_of(r)], out_sems.at[r]).start()
            total = None
            for weight, index in zip(parts("qkv")[:2], place.order[:2]):
                term = dot(normed[rows_of(r), span(index * depth, depth)], weight[...], NN)
                total = term if total is None else total + term
            acc[rows_of(r), :] = total
        own_in_ref[...] = full[span(place.block * piece, piece), :]
        pass_on("out")

        cot_gather = ColumnGather(place, block_ref, cot_out, gather_sems)

        def forward_cot():
            for r in range(SLICES):
                cot_gather.forward(r)

        @pl.when(place.straight)
        def _():
            cot_own().wait()
            cot_gather.start()
            go("ga")

        got("qkv")
        half = size // 2

        def project(r, carry):
            rows = span(r * half, half)
            total = acc[rows, :]
            for weight, index in zip(parts("qkv")[2:], place.order[2:]):
                total = total + dot(normed[rows, span(index * depth, depth)], weight[...], NN)
            cos, sin = cos_ref[rows, :], sin_ref[rows, :]
            for h in range(heads):
                for part in range(3):
                    value = total[:, (3 * h + part) * hd:(3 * h + part + 1) * hd]
                    if part < 2:
                        value = value * cos + pltpu.roll(value, hd // 2, 1) * sin
                    qkv_ref[rows, pl.ds((3 * h + part) * hd, hd)] = value.astype(BF)
            return carry

        lax.fori_loop(0, tokens // half, project, 0)
        @pl.when(crossed)
        def _():
            cot_swap().wait_recv()
            cot_gather.start()
            go("ga")
            cot_swap().wait_send()
            for r in range(SLICES):
                swap_copy(r, 1 - c).wait_send()

        pl.when(place.straight)(forward_cot)

        bound = prefix_ref[0:1, 0:1]

        def head(h, carry):
            base = h * 3 * hd
            for i in range(tokens // bq):
                first = i * bq
                q = qkv_ref[first:first + bq, span(base, hd)]
                count = max(i + 1, tokens // 2 // bk)

                def step(masked, j, state, first=first, q=q):
                    top, tot, out = state
                    rows = span(j * bk, bk)
                    s = dot(q, qkv_ref[rows, span(base + hd, hd)], NT) * scale
                    if masked:
                        kp = j * bk + lax.broadcasted_iota(jnp.int32, (bq, bk), 1)
                        qp = first + lax.broadcasted_iota(jnp.int32, (bq, bk), 0)
                        s = jnp.where(kp < jnp.maximum(qp + 1, bound), s, NEG)
                    new = jnp.maximum(top, jnp.max(s, axis=1, keepdims=True))
                    alpha = jnp.exp(top - new)
                    p = jnp.exp(s - new)
                    tot = tot * alpha + jnp.sum(p, axis=1, keepdims=True)
                    out = out * alpha + dot(p.astype(BF), qkv_ref[rows, span(base + 2 * hd, hd)], NN)
                    return new, tot, out

                state = (jnp.full((bq, 1), NEG, F32), jnp.zeros((bq, 1), F32), jnp.zeros((bq, hd), F32))
                state = lax.fori_loop(0, i, functools.partial(step, False), state)
                top, tot, out = lax.fori_loop(i, count, functools.partial(step, True), state)
                mixed_ref[first:first + bq, span(h * hd, hd)] = (out / tot).astype(BF)
                lse = jnp.broadcast_to(top + jnp.log(tot), (bq, 128))
                lse_ref[h, :, first:first + bq] = lse.T[0:8, :]
            return carry

        lax.fori_loop(0, heads, head, 0)
        go("gb")
        got("out")
        pl.when(crossed)(forward_cot)
        pass_on("ga")

        for r in range(SLICES):
            pltpu.make_async_copy(normed.at[rows_of(r)], normed_in_out.at[rows_of(r)], out_sems.at[r]).wait()
            for slot in range(3):
                gather.near(slot, r, mine).wait_send()
            for slot in range(4):
                sib(slot, r, c, mine).wait_send()
        for device in (place.sibling, place.across, place.along):
            pl.semaphore_signal(phase, inc=1, device_id=device, device_id_type=MESH)
        pl.semaphore_wait(phase, 3)

        class Blocks:
            def __init__(self, first, count):
                self.first, self.shape = first, (count, piece, width)

            def rows(self, index):
                if isinstance(index, tuple):
                    step, inside, *rest = index
                    start = (self.first + step) * piece + inside.start
                    return (pl.ds(pl.multiple_of(start, 16), inside.size), *rest)
                return (span((self.first + index) * piece, piece),)

            @property
            def at(self):
                return At(self)

            def __getitem__(self, index):
                return arena[self.rows(index)]

            def __setitem__(self, index, value):
                arena[self.rows(index)] = value

        class At:
            def __init__(self, blocks):
                self.blocks = blocks

            def __getitem__(self, index):
                return arena.at[self.blocks.rows(index)]

        buffers, first = [], 0
        for count in (4, 4, 2, 3, 3):
            buffers.append(Blocks(first, count))
            first += count

        def last(rows, total):
            middle = own_in_ref[rows, :].astype(F32) + total
            middle_ref[rows, :] = middle
            normed_own[rows, :] = row_norm(middle)[0].astype(BF)

        def after_z():
            go("ua")
            go("ub")
            pass_on("gb")
            got("ga")

        reduce_body(
            place, product(place, mixed_ref, parts("out"), False), last, [*buffers, *reduce_sems_],
            after_z=after_z, split=0,
        )

        full = arena.at[pl.ds(2 * tokens, tokens)]
        slopes_ref = arena.at[pl.ds(0, tokens)]
        hidden_ref = arena.at[pl.ds(tokens, tokens), pl.ds(0, hidden)]
        columns = (("ga", "ua"), ("gb", "ub"))
        waiting = []

        def fill(owner, which):
            rows = span(owner * piece, piece)
            gates, ups = (parts(name) for name in columns[which])

            def step(t, carry):
                taken = span(t * tile, tile)
                gate = up = None
                for gate_weight, up_weight, index in zip(gates, ups, place.order):
                    deep = gate_weight.shape[0]
                    value = full[rows, span(index * deep, deep)]
                    terms = dot(value, gate_weight[:, taken], NN), dot(value, up_weight[:, taken], NN)
                    gate, up = terms if gate is None else (gate + terms[0], up + terms[1])
                cols = span(which * part_width + t * tile, tile)
                up_cols = span(hidden + which * part_width + t * tile, tile)
                sig = 1.0 / (1.0 + jnp.exp(-gate))
                active = gate * sig
                hidden_ref[rows, cols] = (active * up).astype(BF)
                slopes_ref[rows, cols] = (up * sig * (1.0 + gate * (1.0 - sig))).astype(BF)
                slopes_ref[rows, up_cols] = active.astype(BF)
                return carry

            lax.fori_loop(0, part_width // tile, step, 0)

        def begin():
            go("da")
            go("db")

        def process(owner):
            waiting.append(owner)
            if len(waiting) == 1:
                pass_on("ua")
                got("gb")
                got("ua")
            fill(owner, 0)
            if len(waiting) == 3:
                pass_on("ub")
                got("ub")
                for earlier in waiting:
                    fill(earlier, 1)
            elif len(waiting) > 3:
                fill(owner, 1)

        gather_body(place, normed_own, full, feed_sems, process, begin=begin, split=0)
        for i, (ref, out) in enumerate(((full, normed_mid_out), (hidden_ref, hidden_out), (slopes_ref, slopes_out))):
            pltpu.make_async_copy(ref, out, out_sems.at[SLICES + i]).start()
        pass_on("da")
        cot_gather.finish()
        z_moves["db"].wait_recv()
        stores("db")[0].start()
        got("da")
        for i, (ref, out) in enumerate(((full, normed_mid_out), (hidden_ref, hidden_out), (slopes_ref, slopes_out))):
            pltpu.make_async_copy(ref, out, out_sems.at[SLICES + i]).wait()
        for move in (*z_moves.values(), *y_moves.values()):
            move.wait_send()
        for name in names:
            for copy in stores(name):
                copy.wait()

    def half_shape(weight):
        return jax.ShapeDtypeStruct((2, *weight.shape), BF)

    shape = jax.ShapeDtypeStruct
    outs = [
        *(half_shape(weight) for weight in weights),
        *(half_shape(weight) for weight in weights[:7]),
        shape((tokens, inner), BF),
        shape((tokens, heads * hd), BF),
        shape((heads, 8, tokens), F32),
        shape((piece, width), BF),
        shape((piece, width), F32),
        shape((tokens, width), BF),
        shape((tokens, width), BF),
        shape((tokens, width), BF),
        shape((tokens, hidden), BF),
        shape((tokens, 2 * hidden), BF),
    ]
    column_sems = [DMA((3, SLICES)), DMA((3, SLICES)), DMA((4,)), DMA((4,)), DMA((1,))]
    start_sems = [DMA((3, SLICES)), DMA((3, SLICES)), DMA((4, SLICES)), DMA((4, SLICES)), DMA((1,))]
    result = pl.pallas_call(
        kernel,
        out_shape=outs,
        in_specs=[ANYWHERE, ANYWHERE, VMEM_WHOLE, VMEM_WHOLE, VMEM_WHOLE] + [ANYWHERE] * 8,
        out_specs=[ANYWHERE] * 15 + [VMEM_WHOLE] * 5 + [ANYWHERE] * 5,
        scratch_shapes=[
            pltpu.VMEM((3 * tokens, width), BF),
            pltpu.VMEM((tokens, inner), F32),
            pltpu.VMEM((tokens, slice_width), BF),
            pltpu.VMEM((piece, width), BF),
            *(pltpu.VMEM((2, 2, *weight.shape), BF) for weight in weights[:7]),
            pltpu.VMEM((1, 2, *weights[7].shape), BF),
            DMA((8, 4)), DMA((8, 4)), DMA((8, 2)), DMA((SLICES + 3,)), DMA((SLICES + 1,)), DMA((SLICES + 1,)),
            pltpu.SemaphoreType.REGULAR,
            *start_sems, *column_sems, *reduce_sems(), *gather_scratch(),
        ],
        compiler_params=pltpu.CompilerParams(collective_id=ident, has_side_effects=True, vmem_limit_bytes=63 << 20),
        cost_estimate=pl.CostEstimate(
            flops=100 << 30, bytes_accessed=100 << 20, transcendentals=heads * tokens * tokens
        ),
        name="front",
    )(inputs, cot, prefix, *tables, *weights)
    return result[:8], result[8:15], result[15:]


BLOCKS = [(core, zl, x) for core in (0, 1) for zl in (0, 1) for x in (0, 1)]


def spread_greet(place, barrier):
    for core, zl, x in BLOCKS:
        mine = jnp.logical_and(place.straight, core * 4 + zl * 2 + x == place.block)

        @pl.when(jnp.logical_not(mine))
        def _(core=core, zl=zl, x=x):
            pl.semaphore_signal(
                barrier, inc=1, device_id=(place.y, core, place.c, zl, x), device_id_type=MESH
            )

    return 8 - jnp.where(place.straight, 1, 0)


def spread_scratch():
    return [DMA((8,)), DMA((8,)), DMA((1,))]


def spread_shape(piece):
    return jax.ShapeDtypeStruct((piece.shape[0] * 8, piece.shape[1] // 8), piece.dtype)


class Spread:
    def __init__(self, place, src, dst, sems):
        self.place, self.src, self.dst = place, src, dst
        self.send, self.recv, self.own = sems
        self.piece, self.width = src.shape[0], src.shape[1] // 8

    def copy(self, f):
        place = self.place
        return remote(
            self.src.at[:, pl.ds(f * self.width, self.width)], self.dst.at[span(place.block * self.piece, self.piece)],
            self.send.at[f], self.recv.at[place.block], (place.y, place.zh, *BLOCKS[f]),
        )

    def incoming(self, f):
        core, zl, x = BLOCKS[f]
        place = self.place
        return remote(
            self.src.at[:, pl.ds(f * self.width, self.width)], self.dst.at[pl.ds(f * self.piece, self.piece)],
            self.send.at[f], self.recv.at[f], (place.y, core, place.c, zl, x),
        )

    def own_copy(self):
        block = self.place.block
        return pltpu.make_async_copy(
            self.src.at[:, span(block * self.width, self.width)], self.dst.at[span(block * self.piece, self.piece)],
            self.own.at[0],
        )

    def each(self, act):
        for f in range(8):
            mine = jnp.logical_and(self.place.straight, self.place.block == f)
            pl.when(jnp.logical_not(mine))(functools.partial(act, f))

    def start(self):
        self.each(lambda f: self.copy(f).start())
        pl.when(self.place.straight)(lambda: self.own_copy().start())

    def wait(self):
        self.each(lambda f: self.incoming(f).wait_recv())
        self.each(lambda f: self.copy(f).wait_send())
        pl.when(self.place.straight)(lambda: self.own_copy().wait())


def rear_call(branch_own, out_halves, qkv_halves, qkv, mixed, lse, prefix, tables, grad_middle, own_in, ready, normed_in,
              gate_sum, up_own, up_other, heads, hd, ident):
    tokens, inner = qkv.shape
    piece, width = branch_own.shape
    inner_out = mixed.shape[1]
    block = width // 4
    tile = 256

    def kernel(
        branch_ref, out_1, out_2, qkv_1, qkv_2, qkv_ref, mixed_ref, lse_ref, prefix_ref, cos_ref, sin_ref, middle_ref,
        own_in_ref, ready_ref, normed_in_ref, gate_ref, up_own_ref, up_other_ref,
        gate_out, up_out, out_out, qkv_out, ready_out, result_out,
        full, grad_mixed, grad_rows, flipped, dk_ref, dv_ref, up_moved, out_grads, qkv_grads,
        y_sems, z_sems, load_sem, *sems
    ):
        place = Place()
        y = place.y
        reduce_refs, sems = sems[:9], sems[9:]
        gather_sems, ready_sems, result_sems = sems[:4], sems[4:7], sems[7:10]
        place.meet(spread_greet)
        y_up = Beyond(place, up_other_ref, up_moved, y_sems.at[0])
        y_out = Beyond(place, out_grads.at[0], out_grads.at[2], y_sems.at[1])
        y_qkv = Beyond(place, qkv_grads.at[0], qkv_grads.at[2], y_sems.at[2])
        z_gate = GradHalf(place, gate_ref, gate_out, z_sems.at[0])
        z_up = GradHalf(place, up_moved, up_out, z_sems.at[1])
        z_out = GradHalf(place, out_grads.at[1], out_out, z_sems.at[2])
        z_qkv = GradHalf(place, qkv_grads.at[1], qkv_out, z_sems.at[3])
        y_up.start()

        def add(own, moved, rows):
            def step(i, carry):
                where = span(i * 64, 64)
                for j in (0, 1):
                    total = own[j, where, :].astype(F32) + moved[j, where, :].astype(F32)
                    own[j, where, :] = total.astype(BF)
                return carry

            lax.fori_loop(0, rows // 64, step, 0)

        result_ref = full.at[pl.ds(0, piece)]

        out_parts = quarters(out_1, out_2)

        def process(owner):
            rows = span(owner * piece, piece)
            total = None
            for weight, index in zip(out_parts, place.order):
                part = dot(full[rows, span(index * block, block)], weight[...], NT)
                total = part if total is None else total + part
            grad_mixed[rows, :] = total.astype(BF)

        gather_body(place, branch_ref, full, gather_sems, process, begin=z_gate.start, split=0)
        ready_spread = Spread(place, ready_ref, ready_out, ready_sems)
        y_up.wait_recv()
        add(up_moved, up_own_ref, up_own.shape[1])
        z_up.start()
        ready_spread.start()

        def flip(source, columns):
            def step(i, carry):
                rows = span(i * tile, tile)
                flipped[0:columns, rows] = source[rows, :].T
                return carry

            lax.fori_loop(0, tokens // tile, step, 0)

        def weigh(grads, side, which, columns):
            def step(n, carry):
                i, m = n // (columns // tile), lax.rem(n, columns // tile)
                rows = span(m * tile, tile)
                value = dot(flipped[rows, :], full[:, span((which * 2 + i) * block, block)], NN)
                grads[side, i, rows, :] = value.astype(BF)
                return carry

            lax.fori_loop(0, 2 * (columns // tile), step, 0)

        flip(mixed_ref, inner_out)
        weigh(out_grads, 0, 1 - y, inner_out)
        y_out.start()
        weigh(out_grads, 1, y, inner_out)
        load = pltpu.make_async_copy(normed_in_ref, full, load_sem.at[0])
        load.start()
        attend_back_body(
            qkv_ref, mixed_ref, grad_mixed, lse_ref, prefix_ref[0:1, 0:1], cos_ref, sin_ref, grad_rows, dk_ref, dv_ref,
            heads, hd,
        )
        load.wait()

        def last(rows, total):
            value = back_rows(middle_ref[rows, :], own_in_ref[rows, :].astype(F32), total)
            result_ref[rows, :] = value.astype(BF)

        def before_z():
            flip(grad_rows, inner)
            weigh(qkv_grads, 0, 1 - y, inner)
            y_qkv.start()

        def after_z():
            y_out.wait_recv()
            add(out_grads.at[1], out_grads.at[2], inner_out)
            z_out.start()
            weigh(qkv_grads, 1, y, inner)

        reduce_body(
            place, product(place, grad_rows, quarters(qkv_1, qkv_2), True), last, reduce_refs,
            before_z=before_z, after_z=after_z, split=0,
        )
        result_spread = Spread(place, result_ref, result_out, result_sems)
        result_spread.start()
        y_qkv.wait_recv()
        add(qkv_grads.at[1], qkv_grads.at[2], inner)
        z_qkv.start()
        for move in (z_gate, z_up, z_out, z_qkv):
            move.wait_recv()
        ready_spread.wait()
        result_spread.wait()
        for move in (y_up, y_out, y_qkv, z_gate, z_up, z_out, z_qkv):
            move.wait_send()

    shape = jax.ShapeDtypeStruct
    spread = spread_shape(ready)
    return pl.pallas_call(
        kernel,
        out_shape=[
            shape(gate_sum.shape, BF), shape(up_own.shape, BF), shape((2, inner_out, block), BF),
            shape((2, inner, block), BF), spread, spread,
        ],
        in_specs=[VMEM_WHOLE] * 14 + [ANYWHERE, ANYWHERE, VMEM_WHOLE, ANYWHERE],
        out_specs=[ANYWHERE] * 6,
        scratch_shapes=[
            pltpu.VMEM((tokens, width), BF),
            pltpu.VMEM((tokens, inner_out), BF),
            pltpu.VMEM((tokens, inner), BF),
            pltpu.VMEM((inner, tokens), BF),
            pltpu.VMEM((tokens, hd), F32),
            pltpu.VMEM((tokens, hd), F32),
            pltpu.VMEM(up_own.shape, BF),
            pltpu.VMEM((3, 2, inner_out, block), BF),
            pltpu.VMEM((3, 2, inner, block), BF),
            DMA((3, 4)), DMA((4, 4)), DMA((1,)),
            *reduce_scratch(piece, width), *gather_scratch(), *spread_scratch(), *spread_scratch(),
        ],
        compiler_params=pltpu.CompilerParams(
            collective_id=ident, has_side_effects=True, vmem_limit_bytes=(64 << 20) - (64 << 10)
        ),
        cost_estimate=pl.CostEstimate(flops=100 << 30, bytes_accessed=100 << 20, transcendentals=heads * tokens * tokens),
        name="rear",
    )(
        branch_own, *out_halves, *qkv_halves, qkv, mixed, lse, prefix, *tables, grad_middle, own_in, ready, normed_in,
        gate_sum, up_own, up_other,
    )


def local_fine(inputs, prefix_len, w_qkv, w_out, w_up_gate, w_down, cotangent):
    heads, hd = w_qkv.shape[1], w_qkv.shape[2] // 3
    hidden_width = w_down.shape[0]
    tokens = inputs.shape[0]
    y = lax.axis_index("y")
    prefix_len = lax.ppermute(prefix_len, ("core", "zh"), [(0, 0), (1, 2), (2, 1), (3, 3)])
    prefix = jnp.broadcast_to(prefix_len[:, None], (8, 128))
    cosine, sine = rope_tables(tokens, hd)
    tables = (jnp.concatenate([cosine, cosine], axis=1), jnp.concatenate([-sine, sine], axis=1))
    part = hidden_width // 2
    ga, gb = w_up_gate[:, 0, :part], w_up_gate[:, 0, part:]
    ua, ub = w_up_gate[:, 1, :part], w_up_gate[:, 1, part:]
    da, db = w_down[:part], w_down[part:]

    weights = (w_qkv.reshape(w_qkv.shape[0], -1), w_out, ga, gb, ua, ub, da, db)
    firsts, seconds, results = front_call(inputs, cotangent, prefix, tables, weights, heads, hd, 1)
    qkv_1, out_1, ga_1, gb_1, ua_1, ub_1, da_1, db_1 = firsts
    qkv_2, out_2, ga_2, gb_2, ua_2, ub_2, da_2 = seconds
    qkv, mixed, lse, own_in, middle, normed_in, cot_full, normed_mid, hidden, slopes = results
    gates = (ga_1, ga_2, gb_1, gb_2)

    block = cot_full.shape[1] // 4

    def down_block(index):
        cut = lax.dynamic_slice_in_dim(cot_full, index * block, block, 1)
        return mm("tf,td->fd", hidden, cut).astype(BF)

    owns = [down_block(2 * y + i) for i in (0, 1)]
    others = [down_block(2 * (1 - y) + i) for i in (0, 1)]
    (grad_middle, branch_own, grad_gate_up, gate_other), (db_2, *moved) = middle_call(
        cot_full, slopes, gates, (ua_1, ua_2, ub_1, ub_2), (da_1, da_2), db_1, normed_mid,
        [("beyond", db_1), *(("beyond", other) for other in others)], middle, 5,
    )
    outputs, down_final, gate_sum, up_own, up_other = down_call(
        hidden, (da_1, db_1), (da_2, db_2), middle, owns, moved, normed_mid, grad_gate_up, gate_other, 6
    )
    gate_final, up_final, out_final, qkv_final, outputs, input_grad = rear_call(
        branch_own, (out_1, out_2), (qkv_1, qkv_2), qkv, mixed, lse, prefix, tables, grad_middle, own_in, outputs,
        normed_in, gate_sum, up_own, up_other, heads, hd, 7,
    )

    def summed(parts):
        return parts[0].astype(F32) + parts[1].astype(F32)

    return (
        outputs,
        input_grad.astype(F32),
        summed(qkv_final).T.reshape(-1, heads, 3 * hd),
        summed(out_final),
        jnp.stack([summed(gate_final), summed(up_final)], axis=1),
        summed(down_final),
    )


def solution(mesh):
    row_size, col_size = mesh.shape["row"], mesh.shape["col"]
    fine = (row_size, col_size) == (4, 8)
    if fine:
        names, shape, body = AXES, (2,) * 5, local_fine
        row, col = AXES[:2], AXES[2:]
    else:
        names = ("rmaj", "core", "cmaj", "cmin")
        shape = (row_size // 2, 2, 4, col_size // 4)
        body = functools.partial(local, shape[3] == 2)
        row, col = names[:2], names[2:]
    outs = (P(row, col), P(row, col), P(row, col, None), P(col, row), P(row, None, col), P(col, row))
    return jax.shard_map(
        body,
        mesh=Mesh(mesh.devices.reshape(shape), names),
        in_specs=(P(row, col), P(row), P(row, col, None), P(col, row), P(row, None, col), P(col, row), P(row, col)),
        out_specs=outs,
        check_vma=False,
    )
```

```python
import functools

import jax
import jax.numpy as jnp
from jax import lax
from jax.experimental import pallas as pl
from jax.experimental.pallas import tpu as pltpu
from jax.sharding import Mesh
from jax.sharding import PartitionSpec as P

EPSILON = 1e-05
NEG = -1e30
F32 = jnp.float32
BF = jnp.bfloat16
NN = (((1,), (0,)), ((), ()))
NT = (((1,), (1,)), ((), ()))
TN = (((0,), (0,)), ((), ()))
def dot(a, b, dims):
    return lax.dot_general(a, b, dims, preferred_element_type=F32)

def fwd_kernel(prefix_ref, q_ref, k_ref, v_ref, o_ref, lse_ref, *, bq, bk, scale):
    i = pl.program_id(1)
    first = i * bq
    prefix = prefix_ref[0]
    q = q_ref[...]
    limit = jnp.maximum(first + bq, prefix)
    total = (limit + bk - 1) // bk
    clear = jnp.maximum(first, prefix) // bk
    def step(masked, j, carry):
        top, tot, acc = carry
        rows = pl.ds(pl.multiple_of(j * bk, bk), bk)
        s = dot(q, k_ref[rows, :], NT) * scale
        if masked:
            kp = j * bk + lax.broadcasted_iota(jnp.int32, (bq, bk), 1)
            qp = first + lax.broadcasted_iota(jnp.int32, (bq, bk), 0)
            s = jnp.where(kp < jnp.maximum(qp + 1, prefix), s, NEG)
        new = jnp.maximum(top, jnp.max(s, axis=1, keepdims=True))
        alpha = jnp.exp(top - new)
        p = jnp.exp(s - new)
        tot = tot * alpha + jnp.sum(p, axis=1, keepdims=True)
        acc = acc * alpha + dot(p.astype(BF), v_ref[rows, :], NN)
        return new, tot, acc
    carry = (jnp.full((bq, 1), NEG, F32), jnp.zeros((bq, 1), F32), jnp.zeros((bq, q.shape[1]), F32))
    carry = lax.fori_loop(0, clear, functools.partial(step, False), carry)
    top, tot, acc = lax.fori_loop(clear, total, functools.partial(step, True), carry)
    o_ref[...] = (acc / tot).astype(o_ref.dtype)
    lse = jnp.broadcast_to(top + jnp.log(tot), (bq, 128))
    lse_ref[0] = lse.T[0:8, :]

def attend_fwd(qkv, prefix, heads, *, bq=512, bk=512, hd=128):
    seq = qkv.shape[0]
    return pl.pallas_call(
        functools.partial(fwd_kernel, bq=bq, bk=bk, scale=hd ** -0.5),
        grid_spec=pltpu.PrefetchScalarGridSpec(
            num_scalar_prefetch=1, grid=(heads, seq // bq),
            in_specs=[pl.BlockSpec((bq, hd), lambda h, i, p: (i, 3 * h)),
                      pl.BlockSpec((seq, hd), lambda h, i, p: (0, 3 * h + 1)),
                      pl.BlockSpec((seq, hd), lambda h, i, p: (0, 3 * h + 2))],
            out_specs=[pl.BlockSpec((bq, hd), lambda h, i, p: (i, h)),
                       pl.BlockSpec((1, 8, bq), lambda h, i, p: (h, 0, i))]),
        out_shape=[jax.ShapeDtypeStruct((seq, heads * hd), BF), jax.ShapeDtypeStruct((heads, 8, seq), F32)],
        cost_estimate=pl.CostEstimate(flops=4 * heads * seq * seq * hd, bytes_accessed=8 * heads * seq * hd, transcendentals=heads * seq * seq),
        name="attend_forward",
    )(prefix, qkv, qkv, qkv)

def bwd_kernel(prefix_ref, qkv_ref, o_ref, do_ref, lse_ref, cos_ref, sin_ref, out_ref, dk_ref, dv_ref, delta_ref, *, bq, bk, hd, scale):
    seq = qkv_ref.shape[0]
    prefix = prefix_ref[0]
    dk_ref[...] = jnp.zeros_like(dk_ref)
    dv_ref[...] = jnp.zeros_like(dv_ref)
    def deltas(i, _):
        rows = pl.ds(pl.multiple_of(i * bq, bq), bq)
        prod = (do_ref[rows, :].astype(F32) * o_ref[rows, :].astype(F32)).T
        delta_ref[:, rows] = jnp.broadcast_to(jnp.sum(prod, axis=0, keepdims=True), (8, bq))
        return 0
    lax.fori_loop(0, seq // bq, deltas, 0)
    def unrotate(g, rows):
        cos, sin = cos_ref[rows, :], sin_ref[rows, :]
        half = hd // 2
        a, b = g[:, :half], g[:, half:]
        return jnp.concatenate([a * cos + b * sin, b * cos - a * sin], axis=1)
    def q_step(i, _):
        first = i * bq
        qrows = pl.ds(pl.multiple_of(first, bq), bq)
        q = qkv_ref[qrows, 0:hd]
        do = do_ref[qrows, :]
        lse = lse_ref[0, 0:1, qrows]
        delta = delta_ref[0:1, qrows]
        limit = jnp.maximum(first + bq, prefix)
        total = (limit + bk - 1) // bk
        clear = jnp.maximum(first, prefix) // bk
        def step(masked, j, dq):
            krows = pl.ds(pl.multiple_of(j * bk, bk), bk)
            k = qkv_ref[krows, hd:2 * hd]
            v = qkv_ref[krows, 2 * hd:3 * hd]
            s = dot(k, q, NT) * scale
            p = jnp.exp(s - lse)
            if masked:
                kp = j * bk + lax.broadcasted_iota(jnp.int32, (bk, bq), 0)
                qp = first + lax.broadcasted_iota(jnp.int32, (bk, bq), 1)
                p = jnp.where(kp < jnp.maximum(qp + 1, prefix), p, 0.0)
            dp = dot(v, do, NT)
            dv_ref[krows, :] += dot(p.astype(BF), do, NN)
            ds = (p * (dp - delta)).astype(BF)
            dk_ref[krows, :] += dot(ds, q, NN)
            return dq + dot(ds, k, TN)
        dq = lax.fori_loop(0, clear, functools.partial(step, False), jnp.zeros((bq, hd), F32))
        dq = lax.fori_loop(clear, total, functools.partial(step, True), dq)
        out_ref[qrows, 0:hd] = unrotate(dq * scale, qrows).astype(BF)
        return 0
    lax.fori_loop(0, seq // bq, q_step, 0)
    def fin(i, _):
        rows = pl.ds(pl.multiple_of(i * bq, bq), bq)
        out_ref[rows, hd:2 * hd] = unrotate(dk_ref[rows, :] * scale, rows).astype(BF)
        out_ref[rows, 2 * hd:3 * hd] = dv_ref[rows, :].astype(BF)
        return 0
    lax.fori_loop(0, seq // bq, fin, 0)

def attend_bwd(qkv, mixed, dmixed, lse, prefix, cos, sin, heads, *, bq=512, bk=512, hd=128):
    seq = qkv.shape[0]
    return pl.pallas_call(
        functools.partial(bwd_kernel, bq=bq, bk=bk, hd=hd, scale=hd ** -0.5),
        grid_spec=pltpu.PrefetchScalarGridSpec(
            num_scalar_prefetch=1, grid=(heads,),
            in_specs=[pl.BlockSpec((seq, 3 * hd), lambda h, p: (0, h)),
                      pl.BlockSpec((seq, hd), lambda h, p: (0, h)),
                      pl.BlockSpec((seq, hd), lambda h, p: (0, h)),
                      pl.BlockSpec((1, 8, seq), lambda h, p: (h, 0, 0)),
                      pl.BlockSpec((seq, hd // 2), lambda h, p: (0, 0)),
                      pl.BlockSpec((seq, hd // 2), lambda h, p: (0, 0))],
            out_specs=[pl.BlockSpec((seq, 3 * hd), lambda h, p: (0, h))],
            scratch_shapes=[pltpu.VMEM((seq, hd), F32), pltpu.VMEM((seq, hd), F32), pltpu.VMEM((8, seq), F32)]),
        out_shape=[jax.ShapeDtypeStruct((seq, heads * 3 * hd), BF)],
        cost_estimate=pl.CostEstimate(flops=10 * heads * seq * seq * hd, bytes_accessed=20 * heads * seq * hd, transcendentals=heads * seq * seq),
        name="attend_backward",
    )(prefix, qkv, mixed, dmixed, lse, cos, sin)[0]


def rope_tables(count, head_dim):
    positions = jnp.arange(count, dtype=jnp.int32).astype(F32)
    frequency = 10000.0 ** (-(jnp.arange(head_dim // 2).astype(F32) * 2.0 / head_dim))
    angles = positions[:, None] * frequency[None, :]
    return jnp.cos(angles), jnp.sin(angles)


def rotate(values, cosine, sine):
    half = values.shape[-1] // 2
    a, b = values[..., :half], values[..., half:]
    return jnp.concatenate([a * cosine - b * sine, b * cosine + a * sine], axis=-1)


def norm(values):
    center = values - jnp.mean(values, axis=-1, keepdims=True)
    inv_std = lax.rsqrt(jnp.mean(center * center, axis=-1, keepdims=True) + EPSILON)
    return center * inv_std, inv_std


def norm_back(grad, normed, inv_std):
    mean_grad = jnp.mean(grad, axis=-1, keepdims=True)
    mean_cross = jnp.mean(grad * normed, axis=-1, keepdims=True)
    return inv_std * (grad - mean_grad - normed * mean_cross)


def mm(spec, left, right):
    return jnp.einsum(spec, left, right, preferred_element_type=F32)


def local(swap, inputs, prefix_len, w_qkv, w_out, w_up_gate, w_down, cotangent):
    rows = ("rmaj", "cmin") if swap else ("rmaj", "core")
    cols = ("cmaj", "core") if swap else ("cmaj", "cmin")

    def exchange(value):
        if not swap:
            return value
        return lax.ppermute(value, ("core", "cmin"), [(0, 0), (1, 2), (2, 1), (3, 3)])

    def scatter(value):
        return lax.psum_scatter(value.astype(BF), cols, scatter_dimension=0, tiled=True).astype(F32)

    def spread(value):
        return lax.all_to_all(value, cols, 1, 0, tiled=True)

    prefix_len = exchange(prefix_len)
    inputs, cotangent = exchange(inputs), exchange(cotangent)
    w_qkv, w_out = exchange(w_qkv), exchange(w_out)
    w_up_gate, w_down = exchange(w_up_gate), exchange(w_down)
    tokens = inputs.shape[0]
    heads, head_dim = w_qkv.shape[1], w_qkv.shape[2] // 3
    hidden_width = w_down.shape[0]
    full_in = lax.all_gather(inputs, cols, axis=1, tiled=True)
    width = full_in.shape[1]
    qkv_all = lax.all_gather(w_qkv, rows, axis=0, tiled=True).reshape(width, heads * 3 * head_dim)
    out_all = lax.all_gather(w_out, rows, axis=1, tiled=True)
    up_all = lax.all_gather(w_up_gate, rows, axis=0, tiled=True).reshape(width, 2 * hidden_width)
    down_all = lax.all_gather(w_down, rows, axis=1, tiled=True)
    cot_full = lax.all_gather(cotangent, cols, axis=1, tiled=True)
    piece = tokens // lax.axis_size(cols)
    first = lax.axis_index(cols) * piece
    own_in = lax.dynamic_slice_in_dim(full_in, first, piece, 0).astype(F32)
    own_cot = lax.dynamic_slice_in_dim(cot_full, first, piece, 0).astype(F32)

    normed_in = norm(full_in.astype(F32))[0].astype(BF)
    qkv_rows = mm("td,de->te", normed_in, qkv_all).reshape(tokens, heads, 3, head_dim)
    cosine, sine = rope_tables(tokens, head_dim)
    turned = rotate(qkv_rows[:, :, :2], cosine[:, None, None], sine[:, None, None])
    qkv = jnp.concatenate([turned, qkv_rows[:, :, 2:]], axis=2).astype(BF)
    qkv = qkv.reshape(tokens, heads * 3 * head_dim)
    mixed, lse = attend_fwd(qkv, prefix_len, heads, hd=head_dim)
    middle = own_in + scatter(mm("tc,cd->td", mixed, out_all))
    normed_two, inv_two = norm(middle)
    normed_mid = lax.all_gather(normed_two.astype(BF), cols, axis=0, tiled=True)
    gate_up = mm("td,df->tf", normed_mid, up_all)
    gate, up = gate_up[:, :hidden_width], gate_up[:, hidden_width:]
    sig = jax.nn.sigmoid(gate)
    active = gate * sig
    hidden = (active * up).astype(BF)
    outputs = middle + scatter(mm("tf,fd->td", hidden, down_all))
    outputs = exchange(spread(outputs.astype(BF)))

    grad_hidden = mm("td,fd->tf", cot_full, down_all)
    grad_gate = grad_hidden * up * sig * (1.0 + gate * (1.0 - sig))
    grad_gate_up = jnp.concatenate([grad_gate, grad_hidden * active], axis=1).astype(BF)
    grad_down = mm("tf,td->fd", hidden, cot_full).astype(BF)
    grad_down = lax.psum_scatter(grad_down, rows, scatter_dimension=1, tiled=True)
    grad_up = mm("td,tf->df", normed_mid, grad_gate_up).astype(BF)
    grad_up = lax.psum_scatter(grad_up, rows, scatter_dimension=0, tiled=True)
    grad_normed = scatter(mm("tf,df->td", grad_gate_up, up_all))
    grad_middle = own_cot + norm_back(grad_normed, normed_two, inv_two)
    grad_branch = lax.all_gather(grad_middle.astype(BF), cols, axis=0, tiled=True)
    grad_out = mm("tc,td->cd", mixed, grad_branch).astype(BF)
    grad_out = lax.psum_scatter(grad_out, rows, scatter_dimension=1, tiled=True)
    grad_mixed = mm("td,cd->tc", grad_branch, out_all).astype(BF)
    grad_rows = attend_bwd(qkv, mixed, grad_mixed, lse, prefix_len, cosine, sine, heads, hd=head_dim)
    grad_in = scatter(mm("te,de->td", grad_rows, qkv_all))
    grad_qkv = mm("td,te->de", normed_in, grad_rows).astype(BF)
    grad_qkv = lax.psum_scatter(grad_qkv, rows, scatter_dimension=0, tiled=True)
    normed_own, inv_own = norm(own_in)
    input_grad = grad_middle + norm_back(grad_in, normed_own, inv_own)
    input_grad = exchange(spread(input_grad.astype(BF))).astype(F32)
    return (
        outputs,
        input_grad,
        exchange(grad_qkv).astype(F32).reshape(-1, heads, 3 * head_dim),
        exchange(grad_out).astype(F32),
        exchange(grad_up).astype(F32).reshape(-1, 2, hidden_width),
        exchange(grad_down).astype(F32),
    )


AXES = ("y", "core", "zh", "zl", "x")
GROUP = ("core", "zl", "x")
MESH = pl.DeviceIdType.MESH
DMA = pltpu.SemaphoreType.DMA
VMEM_WHOLE = pl.BlockSpec(memory_space=pltpu.VMEM)
ANYWHERE = pl.BlockSpec(memory_space=pl.ANY)


class Place:
    def __init__(self):
        self.y, self.c, self.zh, self.zl, self.x = (lax.axis_index(name) for name in AXES)
        y, c, zh, zl, x = self.y, self.c, self.zh, self.zl, self.x
        self.sibling = (y, 1 - c, zh, zl, x)
        self.across = (y, c, zh, zl, 1 - x)
        self.along = (y, c, zh, 1 - zl, x)
        self.beyond = (1 - y, c, zh, zl, x)
        self.far = [(y, core, 1 - zh, zl, x) for core in (0, 1)]
        self.far_role = (y, zh, 1 - zh, zl, x)
        self.straight = c == zh
        self.outer = zl == zh
        self.order = [2 * y, 2 * y + 1, 2 * (1 - y), 2 * (1 - y) + 1]
        self.block = c * 4 + zl * 2 + x

    def chip(self, dz, dx):
        return lax.rem(self.zl + dz, 2) * 2 + lax.rem(self.x + dx, 2)

    def meet(self, greet=None):
        devices = [self.sibling, self.across, self.along, self.beyond, *self.far]
        barrier = pltpu.get_barrier_semaphore()
        for device in devices:
            pl.semaphore_signal(barrier, inc=1, device_id=device, device_id_type=MESH)
        more = greet(self, barrier) if greet else 0
        pl.semaphore_wait(barrier, len(devices) + more)


def span(start, size):
    return pl.ds(pl.multiple_of(start, size), size)


def remote(src, dst, send_sem, recv_sem, device):
    return pltpu.make_async_remote_copy(
        src_ref=src, dst_ref=dst, send_sem=send_sem, recv_sem=recv_sem, device_id=device, device_id_type=MESH
    )


class Beyond:
    along_z = False

    def __init__(self, place, src, dst, sem):
        self.copy = remote(src, dst, sem.at[0], sem.at[2], place.beyond)

    def start(self):
        self.copy.start()

    def wait_recv(self):
        self.copy.wait_recv()

    def wait_send(self):
        self.copy.wait_send()


class WeightHalf:
    along_z = True

    def __init__(self, place, src, dst, sem):
        c = place.c
        self.straight = place.straight
        self.outward = remote(src, dst.at[c], sem.at[0], sem.at[2 + c], place.far_role)
        self.aside = remote(src, dst.at[c], sem.at[1], sem.at[2 + c], place.sibling)
        self.here = pltpu.make_async_copy(src, dst.at[c], sem.at[1])
        self.from_sibling = remote(src, dst.at[1 - c], sem.at[1], sem.at[3 - c], place.sibling)
        self.from_far = [remote(src, dst.at[i], sem.at[0], sem.at[2 + i], place.far_role) for i in (0, 1)]

    def start(self):
        self.outward.start()

        @pl.when(self.straight)
        def _():
            self.here.start()

        @pl.when(jnp.logical_not(self.straight))
        def _():
            self.aside.start()

    def wait_recv(self):
        @pl.when(self.straight)
        def _():
            self.here.wait()
            self.from_sibling.wait_recv()

        @pl.when(jnp.logical_not(self.straight))
        def _():
            for copy in self.from_far:
                copy.wait_recv()

    def wait_send(self):
        self.outward.wait_send()

        @pl.when(jnp.logical_not(self.straight))
        def _():
            self.aside.wait_send()


class GradHalf:
    along_z = True

    def __init__(self, place, src, dst, sem):
        c, zh = place.c, place.zh
        self.straight = place.straight
        self.here = pltpu.make_async_copy(src.at[c], dst.at[zh], sem.at[0])
        self.aside = remote(src.at[1 - c], dst.at[zh], sem.at[1], sem.at[2 + zh], place.sibling)
        self.outward = [remote(src.at[i], dst.at[zh], sem.at[i], sem.at[2 + zh], place.far[i]) for i in (0, 1)]
        self.from_sibling = remote(src.at[c], dst.at[zh], sem.at[1], sem.at[2 + zh], place.sibling)
        self.from_far = remote(src.at[c], dst.at[1 - zh], sem.at[0], sem.at[3 - zh], place.far[0])

    def start(self):
        @pl.when(self.straight)
        def _():
            self.here.start()
            self.aside.start()

        @pl.when(jnp.logical_not(self.straight))
        def _():
            for copy in self.outward:
                copy.start()

    def wait_recv(self):
        self.from_far.wait_recv()

        @pl.when(self.straight)
        def _():
            self.here.wait()

        @pl.when(jnp.logical_not(self.straight))
        def _():
            self.from_sibling.wait_recv()

    def wait_send(self):
        @pl.when(self.straight)
        def _():
            self.aside.wait_send()

        @pl.when(jnp.logical_not(self.straight))
        def _():
            for copy in self.outward:
                copy.wait_send()


KINDS = {"beyond": Beyond, "weight": WeightHalf, "grad": GradHalf}


def moved_shape(kind, src):
    shape = (2, *src.shape) if kind == "weight" else src.shape
    return jax.ShapeDtypeStruct(shape, src.dtype)


class Under:
    def __init__(self, place, moves):
        self.place, self.moves = place, moves
        self.z = [move for kind, move in moves if move.along_z]
        self.y = [move for kind, move in moves if not move.along_z and not isinstance(kind, int)]
        self.follow = [(moves[kind][1], move) for kind, move in moves if isinstance(kind, int)]

    def start_y(self):
        for move in self.y:
            move.start()

    def start_z(self, outer=None):
        def start():
            for move in self.z:
                move.start()

        if outer is None:
            start()
        else:
            pl.when(self.place.outer if outer else jnp.logical_not(self.place.outer))(start)

    def start_follow(self):
        for ahead, move in self.follow:
            ahead.wait_recv()
            move.start()

    def end(self, skip=0):
        done = [ahead for ahead, _ in self.follow]
        for _, move in self.moves[skip:]:
            if move not in done:
                move.wait_recv()


def comm_call(
    body, name, ident, inputs, outs, scratch, moves=(), flops=0, transcendentals=0, spaces=None, greet=None
):
    n_in, n_out, n_move = len(inputs), len(outs), len(moves)
    own_source = [i for i, (kind, _) in enumerate(moves) if not isinstance(kind, int)]

    def kernel(*refs):
        ins, refs = refs[:n_in], refs[n_in:]
        sources, refs = refs[:len(own_source)], refs[len(own_source):]
        results, refs = refs[:n_out], refs[n_out:]
        targets, refs = refs[:n_move], refs[n_move:]
        sems, rest = refs[0], refs[1:]
        place = Place()
        place.meet(greet)
        made = []
        for i, (kind, _) in enumerate(moves):
            if isinstance(kind, int):
                made.append((kind, Beyond(place, targets[kind], targets[i], sems.at[i])))
            else:
                made.append((kind, KINDS[kind](place, sources[own_source.index(i)], targets[i], sems.at[i])))
        body(place, ins, results, rest, Under(place, made), targets)
        for _, move in made:
            move.wait_send()

    arrays = [*inputs, *(moves[i][1] for i in own_source)]
    shapes = list(outs)
    moved = []
    for kind, array in moves:
        moved.append(moved[kind] if isinstance(kind, int) else moved_shape(kind, array))
    shapes += moved
    in_specs = (spaces or [VMEM_WHOLE] * n_in) + [ANYWHERE] * len(own_source)
    size = sum(s.size * s.dtype.itemsize for s in (*arrays, *shapes))
    result = pl.pallas_call(
        kernel,
        out_shape=shapes,
        in_specs=in_specs,
        out_specs=[VMEM_WHOLE] * (n_out + n_move),
        scratch_shapes=[DMA((max(n_move, 1), 4)), *scratch],
        compiler_params=pltpu.CompilerParams(
            collective_id=ident, has_side_effects=True, vmem_limit_bytes=(64 << 20) - (64 << 10)
        ),
        cost_estimate=pl.CostEstimate(
            flops=flops + (20 << 30), bytes_accessed=size, transcendentals=transcendentals
        ),
        name=name,
    )(*arrays)
    return result[:n_out], result[n_out:]


def each_rows(count, body, size=32):
    def step(i, carry):
        body(span(i * size, size))
        return carry

    lax.fori_loop(0, count // size, step, 0)


def row_norm(values):
    center = values - jnp.mean(values, axis=-1, keepdims=True)
    inv_std = lax.rsqrt(jnp.mean(center * center, axis=-1, keepdims=True) + EPSILON)
    return center * inv_std, inv_std


SLICES = 4
NORM_ROWS = 64
NORM_UNROLL = 1


def reduce_sems():
    return [DMA((4,)), DMA((4,)), DMA((3, SLICES)), DMA((3, SLICES))]


def reduce_scratch(piece, width):
    return [pltpu.VMEM((count, piece, width), BF) for count in (4, 4, 2, 3, 3)] + reduce_sems()


def nothing():
    pass


def reduce_body(place, compute, last, scratch, begin=nothing, before_z=nothing, after_z=nothing, split=0):
    sib_out, sib_in, own, near_out, near_in, sib_send, sib_recv, near_send, near_recv = scratch
    piece = own.shape[1]
    c = place.c
    size = piece // SLICES
    begin()

    def sib_copy(step):
        return remote(sib_out.at[step], sib_in.at[step], sib_send.at[step], sib_recv.at[step], place.sibling)

    def near_copy(step, r, turned=False):
        device = place.along if step == 2 or turned else place.across
        rows = span(r * size, size)
        return remote(
            near_out.at[step, rows], near_in.at[step, rows], near_send.at[step, r], near_recv.at[step, r], device
        )

    def finish(step):
        slot = step % 2
        sib_copy(step).wait_recv()

        def send(joins, turned, r, carry):
            if joins:
                near_copy(0, r).wait_recv()
            rows = span(r * size, size)
            total = own[slot, rows, :].astype(F32) + sib_in[step, rows, :].astype(F32)
            if joins:
                total = total + near_in[0, rows, :].astype(F32)
            near_out[step, rows, :] = total.astype(BF)
            near_copy(step, r, turned).start()
            return carry

        lax.fori_loop(0, SLICES - split, functools.partial(send, step == 2, False), 0)
        if split:
            lax.fori_loop(SLICES - split, SLICES, functools.partial(send, step == 1, step == 0), 0)

    def step(s, carry):
        target = place.chip(1 - lax.rem(s, 2), 1 - s // 2)
        compute((1 - c) * 4 + target, sib_out.at[s])
        sib_copy(s).start()
        for index in (0, 1):
            @pl.when(s == index + 1)
            def _(index=index):
                finish(index)

        compute(c * 4 + target, own.at[lax.rem(s, 2)])
        return carry

    lax.fori_loop(0, 4, step, 0)
    before_z()
    finish(2)
    after_z()
    sib_copy(3).wait_recv()

    def arrive(r, carry):
        near_copy(1, r).wait_recv()
        near_copy(2, r).wait_recv()

        def final(i, carry):
            rows = span(r * size + i * 16, 16)
            total = own[1, rows, :].astype(F32) + sib_in[3, rows, :].astype(F32)
            last(rows, total + near_in[1, rows, :].astype(F32) + near_in[2, rows, :].astype(F32))
            return carry

        return lax.fori_loop(0, size // 16, final, carry)

    lax.fori_loop(0, SLICES, arrive, 0)
    for s in range(4):
        sib_copy(s).wait_send()

    def sent(r, carry):
        for s in range(3):
            near_copy(s, r).wait_send()
        return carry

    lax.fori_loop(0, SLICES, sent, 0)


def product(place, left_ref, weights, transposed):
    def compute(owner, out_ref):
        piece = out_ref.shape[0]
        left = left_ref[span(owner * piece, piece), :]
        for weight, index in zip(weights, place.order):
            size = weight.shape[0] if transposed else weight.shape[1]
            part = dot(left, weight[...], NT if transposed else NN)
            out_ref[:, span(index * size, size)] = part.astype(out_ref.dtype)

    return compute


def back_rows(base, value, total):
    normed, inv_std = row_norm(value)
    mean_grad = jnp.mean(total, axis=-1, keepdims=True)
    mean_cross = jnp.mean(total * normed, axis=-1, keepdims=True)
    return base + inv_std * (total - mean_grad - normed * mean_cross)


def quarters(first, second):
    return [first.at[0], first.at[1], second.at[0], second.at[1]]


def both_halves(cos_ref, sin_ref, rows):
    cos, sin = cos_ref[rows, :], sin_ref[rows, :]
    return jnp.concatenate([cos, cos], axis=1), jnp.concatenate([-sin, sin], axis=1)


def beside(under):
    def begin():
        under.start_y()
        under.start_z()

    return dict(begin=begin, after_z=under.start_follow)


class Turned:
    def __init__(self, source, stage, sems, flipped):
        self.source, self.stage, self.sems, self.flipped = source, stage, sems, flipped
        self.tile, self.strip = 256, stage.shape[1]
        self.count = flipped.shape[1] // self.strip

    def load(self, i):
        slot = lax.rem(i, 2)
        rows = span(i * self.strip, self.strip)
        return pltpu.make_async_copy(self.source.at[rows], self.stage.at[slot], self.sems.at[slot])

    def turn(self):
        def step(i, carry):
            self.load(i).wait()

            @pl.when(i + 1 < self.count)
            def _():
                self.load(i + 1).start()

            self.flipped[:, span(i * self.strip, self.strip)] = self.stage[lax.rem(i, 2)].T
            return carry

        self.load(0).start()
        lax.fori_loop(0, self.count, step, 0)

    def times(self, right, out, first, offset):
        block, columns = out.shape[1:]
        half = columns // 2
        each = block // self.tile

        def step(n, carry):
            m, t = n // 2, lax.rem(n, 2)
            left = self.flipped[span(first + m * self.tile, self.tile), :]
            value = dot(left, right[:, span(offset + t * half, half)], NN)
            out[m // each, span(lax.rem(m, each) * self.tile, self.tile), span(t * half, half)] = value.astype(BF)
            return carry

        lax.fori_loop(0, 4 * each, step, 0)


def down_call(hidden, firsts, seconds, middle, own, moved, normed, grads, gate_other, ident):
    piece, width = middle.shape
    tokens, both = grads.shape
    part_width = both // 2
    block = width // 4
    tile = 256

    def kernel(
        hidden_ref, first_a, first_b, second_a, second_b, base_ref, own_ref, moved_ref, grads_ref, normed_ref, gate_other,
        result_ref, down_out, gate_out, up_own_out, up_other_out,
        down_sum, stage, flipped, gate_moved, kept, spare,
        y_sems, z_sems, load_sems, store_sems, *reduce_refs
    ):
        place = Place()
        place.meet()
        y = place.y

        turned = Turned(normed_ref, stage, load_sems, flipped)
        for j in (0, 1):
            cols = pl.ds(j * block, block)

            def step(i, carry, j=j, cols=cols):
                upper, rows = i // (own_ref.shape[1] // 64), span(lax.rem(i, own_ref.shape[1] // 64) * 64, 64)
                total = own_ref[upper, rows, cols].astype(F32) + moved_ref[upper, rows, cols].astype(F32)
                down_sum[j, span(i * 64, 64), :] = total.astype(BF)
                return carry

            lax.fori_loop(0, down_sum.shape[1] // 64, step, 0)
        z_down = GradHalf(place, down_sum, down_out, z_sems.at[0])
        y_gate = Beyond(place, gate_other, gate_moved, y_sems.at[0])
        y_gate.start()
        parts = list(zip(quarters(first_a, second_a), quarters(first_b, second_b), place.order))

        def compute(owner, out_ref):
            rows = span(owner * piece, piece)
            for upper, lower, index in parts:
                depth, size = upper.shape
                part = dot(hidden_ref[rows, 0:depth], upper[...], NN) + dot(hidden_ref[rows, depth:], lower[...], NN)
                out_ref[:, span(index * size, size)] = part.astype(out_ref.dtype)

        def last(rows, total):
            result_ref[rows, :] = (base_ref[rows, :] + total).astype(BF)

        def store(out, ref, i):
            return pltpu.make_async_copy(ref, out, store_sems.at[i])

        def after_z():
            turned.turn()
            turned.times(grads_ref, spare, (1 - y) * (width // 2), part_width)
            store(up_other_out, spare, 0).start()
            turned.times(grads_ref, kept, y * (width // 2), 0)
            store(up_other_out, spare, 0).wait()
            turned.times(grads_ref, spare, y * (width // 2), part_width)
            store(up_own_out, spare, 1).start()

        reduce_body(place, compute, last, reduce_refs, begin=z_down.start, after_z=after_z)
        y_gate.wait_recv()
        for i in (0, 1):
            def add(n, carry, i=i):
                rows = span(n * 64, 64)
                kept[i, rows, :] = (kept[i, rows, :].astype(F32) + gate_moved[i, rows, :].astype(F32)).astype(BF)
                return carry

            lax.fori_loop(0, block // 64, add, 0)
        store(gate_out, kept, 2).start()
        z_down.wait_recv()
        store(up_own_out, spare, 1).wait()
        store(gate_out, kept, 2).wait()
        for move in (z_down, y_gate):
            move.wait_send()

    shape = jax.ShapeDtypeStruct
    half = shape((2, block, part_width), BF)
    down_shape = (2, hidden.shape[1], block)
    held = pltpu.VMEM(half.shape, BF)
    return pl.pallas_call(
        kernel,
        out_shape=[shape((piece, width), BF), shape(down_shape, BF), half, half, half],
        in_specs=[VMEM_WHOLE] * 9 + [ANYWHERE] * 2,
        out_specs=[VMEM_WHOLE] + [ANYWHERE] * 4,
        scratch_shapes=[
            pltpu.VMEM(down_shape, BF),
            pltpu.VMEM((2, tile, width), BF),
            pltpu.VMEM((width, tokens), BF),
            held, held, held,
            DMA((1, 4)), DMA((1, 4)), DMA((2,)), DMA((3,)), *reduce_scratch(piece, width),
        ],
        compiler_params=pltpu.CompilerParams(collective_id=ident, has_side_effects=True, vmem_limit_bytes=63 << 20),
        cost_estimate=pl.CostEstimate(flops=60 << 30, bytes_accessed=60 << 20, transcendentals=0),
        name="reduce_down",
    )(hidden, *firsts, *seconds, middle, own, moved, grads, normed, gate_other)


def middle_call(cot, slopes, hidden_rows, gates, ups, downs, down_last, normed, moves, middle, ident):
    piece, width = middle.shape
    tokens, part_width = cot.shape[0], down_last.shape[1]
    hidden = 2 * part_width
    tile = 256
    tiles = part_width // tile

    def body(place, ins, outs, scratch, under, targets):
        cot_hbm, slopes_ref, normed_ref, hidden_ref, ga1, ga2, gb1, gb2, ua1, ua2, ub1, ub2, value_ref, da1, da2, db1 = ins
        total_ref, branch_ref, grad_ref, gate_other, down_own, down_moved = outs
        load_sem, cot_ref, stage, down_other, y_sem, turned_hidden, *rest = scratch
        strip = stage.shape[1]
        under.start_y()
        loads = [
            pltpu.make_async_copy(slopes_ref, grad_ref, load_sem.at[0]),
            pltpu.make_async_copy(cot_hbm, cot_ref, load_sem.at[1]),
        ]
        for load in loads:
            load.start()
        for load in loads:
            load.wait()
        base_ref = stage.at[0]

        def hidden_load(i):
            slot = lax.rem(i, 2)
            return pltpu.make_async_copy(
                hidden_ref.at[span(i * strip, strip)], stage.at[slot, :, pl.ds(0, hidden)], load_sem.at[slot]
            )

        def turn(i, carry):
            hidden_load(i).wait()

            @pl.when(i + 1 < tokens // strip)
            def _():
                hidden_load(i + 1).start()

            value = stage[lax.rem(i, 2), :, 0:hidden].T
            for j in range(hidden // tile):
                turned_hidden[j, :, span(i * strip, strip)] = value[j * tile:(j + 1) * tile]
            return carry

        def down_half(out, which):
            half = width // 4
            each = hidden // 2 // tile

            def step(n, carry):
                m, t = n // 2, lax.rem(n, 2)
                value = dot(turned_hidden[m], cot_ref[:, span(which * 2 * half + t * half, half)], NN)
                out[m // each, span(lax.rem(m, each) * tile, tile), span(t * half, half)] = value.astype(BF)
                return carry

            lax.fori_loop(0, 2 * (hidden // tile), step, 0)

        hidden_load(0).start()
        lax.fori_loop(0, tokens // strip, turn, 0)
        down_half(down_other, 1 - place.y)
        y_down = Beyond(place, down_other, down_moved, y_sem)
        y_down.start()
        rows_in = (quarters(da1, da2), quarters(db1, targets[0]))

        def fill(owner, part):
            rows = span(owner * piece, piece)

            def step(t, carry):
                grad = None
                for weight, index in zip(rows_in[part], place.order):
                    size = weight.shape[1]
                    term = dot(cot_ref[rows, span(index * size, size)], weight[span(t * tile, tile), :], NT)
                    grad = term if grad is None else grad + term
                for offset in (0, hidden):
                    cols = span(offset + part * part_width + t * tile, tile)
                    grad_ref[rows, cols] = (grad * grad_ref[rows, cols].astype(F32)).astype(BF)
                return carry

            lax.fori_loop(0, tiles, step, 0)

        def fill_first(i, carry):
            fill(i, 0)
            return carry

        lax.fori_loop(0, tokens // piece, fill_first, 0)
        under.moves[0][1].wait_recv()
        columns = [quarters(ga1, ga2), quarters(gb1, gb2), quarters(ua1, ua2), quarters(ub1, ub2)]

        def compute(owner, out_ref):
            rows = span(owner * piece, piece)
            fill(owner, 1)
            for quarter, index in enumerate(place.order):
                total = None
                for i, weights in enumerate(columns):
                    weight = weights[quarter]
                    size = weight.shape[0]
                    term = dot(grad_ref[rows, i * part_width:(i + 1) * part_width], weight[...], NT)
                    total = term if total is None else total + term
                out_ref[:, span(index * size, size)] = total.astype(out_ref.dtype)

        def last(rows, total):
            base = base_ref[rows, :].astype(F32)
            grad = back_rows(base, value_ref[rows, :], total)
            total_ref[rows, :] = grad
            branch_ref[rows, :] = grad.astype(BF)

        turned = Turned(normed_ref, stage, load_sem, cot_ref)

        def after_z():
            down_half(down_own, place.y)
            turned.turn()
            base_load = pltpu.make_async_copy(cot_hbm.at[span(place.block * piece, piece)], base_ref, load_sem.at[0])
            base_load.start()
            turned.times(grad_ref, gate_other, (1 - place.y) * (width // 2), 0)
            base_load.wait()

        reduce_body(place, compute, last, rest, after_z=after_z, split=2)
        under.end(skip=1)
        y_down.wait_recv()
        y_down.wait_send()

    shape = functools.partial(jax.ShapeDtypeStruct, (piece, width))
    down_half_shape = jax.ShapeDtypeStruct((2, hidden // 2, width // 2), BF)
    return comm_call(
        body, "reduce_middle", ident, [cot, slopes, normed, hidden_rows, *gates, *ups, middle, *downs, down_last],
        [
            shape(F32), shape(BF), jax.ShapeDtypeStruct((tokens, 2 * hidden), BF),
            jax.ShapeDtypeStruct((2, width // 4, hidden), BF),
            down_half_shape,
            down_half_shape,
        ],
        [
            DMA((2,)), pltpu.VMEM((tokens, width), BF), pltpu.VMEM((2, piece, width), BF),
            pltpu.VMEM(down_half_shape.shape, BF), DMA((4,)),
            pltpu.VMEM((hidden // tile, tile, tokens), BF), *reduce_scratch(piece, width),
        ],
        moves, flops=6 * tokens * hidden * width,
        spaces=[ANYWHERE] * 4 + [VMEM_WHOLE] * 12,
    )


def gather_scratch():
    return [DMA((3, SLICES)), DMA((3, SLICES)), DMA((4,)), DMA((4,))]


def gather_body(place, own_ref, full, sems, process, begin=nothing, follow=nothing, split=0):
    near_send, near_recv, sib_send, sib_recv = sems
    piece = own_ref.shape[0]
    size = piece // SLICES
    c = place.c

    def near_copy(slot, r, target, turned=False):
        where = full.at[span((c * 4 + target) * piece + r * size, size)]
        device = place.along if slot == 2 or turned else place.across
        return remote(where, where, near_send.at[slot, r], near_recv.at[slot, r], device)

    def sib_copy(slot, core, target):
        where = full.at[span((core * 4 + target) * piece, piece)]
        return remote(where, where, sib_send.at[slot], sib_recv.at[slot], place.sibling)

    def slices(act):
        def step(r, carry):
            act(r)
            return carry

        lax.fori_loop(0, SLICES, step, 0)

    mine, x_chip, z_chip, d_chip = place.chip(0, 0), place.chip(0, 1), place.chip(1, 0), place.chip(1, 1)
    full[span((c * 4 + mine) * piece, piece), :] = own_ref[...]
    slices(lambda r: near_copy(2, r, mine).start())
    slices(lambda r: near_copy(1, r, mine).start())
    sib_copy(3, c, mine).start()
    begin()

    def forward(r):
        near_copy(2, r, z_chip).wait_recv()
        if r < SLICES - split:
            near_copy(0, r, z_chip).start()

    process(c * 4 + mine)
    forward(0)
    sib_copy(3, 1 - c, mine).wait_recv()
    process((1 - c) * 4 + mine)
    forward(1)

    def arrived(r):
        near_copy(1, r, x_chip).wait_recv()

    for r in range(SLICES):
        arrived(r)
        if r >= SLICES - split:
            near_copy(0, r, x_chip, True).start()
    sib_copy(1, c, x_chip).start()
    process(c * 4 + x_chip)
    for r in range(2, SLICES):
        forward(r)
    sib_copy(2, c, z_chip).start()
    sib_copy(1, 1 - c, x_chip).wait_recv()
    process((1 - c) * 4 + x_chip)
    process(c * 4 + z_chip)
    follow()
    sib_copy(2, 1 - c, z_chip).wait_recv()
    process((1 - c) * 4 + z_chip)
    slices(lambda r: near_copy(0, r, d_chip).wait_recv())
    sib_copy(0, c, d_chip).start()
    process(c * 4 + d_chip)
    sib_copy(0, 1 - c, d_chip).wait_recv()
    process((1 - c) * 4 + d_chip)
    for slot in range(3):
        slices(lambda r: near_copy(slot, r, mine).wait_send())
    for slot in range(4):
        sib_copy(slot, c, mine).wait_send()


class ColumnGather:
    def __init__(self, place, src, full, sems):
        self.place, self.src, self.full = place, src, full
        self.near_send, self.near_recv, self.sib_send, self.sib_recv, self.own = sems
        self.width = src.shape[1]
        self.size = src.shape[0] // SLICES

    def where(self, core, target):
        return span((core * 4 + target) * self.width, self.width)

    def near(self, slot, r, target, first=False):
        place = self.place
        rows = pl.ds(r * self.size, self.size)
        dst = self.full.at[rows, self.where(place.c, target)]
        src = self.src.at[rows] if first else dst
        device = place.along if slot == 2 else place.across
        return remote(src, dst, self.near_send.at[slot, r], self.near_recv.at[slot, r], device)

    def sib(self, slot, core, target, first=False):
        dst = self.full.at[:, self.where(core, target)]
        src = self.src if first else dst
        return remote(src, dst, self.sib_send.at[slot], self.sib_recv.at[slot], self.place.sibling)

    def chips(self):
        place = self.place
        return place.chip(0, 0), place.chip(0, 1), place.chip(1, 0), place.chip(1, 1)

    def own_copy(self):
        return pltpu.make_async_copy(self.src, self.full.at[:, self.where(self.place.c, self.chips()[0])], self.own.at[0])

    def start(self):
        mine = self.chips()[0]
        self.own_copy().start()
        for slot in (2, 1):
            for r in range(SLICES):
                self.near(slot, r, mine, True).start()
        self.sib(3, self.place.c, mine, True).start()

    def forward(self, r):
        z_chip = self.chips()[2]
        self.near(2, r, z_chip).wait_recv()
        self.near(0, r, z_chip).start()

    def finish(self):
        mine, x_chip, z_chip, d_chip = self.chips()
        c = self.place.c
        self.sib(2, c, z_chip).start()
        for r in range(SLICES):
            self.near(1, r, x_chip).wait_recv()
        self.sib(1, c, x_chip).start()
        for r in range(SLICES):
            self.near(0, r, d_chip).wait_recv()
        self.sib(0, c, d_chip).start()
        self.own_copy().wait()
        for slot, target in enumerate((d_chip, x_chip, z_chip, mine)):
            self.sib(slot, 1 - c, target).wait_recv()
            self.sib(slot, c, mine).wait_send()
        for slot in range(3):
            for r in range(SLICES):
                self.near(slot, r, mine).wait_send()


def attend_back_body(qkv_ref, o_ref, do_ref, lse_ref, bound, cos_ref, sin_ref, out_ref, dk_ref, dv_ref, heads, hd):
    seq = qkv_ref.shape[0]
    bq = bk = min(512, seq // 2)
    scale = hd ** -0.5
    half = hd // 2

    def unrotate(g, rows):
        cos, sin = both_halves(cos_ref, sin_ref, rows)
        return g * cos - pltpu.roll(g, half, 1) * sin

    def head(h, carry):
        base = h * 3 * hd
        own = span(h * hd, hd)
        dk_ref[...] = jnp.zeros_like(dk_ref)
        dv_ref[...] = jnp.zeros_like(dv_ref)
        for i in range(seq // bq):
            first = i * bq
            rows = pl.ds(first, bq)
            q = qkv_ref[rows, span(base, hd)]
            do = do_ref[rows, own]
            row_sums = (do.astype(F32) * o_ref[rows, own].astype(F32)).T
            delta = jnp.sum(row_sums, axis=0, keepdims=True)
            tops = lse_ref[h, 0:1, first:first + bq]
            total = max(i + 1, seq // 2 // bk)

            def step(masked, j, dq, first=first, q=q, do=do, delta=delta, tops=tops):
                keys = span(j * bk, bk)
                k = qkv_ref[keys, span(base + hd, hd)]
                v = qkv_ref[keys, span(base + 2 * hd, hd)]
                p = jnp.exp(dot(k, q, NT) * scale - tops)
                if masked:
                    kp = j * bk + lax.broadcasted_iota(jnp.int32, (bk, bq), 0)
                    qp = first + lax.broadcasted_iota(jnp.int32, (bk, bq), 1)
                    p = jnp.where(kp < jnp.maximum(qp + 1, bound), p, 0.0)
                dv_ref[keys, :] += dot(p.astype(BF), do, NN)
                ds = (p * (dot(v, do, NT) - delta)).astype(BF)
                dk_ref[keys, :] += dot(ds, q, NN)
                return dq + dot(ds, k, TN)

            dq = lax.fori_loop(0, i, functools.partial(step, False), jnp.zeros((bq, hd), F32))
            dq = lax.fori_loop(i, total, functools.partial(step, True), dq)
            out_ref[rows, span(base, hd)] = unrotate(dq * scale, rows).astype(BF)

        def fin(i, carry):
            rows = span(i * bq, bq)
            out_ref[rows, span(base + hd, hd)] = unrotate(dk_ref[rows, :] * scale, rows).astype(BF)
            out_ref[rows, span(base + 2 * hd, hd)] = dv_ref[rows, :].astype(BF)
            return carry

        return lax.fori_loop(0, seq // bq, fin, carry)

    lax.fori_loop(0, heads, head, 0)


def front_call(inputs, cot, prefix, tables, weights, heads, hd, ident):
    names = ("qkv", "out", "ga", "gb", "ua", "ub", "da", "db")
    tokens, slice_width = inputs.shape
    width = slice_width * 8
    piece = tokens // 8
    size = tokens // SLICES
    inner = weights[0].shape[1]
    part_width = weights[2].shape[1]
    hidden = 2 * part_width
    tile = 256
    bq = bk = min(512, tokens // 2)
    scale = hd ** -0.5

    def kernel(in_ref, cot_ref, prefix_ref, cos_ref, sin_ref, *refs):
        sources, refs = refs[:8], refs[8:]
        firsts, seconds, refs = refs[:8], refs[8:15], refs[15:]
        (qkv_ref, mixed_ref, lse_ref, own_in_ref, middle_ref, normed_in_out, cot_out, normed_mid_out, hidden_out,
         slopes_out), refs = refs[:10], refs[10:]
        arena, acc, block_ref, normed_own, *refs = refs
        held, refs = dict(zip(names, refs[:8])), refs[8:]
        z_sems, y_sems, store_sems, out_sems, swap_send, swap_recv, phase, *sems = refs
        start_sems, gather_sems, reduce_sems_, feed_sems = sems[:5], sems[5:10], sems[10:14], sems[14:]
        place = Place()
        c, zl, x = place.c, place.zl, place.x
        place.meet()
        z_moves = {n: WeightHalf(place, sources[i], held[n].at[0], z_sems.at[i]) for i, n in enumerate(names)}
        y_moves = {n: Beyond(place, held[n].at[0], held[n].at[1], y_sems.at[i]) for i, n in enumerate(names[:7])}

        def go(name):
            z_moves[name].start()

        def stores(name):
            i = names.index(name)
            return [
                pltpu.make_async_copy(held[name].at[side], out[i], store_sems.at[i, side])
                for side, out in enumerate((firsts, seconds[:7]))
                if i < len(out)
            ]

        def pass_on(name):
            z_moves[name].wait_recv()
            y_moves[name].start()

        def got(name):
            y_moves[name].wait_recv()
            for copy in stores(name):
                copy.start()

        def parts(name):
            return [held[name].at[side, i] for side in (0, 1) for i in (0, 1)]

        full, normed = arena.at[pl.ds(0, tokens)], arena.at[pl.ds(tokens, tokens)]
        gather = ColumnGather(place, in_ref, full, start_sems)
        crossed = jnp.logical_not(place.straight)
        partner = (place.y, 1 - c, 1 - place.zh, zl, x)
        mine, x_chip, z_chip, d_chip = gather.chips()
        def rows_of(r):
            return pl.ds(r * size, size)

        def swap_copy(r, core):
            where = full.at[rows_of(r), gather.where(core, mine)]
            return remote(in_ref.at[rows_of(r)], where, swap_send.at[r], swap_recv.at[r], partner)

        def own_copy(r):
            where = full.at[rows_of(r), gather.where(c, mine)]
            return pltpu.make_async_copy(in_ref.at[rows_of(r)], where, swap_send.at[r])

        def cot_swap():
            return remote(cot_ref, block_ref, swap_send.at[SLICES], swap_recv.at[SLICES], partner)

        def cot_own():
            return pltpu.make_async_copy(cot_ref, block_ref, swap_send.at[SLICES])

        def sib(slot, r, core, target):
            where = full.at[rows_of(r), gather.where(core, target)]
            return remote(where, where, start_sems[2].at[slot, r], start_sems[3].at[slot, r], place.sibling)

        @pl.when(place.straight)
        def _():
            for r in range(SLICES):
                own_copy(r).start()
            cot_own().start()

        @pl.when(crossed)
        def _():
            for r in range(SLICES):
                swap_copy(r, 1 - c).start()

        for r in range(SLICES):
            @pl.when(place.straight)
            def _(r=r):
                own_copy(r).wait()

            @pl.when(crossed)
            def _(r=r):
                swap_copy(r, c).wait_recv()

            gather.near(2, r, mine).start()
            gather.near(1, r, mine).start()
            sib(3, r, c, mine).start()
        for r in range(SLICES):
            gather.forward(r)
            sib(2, r, c, z_chip).start()
            gather.near(1, r, x_chip).wait_recv()
            sib(1, r, c, x_chip).start()
            if r == 0:
                go("qkv")
        pass_on("qkv")
        go("out")
        pl.when(crossed)(lambda: cot_swap().start())
        depth = held["qkv"].shape[2]
        for r in range(SLICES):
            gather.near(0, r, d_chip).wait_recv()
            sib(0, r, c, d_chip).start()
            for slot, target in enumerate((d_chip, x_chip, z_chip, mine)):
                sib(slot, r, 1 - c, target).wait_recv()

            def norm_rows(i, carry, r=r):
                rows = span(r * size + i * NORM_ROWS, NORM_ROWS)
                normed[rows, :] = row_norm(full[rows, :].astype(F32))[0].astype(BF)
                return carry

            lax.fori_loop(0, size // NORM_ROWS, norm_rows, 0, unroll=NORM_UNROLL)
            pltpu.make_async_copy(normed.at[rows_of(r)], normed_in_out.at[rows_of(r)], out_sems.at[r]).start()
            total = None
            for weight, index in zip(parts("qkv")[:2], place.order[:2]):
                term = dot(normed[rows_of(r), span(index * depth, depth)], weight[...], NN)
                total = term if total is None else total + term
            acc[rows_of(r), :] = total
        own_in_ref[...] = full[span(place.block * piece, piece), :]
        pass_on("out")

        cot_gather = ColumnGather(place, block_ref, cot_out, gather_sems)

        def forward_cot():
            for r in range(SLICES):
                cot_gather.forward(r)

        @pl.when(place.straight)
        def _():
            cot_own().wait()
            cot_gather.start()
            go("ga")

        got("qkv")
        half = size // 2

        def project(r, carry):
            rows = span(r * half, half)
            total = acc[rows, :]
            for weight, index in zip(parts("qkv")[2:], place.order[2:]):
                total = total + dot(normed[rows, span(index * depth, depth)], weight[...], NN)
            cos, sin = both_halves(cos_ref, sin_ref, rows)
            for h in range(heads):
                for part in range(3):
                    value = total[:, (3 * h + part) * hd:(3 * h + part + 1) * hd]
                    if part < 2:
                        value = value * cos + pltpu.roll(value, hd // 2, 1) * sin
                    qkv_ref[rows, pl.ds((3 * h + part) * hd, hd)] = value.astype(BF)
            return carry

        lax.fori_loop(0, tokens // half, project, 0)
        @pl.when(crossed)
        def _():
            cot_swap().wait_recv()
            cot_gather.start()
            go("ga")
            cot_swap().wait_send()
            for r in range(SLICES):
                swap_copy(r, 1 - c).wait_send()

        pl.when(place.straight)(forward_cot)

        bound = prefix_ref[0:1, 0:1]

        def head(h, carry):
            base = h * 3 * hd
            for i in range(tokens // bq):
                first = i * bq
                q = qkv_ref[first:first + bq, span(base, hd)]
                count = max(i + 1, tokens // 2 // bk)

                def step(masked, j, state, first=first, q=q):
                    top, tot, out = state
                    rows = span(j * bk, bk)
                    s = dot(q, qkv_ref[rows, span(base + hd, hd)], NT) * scale
                    if masked:
                        kp = j * bk + lax.broadcasted_iota(jnp.int32, (bq, bk), 1)
                        qp = first + lax.broadcasted_iota(jnp.int32, (bq, bk), 0)
                        s = jnp.where(kp < jnp.maximum(qp + 1, bound), s, NEG)
                    new = jnp.maximum(top, jnp.max(s, axis=1, keepdims=True))
                    alpha = jnp.exp(top - new)
                    p = jnp.exp(s - new)
                    tot = tot * alpha + jnp.sum(p, axis=1, keepdims=True)
                    out = out * alpha + dot(p.astype(BF), qkv_ref[rows, span(base + 2 * hd, hd)], NN)
                    return new, tot, out

                state = (jnp.full((bq, 1), NEG, F32), jnp.zeros((bq, 1), F32), jnp.zeros((bq, hd), F32))
                state = lax.fori_loop(0, i, functools.partial(step, False), state)
                top, tot, out = lax.fori_loop(i, count, functools.partial(step, True), state)
                mixed_ref[first:first + bq, span(h * hd, hd)] = (out / tot).astype(BF)
                lse = jnp.broadcast_to(top + jnp.log(tot), (bq, 128))
                lse_ref[h, :, first:first + bq] = lse.T[0:8, :]
            return carry

        lax.fori_loop(0, heads, head, 0)
        go("gb")
        got("out")
        pl.when(crossed)(forward_cot)
        pass_on("ga")

        for r in range(SLICES):
            pltpu.make_async_copy(normed.at[rows_of(r)], normed_in_out.at[rows_of(r)], out_sems.at[r]).wait()
            for slot in range(3):
                gather.near(slot, r, mine).wait_send()
            for slot in range(4):
                sib(slot, r, c, mine).wait_send()
        for device in (place.sibling, place.across, place.along):
            pl.semaphore_signal(phase, inc=1, device_id=device, device_id_type=MESH)
        pl.semaphore_wait(phase, 3)

        class Blocks:
            def __init__(self, first, count):
                self.first, self.shape = first, (count, piece, width)

            def rows(self, index):
                if isinstance(index, tuple):
                    step, inside, *rest = index
                    start = (self.first + step) * piece + inside.start
                    return (pl.ds(pl.multiple_of(start, 16), inside.size), *rest)
                return (span((self.first + index) * piece, piece),)

            @property
            def at(self):
                return At(self)

            def __getitem__(self, index):
                return arena[self.rows(index)]

            def __setitem__(self, index, value):
                arena[self.rows(index)] = value

        class At:
            def __init__(self, blocks):
                self.blocks = blocks

            def __getitem__(self, index):
                return arena.at[self.blocks.rows(index)]

        buffers, first = [], 0
        for count in (4, 4, 2, 3, 3):
            buffers.append(Blocks(first, count))
            first += count

        def last(rows, total):
            middle = own_in_ref[rows, :].astype(F32) + total
            middle_ref[rows, :] = middle
            normed_own[rows, :] = row_norm(middle)[0].astype(BF)

        def after_z():
            go("ua")
            go("ub")
            pass_on("gb")
            got("ga")

        reduce_body(
            place, product(place, mixed_ref, parts("out"), False), last, [*buffers, *reduce_sems_],
            after_z=after_z, split=0,
        )

        full = arena.at[pl.ds(2 * tokens, tokens)]
        slopes_ref = arena.at[pl.ds(0, tokens)]
        hidden_ref = arena.at[pl.ds(tokens, tokens), pl.ds(0, hidden)]
        columns = (("ga", "ua"), ("gb", "ub"))
        waiting = []

        def fill(owner, which):
            rows = span(owner * piece, piece)
            gates, ups = (parts(name) for name in columns[which])

            def step(t, carry):
                taken = span(t * tile, tile)
                gate = up = None
                for gate_weight, up_weight, index in zip(gates, ups, place.order):
                    deep = gate_weight.shape[0]
                    value = full[rows, span(index * deep, deep)]
                    terms = dot(value, gate_weight[:, taken], NN), dot(value, up_weight[:, taken], NN)
                    gate, up = terms if gate is None else (gate + terms[0], up + terms[1])
                cols = span(which * part_width + t * tile, tile)
                up_cols = span(hidden + which * part_width + t * tile, tile)
                sig = 1.0 / (1.0 + jnp.exp(-gate))
                active = gate * sig
                hidden_ref[rows, cols] = (active * up).astype(BF)
                slopes_ref[rows, cols] = (up * sig * (1.0 + gate * (1.0 - sig))).astype(BF)
                slopes_ref[rows, up_cols] = active.astype(BF)
                return carry

            lax.fori_loop(0, part_width // tile, step, 0)

        def process(owner):
            waiting.append(owner)
            if len(waiting) == 1:
                pass_on("ua")
                got("gb")
                got("ua")
            fill(owner, 0)
            if len(waiting) == 3:
                go("da")
                go("db")
                pass_on("ub")
                got("ub")
                for earlier in waiting:
                    fill(earlier, 1)
            elif len(waiting) > 3:
                fill(owner, 1)

        gather_body(place, normed_own, full, feed_sems, process)
        for i, (ref, out) in enumerate(((full, normed_mid_out), (hidden_ref, hidden_out), (slopes_ref, slopes_out))):
            pltpu.make_async_copy(ref, out, out_sems.at[SLICES + i]).start()
        pass_on("da")
        cot_gather.finish()
        z_moves["db"].wait_recv()
        stores("db")[0].start()
        got("da")
        for i, (ref, out) in enumerate(((full, normed_mid_out), (hidden_ref, hidden_out), (slopes_ref, slopes_out))):
            pltpu.make_async_copy(ref, out, out_sems.at[SLICES + i]).wait()
        for move in (*z_moves.values(), *y_moves.values()):
            move.wait_send()
        for name in names:
            for copy in stores(name):
                copy.wait()

    def half_shape(weight):
        return jax.ShapeDtypeStruct((2, *weight.shape), BF)

    shape = jax.ShapeDtypeStruct
    outs = [
        *(half_shape(weight) for weight in weights),
        *(half_shape(weight) for weight in weights[:7]),
        shape((tokens, inner), BF),
        shape((tokens, heads * hd), BF),
        shape((heads, 8, tokens), F32),
        shape((piece, width), BF),
        shape((piece, width), F32),
        shape((tokens, width), BF),
        shape((tokens, width), BF),
        shape((tokens, width), BF),
        shape((tokens, hidden), BF),
        shape((tokens, 2 * hidden), BF),
    ]
    column_sems = [DMA((3, SLICES)), DMA((3, SLICES)), DMA((4,)), DMA((4,)), DMA((1,))]
    start_sems = [DMA((3, SLICES)), DMA((3, SLICES)), DMA((4, SLICES)), DMA((4, SLICES)), DMA((1,))]
    result = pl.pallas_call(
        kernel,
        out_shape=outs,
        in_specs=[ANYWHERE, ANYWHERE, VMEM_WHOLE, VMEM_WHOLE, VMEM_WHOLE] + [ANYWHERE] * 8,
        out_specs=[ANYWHERE] * 15 + [VMEM_WHOLE] * 5 + [ANYWHERE] * 5,
        scratch_shapes=[
            pltpu.VMEM((3 * tokens, width), BF),
            pltpu.VMEM((tokens, inner), F32),
            pltpu.VMEM((tokens, slice_width), BF),
            pltpu.VMEM((piece, width), BF),
            *(pltpu.VMEM((2, 2, *weight.shape), BF) for weight in weights[:7]),
            pltpu.VMEM((1, 2, *weights[7].shape), BF),
            DMA((8, 4)), DMA((8, 4)), DMA((8, 2)), DMA((SLICES + 3,)), DMA((SLICES + 1,)), DMA((SLICES + 1,)),
            pltpu.SemaphoreType.REGULAR,
            *start_sems, *column_sems, *reduce_sems(), *gather_scratch(),
        ],
        compiler_params=pltpu.CompilerParams(collective_id=ident, has_side_effects=True, vmem_limit_bytes=63 << 20),
        cost_estimate=pl.CostEstimate(
            flops=100 << 30, bytes_accessed=100 << 20, transcendentals=heads * tokens * tokens
        ),
        name="front",
    )(inputs, cot, prefix, *tables, *weights)
    return result[:8], result[8:15], result[15:]


BLOCKS = [(core, zl, x) for core in (0, 1) for zl in (0, 1) for x in (0, 1)]


def spread_greet(place, barrier):
    for core, zl, x in BLOCKS:
        mine = jnp.logical_and(place.straight, core * 4 + zl * 2 + x == place.block)

        @pl.when(jnp.logical_not(mine))
        def _(core=core, zl=zl, x=x):
            pl.semaphore_signal(
                barrier, inc=1, device_id=(place.y, core, place.c, zl, x), device_id_type=MESH
            )

    return 8 - jnp.where(place.straight, 1, 0)


def spread_scratch():
    return [DMA((8,)), DMA((8,)), DMA((1,))]


def spread_shape(piece):
    return jax.ShapeDtypeStruct((piece.shape[0] * 8, piece.shape[1] // 8), piece.dtype)


class Spread:
    def __init__(self, place, src, dst, sems):
        self.place, self.src, self.dst = place, src, dst
        self.send, self.recv, self.own = sems
        self.piece, self.width = src.shape[0], src.shape[1] // 8

    def copy(self, f):
        place = self.place
        return remote(
            self.src.at[:, pl.ds(f * self.width, self.width)], self.dst.at[span(place.block * self.piece, self.piece)],
            self.send.at[f], self.recv.at[place.block], (place.y, place.zh, *BLOCKS[f]),
        )

    def incoming(self, f):
        core, zl, x = BLOCKS[f]
        place = self.place
        return remote(
            self.src.at[:, pl.ds(f * self.width, self.width)], self.dst.at[pl.ds(f * self.piece, self.piece)],
            self.send.at[f], self.recv.at[f], (place.y, core, place.c, zl, x),
        )

    def own_copy(self):
        block = self.place.block
        return pltpu.make_async_copy(
            self.src.at[:, span(block * self.width, self.width)], self.dst.at[span(block * self.piece, self.piece)],
            self.own.at[0],
        )

    def each(self, act):
        for f in range(8):
            mine = jnp.logical_and(self.place.straight, self.place.block == f)
            pl.when(jnp.logical_not(mine))(functools.partial(act, f))

    def start(self):
        self.each(lambda f: self.copy(f).start())
        pl.when(self.place.straight)(lambda: self.own_copy().start())

    def wait(self):
        self.each(lambda f: self.incoming(f).wait_recv())
        self.each(lambda f: self.copy(f).wait_send())
        pl.when(self.place.straight)(lambda: self.own_copy().wait())


def rear_call(branch_own, out_halves, qkv_halves, qkv, mixed, lse, prefix, tables, grad_middle, own_in, ready, normed_in,
              gate_sum, up_own, up_other, heads, hd, ident):
    tokens, inner = qkv.shape
    piece, width = branch_own.shape
    inner_out = mixed.shape[1]
    block = width // 4
    tile = 256

    def kernel(
        branch_ref, out_1, out_2, qkv_1, qkv_2, qkv_ref, mixed_ref, lse_ref, prefix_ref, cos_ref, sin_ref, middle_ref,
        own_in_ref, ready_ref, normed_in_ref, gate_ref, up_own_ref, up_other_ref,
        gate_out, up_out, out_out, qkv_out, ready_out, result_out,
        full, grad_mixed, grad_rows, flipped, dk_ref, dv_ref, up_moved, out_grads, qkv_grads,
        y_sems, z_sems, load_sem, *sems
    ):
        place = Place()
        y = place.y
        reduce_refs, sems = sems[:9], sems[9:]
        gather_sems, ready_sems, result_sems = sems[:4], sems[4:7], sems[7:10]
        place.meet(spread_greet)
        y_up = Beyond(place, up_other_ref, up_moved, y_sems.at[0])
        y_out = Beyond(place, out_grads.at[0], out_grads.at[2], y_sems.at[1])
        y_qkv = Beyond(place, qkv_grads.at[0], qkv_grads.at[2], y_sems.at[2])
        z_gate = GradHalf(place, gate_ref, gate_out, z_sems.at[0])
        z_up = GradHalf(place, up_moved, up_out, z_sems.at[1])
        z_out = GradHalf(place, out_grads.at[1], out_out, z_sems.at[2])
        z_qkv = GradHalf(place, qkv_grads.at[1], qkv_out, z_sems.at[3])
        y_up.start()

        def add(own, moved, rows):
            def step(i, carry):
                where = span(i * 64, 64)
                for j in (0, 1):
                    total = own[j, where, :].astype(F32) + moved[j, where, :].astype(F32)
                    own[j, where, :] = total.astype(BF)
                return carry

            lax.fori_loop(0, rows // 64, step, 0)

        result_ref = full.at[pl.ds(0, piece)]

        out_parts = quarters(out_1, out_2)

        def process(owner):
            rows = span(owner * piece, piece)
            total = None
            for weight, index in zip(out_parts, place.order):
                part = dot(full[rows, span(index * block, block)], weight[...], NT)
                total = part if total is None else total + part
            grad_mixed[rows, :] = total.astype(BF)

        gather_body(place, branch_ref, full, gather_sems, process, begin=z_gate.start, split=0)
        ready_spread = Spread(place, ready_ref, ready_out, ready_sems)
        y_up.wait_recv()
        add(up_moved, up_own_ref, up_own.shape[1])
        z_up.start()
        ready_spread.start()

        def flip(source, columns):
            def step(i, carry):
                rows = span(i * tile, tile)
                flipped[0:columns, rows] = source[rows, :].T
                return carry

            lax.fori_loop(0, tokens // tile, step, 0)

        def weigh(grads, side, which, columns):
            def step(n, carry):
                i, m = n // (columns // tile), lax.rem(n, columns // tile)
                rows = span(m * tile, tile)
                value = dot(flipped[rows, :], full[:, span((which * 2 + i) * block, block)], NN)
                grads[side, i, rows, :] = value.astype(BF)
                return carry

            lax.fori_loop(0, 2 * (columns // tile), step, 0)

        flip(mixed_ref, inner_out)
        weigh(out_grads, 0, 1 - y, inner_out)
        y_out.start()
        weigh(out_grads, 1, y, inner_out)
        load = pltpu.make_async_copy(normed_in_ref, full, load_sem.at[0])
        load.start()
        attend_back_body(
            qkv_ref, mixed_ref, grad_mixed, lse_ref, prefix_ref[0:1, 0:1], cos_ref, sin_ref, grad_rows, dk_ref, dv_ref,
            heads, hd,
        )
        load.wait()

        def last(rows, total):
            value = back_rows(middle_ref[rows, :], own_in_ref[rows, :].astype(F32), total)
            result_ref[rows, :] = value.astype(BF)

        def before_z():
            flip(grad_rows, inner)
            weigh(qkv_grads, 0, 1 - y, inner)
            y_qkv.start()

        def after_z():
            y_out.wait_recv()
            add(out_grads.at[1], out_grads.at[2], inner_out)
            z_out.start()
            weigh(qkv_grads, 1, y, inner)

        reduce_body(
            place, product(place, grad_rows, quarters(qkv_1, qkv_2), True), last, reduce_refs,
            before_z=before_z, after_z=after_z, split=0,
        )
        result_spread = Spread(place, result_ref, result_out, result_sems)
        result_spread.start()
        y_qkv.wait_recv()
        add(qkv_grads.at[1], qkv_grads.at[2], inner)
        z_qkv.start()
        for move in (z_gate, z_up, z_out, z_qkv):
            move.wait_recv()
        ready_spread.wait()
        result_spread.wait()
        for move in (y_up, y_out, y_qkv, z_gate, z_up, z_out, z_qkv):
            move.wait_send()

    shape = jax.ShapeDtypeStruct
    spread = spread_shape(ready)
    return pl.pallas_call(
        kernel,
        out_shape=[
            shape(gate_sum.shape, BF), shape(up_own.shape, BF), shape((2, inner_out, block), BF),
            shape((2, inner, block), BF), spread, spread,
        ],
        in_specs=[VMEM_WHOLE] * 14 + [ANYWHERE, ANYWHERE, VMEM_WHOLE, ANYWHERE],
        out_specs=[ANYWHERE] * 6,
        scratch_shapes=[
            pltpu.VMEM((tokens, width), BF),
            pltpu.VMEM((tokens, inner_out), BF),
            pltpu.VMEM((tokens, inner), BF),
            pltpu.VMEM((inner, tokens), BF),
            pltpu.VMEM((tokens, hd), F32),
            pltpu.VMEM((tokens, hd), F32),
            pltpu.VMEM(up_own.shape, BF),
            pltpu.VMEM((3, 2, inner_out, block), BF),
            pltpu.VMEM((3, 2, inner, block), BF),
            DMA((3, 4)), DMA((4, 4)), DMA((1,)),
            *reduce_scratch(piece, width), *gather_scratch(), *spread_scratch(), *spread_scratch(),
        ],
        compiler_params=pltpu.CompilerParams(
            collective_id=ident, has_side_effects=True, vmem_limit_bytes=(64 << 20) - (64 << 10)
        ),
        cost_estimate=pl.CostEstimate(flops=100 << 30, bytes_accessed=100 << 20, transcendentals=heads * tokens * tokens),
        name="rear",
    )(
        branch_own, *out_halves, *qkv_halves, qkv, mixed, lse, prefix, *tables, grad_middle, own_in, ready, normed_in,
        gate_sum, up_own, up_other,
    )


def local_fine(inputs, prefix_len, w_qkv, w_out, w_up_gate, w_down, cotangent):
    heads, hd = w_qkv.shape[1], w_qkv.shape[2] // 3
    hidden_width = w_down.shape[0]
    tokens = inputs.shape[0]
    y = lax.axis_index("y")
    prefix_len = lax.ppermute(prefix_len, ("core", "zh"), [(0, 0), (1, 2), (2, 1), (3, 3)])
    prefix = jnp.broadcast_to(prefix_len[:, None], (8, 128))
    tables = rope_tables(tokens, hd)
    part = hidden_width // 2
    ga, gb = w_up_gate[:, 0, :part], w_up_gate[:, 0, part:]
    ua, ub = w_up_gate[:, 1, :part], w_up_gate[:, 1, part:]
    da, db = w_down[:part], w_down[part:]

    weights = (w_qkv.reshape(w_qkv.shape[0], -1), w_out, ga, gb, ua, ub, da, db)
    firsts, seconds, results = front_call(inputs, cotangent, prefix, tables, weights, heads, hd, 1)
    qkv_1, out_1, ga_1, gb_1, ua_1, ub_1, da_1, db_1 = firsts
    qkv_2, out_2, ga_2, gb_2, ua_2, ub_2, da_2 = seconds
    qkv, mixed, lse, own_in, middle, normed_in, cot_full, normed_mid, hidden, slopes = results
    gates = (ga_1, ga_2, gb_1, gb_2)

    (grad_middle, branch_own, grad_gate_up, gate_other, down_own, down_moved), (db_2,) = middle_call(
        cot_full, slopes, hidden, gates, (ua_1, ua_2, ub_1, ub_2), (da_1, da_2), db_1, normed_mid,
        [("beyond", db_1)], middle, 5,
    )
    outputs, down_final, gate_sum, up_own, up_other = down_call(
        hidden, (da_1, db_1), (da_2, db_2), middle, down_own, down_moved, normed_mid, grad_gate_up, gate_other, 6
    )
    gate_final, up_final, out_final, qkv_final, outputs, input_grad = rear_call(
        branch_own, (out_1, out_2), (qkv_1, qkv_2), qkv, mixed, lse, prefix, tables, grad_middle, own_in, outputs,
        normed_in, gate_sum, up_own, up_other, heads, hd, 7,
    )

    def summed(parts):
        return parts[0].astype(F32) + parts[1].astype(F32)

    return (
        outputs,
        input_grad.astype(F32),
        summed(qkv_final).T.reshape(-1, heads, 3 * hd),
        summed(out_final),
        jnp.stack([summed(gate_final), summed(up_final)], axis=1),
        summed(down_final),
    )


def solution(mesh):
    row_size, col_size = mesh.shape["row"], mesh.shape["col"]
    fine = (row_size, col_size) == (4, 8)
    if fine:
        names, shape, body = AXES, (2,) * 5, local_fine
        row, col = AXES[:2], AXES[2:]
    else:
        names = ("rmaj", "core", "cmaj", "cmin")
        shape = (row_size // 2, 2, 4, col_size // 4)
        body = functools.partial(local, shape[3] == 2)
        row, col = names[:2], names[2:]
    outs = (P(row, col), P(row, col), P(row, col, None), P(col, row), P(row, None, col), P(col, row))
    return jax.shard_map(
        body,
        mesh=Mesh(mesh.devices.reshape(shape), names),
        in_specs=(P(row, col), P(row), P(row, col, None), P(col, row), P(row, None, col), P(col, row), P(row, col)),
        out_specs=outs,
        check_vma=False,
    )
```

```python
import functools

import jax
import jax.numpy as jnp
from jax import lax
from jax.experimental import pallas as pl
from jax.experimental.pallas import tpu as pltpu
from jax.sharding import Mesh
from jax.sharding import PartitionSpec as P

EPSILON = 1e-05
NEG = -1e30
F32 = jnp.float32
BF = jnp.bfloat16
NN = (((1,), (0,)), ((), ()))
NT = (((1,), (1,)), ((), ()))
TN = (((0,), (0,)), ((), ()))
def dot(a, b, dims):
    return lax.dot_general(a, b, dims, preferred_element_type=F32)

def fwd_kernel(prefix_ref, q_ref, k_ref, v_ref, o_ref, lse_ref, *, bq, bk, scale):
    i = pl.program_id(1)
    first = i * bq
    prefix = prefix_ref[0]
    q = q_ref[...]
    limit = jnp.maximum(first + bq, prefix)
    total = (limit + bk - 1) // bk
    clear = jnp.maximum(first, prefix) // bk
    def step(masked, j, carry):
        top, tot, acc = carry
        rows = pl.ds(pl.multiple_of(j * bk, bk), bk)
        s = dot(q, k_ref[rows, :], NT) * scale
        if masked:
            kp = j * bk + lax.broadcasted_iota(jnp.int32, (bq, bk), 1)
            qp = first + lax.broadcasted_iota(jnp.int32, (bq, bk), 0)
            s = jnp.where(kp < jnp.maximum(qp + 1, prefix), s, NEG)
        new = jnp.maximum(top, jnp.max(s, axis=1, keepdims=True))
        alpha = jnp.exp(top - new)
        p = jnp.exp(s - new)
        tot = tot * alpha + jnp.sum(p, axis=1, keepdims=True)
        acc = acc * alpha + dot(p.astype(BF), v_ref[rows, :], NN)
        return new, tot, acc
    carry = (jnp.full((bq, 1), NEG, F32), jnp.zeros((bq, 1), F32), jnp.zeros((bq, q.shape[1]), F32))
    carry = lax.fori_loop(0, clear, functools.partial(step, False), carry)
    top, tot, acc = lax.fori_loop(clear, total, functools.partial(step, True), carry)
    o_ref[...] = (acc / tot).astype(o_ref.dtype)
    lse = jnp.broadcast_to(top + jnp.log(tot), (bq, 128))
    lse_ref[0] = lse.T[0:8, :]

def attend_fwd(qkv, prefix, heads, *, bq=512, bk=512, hd=128):
    seq = qkv.shape[0]
    return pl.pallas_call(
        functools.partial(fwd_kernel, bq=bq, bk=bk, scale=hd ** -0.5),
        grid_spec=pltpu.PrefetchScalarGridSpec(
            num_scalar_prefetch=1, grid=(heads, seq // bq),
            in_specs=[pl.BlockSpec((bq, hd), lambda h, i, p: (i, 3 * h)),
                      pl.BlockSpec((seq, hd), lambda h, i, p: (0, 3 * h + 1)),
                      pl.BlockSpec((seq, hd), lambda h, i, p: (0, 3 * h + 2))],
            out_specs=[pl.BlockSpec((bq, hd), lambda h, i, p: (i, h)),
                       pl.BlockSpec((1, 8, bq), lambda h, i, p: (h, 0, i))]),
        out_shape=[jax.ShapeDtypeStruct((seq, heads * hd), BF), jax.ShapeDtypeStruct((heads, 8, seq), F32)],
        cost_estimate=pl.CostEstimate(flops=4 * heads * seq * seq * hd, bytes_accessed=8 * heads * seq * hd, transcendentals=heads * seq * seq),
        name="attend_forward",
    )(prefix, qkv, qkv, qkv)

def bwd_kernel(prefix_ref, qkv_ref, o_ref, do_ref, lse_ref, cos_ref, sin_ref, out_ref, dk_ref, dv_ref, delta_ref, *, bq, bk, hd, scale):
    seq = qkv_ref.shape[0]
    prefix = prefix_ref[0]
    dk_ref[...] = jnp.zeros_like(dk_ref)
    dv_ref[...] = jnp.zeros_like(dv_ref)
    def deltas(i, _):
        rows = pl.ds(pl.multiple_of(i * bq, bq), bq)
        prod = (do_ref[rows, :].astype(F32) * o_ref[rows, :].astype(F32)).T
        delta_ref[:, rows] = jnp.broadcast_to(jnp.sum(prod, axis=0, keepdims=True), (8, bq))
        return 0
    lax.fori_loop(0, seq // bq, deltas, 0)
    def unrotate(g, rows):
        cos, sin = cos_ref[rows, :], sin_ref[rows, :]
        half = hd // 2
        a, b = g[:, :half], g[:, half:]
        return jnp.concatenate([a * cos + b * sin, b * cos - a * sin], axis=1)
    def q_step(i, _):
        first = i * bq
        qrows = pl.ds(pl.multiple_of(first, bq), bq)
        q = qkv_ref[qrows, 0:hd]
        do = do_ref[qrows, :]
        lse = lse_ref[0, 0:1, qrows]
        delta = delta_ref[0:1, qrows]
        limit = jnp.maximum(first + bq, prefix)
        total = (limit + bk - 1) // bk
        clear = jnp.maximum(first, prefix) // bk
        def step(masked, j, dq):
            krows = pl.ds(pl.multiple_of(j * bk, bk), bk)
            k = qkv_ref[krows, hd:2 * hd]
            v = qkv_ref[krows, 2 * hd:3 * hd]
            s = dot(k, q, NT) * scale
            p = jnp.exp(s - lse)
            if masked:
                kp = j * bk + lax.broadcasted_iota(jnp.int32, (bk, bq), 0)
                qp = first + lax.broadcasted_iota(jnp.int32, (bk, bq), 1)
                p = jnp.where(kp < jnp.maximum(qp + 1, prefix), p, 0.0)
            dp = dot(v, do, NT)
            dv_ref[krows, :] += dot(p.astype(BF), do, NN)
            ds = (p * (dp - delta)).astype(BF)
            dk_ref[krows, :] += dot(ds, q, NN)
            return dq + dot(ds, k, TN)
        dq = lax.fori_loop(0, clear, functools.partial(step, False), jnp.zeros((bq, hd), F32))
        dq = lax.fori_loop(clear, total, functools.partial(step, True), dq)
        out_ref[qrows, 0:hd] = unrotate(dq * scale, qrows).astype(BF)
        return 0
    lax.fori_loop(0, seq // bq, q_step, 0)
    def fin(i, _):
        rows = pl.ds(pl.multiple_of(i * bq, bq), bq)
        out_ref[rows, hd:2 * hd] = unrotate(dk_ref[rows, :] * scale, rows).astype(BF)
        out_ref[rows, 2 * hd:3 * hd] = dv_ref[rows, :].astype(BF)
        return 0
    lax.fori_loop(0, seq // bq, fin, 0)

def attend_bwd(qkv, mixed, dmixed, lse, prefix, cos, sin, heads, *, bq=512, bk=512, hd=128):
    seq = qkv.shape[0]
    return pl.pallas_call(
        functools.partial(bwd_kernel, bq=bq, bk=bk, hd=hd, scale=hd ** -0.5),
        grid_spec=pltpu.PrefetchScalarGridSpec(
            num_scalar_prefetch=1, grid=(heads,),
            in_specs=[pl.BlockSpec((seq, 3 * hd), lambda h, p: (0, h)),
                      pl.BlockSpec((seq, hd), lambda h, p: (0, h)),
                      pl.BlockSpec((seq, hd), lambda h, p: (0, h)),
                      pl.BlockSpec((1, 8, seq), lambda h, p: (h, 0, 0)),
                      pl.BlockSpec((seq, hd // 2), lambda h, p: (0, 0)),
                      pl.BlockSpec((seq, hd // 2), lambda h, p: (0, 0))],
            out_specs=[pl.BlockSpec((seq, 3 * hd), lambda h, p: (0, h))],
            scratch_shapes=[pltpu.VMEM((seq, hd), F32), pltpu.VMEM((seq, hd), F32), pltpu.VMEM((8, seq), F32)]),
        out_shape=[jax.ShapeDtypeStruct((seq, heads * 3 * hd), BF)],
        cost_estimate=pl.CostEstimate(flops=10 * heads * seq * seq * hd, bytes_accessed=20 * heads * seq * hd, transcendentals=heads * seq * seq),
        name="attend_backward",
    )(prefix, qkv, mixed, dmixed, lse, cos, sin)[0]


def rope_tables(count, head_dim):
    positions = jnp.arange(count, dtype=jnp.int32).astype(F32)
    frequency = 10000.0 ** (-(jnp.arange(head_dim // 2).astype(F32) * 2.0 / head_dim))
    angles = positions[:, None] * frequency[None, :]
    return jnp.cos(angles), jnp.sin(angles)


def rotate(values, cosine, sine):
    half = values.shape[-1] // 2
    a, b = values[..., :half], values[..., half:]
    return jnp.concatenate([a * cosine - b * sine, b * cosine + a * sine], axis=-1)


def norm(values):
    center = values - jnp.mean(values, axis=-1, keepdims=True)
    inv_std = lax.rsqrt(jnp.mean(center * center, axis=-1, keepdims=True) + EPSILON)
    return center * inv_std, inv_std


def norm_back(grad, normed, inv_std):
    mean_grad = jnp.mean(grad, axis=-1, keepdims=True)
    mean_cross = jnp.mean(grad * normed, axis=-1, keepdims=True)
    return inv_std * (grad - mean_grad - normed * mean_cross)


def mm(spec, left, right):
    return jnp.einsum(spec, left, right, preferred_element_type=F32)


def local(swap, inputs, prefix_len, w_qkv, w_out, w_up_gate, w_down, cotangent):
    rows = ("rmaj", "cmin") if swap else ("rmaj", "core")
    cols = ("cmaj", "core") if swap else ("cmaj", "cmin")

    def exchange(value):
        if not swap:
            return value
        return lax.ppermute(value, ("core", "cmin"), [(0, 0), (1, 2), (2, 1), (3, 3)])

    def scatter(value):
        return lax.psum_scatter(value.astype(BF), cols, scatter_dimension=0, tiled=True).astype(F32)

    def spread(value):
        return lax.all_to_all(value, cols, 1, 0, tiled=True)

    prefix_len = exchange(prefix_len)
    inputs, cotangent = exchange(inputs), exchange(cotangent)
    w_qkv, w_out = exchange(w_qkv), exchange(w_out)
    w_up_gate, w_down = exchange(w_up_gate), exchange(w_down)
    tokens = inputs.shape[0]
    heads, head_dim = w_qkv.shape[1], w_qkv.shape[2] // 3
    hidden_width = w_down.shape[0]
    full_in = lax.all_gather(inputs, cols, axis=1, tiled=True)
    width = full_in.shape[1]
    qkv_all = lax.all_gather(w_qkv, rows, axis=0, tiled=True).reshape(width, heads * 3 * head_dim)
    out_all = lax.all_gather(w_out, rows, axis=1, tiled=True)
    up_all = lax.all_gather(w_up_gate, rows, axis=0, tiled=True).reshape(width, 2 * hidden_width)
    down_all = lax.all_gather(w_down, rows, axis=1, tiled=True)
    cot_full = lax.all_gather(cotangent, cols, axis=1, tiled=True)
    piece = tokens // lax.axis_size(cols)
    first = lax.axis_index(cols) * piece
    own_in = lax.dynamic_slice_in_dim(full_in, first, piece, 0).astype(F32)
    own_cot = lax.dynamic_slice_in_dim(cot_full, first, piece, 0).astype(F32)

    normed_in = norm(full_in.astype(F32))[0].astype(BF)
    qkv_rows = mm("td,de->te", normed_in, qkv_all).reshape(tokens, heads, 3, head_dim)
    cosine, sine = rope_tables(tokens, head_dim)
    turned = rotate(qkv_rows[:, :, :2], cosine[:, None, None], sine[:, None, None])
    qkv = jnp.concatenate([turned, qkv_rows[:, :, 2:]], axis=2).astype(BF)
    qkv = qkv.reshape(tokens, heads * 3 * head_dim)
    mixed, lse = attend_fwd(qkv, prefix_len, heads, hd=head_dim)
    middle = own_in + scatter(mm("tc,cd->td", mixed, out_all))
    normed_two, inv_two = norm(middle)
    normed_mid = lax.all_gather(normed_two.astype(BF), cols, axis=0, tiled=True)
    gate_up = mm("td,df->tf", normed_mid, up_all)
    gate, up = gate_up[:, :hidden_width], gate_up[:, hidden_width:]
    sig = jax.nn.sigmoid(gate)
    active = gate * sig
    hidden = (active * up).astype(BF)
    outputs = middle + scatter(mm("tf,fd->td", hidden, down_all))
    outputs = exchange(spread(outputs.astype(BF)))

    grad_hidden = mm("td,fd->tf", cot_full, down_all)
    grad_gate = grad_hidden * up * sig * (1.0 + gate * (1.0 - sig))
    grad_gate_up = jnp.concatenate([grad_gate, grad_hidden * active], axis=1).astype(BF)
    grad_down = mm("tf,td->fd", hidden, cot_full).astype(BF)
    grad_down = lax.psum_scatter(grad_down, rows, scatter_dimension=1, tiled=True)
    grad_up = mm("td,tf->df", normed_mid, grad_gate_up).astype(BF)
    grad_up = lax.psum_scatter(grad_up, rows, scatter_dimension=0, tiled=True)
    grad_normed = scatter(mm("tf,df->td", grad_gate_up, up_all))
    grad_middle = own_cot + norm_back(grad_normed, normed_two, inv_two)
    grad_branch = lax.all_gather(grad_middle.astype(BF), cols, axis=0, tiled=True)
    grad_out = mm("tc,td->cd", mixed, grad_branch).astype(BF)
    grad_out = lax.psum_scatter(grad_out, rows, scatter_dimension=1, tiled=True)
    grad_mixed = mm("td,cd->tc", grad_branch, out_all).astype(BF)
    grad_rows = attend_bwd(qkv, mixed, grad_mixed, lse, prefix_len, cosine, sine, heads, hd=head_dim)
    grad_in = scatter(mm("te,de->td", grad_rows, qkv_all))
    grad_qkv = mm("td,te->de", normed_in, grad_rows).astype(BF)
    grad_qkv = lax.psum_scatter(grad_qkv, rows, scatter_dimension=0, tiled=True)
    normed_own, inv_own = norm(own_in)
    input_grad = grad_middle + norm_back(grad_in, normed_own, inv_own)
    input_grad = exchange(spread(input_grad.astype(BF))).astype(F32)
    return (
        outputs,
        input_grad,
        exchange(grad_qkv).astype(F32).reshape(-1, heads, 3 * head_dim),
        exchange(grad_out).astype(F32),
        exchange(grad_up).astype(F32).reshape(-1, 2, hidden_width),
        exchange(grad_down).astype(F32),
    )


AXES = ("y", "core", "zh", "zl", "x")
GROUP = ("core", "zl", "x")
MESH = pl.DeviceIdType.MESH
DMA = pltpu.SemaphoreType.DMA
VMEM_WHOLE = pl.BlockSpec(memory_space=pltpu.VMEM)
ANYWHERE = pl.BlockSpec(memory_space=pl.ANY)


class Place:
    def __init__(self):
        self.y, self.c, self.zh, self.zl, self.x = (lax.axis_index(name) for name in AXES)
        y, c, zh, zl, x = self.y, self.c, self.zh, self.zl, self.x
        self.sibling = (y, 1 - c, zh, zl, x)
        self.across = (y, c, zh, zl, 1 - x)
        self.along = (y, c, zh, 1 - zl, x)
        self.beyond = (1 - y, c, zh, zl, x)
        self.far = [(y, core, 1 - zh, zl, x) for core in (0, 1)]
        self.far_role = (y, zh, 1 - zh, zl, x)
        self.straight = c == zh
        self.outer = zl == zh
        self.order = [2 * y, 2 * y + 1, 2 * (1 - y), 2 * (1 - y) + 1]
        self.block = c * 4 + zl * 2 + x

    def chip(self, dz, dx):
        return lax.rem(self.zl + dz, 2) * 2 + lax.rem(self.x + dx, 2)

    def meet(self, greet=None):
        devices = [self.sibling, self.across, self.along, self.beyond, *self.far]
        barrier = pltpu.get_barrier_semaphore()
        for device in devices:
            pl.semaphore_signal(barrier, inc=1, device_id=device, device_id_type=MESH)
        more = greet(self, barrier) if greet else 0
        pl.semaphore_wait(barrier, len(devices) + more)


def span(start, size):
    return pl.ds(pl.multiple_of(start, size), size)


def remote(src, dst, send_sem, recv_sem, device):
    return pltpu.make_async_remote_copy(
        src_ref=src, dst_ref=dst, send_sem=send_sem, recv_sem=recv_sem, device_id=device, device_id_type=MESH
    )


class Beyond:
    along_z = False

    def __init__(self, place, src, dst, sem):
        self.copy = remote(src, dst, sem.at[0], sem.at[2], place.beyond)

    def start(self):
        self.copy.start()

    def wait_recv(self):
        self.copy.wait_recv()

    def wait_send(self):
        self.copy.wait_send()


class WeightHalf:
    along_z = True

    def __init__(self, place, src, dst, sem):
        c = place.c
        self.straight = place.straight
        self.outward = remote(src, dst.at[c], sem.at[0], sem.at[2 + c], place.far_role)
        self.aside = remote(src, dst.at[c], sem.at[1], sem.at[2 + c], place.sibling)
        self.here = pltpu.make_async_copy(src, dst.at[c], sem.at[1])
        self.from_sibling = remote(src, dst.at[1 - c], sem.at[1], sem.at[3 - c], place.sibling)
        self.from_far = [remote(src, dst.at[i], sem.at[0], sem.at[2 + i], place.far_role) for i in (0, 1)]

    def start(self):
        self.outward.start()

        @pl.when(self.straight)
        def _():
            self.here.start()

        @pl.when(jnp.logical_not(self.straight))
        def _():
            self.aside.start()

    def wait_recv(self):
        @pl.when(self.straight)
        def _():
            self.here.wait()
            self.from_sibling.wait_recv()

        @pl.when(jnp.logical_not(self.straight))
        def _():
            for copy in self.from_far:
                copy.wait_recv()

    def wait_send(self):
        self.outward.wait_send()

        @pl.when(jnp.logical_not(self.straight))
        def _():
            self.aside.wait_send()


class GradHalf:
    along_z = True

    def __init__(self, place, src, dst, sem):
        c, zh = place.c, place.zh
        self.straight = place.straight
        self.here = pltpu.make_async_copy(src.at[c], dst.at[zh], sem.at[0])
        self.aside = remote(src.at[1 - c], dst.at[zh], sem.at[1], sem.at[2 + zh], place.sibling)
        self.outward = [remote(src.at[i], dst.at[zh], sem.at[i], sem.at[2 + zh], place.far[i]) for i in (0, 1)]
        self.from_sibling = remote(src.at[c], dst.at[zh], sem.at[1], sem.at[2 + zh], place.sibling)
        self.from_far = remote(src.at[c], dst.at[1 - zh], sem.at[0], sem.at[3 - zh], place.far[0])

    def start(self):
        @pl.when(self.straight)
        def _():
            self.here.start()
            self.aside.start()

        @pl.when(jnp.logical_not(self.straight))
        def _():
            for copy in self.outward:
                copy.start()

    def wait_recv(self):
        self.from_far.wait_recv()

        @pl.when(self.straight)
        def _():
            self.here.wait()

        @pl.when(jnp.logical_not(self.straight))
        def _():
            self.from_sibling.wait_recv()

    def wait_send(self):
        @pl.when(self.straight)
        def _():
            self.aside.wait_send()

        @pl.when(jnp.logical_not(self.straight))
        def _():
            for copy in self.outward:
                copy.wait_send()


KINDS = {"beyond": Beyond, "weight": WeightHalf, "grad": GradHalf}


def moved_shape(kind, src):
    shape = (2, *src.shape) if kind == "weight" else src.shape
    return jax.ShapeDtypeStruct(shape, src.dtype)


class Under:
    def __init__(self, place, moves):
        self.place, self.moves = place, moves
        self.z = [move for kind, move in moves if move.along_z]
        self.y = [move for kind, move in moves if not move.along_z and not isinstance(kind, int)]
        self.follow = [(moves[kind][1], move) for kind, move in moves if isinstance(kind, int)]

    def start_y(self):
        for move in self.y:
            move.start()

    def start_z(self, outer=None):
        def start():
            for move in self.z:
                move.start()

        if outer is None:
            start()
        else:
            pl.when(self.place.outer if outer else jnp.logical_not(self.place.outer))(start)

    def start_follow(self):
        for ahead, move in self.follow:
            ahead.wait_recv()
            move.start()

    def end(self, skip=0):
        done = [ahead for ahead, _ in self.follow]
        for _, move in self.moves[skip:]:
            if move not in done:
                move.wait_recv()


def comm_call(
    body, name, ident, inputs, outs, scratch, moves=(), flops=0, transcendentals=0, spaces=None, greet=None
):
    n_in, n_out, n_move = len(inputs), len(outs), len(moves)
    own_source = [i for i, (kind, _) in enumerate(moves) if not isinstance(kind, int)]

    def kernel(*refs):
        ins, refs = refs[:n_in], refs[n_in:]
        sources, refs = refs[:len(own_source)], refs[len(own_source):]
        results, refs = refs[:n_out], refs[n_out:]
        targets, refs = refs[:n_move], refs[n_move:]
        sems, rest = refs[0], refs[1:]
        place = Place()
        place.meet(greet)
        made = []
        for i, (kind, _) in enumerate(moves):
            if isinstance(kind, int):
                made.append((kind, Beyond(place, targets[kind], targets[i], sems.at[i])))
            else:
                made.append((kind, KINDS[kind](place, sources[own_source.index(i)], targets[i], sems.at[i])))
        body(place, ins, results, rest, Under(place, made), targets)
        for _, move in made:
            move.wait_send()

    arrays = [*inputs, *(moves[i][1] for i in own_source)]
    shapes = list(outs)
    moved = []
    for kind, array in moves:
        moved.append(moved[kind] if isinstance(kind, int) else moved_shape(kind, array))
    shapes += moved
    in_specs = (spaces or [VMEM_WHOLE] * n_in) + [ANYWHERE] * len(own_source)
    size = sum(s.size * s.dtype.itemsize for s in (*arrays, *shapes))
    result = pl.pallas_call(
        kernel,
        out_shape=shapes,
        in_specs=in_specs,
        out_specs=[VMEM_WHOLE] * (n_out + n_move),
        scratch_shapes=[DMA((max(n_move, 1), 4)), *scratch],
        compiler_params=pltpu.CompilerParams(
            collective_id=ident, has_side_effects=True, vmem_limit_bytes=(64 << 20) - (64 << 10)
        ),
        cost_estimate=pl.CostEstimate(
            flops=flops + (20 << 30), bytes_accessed=size, transcendentals=transcendentals
        ),
        name=name,
    )(*arrays)
    return result[:n_out], result[n_out:]


def each_rows(count, body, size=32):
    def step(i, carry):
        body(span(i * size, size))
        return carry

    lax.fori_loop(0, count // size, step, 0)


def row_norm(values):
    center = values - jnp.mean(values, axis=-1, keepdims=True)
    inv_std = lax.rsqrt(jnp.mean(center * center, axis=-1, keepdims=True) + EPSILON)
    return center * inv_std, inv_std


SLICES = 4
NORM_ROWS = 64
NORM_UNROLL = 1


def reduce_sems():
    return [DMA((4,)), DMA((4,)), DMA((3, SLICES)), DMA((3, SLICES))]


def reduce_scratch(piece, width):
    return [pltpu.VMEM((count, piece, width), BF) for count in (4, 4, 2, 3, 3)] + reduce_sems()


def nothing():
    pass


def reduce_body(place, compute, last, scratch, begin=nothing, before_z=nothing, after_z=nothing, split=0):
    sib_out, sib_in, own, near_out, near_in, sib_send, sib_recv, near_send, near_recv = scratch
    piece = own.shape[1]
    c = place.c
    size = piece // SLICES
    begin()

    def sib_copy(step):
        return remote(sib_out.at[step], sib_in.at[step], sib_send.at[step], sib_recv.at[step], place.sibling)

    def near_copy(step, r, turned=False):
        device = place.along if step == 2 or turned else place.across
        rows = span(r * size, size)
        return remote(
            near_out.at[step, rows], near_in.at[step, rows], near_send.at[step, r], near_recv.at[step, r], device
        )

    def finish(step):
        slot = step % 2
        sib_copy(step).wait_recv()

        def send(joins, turned, r, carry):
            if joins:
                near_copy(0, r).wait_recv()
            rows = span(r * size, size)
            total = own[slot, rows, :].astype(F32) + sib_in[step, rows, :].astype(F32)
            if joins:
                total = total + near_in[0, rows, :].astype(F32)
            near_out[step, rows, :] = total.astype(BF)
            near_copy(step, r, turned).start()
            return carry

        lax.fori_loop(0, SLICES - split, functools.partial(send, step == 2, False), 0)
        if split:
            lax.fori_loop(SLICES - split, SLICES, functools.partial(send, step == 1, step == 0), 0)

    def step(s, carry):
        target = place.chip(1 - lax.rem(s, 2), 1 - s // 2)
        compute((1 - c) * 4 + target, sib_out.at[s])
        sib_copy(s).start()
        for index in (0, 1):
            @pl.when(s == index + 1)
            def _(index=index):
                finish(index)

        compute(c * 4 + target, own.at[lax.rem(s, 2)])
        return carry

    lax.fori_loop(0, 4, step, 0)
    before_z()
    finish(2)
    after_z()
    sib_copy(3).wait_recv()

    def arrive(r, carry):
        near_copy(1, r).wait_recv()
        near_copy(2, r).wait_recv()

        def final(i, carry):
            rows = span(r * size + i * 16, 16)
            total = own[1, rows, :].astype(F32) + sib_in[3, rows, :].astype(F32)
            last(rows, total + near_in[1, rows, :].astype(F32) + near_in[2, rows, :].astype(F32))
            return carry

        return lax.fori_loop(0, size // 16, final, carry)

    lax.fori_loop(0, SLICES, arrive, 0)
    for s in range(4):
        sib_copy(s).wait_send()

    def sent(r, carry):
        for s in range(3):
            near_copy(s, r).wait_send()
        return carry

    lax.fori_loop(0, SLICES, sent, 0)


def product(place, left_ref, weights, transposed):
    def compute(owner, out_ref):
        piece = out_ref.shape[0]
        left = left_ref[span(owner * piece, piece), :]
        for weight, index in zip(weights, place.order):
            size = weight.shape[0] if transposed else weight.shape[1]
            part = dot(left, weight[...], NT if transposed else NN)
            out_ref[:, span(index * size, size)] = part.astype(out_ref.dtype)

    return compute


def back_rows(base, value, total):
    normed, inv_std = row_norm(value)
    mean_grad = jnp.mean(total, axis=-1, keepdims=True)
    mean_cross = jnp.mean(total * normed, axis=-1, keepdims=True)
    return base + inv_std * (total - mean_grad - normed * mean_cross)


def quarters(first, second):
    return [first.at[0], first.at[1], second.at[0], second.at[1]]


def both_halves(cos_ref, sin_ref, rows):
    cos, sin = cos_ref[rows, :], sin_ref[rows, :]
    return jnp.concatenate([cos, cos], axis=1), jnp.concatenate([-sin, sin], axis=1)


def beside(under):
    def begin():
        under.start_y()
        under.start_z()

    return dict(begin=begin, after_z=under.start_follow)


class Turned:
    def __init__(self, source, stage, sems, flipped):
        self.source, self.stage, self.sems, self.flipped = source, stage, sems, flipped
        self.tile, self.strip = 256, stage.shape[1]
        self.count = flipped.shape[1] // self.strip

    def load(self, i):
        slot = lax.rem(i, 2)
        rows = span(i * self.strip, self.strip)
        return pltpu.make_async_copy(self.source.at[rows], self.stage.at[slot], self.sems.at[slot])

    def turn(self):
        def step(i, carry):
            self.load(i).wait()

            @pl.when(i + 1 < self.count)
            def _():
                self.load(i + 1).start()

            self.flipped[:, span(i * self.strip, self.strip)] = self.stage[lax.rem(i, 2)].T
            return carry

        self.load(0).start()
        lax.fori_loop(0, self.count, step, 0)

    def times(self, right, out, first, offset):
        block, columns = out.shape[1:]
        half = columns // 2
        each = block // self.tile

        def step(n, carry):
            m, t = n // 2, lax.rem(n, 2)
            left = self.flipped[span(first + m * self.tile, self.tile), :]
            value = dot(left, right[:, span(offset + t * half, half)], NN)
            out[m // each, span(lax.rem(m, each) * self.tile, self.tile), span(t * half, half)] = value.astype(BF)
            return carry

        lax.fori_loop(0, 4 * each, step, 0)


def down_call(hidden, firsts, seconds, middle, own, moved, normed, grads, gate_other, ident):
    piece, width = middle.shape
    tokens, both = grads.shape
    part_width = both // 2
    block = width // 4
    tile = 256

    def kernel(
        hidden_ref, first_a, first_b, second_a, second_b, base_ref, own_ref, moved_ref, grads_ref, normed_ref, gate_other,
        result_ref, down_out, gate_out, up_own_out, up_other_out,
        down_sum, stage, flipped, gate_moved, kept, spare,
        y_sems, z_sems, load_sems, store_sems, *reduce_refs
    ):
        place = Place()
        place.meet()
        y = place.y

        turned = Turned(normed_ref, stage, load_sems, flipped)
        for j in (0, 1):
            cols = pl.ds(j * block, block)

            def step(i, carry, j=j, cols=cols):
                upper, rows = i // (own_ref.shape[1] // 64), span(lax.rem(i, own_ref.shape[1] // 64) * 64, 64)
                total = own_ref[upper, rows, cols].astype(F32) + moved_ref[upper, rows, cols].astype(F32)
                down_sum[j, span(i * 64, 64), :] = total.astype(BF)
                return carry

            lax.fori_loop(0, down_sum.shape[1] // 64, step, 0)
        z_down = GradHalf(place, down_sum, down_out, z_sems.at[0])
        y_gate = Beyond(place, gate_other, gate_moved, y_sems.at[0])
        y_gate.start()
        parts = list(zip(quarters(first_a, second_a), quarters(first_b, second_b), place.order))

        def compute(owner, out_ref):
            rows = span(owner * piece, piece)
            for upper, lower, index in parts:
                depth, size = upper.shape
                part = dot(hidden_ref[rows, 0:depth], upper[...], NN) + dot(hidden_ref[rows, depth:], lower[...], NN)
                out_ref[:, span(index * size, size)] = part.astype(out_ref.dtype)

        def last(rows, total):
            result_ref[rows, :] = (base_ref[rows, :] + total).astype(BF)

        def store(out, ref, i):
            return pltpu.make_async_copy(ref, out, store_sems.at[i])

        def after_z():
            turned.turn()
            turned.times(grads_ref, spare, (1 - y) * (width // 2), part_width)
            store(up_other_out, spare, 0).start()
            turned.times(grads_ref, kept, y * (width // 2), 0)
            store(up_other_out, spare, 0).wait()
            turned.times(grads_ref, spare, y * (width // 2), part_width)
            store(up_own_out, spare, 1).start()

        reduce_body(place, compute, last, reduce_refs, begin=z_down.start, after_z=after_z)
        y_gate.wait_recv()
        for i in (0, 1):
            def add(n, carry, i=i):
                rows = span(n * 64, 64)
                kept[i, rows, :] = (kept[i, rows, :].astype(F32) + gate_moved[i, rows, :].astype(F32)).astype(BF)
                return carry

            lax.fori_loop(0, block // 64, add, 0)
        store(gate_out, kept, 2).start()
        z_down.wait_recv()
        store(up_own_out, spare, 1).wait()
        store(gate_out, kept, 2).wait()
        for move in (z_down, y_gate):
            move.wait_send()

    shape = jax.ShapeDtypeStruct
    half = shape((2, block, part_width), BF)
    down_shape = (2, hidden.shape[1], block)
    held = pltpu.VMEM(half.shape, BF)
    return pl.pallas_call(
        kernel,
        out_shape=[shape((piece, width), BF), shape(down_shape, BF), half, half, half],
        in_specs=[VMEM_WHOLE] * 9 + [ANYWHERE] * 2,
        out_specs=[VMEM_WHOLE] + [ANYWHERE] * 4,
        scratch_shapes=[
            pltpu.VMEM(down_shape, BF),
            pltpu.VMEM((2, tile, width), BF),
            pltpu.VMEM((width, tokens), BF),
            held, held, held,
            DMA((1, 4)), DMA((1, 4)), DMA((2,)), DMA((3,)), *reduce_scratch(piece, width),
        ],
        compiler_params=pltpu.CompilerParams(collective_id=ident, has_side_effects=True, vmem_limit_bytes=63 << 20),
        cost_estimate=pl.CostEstimate(flops=60 << 30, bytes_accessed=60 << 20, transcendentals=0),
        name="reduce_down",
    )(hidden, *firsts, *seconds, middle, own, moved, grads, normed, gate_other)


def middle_call(cot, slopes, hidden_rows, gates, ups, downs, down_last, normed, moves, middle, ident):
    piece, width = middle.shape
    tokens, part_width = cot.shape[0], down_last.shape[1]
    hidden = 2 * part_width
    tile = 256
    tiles = part_width // tile

    def body(place, ins, outs, scratch, under, targets):
        cot_hbm, slopes_ref, normed_ref, hidden_ref, ga1, ga2, gb1, gb2, ua1, ua2, ub1, ub2, value_ref, da1, da2, db1 = ins
        total_ref, branch_ref, grad_ref, gate_other, down_own, down_moved = outs
        load_sem, cot_ref, stage, down_other, y_sem, turned_hidden, *rest = scratch
        strip = stage.shape[1]
        under.start_y()
        loads = [
            pltpu.make_async_copy(slopes_ref, grad_ref, load_sem.at[0]),
            pltpu.make_async_copy(cot_hbm, cot_ref, load_sem.at[1]),
        ]
        for load in loads:
            load.start()
        for load in loads:
            load.wait()
        base_ref = stage.at[0]

        def hidden_load(i):
            slot = lax.rem(i, 2)
            return pltpu.make_async_copy(
                hidden_ref.at[span(i * strip, strip)], stage.at[slot, :, pl.ds(0, hidden)], load_sem.at[slot]
            )

        def turn(i, carry):
            hidden_load(i).wait()

            @pl.when(i + 1 < tokens // strip)
            def _():
                hidden_load(i + 1).start()

            value = stage[lax.rem(i, 2), :, 0:hidden].T
            for j in range(hidden // tile):
                turned_hidden[j, :, span(i * strip, strip)] = value[j * tile:(j + 1) * tile]
            return carry

        def down_half(out, which):
            half = width // 4
            each = hidden // 2 // tile

            def step(n, carry):
                m, t = n // 2, lax.rem(n, 2)
                value = dot(turned_hidden[m], cot_ref[:, span(which * 2 * half + t * half, half)], NN)
                out[m // each, span(lax.rem(m, each) * tile, tile), span(t * half, half)] = value.astype(BF)
                return carry

            lax.fori_loop(0, 2 * (hidden // tile), step, 0)

        hidden_load(0).start()
        lax.fori_loop(0, tokens // strip, turn, 0)
        down_half(down_other, 1 - place.y)
        y_down = Beyond(place, down_other, down_moved, y_sem)
        y_down.start()
        rows_in = (quarters(da1, da2), quarters(db1, targets[0]))

        def fill(owner, part):
            rows = span(owner * piece, piece)

            def step(t, carry):
                grad = None
                for weight, index in zip(rows_in[part], place.order):
                    size = weight.shape[1]
                    term = dot(cot_ref[rows, span(index * size, size)], weight[span(t * tile, tile), :], NT)
                    grad = term if grad is None else grad + term
                for offset in (0, hidden):
                    cols = span(offset + part * part_width + t * tile, tile)
                    grad_ref[rows, cols] = (grad * grad_ref[rows, cols].astype(F32)).astype(BF)
                return carry

            lax.fori_loop(0, tiles, step, 0)

        def fill_first(i, carry):
            fill(i, 0)
            return carry

        lax.fori_loop(0, tokens // piece, fill_first, 0)
        under.moves[0][1].wait_recv()
        columns = [quarters(ga1, ga2), quarters(gb1, gb2), quarters(ua1, ua2), quarters(ub1, ub2)]

        def compute(owner, out_ref):
            rows = span(owner * piece, piece)
            fill(owner, 1)
            for quarter, index in enumerate(place.order):
                total = None
                for i, weights in enumerate(columns):
                    weight = weights[quarter]
                    size = weight.shape[0]
                    term = dot(grad_ref[rows, i * part_width:(i + 1) * part_width], weight[...], NT)
                    total = term if total is None else total + term
                out_ref[:, span(index * size, size)] = total.astype(out_ref.dtype)

        def last(rows, total):
            base = base_ref[rows, :].astype(F32)
            grad = back_rows(base, value_ref[rows, :], total)
            total_ref[rows, :] = grad
            branch_ref[rows, :] = grad.astype(BF)

        turned = Turned(normed_ref, stage, load_sem, cot_ref)

        def after_z():
            down_half(down_own, place.y)
            turned.turn()
            base_load = pltpu.make_async_copy(cot_hbm.at[span(place.block * piece, piece)], base_ref, load_sem.at[0])
            base_load.start()
            turned.times(grad_ref, gate_other, (1 - place.y) * (width // 2), 0)
            base_load.wait()

        reduce_body(place, compute, last, rest, after_z=after_z, split=2)
        under.end(skip=1)
        y_down.wait_recv()
        y_down.wait_send()

    shape = functools.partial(jax.ShapeDtypeStruct, (piece, width))
    down_half_shape = jax.ShapeDtypeStruct((2, hidden // 2, width // 2), BF)
    return comm_call(
        body, "reduce_middle", ident, [cot, slopes, normed, hidden_rows, *gates, *ups, middle, *downs, down_last],
        [
            shape(F32), shape(BF), jax.ShapeDtypeStruct((tokens, 2 * hidden), BF),
            jax.ShapeDtypeStruct((2, width // 4, hidden), BF),
            down_half_shape,
            down_half_shape,
        ],
        [
            DMA((2,)), pltpu.VMEM((tokens, width), BF), pltpu.VMEM((2, piece, width), BF),
            pltpu.VMEM(down_half_shape.shape, BF), DMA((4,)),
            pltpu.VMEM((hidden // tile, tile, tokens), BF), *reduce_scratch(piece, width),
        ],
        moves, flops=6 * tokens * hidden * width,
        spaces=[ANYWHERE] * 4 + [VMEM_WHOLE] * 12,
    )


def gather_scratch():
    return [DMA((3, SLICES)), DMA((3, SLICES)), DMA((4,)), DMA((4,))]


def gather_body(place, own_ref, full, sems, process, begin=nothing, follow=nothing, split=0):
    near_send, near_recv, sib_send, sib_recv = sems
    piece = own_ref.shape[0]
    size = piece // SLICES
    c = place.c

    def near_copy(slot, r, target, turned=False):
        where = full.at[span((c * 4 + target) * piece + r * size, size)]
        device = place.along if slot == 2 or turned else place.across
        return remote(where, where, near_send.at[slot, r], near_recv.at[slot, r], device)

    def sib_copy(slot, core, target):
        where = full.at[span((core * 4 + target) * piece, piece)]
        return remote(where, where, sib_send.at[slot], sib_recv.at[slot], place.sibling)

    def slices(act):
        def step(r, carry):
            act(r)
            return carry

        lax.fori_loop(0, SLICES, step, 0)

    mine, x_chip, z_chip, d_chip = place.chip(0, 0), place.chip(0, 1), place.chip(1, 0), place.chip(1, 1)
    full[span((c * 4 + mine) * piece, piece), :] = own_ref[...]
    slices(lambda r: near_copy(2, r, mine).start())
    slices(lambda r: near_copy(1, r, mine).start())
    sib_copy(3, c, mine).start()
    begin()

    def forward(r):
        near_copy(2, r, z_chip).wait_recv()
        if r < SLICES - split:
            near_copy(0, r, z_chip).start()

    process(c * 4 + mine)
    forward(0)
    sib_copy(3, 1 - c, mine).wait_recv()
    process((1 - c) * 4 + mine)
    forward(1)

    def arrived(r):
        near_copy(1, r, x_chip).wait_recv()

    for r in range(SLICES):
        arrived(r)
        if r >= SLICES - split:
            near_copy(0, r, x_chip, True).start()
    sib_copy(1, c, x_chip).start()
    process(c * 4 + x_chip)
    for r in range(2, SLICES):
        forward(r)
    sib_copy(2, c, z_chip).start()
    sib_copy(1, 1 - c, x_chip).wait_recv()
    process((1 - c) * 4 + x_chip)
    process(c * 4 + z_chip)
    follow()
    sib_copy(2, 1 - c, z_chip).wait_recv()
    process((1 - c) * 4 + z_chip)
    slices(lambda r: near_copy(0, r, d_chip).wait_recv())
    sib_copy(0, c, d_chip).start()
    process(c * 4 + d_chip)
    sib_copy(0, 1 - c, d_chip).wait_recv()
    process((1 - c) * 4 + d_chip)
    for slot in range(3):
        slices(lambda r: near_copy(slot, r, mine).wait_send())
    for slot in range(4):
        sib_copy(slot, c, mine).wait_send()


class ColumnGather:
    def __init__(self, place, src, full, sems):
        self.place, self.src, self.full = place, src, full
        self.near_send, self.near_recv, self.sib_send, self.sib_recv, self.own = sems
        self.width = src.shape[1]
        self.size = src.shape[0] // SLICES

    def where(self, core, target):
        return span((core * 4 + target) * self.width, self.width)

    def near(self, slot, r, target, first=False):
        place = self.place
        rows = pl.ds(r * self.size, self.size)
        dst = self.full.at[rows, self.where(place.c, target)]
        src = self.src.at[rows] if first else dst
        device = place.along if slot == 2 else place.across
        return remote(src, dst, self.near_send.at[slot, r], self.near_recv.at[slot, r], device)

    def sib(self, slot, core, target, first=False):
        dst = self.full.at[:, self.where(core, target)]
        src = self.src if first else dst
        return remote(src, dst, self.sib_send.at[slot], self.sib_recv.at[slot], self.place.sibling)

    def chips(self):
        place = self.place
        return place.chip(0, 0), place.chip(0, 1), place.chip(1, 0), place.chip(1, 1)

    def own_copy(self):
        return pltpu.make_async_copy(self.src, self.full.at[:, self.where(self.place.c, self.chips()[0])], self.own.at[0])

    def start(self):
        mine = self.chips()[0]
        self.own_copy().start()
        for slot in (2, 1):
            for r in range(SLICES):
                self.near(slot, r, mine, True).start()
        self.sib(3, self.place.c, mine, True).start()

    def forward(self, r):
        z_chip = self.chips()[2]
        self.near(2, r, z_chip).wait_recv()
        self.near(0, r, z_chip).start()

    def finish(self):
        mine, x_chip, z_chip, d_chip = self.chips()
        c = self.place.c
        self.sib(2, c, z_chip).start()
        for r in range(SLICES):
            self.near(1, r, x_chip).wait_recv()
        self.sib(1, c, x_chip).start()
        for r in range(SLICES):
            self.near(0, r, d_chip).wait_recv()
        self.sib(0, c, d_chip).start()
        self.own_copy().wait()
        for slot, target in enumerate((d_chip, x_chip, z_chip, mine)):
            self.sib(slot, 1 - c, target).wait_recv()
            self.sib(slot, c, mine).wait_send()
        for slot in range(3):
            for r in range(SLICES):
                self.near(slot, r, mine).wait_send()


def attend_back_body(qkv_ref, o_ref, do_ref, lse_ref, bound, cos_ref, sin_ref, out_ref, dk_ref, dv_ref, heads, hd):
    seq = qkv_ref.shape[0]
    bq = bk = min(512, seq // 2)
    scale = hd ** -0.5
    half = hd // 2

    def unrotate(g, rows):
        cos, sin = both_halves(cos_ref, sin_ref, rows)
        return g * cos - pltpu.roll(g, half, 1) * sin

    def head(h, carry):
        base = h * 3 * hd
        own = span(h * hd, hd)
        dk_ref[...] = jnp.zeros_like(dk_ref)
        dv_ref[...] = jnp.zeros_like(dv_ref)
        for i in range(seq // bq):
            first = i * bq
            rows = pl.ds(first, bq)
            q = qkv_ref[rows, span(base, hd)]
            do = do_ref[rows, own]
            row_sums = (do.astype(F32) * o_ref[rows, own].astype(F32)).T
            delta = jnp.sum(row_sums, axis=0, keepdims=True)
            tops = lse_ref[h, 0:1, first:first + bq]
            total = max(i + 1, seq // 2 // bk)

            def step(masked, j, dq, first=first, q=q, do=do, delta=delta, tops=tops):
                keys = span(j * bk, bk)
                k = qkv_ref[keys, span(base + hd, hd)]
                v = qkv_ref[keys, span(base + 2 * hd, hd)]
                p = jnp.exp(dot(k, q, NT) * scale - tops)
                if masked:
                    kp = j * bk + lax.broadcasted_iota(jnp.int32, (bk, bq), 0)
                    qp = first + lax.broadcasted_iota(jnp.int32, (bk, bq), 1)
                    p = jnp.where(kp < jnp.maximum(qp + 1, bound), p, 0.0)
                dv_ref[keys, :] += dot(p.astype(BF), do, NN)
                ds = (p * (dot(v, do, NT) - delta)).astype(BF)
                dk_ref[keys, :] += dot(ds, q, NN)
                return dq + dot(ds, k, TN)

            dq = lax.fori_loop(0, i, functools.partial(step, False), jnp.zeros((bq, hd), F32))
            dq = lax.fori_loop(i, total, functools.partial(step, True), dq)
            out_ref[rows, span(base, hd)] = unrotate(dq * scale, rows).astype(BF)

        def fin(i, carry):
            rows = span(i * bq, bq)
            out_ref[rows, span(base + hd, hd)] = unrotate(dk_ref[rows, :] * scale, rows).astype(BF)
            out_ref[rows, span(base + 2 * hd, hd)] = dv_ref[rows, :].astype(BF)
            return carry

        return lax.fori_loop(0, seq // bq, fin, carry)

    lax.fori_loop(0, heads, head, 0)


def front_call(inputs, cot, prefix, tables, weights, heads, hd, ident):
    names = ("qkv", "out", "ga", "gb", "ua", "ub", "da", "db")
    tokens, slice_width = inputs.shape
    width = slice_width * 8
    piece = tokens // 8
    size = tokens // SLICES
    inner = weights[0].shape[1]
    part_width = weights[2].shape[1]
    hidden = 2 * part_width
    tile = 256
    bq = bk = min(512, tokens // 2)
    scale = hd ** -0.5

    def kernel(in_ref, cot_ref, prefix_ref, cos_ref, sin_ref, *refs):
        sources, refs = refs[:8], refs[8:]
        firsts, seconds, refs = refs[:8], refs[8:15], refs[15:]
        (qkv_ref, mixed_ref, lse_ref, own_in_ref, middle_ref, normed_in_out, cot_out, normed_mid_out, hidden_out,
         slopes_out), refs = refs[:10], refs[10:]
        arena, acc, block_ref, normed_own, *refs = refs
        held, refs = dict(zip(names, refs[:8])), refs[8:]
        z_sems, y_sems, store_sems, out_sems, swap_send, swap_recv, phase, *sems = refs
        start_sems, gather_sems, reduce_sems_, feed_sems = sems[:5], sems[5:10], sems[10:14], sems[14:]
        place = Place()
        c, zl, x = place.c, place.zl, place.x
        place.meet()
        z_moves = {n: WeightHalf(place, sources[i], held[n].at[0], z_sems.at[i]) for i, n in enumerate(names)}
        y_moves = {n: Beyond(place, held[n].at[0], held[n].at[1], y_sems.at[i]) for i, n in enumerate(names[:7])}

        def go(name):
            z_moves[name].start()

        def stores(name):
            i = names.index(name)
            return [
                pltpu.make_async_copy(held[name].at[side], out[i], store_sems.at[i, side])
                for side, out in enumerate((firsts, seconds[:7]))
                if i < len(out)
            ]

        def pass_on(name):
            z_moves[name].wait_recv()
            y_moves[name].start()

        def got(name):
            y_moves[name].wait_recv()
            for copy in stores(name):
                copy.start()

        def parts(name):
            return [held[name].at[side, i] for side in (0, 1) for i in (0, 1)]

        full, normed = arena.at[pl.ds(0, tokens)], arena.at[pl.ds(tokens, tokens)]
        gather = ColumnGather(place, in_ref, full, start_sems)
        crossed = jnp.logical_not(place.straight)
        partner = (place.y, 1 - c, 1 - place.zh, zl, x)
        mine, x_chip, z_chip, d_chip = gather.chips()
        def rows_of(r):
            return pl.ds(r * size, size)

        def swap_copy(r, core):
            where = full.at[rows_of(r), gather.where(core, mine)]
            return remote(in_ref.at[rows_of(r)], where, swap_send.at[r], swap_recv.at[r], partner)

        def own_copy(r):
            where = full.at[rows_of(r), gather.where(c, mine)]
            return pltpu.make_async_copy(in_ref.at[rows_of(r)], where, swap_send.at[r])

        def cot_swap():
            return remote(cot_ref, block_ref, swap_send.at[SLICES], swap_recv.at[SLICES], partner)

        def cot_own():
            return pltpu.make_async_copy(cot_ref, block_ref, swap_send.at[SLICES])

        def sib(slot, r, core, target):
            where = full.at[rows_of(r), gather.where(core, target)]
            return remote(where, where, start_sems[2].at[slot, r], start_sems[3].at[slot, r], place.sibling)

        @pl.when(place.straight)
        def _():
            for r in range(SLICES):
                own_copy(r).start()
            cot_own().start()

        @pl.when(crossed)
        def _():
            for r in range(SLICES):
                swap_copy(r, 1 - c).start()

        for r in range(SLICES):
            @pl.when(place.straight)
            def _(r=r):
                own_copy(r).wait()

            @pl.when(crossed)
            def _(r=r):
                swap_copy(r, c).wait_recv()

            gather.near(2, r, mine).start()
            gather.near(1, r, mine).start()
            sib(3, r, c, mine).start()
        for r in range(SLICES):
            gather.forward(r)
            sib(2, r, c, z_chip).start()
            gather.near(1, r, x_chip).wait_recv()
            sib(1, r, c, x_chip).start()
            if r == 0:
                go("qkv")
        pass_on("qkv")
        go("out")
        pl.when(crossed)(lambda: cot_swap().start())
        depth = held["qkv"].shape[2]
        for r in range(SLICES):
            gather.near(0, r, d_chip).wait_recv()
            sib(0, r, c, d_chip).start()
            for slot, target in enumerate((d_chip, x_chip, z_chip, mine)):
                sib(slot, r, 1 - c, target).wait_recv()

            def norm_rows(i, carry, r=r):
                rows = span(r * size + i * NORM_ROWS, NORM_ROWS)
                normed[rows, :] = row_norm(full[rows, :].astype(F32))[0].astype(BF)
                return carry

            lax.fori_loop(0, size // NORM_ROWS, norm_rows, 0, unroll=NORM_UNROLL)
            pltpu.make_async_copy(normed.at[rows_of(r)], normed_in_out.at[rows_of(r)], out_sems.at[r]).start()
            total = None
            for weight, index in zip(parts("qkv")[:2], place.order[:2]):
                term = dot(normed[rows_of(r), span(index * depth, depth)], weight[...], NN)
                total = term if total is None else total + term
            acc[rows_of(r), :] = total
        own_in_ref[...] = full[span(place.block * piece, piece), :]
        pass_on("out")

        cot_gather = ColumnGather(place, block_ref, cot_out, gather_sems)

        def forward_cot():
            for r in range(SLICES):
                cot_gather.forward(r)

        @pl.when(place.straight)
        def _():
            cot_own().wait()
            cot_gather.start()
            go("ga")

        got("qkv")
        half = size // 2

        def project(r, carry):
            rows = span(r * half, half)
            total = acc[rows, :]
            for weight, index in zip(parts("qkv")[2:], place.order[2:]):
                total = total + dot(normed[rows, span(index * depth, depth)], weight[...], NN)
            cos, sin = both_halves(cos_ref, sin_ref, rows)
            for h in range(heads):
                for part in range(3):
                    value = total[:, (3 * h + part) * hd:(3 * h + part + 1) * hd]
                    if part < 2:
                        value = value * cos + pltpu.roll(value, hd // 2, 1) * sin
                    qkv_ref[rows, pl.ds((3 * h + part) * hd, hd)] = value.astype(BF)
            return carry

        lax.fori_loop(0, tokens // half, project, 0)
        @pl.when(crossed)
        def _():
            cot_swap().wait_recv()
            cot_gather.start()
            go("ga")
            cot_swap().wait_send()
            for r in range(SLICES):
                swap_copy(r, 1 - c).wait_send()

        pl.when(place.straight)(forward_cot)

        bound = prefix_ref[0:1, 0:1]

        def head(h, carry):
            base = h * 3 * hd
            for i in range(tokens // bq):
                first = i * bq
                q = qkv_ref[first:first + bq, span(base, hd)]
                count = max(i + 1, tokens // 2 // bk)

                def step(masked, j, state, first=first, q=q):
                    top, tot, out = state
                    rows = span(j * bk, bk)
                    s = dot(q, qkv_ref[rows, span(base + hd, hd)], NT) * scale
                    if masked:
                        kp = j * bk + lax.broadcasted_iota(jnp.int32, (bq, bk), 1)
                        qp = first + lax.broadcasted_iota(jnp.int32, (bq, bk), 0)
                        s = jnp.where(kp < jnp.maximum(qp + 1, bound), s, NEG)
                    new = jnp.maximum(top, jnp.max(s, axis=1, keepdims=True))
                    alpha = jnp.exp(top - new)
                    p = jnp.exp(s - new)
                    tot = tot * alpha + jnp.sum(p, axis=1, keepdims=True)
                    out = out * alpha + dot(p.astype(BF), qkv_ref[rows, span(base + 2 * hd, hd)], NN)
                    return new, tot, out

                state = (jnp.full((bq, 1), NEG, F32), jnp.zeros((bq, 1), F32), jnp.zeros((bq, hd), F32))
                state = lax.fori_loop(0, i, functools.partial(step, False), state)
                top, tot, out = lax.fori_loop(i, count, functools.partial(step, True), state)
                mixed_ref[first:first + bq, span(h * hd, hd)] = (out / tot).astype(BF)
                lse = jnp.broadcast_to(top + jnp.log(tot), (bq, 128))
                lse_ref[h, :, first:first + bq] = lse.T[0:8, :]
            return carry

        lax.fori_loop(0, heads, head, 0)
        go("gb")
        got("out")
        pl.when(crossed)(forward_cot)
        pass_on("ga")

        for r in range(SLICES):
            pltpu.make_async_copy(normed.at[rows_of(r)], normed_in_out.at[rows_of(r)], out_sems.at[r]).wait()
            for slot in range(3):
                gather.near(slot, r, mine).wait_send()
            for slot in range(4):
                sib(slot, r, c, mine).wait_send()
        for device in (place.sibling, place.across, place.along):
            pl.semaphore_signal(phase, inc=1, device_id=device, device_id_type=MESH)
        pl.semaphore_wait(phase, 3)

        class Blocks:
            def __init__(self, first, count):
                self.first, self.shape = first, (count, piece, width)

            def rows(self, index):
                if isinstance(index, tuple):
                    step, inside, *rest = index
                    start = (self.first + step) * piece + inside.start
                    return (pl.ds(pl.multiple_of(start, 16), inside.size), *rest)
                return (span((self.first + index) * piece, piece),)

            @property
            def at(self):
                return At(self)

            def __getitem__(self, index):
                return arena[self.rows(index)]

            def __setitem__(self, index, value):
                arena[self.rows(index)] = value

        class At:
            def __init__(self, blocks):
                self.blocks = blocks

            def __getitem__(self, index):
                return arena.at[self.blocks.rows(index)]

        buffers, first = [], 0
        for count in (4, 4, 2, 3, 3):
            buffers.append(Blocks(first, count))
            first += count

        def last(rows, total):
            middle = own_in_ref[rows, :].astype(F32) + total
            middle_ref[rows, :] = middle
            normed_own[rows, :] = row_norm(middle)[0].astype(BF)

        def after_z():
            go("ua")
            go("ub")
            pass_on("gb")
            got("ga")

        reduce_body(
            place, product(place, mixed_ref, parts("out"), False), last, [*buffers, *reduce_sems_],
            after_z=after_z, split=0,
        )

        full = arena.at[pl.ds(2 * tokens, tokens)]
        slopes_ref = arena.at[pl.ds(0, tokens)]
        hidden_ref = arena.at[pl.ds(tokens, tokens), pl.ds(0, hidden)]
        columns = (("ga", "ua"), ("gb", "ub"))
        waiting = []

        def fill(owner, which):
            rows = span(owner * piece, piece)
            gates, ups = (parts(name) for name in columns[which])

            def step(t, carry):
                taken = span(t * tile, tile)
                gate = up = None
                for gate_weight, up_weight, index in zip(gates, ups, place.order):
                    deep = gate_weight.shape[0]
                    value = full[rows, span(index * deep, deep)]
                    terms = dot(value, gate_weight[:, taken], NN), dot(value, up_weight[:, taken], NN)
                    gate, up = terms if gate is None else (gate + terms[0], up + terms[1])
                cols = span(which * part_width + t * tile, tile)
                up_cols = span(hidden + which * part_width + t * tile, tile)
                sig = 1.0 / (1.0 + jnp.exp(-gate))
                active = gate * sig
                hidden_ref[rows, cols] = (active * up).astype(BF)
                slopes_ref[rows, cols] = (up * sig * (1.0 + gate * (1.0 - sig))).astype(BF)
                slopes_ref[rows, up_cols] = active.astype(BF)
                return carry

            lax.fori_loop(0, part_width // tile, step, 0)

        def process(owner):
            waiting.append(owner)
            if len(waiting) == 1:
                pass_on("ua")
                got("gb")
                got("ua")
            fill(owner, 0)
            if len(waiting) == 3:
                go("da")
                go("db")
                pass_on("ub")
                got("ub")
                for earlier in waiting:
                    fill(earlier, 1)
            elif len(waiting) > 3:
                fill(owner, 1)

        gather_body(place, normed_own, full, feed_sems, process)
        for i, (ref, out) in enumerate(((full, normed_mid_out), (hidden_ref, hidden_out), (slopes_ref, slopes_out))):
            pltpu.make_async_copy(ref, out, out_sems.at[SLICES + i]).start()
        pass_on("da")
        cot_gather.finish()
        z_moves["db"].wait_recv()
        stores("db")[0].start()
        got("da")
        for i, (ref, out) in enumerate(((full, normed_mid_out), (hidden_ref, hidden_out), (slopes_ref, slopes_out))):
            pltpu.make_async_copy(ref, out, out_sems.at[SLICES + i]).wait()
        for move in (*z_moves.values(), *y_moves.values()):
            move.wait_send()
        for name in names:
            for copy in stores(name):
                copy.wait()

    def half_shape(weight):
        return jax.ShapeDtypeStruct((2, *weight.shape), BF)

    shape = jax.ShapeDtypeStruct
    outs = [
        *(half_shape(weight) for weight in weights),
        *(half_shape(weight) for weight in weights[:7]),
        shape((tokens, inner), BF),
        shape((tokens, heads * hd), BF),
        shape((heads, 8, tokens), F32),
        shape((piece, width), BF),
        shape((piece, width), F32),
        shape((tokens, width), BF),
        shape((tokens, width), BF),
        shape((tokens, width), BF),
        shape((tokens, hidden), BF),
        shape((tokens, 2 * hidden), BF),
    ]
    column_sems = [DMA((3, SLICES)), DMA((3, SLICES)), DMA((4,)), DMA((4,)), DMA((1,))]
    start_sems = [DMA((3, SLICES)), DMA((3, SLICES)), DMA((4, SLICES)), DMA((4, SLICES)), DMA((1,))]
    result = pl.pallas_call(
        kernel,
        out_shape=outs,
        in_specs=[ANYWHERE, ANYWHERE, VMEM_WHOLE, VMEM_WHOLE, VMEM_WHOLE] + [ANYWHERE] * 8,
        out_specs=[ANYWHERE] * 15 + [VMEM_WHOLE] * 5 + [ANYWHERE] * 5,
        scratch_shapes=[
            pltpu.VMEM((3 * tokens, width), BF),
            pltpu.VMEM((tokens, inner), F32),
            pltpu.VMEM((tokens, slice_width), BF),
            pltpu.VMEM((piece, width), BF),
            *(pltpu.VMEM((2, 2, *weight.shape), BF) for weight in weights[:7]),
            pltpu.VMEM((1, 2, *weights[7].shape), BF),
            DMA((8, 4)), DMA((8, 4)), DMA((8, 2)), DMA((SLICES + 3,)), DMA((SLICES + 1,)), DMA((SLICES + 1,)),
            pltpu.SemaphoreType.REGULAR,
            *start_sems, *column_sems, *reduce_sems(), *gather_scratch(),
        ],
        compiler_params=pltpu.CompilerParams(collective_id=ident, has_side_effects=True, vmem_limit_bytes=63 << 20),
        cost_estimate=pl.CostEstimate(
            flops=100 << 30, bytes_accessed=100 << 20, transcendentals=heads * tokens * tokens
        ),
        name="front",
    )(inputs, cot, prefix, *tables, *weights)
    return result[:8], result[8:15], result[15:]


BLOCKS = [(core, zl, x) for core in (0, 1) for zl in (0, 1) for x in (0, 1)]


def spread_greet(place, barrier):
    for core, zl, x in BLOCKS:
        mine = jnp.logical_and(place.straight, core * 4 + zl * 2 + x == place.block)

        @pl.when(jnp.logical_not(mine))
        def _(core=core, zl=zl, x=x):
            pl.semaphore_signal(
                barrier, inc=1, device_id=(place.y, core, place.c, zl, x), device_id_type=MESH
            )

    return 8 - jnp.where(place.straight, 1, 0)


def spread_scratch():
    return [DMA((8,)), DMA((8,)), DMA((1,))]


def spread_shape(piece):
    return jax.ShapeDtypeStruct((piece.shape[0] * 8, piece.shape[1] // 8), piece.dtype)


class Spread:
    def __init__(self, place, src, dst, sems):
        self.place, self.src, self.dst = place, src, dst
        self.send, self.recv, self.own = sems
        self.piece, self.width = src.shape[0], src.shape[1] // 8

    def copy(self, f):
        place = self.place
        return remote(
            self.src.at[:, pl.ds(f * self.width, self.width)], self.dst.at[span(place.block * self.piece, self.piece)],
            self.send.at[f], self.recv.at[place.block], (place.y, place.zh, *BLOCKS[f]),
        )

    def incoming(self, f):
        core, zl, x = BLOCKS[f]
        place = self.place
        return remote(
            self.src.at[:, pl.ds(f * self.width, self.width)], self.dst.at[pl.ds(f * self.piece, self.piece)],
            self.send.at[f], self.recv.at[f], (place.y, core, place.c, zl, x),
        )

    def own_copy(self):
        block = self.place.block
        return pltpu.make_async_copy(
            self.src.at[:, span(block * self.width, self.width)], self.dst.at[span(block * self.piece, self.piece)],
            self.own.at[0],
        )

    def each(self, act):
        for f in range(8):
            mine = jnp.logical_and(self.place.straight, self.place.block == f)
            pl.when(jnp.logical_not(mine))(functools.partial(act, f))

    def start(self):
        self.each(lambda f: self.copy(f).start())
        pl.when(self.place.straight)(lambda: self.own_copy().start())

    def wait(self):
        self.each(lambda f: self.incoming(f).wait_recv())
        self.each(lambda f: self.copy(f).wait_send())
        pl.when(self.place.straight)(lambda: self.own_copy().wait())


def rear_call(branch_own, out_halves, qkv_halves, qkv, mixed, lse, prefix, tables, grad_middle, own_in, ready, normed_in,
              gate_sum, up_own, up_other, heads, hd, ident):
    tokens, inner = qkv.shape
    piece, width = branch_own.shape
    inner_out = mixed.shape[1]
    block = width // 4
    tile = 256

    def kernel(
        branch_ref, out_1, out_2, qkv_1, qkv_2, qkv_ref, mixed_ref, lse_ref, prefix_ref, cos_ref, sin_ref, middle_ref,
        own_in_ref, ready_ref, normed_in_ref, gate_ref, up_own_ref, up_other_ref,
        gate_out, up_out, out_out, qkv_out, ready_out, result_out,
        full, grad_mixed, grad_rows, flipped, dk_ref, dv_ref, up_moved, out_grads, qkv_grads,
        y_sems, z_sems, load_sem, *sems
    ):
        place = Place()
        y = place.y
        reduce_refs, sems = sems[:9], sems[9:]
        gather_sems, ready_sems, result_sems = sems[:4], sems[4:7], sems[7:10]
        place.meet(spread_greet)
        y_up = Beyond(place, up_other_ref, up_moved, y_sems.at[0])
        y_out = Beyond(place, out_grads.at[0], out_grads.at[2], y_sems.at[1])
        y_qkv = Beyond(place, qkv_grads.at[0], qkv_grads.at[2], y_sems.at[2])
        z_gate = GradHalf(place, gate_ref, gate_out, z_sems.at[0])
        z_up = GradHalf(place, up_moved, up_out, z_sems.at[1])
        z_out = GradHalf(place, out_grads.at[1], out_out, z_sems.at[2])
        z_qkv = GradHalf(place, qkv_grads.at[1], qkv_out, z_sems.at[3])
        y_up.start()

        def add(own, moved, rows):
            def step(i, carry):
                where = span(i * 64, 64)
                for j in (0, 1):
                    total = own[j, where, :].astype(F32) + moved[j, where, :].astype(F32)
                    own[j, where, :] = total.astype(BF)
                return carry

            lax.fori_loop(0, rows // 64, step, 0)

        result_ref = full.at[pl.ds(0, piece)]

        out_parts = quarters(out_1, out_2)

        def process(owner):
            rows = span(owner * piece, piece)
            total = None
            for weight, index in zip(out_parts, place.order):
                part = dot(full[rows, span(index * block, block)], weight[...], NT)
                total = part if total is None else total + part
            grad_mixed[rows, :] = total.astype(BF)

        gather_body(place, branch_ref, full, gather_sems, process, begin=z_gate.start, split=0)
        ready_spread = Spread(place, ready_ref, ready_out, ready_sems)
        y_up.wait_recv()
        add(up_moved, up_own_ref, up_own.shape[1])
        z_up.start()

        def flip(source, columns):
            def step(i, carry):
                rows = span(i * tile, tile)
                flipped[0:columns, rows] = source[rows, :].T
                return carry

            lax.fori_loop(0, tokens // tile, step, 0)

        def weigh(grads, side, which, columns):
            def step(n, carry):
                i, m = n // (columns // tile), lax.rem(n, columns // tile)
                rows = span(m * tile, tile)
                value = dot(flipped[rows, :], full[:, span((which * 2 + i) * block, block)], NN)
                grads[side, i, rows, :] = value.astype(BF)
                return carry

            lax.fori_loop(0, 2 * (columns // tile), step, 0)

        flip(mixed_ref, inner_out)
        weigh(out_grads, 0, 1 - y, inner_out)
        y_out.start()
        weigh(out_grads, 1, y, inner_out)
        load = pltpu.make_async_copy(normed_in_ref, full, load_sem.at[0])
        load.start()
        attend_back_body(
            qkv_ref, mixed_ref, grad_mixed, lse_ref, prefix_ref[0:1, 0:1], cos_ref, sin_ref, grad_rows, dk_ref, dv_ref,
            heads, hd,
        )
        load.wait()
        ready_spread.start()

        def last(rows, total):
            value = back_rows(middle_ref[rows, :], own_in_ref[rows, :].astype(F32), total)
            result_ref[rows, :] = value.astype(BF)

        def after_z():
            flip(grad_rows, inner)
            weigh(qkv_grads, 0, 1 - y, inner)
            y_qkv.start()
            y_out.wait_recv()
            add(out_grads.at[1], out_grads.at[2], inner_out)
            z_out.start()
            weigh(qkv_grads, 1, y, inner)

        reduce_body(
            place, product(place, grad_rows, quarters(qkv_1, qkv_2), True), last, reduce_refs,
            after_z=after_z, split=0,
        )
        result_spread = Spread(place, result_ref, result_out, result_sems)
        result_spread.start()
        y_qkv.wait_recv()
        add(qkv_grads.at[1], qkv_grads.at[2], inner)
        z_qkv.start()
        for move in (z_gate, z_up, z_out, z_qkv):
            move.wait_recv()
        ready_spread.wait()
        result_spread.wait()
        for move in (y_up, y_out, y_qkv, z_gate, z_up, z_out, z_qkv):
            move.wait_send()

    shape = jax.ShapeDtypeStruct
    spread = spread_shape(ready)
    return pl.pallas_call(
        kernel,
        out_shape=[
            shape(gate_sum.shape, BF), shape(up_own.shape, BF), shape((2, inner_out, block), BF),
            shape((2, inner, block), BF), spread, spread,
        ],
        in_specs=[VMEM_WHOLE] * 14 + [ANYWHERE, ANYWHERE, VMEM_WHOLE, ANYWHERE],
        out_specs=[ANYWHERE] * 6,
        scratch_shapes=[
            pltpu.VMEM((tokens, width), BF),
            pltpu.VMEM((tokens, inner_out), BF),
            pltpu.VMEM((tokens, inner), BF),
            pltpu.VMEM((inner, tokens), BF),
            pltpu.VMEM((tokens, hd), F32),
            pltpu.VMEM((tokens, hd), F32),
            pltpu.VMEM(up_own.shape, BF),
            pltpu.VMEM((3, 2, inner_out, block), BF),
            pltpu.VMEM((3, 2, inner, block), BF),
            DMA((3, 4)), DMA((4, 4)), DMA((1,)),
            *reduce_scratch(piece, width), *gather_scratch(), *spread_scratch(), *spread_scratch(),
        ],
        compiler_params=pltpu.CompilerParams(
            collective_id=ident, has_side_effects=True, vmem_limit_bytes=(64 << 20) - (64 << 10)
        ),
        cost_estimate=pl.CostEstimate(flops=100 << 30, bytes_accessed=100 << 20, transcendentals=heads * tokens * tokens),
        name="rear",
    )(
        branch_own, *out_halves, *qkv_halves, qkv, mixed, lse, prefix, *tables, grad_middle, own_in, ready, normed_in,
        gate_sum, up_own, up_other,
    )


def local_fine(inputs, prefix_len, w_qkv, w_out, w_up_gate, w_down, cotangent):
    heads, hd = w_qkv.shape[1], w_qkv.shape[2] // 3
    hidden_width = w_down.shape[0]
    tokens = inputs.shape[0]
    y = lax.axis_index("y")
    prefix_len = lax.ppermute(prefix_len, ("core", "zh"), [(0, 0), (1, 2), (2, 1), (3, 3)])
    prefix = jnp.broadcast_to(prefix_len[:, None], (8, 128))
    tables = rope_tables(tokens, hd)
    part = hidden_width // 2
    ga, gb = w_up_gate[:, 0, :part], w_up_gate[:, 0, part:]
    ua, ub = w_up_gate[:, 1, :part], w_up_gate[:, 1, part:]
    da, db = w_down[:part], w_down[part:]

    weights = (w_qkv.reshape(w_qkv.shape[0], -1), w_out, ga, gb, ua, ub, da, db)
    firsts, seconds, results = front_call(inputs, cotangent, prefix, tables, weights, heads, hd, 1)
    qkv_1, out_1, ga_1, gb_1, ua_1, ub_1, da_1, db_1 = firsts
    qkv_2, out_2, ga_2, gb_2, ua_2, ub_2, da_2 = seconds
    qkv, mixed, lse, own_in, middle, normed_in, cot_full, normed_mid, hidden, slopes = results
    gates = (ga_1, ga_2, gb_1, gb_2)

    (grad_middle, branch_own, grad_gate_up, gate_other, down_own, down_moved), (db_2,) = middle_call(
        cot_full, slopes, hidden, gates, (ua_1, ua_2, ub_1, ub_2), (da_1, da_2), db_1, normed_mid,
        [("beyond", db_1)], middle, 5,
    )
    outputs, down_final, gate_sum, up_own, up_other = down_call(
        hidden, (da_1, db_1), (da_2, db_2), middle, down_own, down_moved, normed_mid, grad_gate_up, gate_other, 6
    )
    gate_final, up_final, out_final, qkv_final, outputs, input_grad = rear_call(
        branch_own, (out_1, out_2), (qkv_1, qkv_2), qkv, mixed, lse, prefix, tables, grad_middle, own_in, outputs,
        normed_in, gate_sum, up_own, up_other, heads, hd, 7,
    )

    def summed(parts):
        return parts[0].astype(F32) + parts[1].astype(F32)

    return (
        outputs,
        input_grad.astype(F32),
        summed(qkv_final).T.reshape(-1, heads, 3 * hd),
        summed(out_final),
        jnp.stack([summed(gate_final), summed(up_final)], axis=1),
        summed(down_final),
    )


def solution(mesh):
    row_size, col_size = mesh.shape["row"], mesh.shape["col"]
    fine = (row_size, col_size) == (4, 8)
    if fine:
        names, shape, body = AXES, (2,) * 5, local_fine
        row, col = AXES[:2], AXES[2:]
    else:
        names = ("rmaj", "core", "cmaj", "cmin")
        shape = (row_size // 2, 2, 4, col_size // 4)
        body = functools.partial(local, shape[3] == 2)
        row, col = names[:2], names[2:]
    outs = (P(row, col), P(row, col), P(row, col, None), P(col, row), P(row, None, col), P(col, row))
    return jax.shard_map(
        body,
        mesh=Mesh(mesh.devices.reshape(shape), names),
        in_specs=(P(row, col), P(row), P(row, col, None), P(col, row), P(row, None, col), P(col, row), P(row, col)),
        out_specs=outs,
        check_vma=False,
    )
```

```python
import functools

import jax
import jax.numpy as jnp
from jax import lax
from jax.experimental import pallas as pl
from jax.experimental.pallas import tpu as pltpu
from jax.sharding import Mesh
from jax.sharding import PartitionSpec as P

EPSILON = 1e-05
NEG = -1e30
F32 = jnp.float32
BF = jnp.bfloat16
NN = (((1,), (0,)), ((), ()))
NT = (((1,), (1,)), ((), ()))
TN = (((0,), (0,)), ((), ()))
def dot(a, b, dims):
    return lax.dot_general(a, b, dims, preferred_element_type=F32)

def fwd_kernel(prefix_ref, q_ref, k_ref, v_ref, o_ref, lse_ref, *, bq, bk, scale):
    i = pl.program_id(1)
    first = i * bq
    prefix = prefix_ref[0]
    q = q_ref[...]
    limit = jnp.maximum(first + bq, prefix)
    total = (limit + bk - 1) // bk
    clear = jnp.maximum(first, prefix) // bk
    def step(masked, j, carry):
        top, tot, acc = carry
        rows = pl.ds(pl.multiple_of(j * bk, bk), bk)
        s = dot(q, k_ref[rows, :], NT) * scale
        if masked:
            kp = j * bk + lax.broadcasted_iota(jnp.int32, (bq, bk), 1)
            qp = first + lax.broadcasted_iota(jnp.int32, (bq, bk), 0)
            s = jnp.where(kp < jnp.maximum(qp + 1, prefix), s, NEG)
        new = jnp.maximum(top, jnp.max(s, axis=1, keepdims=True))
        alpha = jnp.exp(top - new)
        p = jnp.exp(s - new)
        tot = tot * alpha + jnp.sum(p, axis=1, keepdims=True)
        acc = acc * alpha + dot(p.astype(BF), v_ref[rows, :], NN)
        return new, tot, acc
    carry = (jnp.full((bq, 1), NEG, F32), jnp.zeros((bq, 1), F32), jnp.zeros((bq, q.shape[1]), F32))
    carry = lax.fori_loop(0, clear, functools.partial(step, False), carry)
    top, tot, acc = lax.fori_loop(clear, total, functools.partial(step, True), carry)
    o_ref[...] = (acc / tot).astype(o_ref.dtype)
    lse = jnp.broadcast_to(top + jnp.log(tot), (bq, 128))
    lse_ref[0] = lse.T[0:8, :]

def attend_fwd(qkv, prefix, heads, *, bq=512, bk=512, hd=128):
    seq = qkv.shape[0]
    return pl.pallas_call(
        functools.partial(fwd_kernel, bq=bq, bk=bk, scale=hd ** -0.5),
        grid_spec=pltpu.PrefetchScalarGridSpec(
            num_scalar_prefetch=1, grid=(heads, seq // bq),
            in_specs=[pl.BlockSpec((bq, hd), lambda h, i, p: (i, 3 * h)),
                      pl.BlockSpec((seq, hd), lambda h, i, p: (0, 3 * h + 1)),
                      pl.BlockSpec((seq, hd), lambda h, i, p: (0, 3 * h + 2))],
            out_specs=[pl.BlockSpec((bq, hd), lambda h, i, p: (i, h)),
                       pl.BlockSpec((1, 8, bq), lambda h, i, p: (h, 0, i))]),
        out_shape=[jax.ShapeDtypeStruct((seq, heads * hd), BF), jax.ShapeDtypeStruct((heads, 8, seq), F32)],
        cost_estimate=pl.CostEstimate(flops=4 * heads * seq * seq * hd, bytes_accessed=8 * heads * seq * hd, transcendentals=heads * seq * seq),
        name="attend_forward",
    )(prefix, qkv, qkv, qkv)

def bwd_kernel(prefix_ref, qkv_ref, o_ref, do_ref, lse_ref, cos_ref, sin_ref, out_ref, dk_ref, dv_ref, delta_ref, *, bq, bk, hd, scale):
    seq = qkv_ref.shape[0]
    prefix = prefix_ref[0]
    dk_ref[...] = jnp.zeros_like(dk_ref)
    dv_ref[...] = jnp.zeros_like(dv_ref)
    def deltas(i, _):
        rows = pl.ds(pl.multiple_of(i * bq, bq), bq)
        prod = (do_ref[rows, :].astype(F32) * o_ref[rows, :].astype(F32)).T
        delta_ref[:, rows] = jnp.broadcast_to(jnp.sum(prod, axis=0, keepdims=True), (8, bq))
        return 0
    lax.fori_loop(0, seq // bq, deltas, 0)
    def unrotate(g, rows):
        cos, sin = cos_ref[rows, :], sin_ref[rows, :]
        half = hd // 2
        a, b = g[:, :half], g[:, half:]
        return jnp.concatenate([a * cos + b * sin, b * cos - a * sin], axis=1)
    def q_step(i, _):
        first = i * bq
        qrows = pl.ds(pl.multiple_of(first, bq), bq)
        q = qkv_ref[qrows, 0:hd]
        do = do_ref[qrows, :]
        lse = lse_ref[0, 0:1, qrows]
        delta = delta_ref[0:1, qrows]
        limit = jnp.maximum(first + bq, prefix)
        total = (limit + bk - 1) // bk
        clear = jnp.maximum(first, prefix) // bk
        def step(masked, j, dq):
            krows = pl.ds(pl.multiple_of(j * bk, bk), bk)
            k = qkv_ref[krows, hd:2 * hd]
            v = qkv_ref[krows, 2 * hd:3 * hd]
            s = dot(k, q, NT) * scale
            p = jnp.exp(s - lse)
            if masked:
                kp = j * bk + lax.broadcasted_iota(jnp.int32, (bk, bq), 0)
                qp = first + lax.broadcasted_iota(jnp.int32, (bk, bq), 1)
                p = jnp.where(kp < jnp.maximum(qp + 1, prefix), p, 0.0)
            dp = dot(v, do, NT)
            dv_ref[krows, :] += dot(p.astype(BF), do, NN)
            ds = (p * (dp - delta)).astype(BF)
            dk_ref[krows, :] += dot(ds, q, NN)
            return dq + dot(ds, k, TN)
        dq = lax.fori_loop(0, clear, functools.partial(step, False), jnp.zeros((bq, hd), F32))
        dq = lax.fori_loop(clear, total, functools.partial(step, True), dq)
        out_ref[qrows, 0:hd] = unrotate(dq * scale, qrows).astype(BF)
        return 0
    lax.fori_loop(0, seq // bq, q_step, 0)
    def fin(i, _):
        rows = pl.ds(pl.multiple_of(i * bq, bq), bq)
        out_ref[rows, hd:2 * hd] = unrotate(dk_ref[rows, :] * scale, rows).astype(BF)
        out_ref[rows, 2 * hd:3 * hd] = dv_ref[rows, :].astype(BF)
        return 0
    lax.fori_loop(0, seq // bq, fin, 0)

def attend_bwd(qkv, mixed, dmixed, lse, prefix, cos, sin, heads, *, bq=512, bk=512, hd=128):
    seq = qkv.shape[0]
    return pl.pallas_call(
        functools.partial(bwd_kernel, bq=bq, bk=bk, hd=hd, scale=hd ** -0.5),
        grid_spec=pltpu.PrefetchScalarGridSpec(
            num_scalar_prefetch=1, grid=(heads,),
            in_specs=[pl.BlockSpec((seq, 3 * hd), lambda h, p: (0, h)),
                      pl.BlockSpec((seq, hd), lambda h, p: (0, h)),
                      pl.BlockSpec((seq, hd), lambda h, p: (0, h)),
                      pl.BlockSpec((1, 8, seq), lambda h, p: (h, 0, 0)),
                      pl.BlockSpec((seq, hd // 2), lambda h, p: (0, 0)),
                      pl.BlockSpec((seq, hd // 2), lambda h, p: (0, 0))],
            out_specs=[pl.BlockSpec((seq, 3 * hd), lambda h, p: (0, h))],
            scratch_shapes=[pltpu.VMEM((seq, hd), F32), pltpu.VMEM((seq, hd), F32), pltpu.VMEM((8, seq), F32)]),
        out_shape=[jax.ShapeDtypeStruct((seq, heads * 3 * hd), BF)],
        cost_estimate=pl.CostEstimate(flops=10 * heads * seq * seq * hd, bytes_accessed=20 * heads * seq * hd, transcendentals=heads * seq * seq),
        name="attend_backward",
    )(prefix, qkv, mixed, dmixed, lse, cos, sin)[0]


def rope_tables(count, head_dim):
    positions = jnp.arange(count, dtype=jnp.int32).astype(F32)
    frequency = 10000.0 ** (-(jnp.arange(head_dim // 2).astype(F32) * 2.0 / head_dim))
    angles = positions[:, None] * frequency[None, :]
    return jnp.cos(angles), jnp.sin(angles)


def rotate(values, cosine, sine):
    half = values.shape[-1] // 2
    a, b = values[..., :half], values[..., half:]
    return jnp.concatenate([a * cosine - b * sine, b * cosine + a * sine], axis=-1)


def norm(values):
    center = values - jnp.mean(values, axis=-1, keepdims=True)
    inv_std = lax.rsqrt(jnp.mean(center * center, axis=-1, keepdims=True) + EPSILON)
    return center * inv_std, inv_std


def norm_back(grad, normed, inv_std):
    mean_grad = jnp.mean(grad, axis=-1, keepdims=True)
    mean_cross = jnp.mean(grad * normed, axis=-1, keepdims=True)
    return inv_std * (grad - mean_grad - normed * mean_cross)


def mm(spec, left, right):
    return jnp.einsum(spec, left, right, preferred_element_type=F32)


def local(swap, inputs, prefix_len, w_qkv, w_out, w_up_gate, w_down, cotangent):
    rows = ("rmaj", "cmin") if swap else ("rmaj", "core")
    cols = ("cmaj", "core") if swap else ("cmaj", "cmin")

    def exchange(value):
        if not swap:
            return value
        return lax.ppermute(value, ("core", "cmin"), [(0, 0), (1, 2), (2, 1), (3, 3)])

    def scatter(value):
        return lax.psum_scatter(value.astype(BF), cols, scatter_dimension=0, tiled=True).astype(F32)

    def spread(value):
        return lax.all_to_all(value, cols, 1, 0, tiled=True)

    prefix_len = exchange(prefix_len)
    inputs, cotangent = exchange(inputs), exchange(cotangent)
    w_qkv, w_out = exchange(w_qkv), exchange(w_out)
    w_up_gate, w_down = exchange(w_up_gate), exchange(w_down)
    tokens = inputs.shape[0]
    heads, head_dim = w_qkv.shape[1], w_qkv.shape[2] // 3
    hidden_width = w_down.shape[0]
    full_in = lax.all_gather(inputs, cols, axis=1, tiled=True)
    width = full_in.shape[1]
    qkv_all = lax.all_gather(w_qkv, rows, axis=0, tiled=True).reshape(width, heads * 3 * head_dim)
    out_all = lax.all_gather(w_out, rows, axis=1, tiled=True)
    up_all = lax.all_gather(w_up_gate, rows, axis=0, tiled=True).reshape(width, 2 * hidden_width)
    down_all = lax.all_gather(w_down, rows, axis=1, tiled=True)
    cot_full = lax.all_gather(cotangent, cols, axis=1, tiled=True)
    piece = tokens // lax.axis_size(cols)
    first = lax.axis_index(cols) * piece
    own_in = lax.dynamic_slice_in_dim(full_in, first, piece, 0).astype(F32)
    own_cot = lax.dynamic_slice_in_dim(cot_full, first, piece, 0).astype(F32)

    normed_in = norm(full_in.astype(F32))[0].astype(BF)
    qkv_rows = mm("td,de->te", normed_in, qkv_all).reshape(tokens, heads, 3, head_dim)
    cosine, sine = rope_tables(tokens, head_dim)
    turned = rotate(qkv_rows[:, :, :2], cosine[:, None, None], sine[:, None, None])
    qkv = jnp.concatenate([turned, qkv_rows[:, :, 2:]], axis=2).astype(BF)
    qkv = qkv.reshape(tokens, heads * 3 * head_dim)
    mixed, lse = attend_fwd(qkv, prefix_len, heads, hd=head_dim)
    middle = own_in + scatter(mm("tc,cd->td", mixed, out_all))
    normed_two, inv_two = norm(middle)
    normed_mid = lax.all_gather(normed_two.astype(BF), cols, axis=0, tiled=True)
    gate_up = mm("td,df->tf", normed_mid, up_all)
    gate, up = gate_up[:, :hidden_width], gate_up[:, hidden_width:]
    sig = jax.nn.sigmoid(gate)
    active = gate * sig
    hidden = (active * up).astype(BF)
    outputs = middle + scatter(mm("tf,fd->td", hidden, down_all))
    outputs = exchange(spread(outputs.astype(BF)))

    grad_hidden = mm("td,fd->tf", cot_full, down_all)
    grad_gate = grad_hidden * up * sig * (1.0 + gate * (1.0 - sig))
    grad_gate_up = jnp.concatenate([grad_gate, grad_hidden * active], axis=1).astype(BF)
    grad_down = mm("tf,td->fd", hidden, cot_full).astype(BF)
    grad_down = lax.psum_scatter(grad_down, rows, scatter_dimension=1, tiled=True)
    grad_up = mm("td,tf->df", normed_mid, grad_gate_up).astype(BF)
    grad_up = lax.psum_scatter(grad_up, rows, scatter_dimension=0, tiled=True)
    grad_normed = scatter(mm("tf,df->td", grad_gate_up, up_all))
    grad_middle = own_cot + norm_back(grad_normed, normed_two, inv_two)
    grad_branch = lax.all_gather(grad_middle.astype(BF), cols, axis=0, tiled=True)
    grad_out = mm("tc,td->cd", mixed, grad_branch).astype(BF)
    grad_out = lax.psum_scatter(grad_out, rows, scatter_dimension=1, tiled=True)
    grad_mixed = mm("td,cd->tc", grad_branch, out_all).astype(BF)
    grad_rows = attend_bwd(qkv, mixed, grad_mixed, lse, prefix_len, cosine, sine, heads, hd=head_dim)
    grad_in = scatter(mm("te,de->td", grad_rows, qkv_all))
    grad_qkv = mm("td,te->de", normed_in, grad_rows).astype(BF)
    grad_qkv = lax.psum_scatter(grad_qkv, rows, scatter_dimension=0, tiled=True)
    normed_own, inv_own = norm(own_in)
    input_grad = grad_middle + norm_back(grad_in, normed_own, inv_own)
    input_grad = exchange(spread(input_grad.astype(BF))).astype(F32)
    return (
        outputs,
        input_grad,
        exchange(grad_qkv).astype(F32).reshape(-1, heads, 3 * head_dim),
        exchange(grad_out).astype(F32),
        exchange(grad_up).astype(F32).reshape(-1, 2, hidden_width),
        exchange(grad_down).astype(F32),
    )


AXES = ("y", "core", "zh", "zl", "x")
GROUP = ("core", "zl", "x")
MESH = pl.DeviceIdType.MESH
DMA = pltpu.SemaphoreType.DMA
VMEM_WHOLE = pl.BlockSpec(memory_space=pltpu.VMEM)
ANYWHERE = pl.BlockSpec(memory_space=pl.ANY)


class Place:
    def __init__(self):
        self.y, self.c, self.zh, self.zl, self.x = (lax.axis_index(name) for name in AXES)
        y, c, zh, zl, x = self.y, self.c, self.zh, self.zl, self.x
        self.sibling = (y, 1 - c, zh, zl, x)
        self.across = (y, c, zh, zl, 1 - x)
        self.along = (y, c, zh, 1 - zl, x)
        self.beyond = (1 - y, c, zh, zl, x)
        self.far = [(y, core, 1 - zh, zl, x) for core in (0, 1)]
        self.far_role = (y, zh, 1 - zh, zl, x)
        self.straight = c == zh
        self.outer = zl == zh
        self.order = [2 * y, 2 * y + 1, 2 * (1 - y), 2 * (1 - y) + 1]
        self.block = c * 4 + zl * 2 + x

    def chip(self, dz, dx):
        return lax.rem(self.zl + dz, 2) * 2 + lax.rem(self.x + dx, 2)

    def meet(self, greet=None):
        devices = [self.sibling, self.across, self.along, self.beyond, *self.far]
        barrier = pltpu.get_barrier_semaphore()
        for device in devices:
            pl.semaphore_signal(barrier, inc=1, device_id=device, device_id_type=MESH)
        more = greet(self, barrier) if greet else 0
        pl.semaphore_wait(barrier, len(devices) + more)


def span(start, size):
    return pl.ds(pl.multiple_of(start, size), size)


def remote(src, dst, send_sem, recv_sem, device):
    return pltpu.make_async_remote_copy(
        src_ref=src, dst_ref=dst, send_sem=send_sem, recv_sem=recv_sem, device_id=device, device_id_type=MESH
    )


class Beyond:
    along_z = False

    def __init__(self, place, src, dst, sem):
        self.copy = remote(src, dst, sem.at[0], sem.at[2], place.beyond)

    def start(self):
        self.copy.start()

    def wait_recv(self):
        self.copy.wait_recv()

    def wait_send(self):
        self.copy.wait_send()


class WeightHalf:
    along_z = True

    def __init__(self, place, src, dst, sem):
        c = place.c
        self.straight = place.straight
        self.outward = remote(src, dst.at[c], sem.at[0], sem.at[2 + c], place.far_role)
        self.aside = remote(src, dst.at[c], sem.at[1], sem.at[2 + c], place.sibling)
        self.here = pltpu.make_async_copy(src, dst.at[c], sem.at[1])
        self.from_sibling = remote(src, dst.at[1 - c], sem.at[1], sem.at[3 - c], place.sibling)
        self.from_far = [remote(src, dst.at[i], sem.at[0], sem.at[2 + i], place.far_role) for i in (0, 1)]

    def start(self):
        self.outward.start()

        @pl.when(self.straight)
        def _():
            self.here.start()

        @pl.when(jnp.logical_not(self.straight))
        def _():
            self.aside.start()

    def wait_recv(self):
        @pl.when(self.straight)
        def _():
            self.here.wait()
            self.from_sibling.wait_recv()

        @pl.when(jnp.logical_not(self.straight))
        def _():
            for copy in self.from_far:
                copy.wait_recv()

    def wait_send(self):
        self.outward.wait_send()

        @pl.when(jnp.logical_not(self.straight))
        def _():
            self.aside.wait_send()


class GradHalf:
    along_z = True

    def __init__(self, place, src, dst, sem):
        c, zh = place.c, place.zh
        self.straight = place.straight
        self.here = pltpu.make_async_copy(src.at[c], dst.at[zh], sem.at[0])
        self.aside = remote(src.at[1 - c], dst.at[zh], sem.at[1], sem.at[2 + zh], place.sibling)
        self.outward = [remote(src.at[i], dst.at[zh], sem.at[i], sem.at[2 + zh], place.far[i]) for i in (0, 1)]
        self.from_sibling = remote(src.at[c], dst.at[zh], sem.at[1], sem.at[2 + zh], place.sibling)
        self.from_far = remote(src.at[c], dst.at[1 - zh], sem.at[0], sem.at[3 - zh], place.far[0])

    def start(self):
        @pl.when(self.straight)
        def _():
            self.here.start()
            self.aside.start()

        @pl.when(jnp.logical_not(self.straight))
        def _():
            for copy in self.outward:
                copy.start()

    def wait_recv(self):
        self.from_far.wait_recv()

        @pl.when(self.straight)
        def _():
            self.here.wait()

        @pl.when(jnp.logical_not(self.straight))
        def _():
            self.from_sibling.wait_recv()

    def wait_send(self):
        @pl.when(self.straight)
        def _():
            self.aside.wait_send()

        @pl.when(jnp.logical_not(self.straight))
        def _():
            for copy in self.outward:
                copy.wait_send()


KINDS = {"beyond": Beyond, "weight": WeightHalf, "grad": GradHalf}


def moved_shape(kind, src):
    shape = (2, *src.shape) if kind == "weight" else src.shape
    return jax.ShapeDtypeStruct(shape, src.dtype)


class Under:
    def __init__(self, place, moves):
        self.place, self.moves = place, moves
        self.z = [move for kind, move in moves if move.along_z]
        self.y = [move for kind, move in moves if not move.along_z and not isinstance(kind, int)]
        self.follow = [(moves[kind][1], move) for kind, move in moves if isinstance(kind, int)]

    def start_y(self):
        for move in self.y:
            move.start()

    def start_z(self, outer=None):
        def start():
            for move in self.z:
                move.start()

        if outer is None:
            start()
        else:
            pl.when(self.place.outer if outer else jnp.logical_not(self.place.outer))(start)

    def start_follow(self):
        for ahead, move in self.follow:
            ahead.wait_recv()
            move.start()

    def end(self, skip=0):
        done = [ahead for ahead, _ in self.follow]
        for _, move in self.moves[skip:]:
            if move not in done:
                move.wait_recv()


def comm_call(
    body, name, ident, inputs, outs, scratch, moves=(), flops=0, transcendentals=0, spaces=None, greet=None
):
    n_in, n_out, n_move = len(inputs), len(outs), len(moves)
    own_source = [i for i, (kind, _) in enumerate(moves) if not isinstance(kind, int)]

    def kernel(*refs):
        ins, refs = refs[:n_in], refs[n_in:]
        sources, refs = refs[:len(own_source)], refs[len(own_source):]
        results, refs = refs[:n_out], refs[n_out:]
        targets, refs = refs[:n_move], refs[n_move:]
        sems, rest = refs[0], refs[1:]
        place = Place()
        place.meet(greet)
        made = []
        for i, (kind, _) in enumerate(moves):
            if isinstance(kind, int):
                made.append((kind, Beyond(place, targets[kind], targets[i], sems.at[i])))
            else:
                made.append((kind, KINDS[kind](place, sources[own_source.index(i)], targets[i], sems.at[i])))
        body(place, ins, results, rest, Under(place, made), targets)
        for _, move in made:
            move.wait_send()

    arrays = [*inputs, *(moves[i][1] for i in own_source)]
    shapes = list(outs)
    moved = []
    for kind, array in moves:
        moved.append(moved[kind] if isinstance(kind, int) else moved_shape(kind, array))
    shapes += moved
    in_specs = (spaces or [VMEM_WHOLE] * n_in) + [ANYWHERE] * len(own_source)
    size = sum(s.size * s.dtype.itemsize for s in (*arrays, *shapes))
    result = pl.pallas_call(
        kernel,
        out_shape=shapes,
        in_specs=in_specs,
        out_specs=[VMEM_WHOLE] * (n_out + n_move),
        scratch_shapes=[DMA((max(n_move, 1), 4)), *scratch],
        compiler_params=pltpu.CompilerParams(
            collective_id=ident, has_side_effects=True, vmem_limit_bytes=(64 << 20) - (64 << 10)
        ),
        cost_estimate=pl.CostEstimate(
            flops=flops + (20 << 30), bytes_accessed=size, transcendentals=transcendentals
        ),
        name=name,
    )(*arrays)
    return result[:n_out], result[n_out:]


def each_rows(count, body, size=32):
    def step(i, carry):
        body(span(i * size, size))
        return carry

    lax.fori_loop(0, count // size, step, 0)


def row_norm(values):
    center = values - jnp.mean(values, axis=-1, keepdims=True)
    inv_std = lax.rsqrt(jnp.mean(center * center, axis=-1, keepdims=True) + EPSILON)
    return center * inv_std, inv_std


SLICES = 4
NORM_ROWS = 64
NORM_UNROLL = 1


def reduce_sems():
    return [DMA((4,)), DMA((4,)), DMA((3, SLICES)), DMA((3, SLICES))]


def reduce_scratch(piece, width):
    return [pltpu.VMEM((count, piece, width), BF) for count in (4, 4, 2, 3, 3)] + reduce_sems()


def nothing():
    pass


def reduce_body(place, compute, last, scratch, begin=nothing, before_z=nothing, after_z=nothing, split=0):
    sib_out, sib_in, own, near_out, near_in, sib_send, sib_recv, near_send, near_recv = scratch
    piece = own.shape[1]
    c = place.c
    size = piece // SLICES
    begin()

    def sib_copy(step):
        return remote(sib_out.at[step], sib_in.at[step], sib_send.at[step], sib_recv.at[step], place.sibling)

    def near_copy(step, r, turned=False):
        device = place.along if step == 2 or turned else place.across
        rows = span(r * size, size)
        return remote(
            near_out.at[step, rows], near_in.at[step, rows], near_send.at[step, r], near_recv.at[step, r], device
        )

    def finish(step):
        slot = step % 2
        sib_copy(step).wait_recv()

        def send(joins, turned, r, carry):
            if joins:
                near_copy(0, r).wait_recv()
            rows = span(r * size, size)
            total = own[slot, rows, :].astype(F32) + sib_in[step, rows, :].astype(F32)
            if joins:
                total = total + near_in[0, rows, :].astype(F32)
            near_out[step, rows, :] = total.astype(BF)
            near_copy(step, r, turned).start()
            return carry

        lax.fori_loop(0, SLICES - split, functools.partial(send, step == 2, False), 0)
        if split:
            lax.fori_loop(SLICES - split, SLICES, functools.partial(send, step == 1, step == 0), 0)

    def step(s, carry):
        target = place.chip(1 - lax.rem(s, 2), 1 - s // 2)
        compute((1 - c) * 4 + target, sib_out.at[s])
        sib_copy(s).start()
        for index in (0, 1):
            @pl.when(s == index + 1)
            def _(index=index):
                finish(index)

        compute(c * 4 + target, own.at[lax.rem(s, 2)])
        return carry

    lax.fori_loop(0, 4, step, 0)
    before_z()
    finish(2)
    after_z()
    sib_copy(3).wait_recv()

    def arrive(r, carry):
        near_copy(1, r).wait_recv()
        near_copy(2, r).wait_recv()

        def final(i, carry):
            rows = span(r * size + i * 16, 16)
            total = own[1, rows, :].astype(F32) + sib_in[3, rows, :].astype(F32)
            last(rows, total + near_in[1, rows, :].astype(F32) + near_in[2, rows, :].astype(F32))
            return carry

        return lax.fori_loop(0, size // 16, final, carry)

    lax.fori_loop(0, SLICES, arrive, 0)
    for s in range(4):
        sib_copy(s).wait_send()

    def sent(r, carry):
        for s in range(3):
            near_copy(s, r).wait_send()
        return carry

    lax.fori_loop(0, SLICES, sent, 0)


def product(place, left_ref, weights, transposed):
    def compute(owner, out_ref):
        piece = out_ref.shape[0]
        left = left_ref[span(owner * piece, piece), :]
        for weight, index in zip(weights, place.order):
            size = weight.shape[0] if transposed else weight.shape[1]
            part = dot(left, weight[...], NT if transposed else NN)
            out_ref[:, span(index * size, size)] = part.astype(out_ref.dtype)

    return compute


def back_rows(base, value, total):
    normed, inv_std = row_norm(value)
    mean_grad = jnp.mean(total, axis=-1, keepdims=True)
    mean_cross = jnp.mean(total * normed, axis=-1, keepdims=True)
    return base + inv_std * (total - mean_grad - normed * mean_cross)


def quarters(first, second):
    return [first.at[0], first.at[1], second.at[0], second.at[1]]


def both_halves(cos_ref, sin_ref, rows):
    cos, sin = cos_ref[rows, :], sin_ref[rows, :]
    return jnp.concatenate([cos, cos], axis=1), jnp.concatenate([-sin, sin], axis=1)


def beside(under):
    def begin():
        under.start_y()
        under.start_z()

    return dict(begin=begin, after_z=under.start_follow)


class Turned:
    def __init__(self, source, stage, sems, flipped):
        self.source, self.stage, self.sems, self.flipped = source, stage, sems, flipped
        self.tile, self.strip = 256, stage.shape[1]
        self.count = flipped.shape[1] // self.strip

    def load(self, i):
        slot = lax.rem(i, 2)
        rows = span(i * self.strip, self.strip)
        return pltpu.make_async_copy(self.source.at[rows], self.stage.at[slot], self.sems.at[slot])

    def turn(self):
        def step(i, carry):
            self.load(i).wait()

            @pl.when(i + 1 < self.count)
            def _():
                self.load(i + 1).start()

            self.flipped[:, span(i * self.strip, self.strip)] = self.stage[lax.rem(i, 2)].T
            return carry

        self.load(0).start()
        lax.fori_loop(0, self.count, step, 0)

    def times(self, right, out, first, offset):
        block, columns = out.shape[1:]
        half = columns // 2
        each = block // self.tile

        def step(n, carry):
            m, t = n // 2, lax.rem(n, 2)
            left = self.flipped[span(first + m * self.tile, self.tile), :]
            value = dot(left, right[:, span(offset + t * half, half)], NN)
            out[m // each, span(lax.rem(m, each) * self.tile, self.tile), span(t * half, half)] = value.astype(BF)
            return carry

        lax.fori_loop(0, 4 * each, step, 0)


def down_call(hidden, firsts, seconds, middle, own, moved, normed, grads, gate_other, ident):
    piece, width = middle.shape
    tokens, both = grads.shape
    part_width = both // 2
    block = width // 4
    tile = 256

    def kernel(
        hidden_ref, first_a, first_b, second_a, second_b, base_ref, own_ref, moved_ref, grads_ref, normed_ref, gate_other,
        result_ref, down_out, gate_out, up_own_out, up_other_out,
        down_sum, stage, flipped, gate_moved, kept, spare,
        y_sems, z_sems, load_sems, store_sems, *reduce_refs
    ):
        place = Place()
        place.meet()
        y = place.y

        turned = Turned(normed_ref, stage, load_sems, flipped)
        for j in (0, 1):
            cols = pl.ds(j * block, block)

            def step(i, carry, j=j, cols=cols):
                upper, rows = i // (own_ref.shape[1] // 64), span(lax.rem(i, own_ref.shape[1] // 64) * 64, 64)
                total = own_ref[upper, rows, cols].astype(F32) + moved_ref[upper, rows, cols].astype(F32)
                down_sum[j, span(i * 64, 64), :] = total.astype(BF)
                return carry

            lax.fori_loop(0, down_sum.shape[1] // 64, step, 0)
        z_down = GradHalf(place, down_sum, down_out, z_sems.at[0])
        y_gate = Beyond(place, gate_other, gate_moved, y_sems.at[0])
        y_gate.start()
        parts = list(zip(quarters(first_a, second_a), quarters(first_b, second_b), place.order))

        def compute(owner, out_ref):
            rows = span(owner * piece, piece)
            for upper, lower, index in parts:
                depth, size = upper.shape
                part = dot(hidden_ref[rows, 0:depth], upper[...], NN) + dot(hidden_ref[rows, depth:], lower[...], NN)
                out_ref[:, span(index * size, size)] = part.astype(out_ref.dtype)

        def last(rows, total):
            result_ref[rows, :] = (base_ref[rows, :] + total).astype(BF)

        def store(out, ref, i):
            return pltpu.make_async_copy(ref, out, store_sems.at[i])

        def after_z():
            turned.turn()
            turned.times(grads_ref, spare, (1 - y) * (width // 2), part_width)
            store(up_other_out, spare, 0).start()
            turned.times(grads_ref, kept, y * (width // 2), 0)
            store(up_other_out, spare, 0).wait()
            turned.times(grads_ref, spare, y * (width // 2), part_width)
            store(up_own_out, spare, 1).start()

        reduce_body(place, compute, last, reduce_refs, begin=z_down.start, after_z=after_z)
        y_gate.wait_recv()
        for i in (0, 1):
            def add(n, carry, i=i):
                rows = span(n * 64, 64)
                kept[i, rows, :] = (kept[i, rows, :].astype(F32) + gate_moved[i, rows, :].astype(F32)).astype(BF)
                return carry

            lax.fori_loop(0, block // 64, add, 0)
        store(gate_out, kept, 2).start()
        z_down.wait_recv()
        store(up_own_out, spare, 1).wait()
        store(gate_out, kept, 2).wait()
        for move in (z_down, y_gate):
            move.wait_send()

    shape = jax.ShapeDtypeStruct
    half = shape((2, block, part_width), BF)
    down_shape = (2, hidden.shape[1], block)
    held = pltpu.VMEM(half.shape, BF)
    return pl.pallas_call(
        kernel,
        out_shape=[shape((piece, width), BF), shape(down_shape, BF), half, half, half],
        in_specs=[VMEM_WHOLE] * 9 + [ANYWHERE] * 2,
        out_specs=[VMEM_WHOLE] + [ANYWHERE] * 4,
        scratch_shapes=[
            pltpu.VMEM(down_shape, BF),
            pltpu.VMEM((2, tile, width), BF),
            pltpu.VMEM((width, tokens), BF),
            held, held, held,
            DMA((1, 4)), DMA((1, 4)), DMA((2,)), DMA((3,)), *reduce_scratch(piece, width),
        ],
        compiler_params=pltpu.CompilerParams(collective_id=ident, has_side_effects=True, vmem_limit_bytes=63 << 20),
        cost_estimate=pl.CostEstimate(flops=60 << 30, bytes_accessed=60 << 20, transcendentals=0),
        name="reduce_down",
    )(hidden, *firsts, *seconds, middle, own, moved, grads, normed, gate_other)


def middle_call(cot, slopes, hidden_rows, gates, ups, downs, down_last, normed, moves, middle, ident):
    piece, width = middle.shape
    tokens, part_width = cot.shape[0], down_last.shape[1]
    hidden = 2 * part_width
    tile = 256
    tiles = part_width // tile

    def body(place, ins, outs, scratch, under, targets):
        cot_hbm, slopes_ref, normed_ref, hidden_ref, ga1, ga2, gb1, gb2, ua1, ua2, ub1, ub2, value_ref, da1, da2, db1 = ins
        total_ref, branch_ref, grad_ref, gate_other, down_own, down_moved = outs
        load_sem, cot_ref, stage, down_other, y_sem, turned_hidden, *rest = scratch
        strip = stage.shape[1]
        under.start_y()
        loads = [
            pltpu.make_async_copy(slopes_ref, grad_ref, load_sem.at[0]),
            pltpu.make_async_copy(cot_hbm, cot_ref, load_sem.at[1]),
        ]
        for load in loads:
            load.start()
        for load in loads:
            load.wait()
        base_ref = stage.at[0]

        def hidden_load(i):
            slot = lax.rem(i, 2)
            return pltpu.make_async_copy(
                hidden_ref.at[span(i * strip, strip)], stage.at[slot, :, pl.ds(0, hidden)], load_sem.at[slot]
            )

        def turn(i, carry):
            hidden_load(i).wait()

            @pl.when(i + 1 < tokens // strip)
            def _():
                hidden_load(i + 1).start()

            value = stage[lax.rem(i, 2), :, 0:hidden].T
            for j in range(hidden // tile):
                turned_hidden[j, :, span(i * strip, strip)] = value[j * tile:(j + 1) * tile]
            return carry

        def down_half(out, which):
            half = width // 4
            each = hidden // 2 // tile

            def step(n, carry):
                m, t = n // 2, lax.rem(n, 2)
                value = dot(turned_hidden[m], cot_ref[:, span(which * 2 * half + t * half, half)], NN)
                out[m // each, span(lax.rem(m, each) * tile, tile), span(t * half, half)] = value.astype(BF)
                return carry

            lax.fori_loop(0, 2 * (hidden // tile), step, 0)

        hidden_load(0).start()
        lax.fori_loop(0, tokens // strip, turn, 0)
        down_half(down_other, 1 - place.y)
        y_down = Beyond(place, down_other, down_moved, y_sem)
        y_down.start()
        rows_in = (quarters(da1, da2), quarters(db1, targets[0]))

        def fill(owner, part):
            rows = span(owner * piece, piece)

            def step(t, carry):
                grad = None
                for weight, index in zip(rows_in[part], place.order):
                    size = weight.shape[1]
                    term = dot(cot_ref[rows, span(index * size, size)], weight[span(t * tile, tile), :], NT)
                    grad = term if grad is None else grad + term
                for offset in (0, hidden):
                    cols = span(offset + part * part_width + t * tile, tile)
                    grad_ref[rows, cols] = (grad * grad_ref[rows, cols].astype(F32)).astype(BF)
                return carry

            lax.fori_loop(0, tiles, step, 0)

        def fill_first(i, carry):
            fill(i, 0)
            return carry

        lax.fori_loop(0, tokens // piece, fill_first, 0)
        under.moves[0][1].wait_recv()
        columns = [quarters(ga1, ga2), quarters(gb1, gb2), quarters(ua1, ua2), quarters(ub1, ub2)]

        def compute(owner, out_ref):
            rows = span(owner * piece, piece)
            fill(owner, 1)
            for quarter, index in enumerate(place.order):
                total = None
                for i, weights in enumerate(columns):
                    weight = weights[quarter]
                    size = weight.shape[0]
                    term = dot(grad_ref[rows, i * part_width:(i + 1) * part_width], weight[...], NT)
                    total = term if total is None else total + term
                out_ref[:, span(index * size, size)] = total.astype(out_ref.dtype)

        def last(rows, total):
            base = base_ref[rows, :].astype(F32)
            grad = back_rows(base, value_ref[rows, :], total)
            total_ref[rows, :] = grad
            branch_ref[rows, :] = grad.astype(BF)

        turned = Turned(normed_ref, stage, load_sem, cot_ref)

        def after_z():
            down_half(down_own, place.y)
            turned.turn()
            base_load = pltpu.make_async_copy(cot_hbm.at[span(place.block * piece, piece)], base_ref, load_sem.at[0])
            base_load.start()
            turned.times(grad_ref, gate_other, (1 - place.y) * (width // 2), 0)
            base_load.wait()

        reduce_body(place, compute, last, rest, after_z=after_z, split=2)
        under.end(skip=1)
        y_down.wait_recv()
        y_down.wait_send()

    shape = functools.partial(jax.ShapeDtypeStruct, (piece, width))
    down_half_shape = jax.ShapeDtypeStruct((2, hidden // 2, width // 2), BF)
    return comm_call(
        body, "reduce_middle", ident, [cot, slopes, normed, hidden_rows, *gates, *ups, middle, *downs, down_last],
        [
            shape(F32), shape(BF), jax.ShapeDtypeStruct((tokens, 2 * hidden), BF),
            jax.ShapeDtypeStruct((2, width // 4, hidden), BF),
            down_half_shape,
            down_half_shape,
        ],
        [
            DMA((2,)), pltpu.VMEM((tokens, width), BF), pltpu.VMEM((2, piece, width), BF),
            pltpu.VMEM(down_half_shape.shape, BF), DMA((4,)),
            pltpu.VMEM((hidden // tile, tile, tokens), BF), *reduce_scratch(piece, width),
        ],
        moves, flops=6 * tokens * hidden * width,
        spaces=[ANYWHERE] * 4 + [VMEM_WHOLE] * 12,
    )


def gather_scratch():
    return [DMA((3, SLICES)), DMA((3, SLICES)), DMA((4,)), DMA((4,))]


def gather_body(place, own_ref, full, sems, process, begin=nothing, follow=nothing, split=0):
    near_send, near_recv, sib_send, sib_recv = sems
    piece = own_ref.shape[0]
    size = piece // SLICES
    c = place.c

    def near_copy(slot, r, target, turned=False):
        where = full.at[span((c * 4 + target) * piece + r * size, size)]
        device = place.along if slot == 2 or turned else place.across
        return remote(where, where, near_send.at[slot, r], near_recv.at[slot, r], device)

    def sib_copy(slot, core, target):
        where = full.at[span((core * 4 + target) * piece, piece)]
        return remote(where, where, sib_send.at[slot], sib_recv.at[slot], place.sibling)

    def slices(act):
        def step(r, carry):
            act(r)
            return carry

        lax.fori_loop(0, SLICES, step, 0)

    mine, x_chip, z_chip, d_chip = place.chip(0, 0), place.chip(0, 1), place.chip(1, 0), place.chip(1, 1)
    full[span((c * 4 + mine) * piece, piece), :] = own_ref[...]
    slices(lambda r: near_copy(2, r, mine).start())
    slices(lambda r: near_copy(1, r, mine).start())
    sib_copy(3, c, mine).start()
    begin()

    def forward(r):
        near_copy(2, r, z_chip).wait_recv()
        if r < SLICES - split:
            near_copy(0, r, z_chip).start()

    process(c * 4 + mine)
    forward(0)
    sib_copy(3, 1 - c, mine).wait_recv()
    process((1 - c) * 4 + mine)
    forward(1)

    def arrived(r):
        near_copy(1, r, x_chip).wait_recv()

    for r in range(SLICES):
        arrived(r)
        if r >= SLICES - split:
            near_copy(0, r, x_chip, True).start()
    sib_copy(1, c, x_chip).start()
    process(c * 4 + x_chip)
    for r in range(2, SLICES):
        forward(r)
    sib_copy(2, c, z_chip).start()
    sib_copy(1, 1 - c, x_chip).wait_recv()
    process((1 - c) * 4 + x_chip)
    process(c * 4 + z_chip)
    follow()
    sib_copy(2, 1 - c, z_chip).wait_recv()
    process((1 - c) * 4 + z_chip)
    slices(lambda r: near_copy(0, r, d_chip).wait_recv())
    sib_copy(0, c, d_chip).start()
    process(c * 4 + d_chip)
    sib_copy(0, 1 - c, d_chip).wait_recv()
    process((1 - c) * 4 + d_chip)
    for slot in range(3):
        slices(lambda r: near_copy(slot, r, mine).wait_send())
    for slot in range(4):
        sib_copy(slot, c, mine).wait_send()


class ColumnGather:
    def __init__(self, place, src, full, sems):
        self.place, self.src, self.full = place, src, full
        self.near_send, self.near_recv, self.sib_send, self.sib_recv, self.own = sems
        self.width = src.shape[1]
        self.size = src.shape[0] // SLICES

    def where(self, core, target):
        return span((core * 4 + target) * self.width, self.width)

    def near(self, slot, r, target, first=False):
        place = self.place
        rows = pl.ds(r * self.size, self.size)
        dst = self.full.at[rows, self.where(place.c, target)]
        src = self.src.at[rows] if first else dst
        device = place.along if slot == 2 else place.across
        return remote(src, dst, self.near_send.at[slot, r], self.near_recv.at[slot, r], device)

    def sib(self, slot, core, target, first=False):
        dst = self.full.at[:, self.where(core, target)]
        src = self.src if first else dst
        return remote(src, dst, self.sib_send.at[slot], self.sib_recv.at[slot], self.place.sibling)

    def chips(self):
        place = self.place
        return place.chip(0, 0), place.chip(0, 1), place.chip(1, 0), place.chip(1, 1)

    def own_copy(self):
        return pltpu.make_async_copy(self.src, self.full.at[:, self.where(self.place.c, self.chips()[0])], self.own.at[0])

    def start(self):
        mine = self.chips()[0]
        self.own_copy().start()
        for slot in (2, 1):
            for r in range(SLICES):
                self.near(slot, r, mine, True).start()
        self.sib(3, self.place.c, mine, True).start()

    def forward(self, r):
        z_chip = self.chips()[2]
        self.near(2, r, z_chip).wait_recv()
        self.near(0, r, z_chip).start()

    def finish(self):
        mine, x_chip, z_chip, d_chip = self.chips()
        c = self.place.c
        self.sib(2, c, z_chip).start()
        for r in range(SLICES):
            self.near(1, r, x_chip).wait_recv()
        self.sib(1, c, x_chip).start()
        for r in range(SLICES):
            self.near(0, r, d_chip).wait_recv()
        self.sib(0, c, d_chip).start()
        self.own_copy().wait()
        for slot, target in enumerate((d_chip, x_chip, z_chip, mine)):
            self.sib(slot, 1 - c, target).wait_recv()
            self.sib(slot, c, mine).wait_send()
        for slot in range(3):
            for r in range(SLICES):
                self.near(slot, r, mine).wait_send()


def attend_back_body(qkv_ref, o_ref, do_ref, lse_ref, bound, cos_ref, sin_ref, out_ref, dk_ref, dv_ref, heads, hd):
    seq = qkv_ref.shape[0]
    bq = bk = min(512, seq // 2)
    scale = hd ** -0.5
    half = hd // 2

    def unrotate(g, rows):
        cos, sin = both_halves(cos_ref, sin_ref, rows)
        return g * cos - pltpu.roll(g, half, 1) * sin

    def head(h, carry):
        base = h * 3 * hd
        own = span(h * hd, hd)
        dk_ref[...] = jnp.zeros_like(dk_ref)
        dv_ref[...] = jnp.zeros_like(dv_ref)
        for i in range(seq // bq):
            first = i * bq
            rows = pl.ds(first, bq)
            q = qkv_ref[rows, span(base, hd)]
            do = do_ref[rows, own]
            row_sums = (do.astype(F32) * o_ref[rows, own].astype(F32)).T
            delta = jnp.sum(row_sums, axis=0, keepdims=True)
            tops = lse_ref[h, 0:1, first:first + bq]
            total = max(i + 1, seq // 2 // bk)

            def step(masked, j, dq, first=first, q=q, do=do, delta=delta, tops=tops):
                keys = span(j * bk, bk)
                k = qkv_ref[keys, span(base + hd, hd)]
                v = qkv_ref[keys, span(base + 2 * hd, hd)]
                p = jnp.exp(dot(k, q, NT) * scale - tops)
                if masked:
                    kp = j * bk + lax.broadcasted_iota(jnp.int32, (bk, bq), 0)
                    qp = first + lax.broadcasted_iota(jnp.int32, (bk, bq), 1)
                    p = jnp.where(kp < jnp.maximum(qp + 1, bound), p, 0.0)
                dv_ref[keys, :] += dot(p.astype(BF), do, NN)
                ds = (p * (dot(v, do, NT) - delta)).astype(BF)
                dk_ref[keys, :] += dot(ds, q, NN)
                return dq + dot(ds, k, TN)

            dq = lax.fori_loop(0, i, functools.partial(step, False), jnp.zeros((bq, hd), F32))
            dq = lax.fori_loop(i, total, functools.partial(step, True), dq)
            out_ref[rows, span(base, hd)] = unrotate(dq * scale, rows).astype(BF)

        def fin(i, carry):
            rows = span(i * bq, bq)
            out_ref[rows, span(base + hd, hd)] = unrotate(dk_ref[rows, :] * scale, rows).astype(BF)
            out_ref[rows, span(base + 2 * hd, hd)] = dv_ref[rows, :].astype(BF)
            return carry

        return lax.fori_loop(0, seq // bq, fin, carry)

    lax.fori_loop(0, heads, head, 0)


def front_call(inputs, cot, prefix, tables, weights, heads, hd, ident):
    names = ("qkv", "out", "ga", "gb", "ua", "ub", "da", "db")
    tokens, slice_width = inputs.shape
    width = slice_width * 8
    piece = tokens // 8
    size = tokens // SLICES
    inner = weights[0].shape[1]
    part_width = weights[2].shape[1]
    hidden = 2 * part_width
    tile = 256
    bq = bk = min(512, tokens // 2)
    scale = hd ** -0.5

    def kernel(in_ref, cot_ref, prefix_ref, cos_ref, sin_ref, *refs):
        sources, refs = refs[:8], refs[8:]
        firsts, seconds, refs = refs[:8], refs[8:15], refs[15:]
        (qkv_ref, mixed_ref, lse_ref, own_in_ref, middle_ref, normed_in_out, cot_out, normed_mid_out, hidden_out,
         slopes_out), refs = refs[:10], refs[10:]
        arena, acc, block_ref, normed_own, *refs = refs
        held, refs = dict(zip(names, refs[:8])), refs[8:]
        z_sems, y_sems, store_sems, out_sems, swap_send, swap_recv, phase, *sems = refs
        start_sems, gather_sems, reduce_sems_, feed_sems = sems[:5], sems[5:10], sems[10:14], sems[14:]
        place = Place()
        c, zl, x = place.c, place.zl, place.x
        place.meet()
        z_moves = {n: WeightHalf(place, sources[i], held[n].at[0], z_sems.at[i]) for i, n in enumerate(names)}
        y_moves = {n: Beyond(place, held[n].at[0], held[n].at[1], y_sems.at[i]) for i, n in enumerate(names[:7])}

        def go(name):
            z_moves[name].start()

        def stores(name):
            i = names.index(name)
            return [
                pltpu.make_async_copy(held[name].at[side], out[i], store_sems.at[i, side])
                for side, out in enumerate((firsts, seconds[:7]))
                if i < len(out)
            ]

        def pass_on(name):
            z_moves[name].wait_recv()
            y_moves[name].start()

        def got(name):
            y_moves[name].wait_recv()
            for copy in stores(name):
                copy.start()

        def parts(name):
            return [held[name].at[side, i] for side in (0, 1) for i in (0, 1)]

        full, normed = arena.at[pl.ds(0, tokens)], arena.at[pl.ds(tokens, tokens)]
        gather = ColumnGather(place, in_ref, full, start_sems)
        crossed = jnp.logical_not(place.straight)
        partner = (place.y, 1 - c, 1 - place.zh, zl, x)
        mine, x_chip, z_chip, d_chip = gather.chips()
        def rows_of(r):
            return pl.ds(r * size, size)

        def swap_copy(r, core):
            where = full.at[rows_of(r), gather.where(core, mine)]
            return remote(in_ref.at[rows_of(r)], where, swap_send.at[r], swap_recv.at[r], partner)

        def own_copy(r):
            where = full.at[rows_of(r), gather.where(c, mine)]
            return pltpu.make_async_copy(in_ref.at[rows_of(r)], where, swap_send.at[r])

        def cot_swap():
            return remote(cot_ref, block_ref, swap_send.at[SLICES], swap_recv.at[SLICES], partner)

        def cot_own():
            return pltpu.make_async_copy(cot_ref, block_ref, swap_send.at[SLICES])

        def sib(slot, r, core, target):
            where = full.at[rows_of(r), gather.where(core, target)]
            return remote(where, where, start_sems[2].at[slot, r], start_sems[3].at[slot, r], place.sibling)

        @pl.when(place.straight)
        def _():
            for r in range(SLICES):
                own_copy(r).start()
            cot_own().start()

        @pl.when(crossed)
        def _():
            for r in range(SLICES):
                swap_copy(r, 1 - c).start()

        for r in range(SLICES):
            @pl.when(place.straight)
            def _(r=r):
                own_copy(r).wait()

            @pl.when(crossed)
            def _(r=r):
                swap_copy(r, c).wait_recv()

            gather.near(2, r, mine).start()
            gather.near(1, r, mine).start()
            sib(3, r, c, mine).start()
        for r in range(SLICES):
            gather.forward(r)
            sib(2, r, c, z_chip).start()
            gather.near(1, r, x_chip).wait_recv()
            sib(1, r, c, x_chip).start()
            if r == 0:
                go("qkv")
        pass_on("qkv")
        go("out")
        pl.when(crossed)(lambda: cot_swap().start())
        depth = held["qkv"].shape[2]
        for r in range(SLICES):
            gather.near(0, r, d_chip).wait_recv()
            sib(0, r, c, d_chip).start()
            for slot, target in enumerate((d_chip, x_chip, z_chip, mine)):
                sib(slot, r, 1 - c, target).wait_recv()

            def norm_rows(i, carry, r=r):
                rows = span(r * size + i * NORM_ROWS, NORM_ROWS)
                normed[rows, :] = row_norm(full[rows, :].astype(F32))[0].astype(BF)
                return carry

            lax.fori_loop(0, size // NORM_ROWS, norm_rows, 0, unroll=NORM_UNROLL)
            pltpu.make_async_copy(normed.at[rows_of(r)], normed_in_out.at[rows_of(r)], out_sems.at[r]).start()
            total = None
            for weight, index in zip(parts("qkv")[:2], place.order[:2]):
                term = dot(normed[rows_of(r), span(index * depth, depth)], weight[...], NN)
                total = term if total is None else total + term
            acc[rows_of(r), :] = total
        own_in_ref[...] = full[span(place.block * piece, piece), :]
        pass_on("out")

        cot_gather = ColumnGather(place, block_ref, cot_out, gather_sems)

        def forward_cot():
            for r in range(SLICES):
                cot_gather.forward(r)

        @pl.when(place.straight)
        def _():
            cot_own().wait()
            cot_gather.start()
            go("ga")

        got("qkv")
        half = size // 2

        def project(r, carry):
            rows = span(r * half, half)
            total = acc[rows, :]
            for weight, index in zip(parts("qkv")[2:], place.order[2:]):
                total = total + dot(normed[rows, span(index * depth, depth)], weight[...], NN)
            cos, sin = both_halves(cos_ref, sin_ref, rows)
            for h in range(heads):
                for part in range(3):
                    value = total[:, (3 * h + part) * hd:(3 * h + part + 1) * hd]
                    if part < 2:
                        value = value * cos + pltpu.roll(value, hd // 2, 1) * sin
                    qkv_ref[rows, pl.ds((3 * h + part) * hd, hd)] = value.astype(BF)
            return carry

        lax.fori_loop(0, tokens // half, project, 0)
        @pl.when(crossed)
        def _():
            cot_swap().wait_recv()
            cot_gather.start()
            go("ga")
            cot_swap().wait_send()
            for r in range(SLICES):
                swap_copy(r, 1 - c).wait_send()

        pl.when(place.straight)(forward_cot)

        bound = prefix_ref[0:1, 0:1]

        def head(h, carry):
            base = h * 3 * hd
            for i in range(tokens // bq):
                first = i * bq
                q = qkv_ref[first:first + bq, span(base, hd)]
                count = max(i + 1, tokens // 2 // bk)

                def step(masked, j, state, first=first, q=q):
                    top, tot, out = state
                    rows = span(j * bk, bk)
                    s = dot(q, qkv_ref[rows, span(base + hd, hd)], NT) * scale
                    if masked:
                        kp = j * bk + lax.broadcasted_iota(jnp.int32, (bq, bk), 1)
                        qp = first + lax.broadcasted_iota(jnp.int32, (bq, bk), 0)
                        s = jnp.where(kp < jnp.maximum(qp + 1, bound), s, NEG)
                    new = jnp.maximum(top, jnp.max(s, axis=1, keepdims=True))
                    alpha = jnp.exp(top - new)
                    p = jnp.exp(s - new)
                    tot = tot * alpha + jnp.sum(p, axis=1, keepdims=True)
                    out = out * alpha + dot(p.astype(BF), qkv_ref[rows, span(base + 2 * hd, hd)], NN)
                    return new, tot, out

                state = (jnp.full((bq, 1), NEG, F32), jnp.zeros((bq, 1), F32), jnp.zeros((bq, hd), F32))
                state = lax.fori_loop(0, i, functools.partial(step, False), state)
                top, tot, out = lax.fori_loop(i, count, functools.partial(step, True), state)
                mixed_ref[first:first + bq, span(h * hd, hd)] = (out / tot).astype(BF)
                lse = jnp.broadcast_to(top + jnp.log(tot), (bq, 128))
                lse_ref[h, :, first:first + bq] = lse.T[0:8, :]
            return carry

        lax.fori_loop(0, heads, head, 0)
        go("gb")
        got("out")
        pl.when(crossed)(forward_cot)
        pass_on("ga")

        for r in range(SLICES):
            pltpu.make_async_copy(normed.at[rows_of(r)], normed_in_out.at[rows_of(r)], out_sems.at[r]).wait()
            for slot in range(3):
                gather.near(slot, r, mine).wait_send()
            for slot in range(4):
                sib(slot, r, c, mine).wait_send()
        for device in (place.sibling, place.across, place.along):
            pl.semaphore_signal(phase, inc=1, device_id=device, device_id_type=MESH)
        pl.semaphore_wait(phase, 3)

        class Blocks:
            def __init__(self, first, count):
                self.first, self.shape = first, (count, piece, width)

            def rows(self, index):
                if isinstance(index, tuple):
                    step, inside, *rest = index
                    start = (self.first + step) * piece + inside.start
                    return (pl.ds(pl.multiple_of(start, 16), inside.size), *rest)
                return (span((self.first + index) * piece, piece),)

            @property
            def at(self):
                return At(self)

            def __getitem__(self, index):
                return arena[self.rows(index)]

            def __setitem__(self, index, value):
                arena[self.rows(index)] = value

        class At:
            def __init__(self, blocks):
                self.blocks = blocks

            def __getitem__(self, index):
                return arena.at[self.blocks.rows(index)]

        buffers, first = [], 0
        for count in (4, 4, 2, 3, 3):
            buffers.append(Blocks(first, count))
            first += count

        def last(rows, total):
            middle = own_in_ref[rows, :].astype(F32) + total
            middle_ref[rows, :] = middle
            normed_own[rows, :] = row_norm(middle)[0].astype(BF)

        def after_z():
            go("ua")
            go("ub")
            pass_on("gb")
            got("ga")

        reduce_body(
            place, product(place, mixed_ref, parts("out"), False), last, [*buffers, *reduce_sems_],
            after_z=after_z, split=0,
        )

        full = arena.at[pl.ds(2 * tokens, tokens)]
        slopes_ref = arena.at[pl.ds(0, tokens)]
        hidden_ref = arena.at[pl.ds(tokens, tokens), pl.ds(0, hidden)]
        columns = (("ga", "ua"), ("gb", "ub"))
        waiting = []

        def fill(owner, which):
            rows = span(owner * piece, piece)
            gates, ups = (parts(name) for name in columns[which])

            def step(t, carry):
                taken = span(t * tile, tile)
                gate = up = None
                for gate_weight, up_weight, index in zip(gates, ups, place.order):
                    deep = gate_weight.shape[0]
                    value = full[rows, span(index * deep, deep)]
                    terms = dot(value, gate_weight[:, taken], NN), dot(value, up_weight[:, taken], NN)
                    gate, up = terms if gate is None else (gate + terms[0], up + terms[1])
                cols = span(which * part_width + t * tile, tile)
                up_cols = span(hidden + which * part_width + t * tile, tile)
                sig = 1.0 / (1.0 + jnp.exp(-gate))
                active = gate * sig
                hidden_ref[rows, cols] = (active * up).astype(BF)
                slopes_ref[rows, cols] = (up * sig * (1.0 + gate * (1.0 - sig))).astype(BF)
                slopes_ref[rows, up_cols] = active.astype(BF)
                return carry

            lax.fori_loop(0, part_width // tile, step, 0)

        def process(owner):
            waiting.append(owner)
            if len(waiting) == 1:
                pass_on("ua")
                got("gb")
                got("ua")
            fill(owner, 0)
            if len(waiting) == 3:
                go("da")
                pass_on("ub")
                got("ub")
                for earlier in waiting:
                    fill(earlier, 1)
            elif len(waiting) > 3:
                if len(waiting) == 4:
                    go("db")
                fill(owner, 1)

        gather_body(place, normed_own, full, feed_sems, process)
        for i, (ref, out) in enumerate(((full, normed_mid_out), (hidden_ref, hidden_out), (slopes_ref, slopes_out))):
            pltpu.make_async_copy(ref, out, out_sems.at[SLICES + i]).start()
        pass_on("da")
        cot_gather.finish()
        z_moves["db"].wait_recv()
        stores("db")[0].start()
        got("da")
        for i, (ref, out) in enumerate(((full, normed_mid_out), (hidden_ref, hidden_out), (slopes_ref, slopes_out))):
            pltpu.make_async_copy(ref, out, out_sems.at[SLICES + i]).wait()
        for move in (*z_moves.values(), *y_moves.values()):
            move.wait_send()
        for name in names:
            for copy in stores(name):
                copy.wait()

    def half_shape(weight):
        return jax.ShapeDtypeStruct((2, *weight.shape), BF)

    shape = jax.ShapeDtypeStruct
    outs = [
        *(half_shape(weight) for weight in weights),
        *(half_shape(weight) for weight in weights[:7]),
        shape((tokens, inner), BF),
        shape((tokens, heads * hd), BF),
        shape((heads, 8, tokens), F32),
        shape((piece, width), BF),
        shape((piece, width), F32),
        shape((tokens, width), BF),
        shape((tokens, width), BF),
        shape((tokens, width), BF),
        shape((tokens, hidden), BF),
        shape((tokens, 2 * hidden), BF),
    ]
    column_sems = [DMA((3, SLICES)), DMA((3, SLICES)), DMA((4,)), DMA((4,)), DMA((1,))]
    start_sems = [DMA((3, SLICES)), DMA((3, SLICES)), DMA((4, SLICES)), DMA((4, SLICES)), DMA((1,))]
    result = pl.pallas_call(
        kernel,
        out_shape=outs,
        in_specs=[ANYWHERE, ANYWHERE, VMEM_WHOLE, VMEM_WHOLE, VMEM_WHOLE] + [ANYWHERE] * 8,
        out_specs=[ANYWHERE] * 15 + [VMEM_WHOLE] * 5 + [ANYWHERE] * 5,
        scratch_shapes=[
            pltpu.VMEM((3 * tokens, width), BF),
            pltpu.VMEM((tokens, inner), F32),
            pltpu.VMEM((tokens, slice_width), BF),
            pltpu.VMEM((piece, width), BF),
            *(pltpu.VMEM((2, 2, *weight.shape), BF) for weight in weights[:7]),
            pltpu.VMEM((1, 2, *weights[7].shape), BF),
            DMA((8, 4)), DMA((8, 4)), DMA((8, 2)), DMA((SLICES + 3,)), DMA((SLICES + 1,)), DMA((SLICES + 1,)),
            pltpu.SemaphoreType.REGULAR,
            *start_sems, *column_sems, *reduce_sems(), *gather_scratch(),
        ],
        compiler_params=pltpu.CompilerParams(collective_id=ident, has_side_effects=True, vmem_limit_bytes=63 << 20),
        cost_estimate=pl.CostEstimate(
            flops=100 << 30, bytes_accessed=100 << 20, transcendentals=heads * tokens * tokens
        ),
        name="front",
    )(inputs, cot, prefix, *tables, *weights)
    return result[:8], result[8:15], result[15:]


BLOCKS = [(core, zl, x) for core in (0, 1) for zl in (0, 1) for x in (0, 1)]


def spread_greet(place, barrier):
    for core, zl, x in BLOCKS:
        mine = jnp.logical_and(place.straight, core * 4 + zl * 2 + x == place.block)

        @pl.when(jnp.logical_not(mine))
        def _(core=core, zl=zl, x=x):
            pl.semaphore_signal(
                barrier, inc=1, device_id=(place.y, core, place.c, zl, x), device_id_type=MESH
            )

    return 8 - jnp.where(place.straight, 1, 0)


def spread_scratch():
    return [DMA((8,)), DMA((8,)), DMA((1,))]


def spread_shape(piece):
    return jax.ShapeDtypeStruct((piece.shape[0] * 8, piece.shape[1] // 8), piece.dtype)


class Spread:
    def __init__(self, place, src, dst, sems):
        self.place, self.src, self.dst = place, src, dst
        self.send, self.recv, self.own = sems
        self.piece, self.width = src.shape[0], src.shape[1] // 8

    def copy(self, f):
        place = self.place
        return remote(
            self.src.at[:, pl.ds(f * self.width, self.width)], self.dst.at[span(place.block * self.piece, self.piece)],
            self.send.at[f], self.recv.at[place.block], (place.y, place.zh, *BLOCKS[f]),
        )

    def incoming(self, f):
        core, zl, x = BLOCKS[f]
        place = self.place
        return remote(
            self.src.at[:, pl.ds(f * self.width, self.width)], self.dst.at[pl.ds(f * self.piece, self.piece)],
            self.send.at[f], self.recv.at[f], (place.y, core, place.c, zl, x),
        )

    def own_copy(self):
        block = self.place.block
        return pltpu.make_async_copy(
            self.src.at[:, span(block * self.width, self.width)], self.dst.at[span(block * self.piece, self.piece)],
            self.own.at[0],
        )

    def each(self, act):
        for f in range(8):
            mine = jnp.logical_and(self.place.straight, self.place.block == f)
            pl.when(jnp.logical_not(mine))(functools.partial(act, f))

    def start(self):
        self.each(lambda f: self.copy(f).start())
        pl.when(self.place.straight)(lambda: self.own_copy().start())

    def wait(self):
        self.each(lambda f: self.incoming(f).wait_recv())
        self.each(lambda f: self.copy(f).wait_send())
        pl.when(self.place.straight)(lambda: self.own_copy().wait())


def rear_call(branch_own, out_halves, qkv_halves, qkv, mixed, lse, prefix, tables, grad_middle, own_in, ready, normed_in,
              gate_sum, up_own, up_other, heads, hd, ident):
    tokens, inner = qkv.shape
    piece, width = branch_own.shape
    inner_out = mixed.shape[1]
    block = width // 4
    tile = 256

    def kernel(
        branch_ref, out_1, out_2, qkv_1, qkv_2, qkv_ref, mixed_ref, lse_ref, prefix_ref, cos_ref, sin_ref, middle_ref,
        own_in_ref, ready_ref, normed_in_ref, gate_ref, up_own_ref, up_other_ref,
        gate_out, up_out, out_out, qkv_out, ready_out, result_out,
        full, grad_mixed, grad_rows, flipped, dk_ref, dv_ref, up_moved, out_grads, qkv_grads,
        y_sems, z_sems, load_sem, *sems
    ):
        place = Place()
        y = place.y
        reduce_refs, sems = sems[:9], sems[9:]
        gather_sems, ready_sems, result_sems = sems[:4], sems[4:7], sems[7:10]
        place.meet(spread_greet)
        y_up = Beyond(place, up_other_ref, up_moved, y_sems.at[0])
        y_out = Beyond(place, out_grads.at[0], out_grads.at[2], y_sems.at[1])
        y_qkv = Beyond(place, qkv_grads.at[0], qkv_grads.at[2], y_sems.at[2])
        z_gate = GradHalf(place, gate_ref, gate_out, z_sems.at[0])
        z_up = GradHalf(place, up_moved, up_out, z_sems.at[1])
        z_out = GradHalf(place, out_grads.at[1], out_out, z_sems.at[2])
        z_qkv = GradHalf(place, qkv_grads.at[1], qkv_out, z_sems.at[3])
        y_up.start()

        def add(own, moved, rows):
            def step(i, carry):
                where = span(i * 64, 64)
                for j in (0, 1):
                    total = own[j, where, :].astype(F32) + moved[j, where, :].astype(F32)
                    own[j, where, :] = total.astype(BF)
                return carry

            lax.fori_loop(0, rows // 64, step, 0)

        result_ref = full.at[pl.ds(0, piece)]

        out_parts = quarters(out_1, out_2)

        def process(owner):
            rows = span(owner * piece, piece)
            total = None
            for weight, index in zip(out_parts, place.order):
                part = dot(full[rows, span(index * block, block)], weight[...], NT)
                total = part if total is None else total + part
            grad_mixed[rows, :] = total.astype(BF)

        gather_body(place, branch_ref, full, gather_sems, process, begin=z_gate.start, split=0)
        ready_spread = Spread(place, ready_ref, ready_out, ready_sems)
        y_up.wait_recv()
        add(up_moved, up_own_ref, up_own.shape[1])
        z_up.start()

        def flip(source, columns):
            def step(i, carry):
                rows = span(i * tile, tile)
                flipped[0:columns, rows] = source[rows, :].T
                return carry

            lax.fori_loop(0, tokens // tile, step, 0)

        def weigh(grads, side, which, columns):
            def step(n, carry):
                i, m = n // (columns // tile), lax.rem(n, columns // tile)
                rows = span(m * tile, tile)
                value = dot(flipped[rows, :], full[:, span((which * 2 + i) * block, block)], NN)
                grads[side, i, rows, :] = value.astype(BF)
                return carry

            lax.fori_loop(0, 2 * (columns // tile), step, 0)

        flip(mixed_ref, inner_out)
        weigh(out_grads, 0, 1 - y, inner_out)
        y_out.start()
        weigh(out_grads, 1, y, inner_out)
        load = pltpu.make_async_copy(normed_in_ref, full, load_sem.at[0])
        load.start()
        attend_back_body(
            qkv_ref, mixed_ref, grad_mixed, lse_ref, prefix_ref[0:1, 0:1], cos_ref, sin_ref, grad_rows, dk_ref, dv_ref,
            heads, hd,
        )
        load.wait()
        ready_spread.start()

        def last(rows, total):
            value = back_rows(middle_ref[rows, :], own_in_ref[rows, :].astype(F32), total)
            result_ref[rows, :] = value.astype(BF)

        def after_z():
            flip(grad_rows, inner)
            weigh(qkv_grads, 0, 1 - y, inner)
            y_qkv.start()
            y_out.wait_recv()
            add(out_grads.at[1], out_grads.at[2], inner_out)
            z_out.start()
            weigh(qkv_grads, 1, y, inner)

        reduce_body(
            place, product(place, grad_rows, quarters(qkv_1, qkv_2), True), last, reduce_refs,
            after_z=after_z, split=0,
        )
        result_spread = Spread(place, result_ref, result_out, result_sems)
        result_spread.start()
        y_qkv.wait_recv()
        add(qkv_grads.at[1], qkv_grads.at[2], inner)
        z_qkv.start()
        for move in (z_gate, z_up, z_out, z_qkv):
            move.wait_recv()
        ready_spread.wait()
        result_spread.wait()
        for move in (y_up, y_out, y_qkv, z_gate, z_up, z_out, z_qkv):
            move.wait_send()

    shape = jax.ShapeDtypeStruct
    spread = spread_shape(ready)
    return pl.pallas_call(
        kernel,
        out_shape=[
            shape(gate_sum.shape, BF), shape(up_own.shape, BF), shape((2, inner_out, block), BF),
            shape((2, inner, block), BF), spread, spread,
        ],
        in_specs=[VMEM_WHOLE] * 14 + [ANYWHERE, ANYWHERE, VMEM_WHOLE, ANYWHERE],
        out_specs=[ANYWHERE] * 6,
        scratch_shapes=[
            pltpu.VMEM((tokens, width), BF),
            pltpu.VMEM((tokens, inner_out), BF),
            pltpu.VMEM((tokens, inner), BF),
            pltpu.VMEM((inner, tokens), BF),
            pltpu.VMEM((tokens, hd), F32),
            pltpu.VMEM((tokens, hd), F32),
            pltpu.VMEM(up_own.shape, BF),
            pltpu.VMEM((3, 2, inner_out, block), BF),
            pltpu.VMEM((3, 2, inner, block), BF),
            DMA((3, 4)), DMA((4, 4)), DMA((1,)),
            *reduce_scratch(piece, width), *gather_scratch(), *spread_scratch(), *spread_scratch(),
        ],
        compiler_params=pltpu.CompilerParams(
            collective_id=ident, has_side_effects=True, vmem_limit_bytes=(64 << 20) - (64 << 10)
        ),
        cost_estimate=pl.CostEstimate(flops=100 << 30, bytes_accessed=100 << 20, transcendentals=heads * tokens * tokens),
        name="rear",
    )(
        branch_own, *out_halves, *qkv_halves, qkv, mixed, lse, prefix, *tables, grad_middle, own_in, ready, normed_in,
        gate_sum, up_own, up_other,
    )


def local_fine(inputs, prefix_len, w_qkv, w_out, w_up_gate, w_down, cotangent):
    heads, hd = w_qkv.shape[1], w_qkv.shape[2] // 3
    hidden_width = w_down.shape[0]
    tokens = inputs.shape[0]
    y = lax.axis_index("y")
    prefix_len = lax.ppermute(prefix_len, ("core", "zh"), [(0, 0), (1, 2), (2, 1), (3, 3)])
    prefix = jnp.broadcast_to(prefix_len[:, None], (8, 128))
    tables = rope_tables(tokens, hd)
    part = hidden_width // 2
    ga, gb = w_up_gate[:, 0, :part], w_up_gate[:, 0, part:]
    ua, ub = w_up_gate[:, 1, :part], w_up_gate[:, 1, part:]
    da, db = w_down[:part], w_down[part:]

    weights = (w_qkv.reshape(w_qkv.shape[0], -1), w_out, ga, gb, ua, ub, da, db)
    firsts, seconds, results = front_call(inputs, cotangent, prefix, tables, weights, heads, hd, 1)
    qkv_1, out_1, ga_1, gb_1, ua_1, ub_1, da_1, db_1 = firsts
    qkv_2, out_2, ga_2, gb_2, ua_2, ub_2, da_2 = seconds
    qkv, mixed, lse, own_in, middle, normed_in, cot_full, normed_mid, hidden, slopes = results
    gates = (ga_1, ga_2, gb_1, gb_2)

    (grad_middle, branch_own, grad_gate_up, gate_other, down_own, down_moved), (db_2,) = middle_call(
        cot_full, slopes, hidden, gates, (ua_1, ua_2, ub_1, ub_2), (da_1, da_2), db_1, normed_mid,
        [("beyond", db_1)], middle, 5,
    )
    outputs, down_final, gate_sum, up_own, up_other = down_call(
        hidden, (da_1, db_1), (da_2, db_2), middle, down_own, down_moved, normed_mid, grad_gate_up, gate_other, 6
    )
    gate_final, up_final, out_final, qkv_final, outputs, input_grad = rear_call(
        branch_own, (out_1, out_2), (qkv_1, qkv_2), qkv, mixed, lse, prefix, tables, grad_middle, own_in, outputs,
        normed_in, gate_sum, up_own, up_other, heads, hd, 7,
    )

    def summed(parts):
        return parts[0].astype(F32) + parts[1].astype(F32)

    return (
        outputs,
        input_grad.astype(F32),
        summed(qkv_final).T.reshape(-1, heads, 3 * hd),
        summed(out_final),
        jnp.stack([summed(gate_final), summed(up_final)], axis=1),
        summed(down_final),
    )


def solution(mesh):
    row_size, col_size = mesh.shape["row"], mesh.shape["col"]
    fine = (row_size, col_size) == (4, 8)
    if fine:
        names, shape, body = AXES, (2,) * 5, local_fine
        row, col = AXES[:2], AXES[2:]
    else:
        names = ("rmaj", "core", "cmaj", "cmin")
        shape = (row_size // 2, 2, 4, col_size // 4)
        body = functools.partial(local, shape[3] == 2)
        row, col = names[:2], names[2:]
    outs = (P(row, col), P(row, col), P(row, col, None), P(col, row), P(row, None, col), P(col, row))
    return jax.shard_map(
        body,
        mesh=Mesh(mesh.devices.reshape(shape), names),
        in_specs=(P(row, col), P(row), P(row, col, None), P(col, row), P(row, None, col), P(col, row), P(row, col)),
        out_specs=outs,
        check_vma=False,
    )
```
